32 devices in a mesh: dp: 16 (over z, x, core), seq: 2 (over y).
Axes of the slice: x: 2, y: 2, z: 4, core: 2. Of those that a mesh axis runs over, the one named last changes fastest.
Arguments:
- gene_ids: int32 [16, 2048], P('dp', 'seq'), may hold values from 0 to 9215, as said below
- homolog_ids: int32 [16, 2048], P('dp', 'seq'), may hold values from 0 to 9215, as said below
- knowledge_ids: int32 [16, 2048], P('dp', 'seq'), may hold values from 0 to 9215, as said below
- expr_bins: int32 [16, 2048], P('dp', 'seq'), may hold values from 0 to 127
- species: int32 [16], P('dp'), may hold values from 0 to 1, as said below
- cell_lengths: int32 [16], P('dp'), may hold values from 1025 to 2048, as said below
- gene_table: bfloat16 [9216, 768], P(('dp', 'seq')), may hold values from -4.1875 to 4.1875
- knowledge_tables: bfloat16 [4, 9216, 768], P(None, ('dp', 'seq')), may hold values from -2.09375 to 2.09375
- expr_table: bfloat16 [128, 768], replicated, may hold values from -4.1875 to 4.1875
- w_query: bfloat16 [768, 768], replicated, may hold values from -0.21875 to 0.21875
- b_query: float32 [768], replicated, may hold values from -1.8 to 1.8
- w_key: bfloat16 [768, 768], replicated, may hold values from -0.21875 to 0.21875
- w_value: bfloat16 [768, 768], replicated, may hold values from -0.21875 to 0.21875
- b_value: float32 [768], replicated, may hold values from -1.8 to 1.8
- w_out: bfloat16 [768, 768], replicated, may hold values from -2.5 to 2.5
- b_out: float32 [768], replicated, may hold values from -1.8 to 1.8
- gain_one: float32 [768], replicated, may hold values from 0.1 to 1.9
- shift_one: float32 [768], replicated, may hold values from -1.8 to 1.8
- w_up: bfloat16 [768, 3072], replicated, may hold values from -0.21875 to 0.21875
- b_up: float32 [3072], replicated, may hold values from -1.8 to 1.8
- w_down: bfloat16 [3072, 768], replicated, may hold values from -0.109375 to 0.109375
- b_down: float32 [768], replicated, may hold values from -1.8 to 1.8
- gain_two: float32 [768], replicated, may hold values from 0.1 to 1.9
- shift_two: float32 [768], replicated, may hold values from -1.8 to 1.8
- cotangent: bfloat16 [16, 2048, 768], P('dp', 'seq'), may hold values from -6 to 6
Outputs:
- layer_output: bfloat16 [16, 2048, 768], P('dp', 'seq')
- gene_table_grad: float32 [9216, 768], P(('dp', 'seq'))
- knowledge_grad: float32 [9216, 768], P(('dp', 'seq'))
- expr_table_grad: float32 [128, 768], replicated
- w_query_grad: float32 [768, 768], replicated
- b_query_grad: float32 [768], replicated
- w_key_grad: float32 [768, 768], replicated
- w_value_grad: float32 [768, 768], replicated
- b_value_grad: float32 [768], replicated
- w_out_grad: float32 [768, 768], replicated
- b_out_grad: float32 [768], replicated
- gain_one_grad: float32 [768], replicated
- shift_one_grad: float32 [768], replicated
- w_up_grad: float32 [768, 3072], replicated
- b_up_grad: float32 [3072], replicated
- w_down_grad: float32 [3072, 768], replicated
- b_down_grad: float32 [768], replicated
- gain_two_grad: float32 [768], replicated
- shift_two_grad: float32 [768], replicated
- row_counts: int32 [2, 9216], P(None, ('dp', 'seq'))
The draws below stay inside these ranges and needn't reach their ends.
Inputs may be any that keep to these rules, and one draw needn't show every extreme that they name: Of the 1024 genes that one device holds (the cells of its dp index, the positions of its seq index), at most 64 have an id in one block of 288 rows (ids r * 288 to (r + 1) * 288 - 1); in every draw one block has exactly 64 from every device. A gene's gene_ids and homolog_ids lie in the same block. `homolog_ids`: as gene_ids: at most 64 of one device's genes in one block of 288 rows, one block reaching 64 from every device, and the same block as gene_ids for every gene. `knowledge_ids`: at most 64 of one device's genes in one block of 288 rows; in every draw one block has exactly 64 from every device. `species`: exactly a quarter of the cells, rounded down and at least one, have 1. `cell_lengths`: one cell has 2048 and one has 1025.
All inputs are finite; a program needn't handle non-finite values.
Results may differ from the reference program's by a relative error of at most 0.015.
The reference program's roundings to bfloat16 on the way count: a program that leaves them out, or rounds other values in their place, can miss the bound.
Values may be sent and summed in bfloat16 or wider, within the bound.
No kernel may reach another device: no remote copies, remote signals or barrier semaphores. Data moves between devices by JAX's collectives and lax.ppermute only.
A program may use at most 192 MiB of HBM per device.

```python
import jax
import jax.numpy as jnp
from jax import lax

D = 768
HEADS = 12
HEAD_DIM = 64
FF = 3072
LEN = 2048
CELLS_DEV = 1
ROWS_DEV = 288
BINS = 128
CELLS = 16
HALF = 1024
LOOK = 1024
CAP = 64
VOCAB = 9216
N_DP = 16
N_SEQ = 2
DEVICES = 32


def owner_layout(key):
    heavy_owner = jax.random.randint(jax.random.fold_in(key, 1), (), 0, DEVICES)

    def one_device(device):
        device_key = jax.random.fold_in(key, device + 2)
        spread = jax.random.permutation(device_key, DEVICES * CAP - CAP)[:LOOK - CAP]
        others = (spread // CAP).astype(jnp.int32)
        others = others + (others >= heavy_owner).astype(jnp.int32)
        joined = jnp.concatenate([jnp.full((CAP,), heavy_owner, jnp.int32), others])
        return jax.random.permutation(jax.random.fold_in(device_key, 7), joined)
    layout = jax.vmap(one_device)(jnp.arange(DEVICES))
    layout = layout.reshape(N_DP, N_SEQ, CELLS_DEV, HALF).transpose(0, 2, 1, 3)
    return layout.reshape(CELLS, LEN).astype(jnp.int32)


def draw_gene_ids(key, part):
    blocks = owner_layout(jax.random.fold_in(key, 11))
    within = jax.random.randint(jax.random.fold_in(key, 12), (CELLS, LEN), 0, ROWS_DEV)
    return (blocks * ROWS_DEV + within).astype(jnp.int32)


def draw_homolog_ids(key, part):
    blocks = owner_layout(jax.random.fold_in(key, 11))
    within = jax.random.randint(jax.random.fold_in(key, 13), (CELLS, LEN), 0, ROWS_DEV)
    return (blocks * ROWS_DEV + within).astype(jnp.int32)


def draw_knowledge_ids(key, part):
    blocks = owner_layout(jax.random.fold_in(key, 21))
    within = jax.random.randint(jax.random.fold_in(key, 22), (CELLS, LEN), 0, ROWS_DEV)
    return (blocks * ROWS_DEV + within).astype(jnp.int32)


def draw_species(key, part):
    order = jax.random.permutation(jax.random.fold_in(key, 31), CELLS)
    return (order < max(1, CELLS // 4)).astype(jnp.int32)


def draw_cell_lengths(key, part):
    drawn = jax.random.randint(jax.random.fold_in(key, 41), (CELLS,), HALF + 1, LEN + 1)
    order = jax.random.permutation(jax.random.fold_in(key, 42), CELLS)
    drawn = jnp.where(order == 0, LEN, drawn)
    drawn = jnp.where(order == 1, HALF + 1, drawn)
    return drawn.astype(jnp.int32)


def touch_ends(entries, own_key, least, largest):
    spot = [jax.random.randint(jax.random.fold_in(own_key, axis), (), 0, length) for axis, length in enumerate(entries.shape)]
    widest = entries.shape.index(max(entries.shape))
    next_to = spot[:widest] + [(spot[widest] + 1) % entries.shape[widest]] + spot[widest + 1:]
    return entries.at[tuple(spot)].set(least).at[tuple(next_to)].set(largest)


def shard_levels(key, shape, pieces, low, top_value):
    level = 1.0
    for axis_at, shards_of in pieces:
        heights = jax.random.uniform(jax.random.fold_in(jax.random.fold_in(key, 6), axis_at), (shards_of,), jnp.float32, low / len(pieces), top_value / len(pieces))
        level = level * jnp.repeat(jnp.exp(heights), shape[axis_at] // shards_of).reshape((-1,) + (1,) * (len(shape) - 1 - axis_at))
    return level


def normal_values(key, dims, scale, reach, shards=(), dtype=jnp.bfloat16):
    values = jax.random.normal(key, dims, jnp.float32) * scale
    if len(shards) > 0:
        values = shard_levels(key, dims, shards, -0.22, 0.18) * values
    return jnp.clip(values, min=-reach, max=reach).astype(dtype)


def setup_inputs(seed: int = 0) -> dict:
    splits = jax.random.split(jax.random.key(seed), 26)
    return {
        "gene_ids": draw_gene_ids(jax.random.fold_in(splits[25], 71), 0),
        "homolog_ids": draw_homolog_ids(jax.random.fold_in(splits[25], 71), 0),
        "knowledge_ids": draw_knowledge_ids(jax.random.fold_in(splits[25], 71), 0),
        "expr_bins": touch_ends(jax.random.randint(splits[3], (CELLS, LEN), 0, BINS), jax.random.fold_in(splits[3], 1), 0, BINS - 1).astype(jnp.int32),
        "species": draw_species(jax.random.fold_in(splits[25], 71), 0),
        "cell_lengths": draw_cell_lengths(jax.random.fold_in(splits[25], 71), 0),
        "gene_table": normal_values(splits[6], (VOCAB, D), 0.7, 4.1875, ((0, 32),)),
        "knowledge_tables": normal_values(splits[7], (4, VOCAB, D), 0.35, 2.09375, ((1, 32),)),
        "expr_table": normal_values(splits[8], (BINS, D), 0.7, 4.1875),
        "w_query": normal_values(splits[9], (D, D), D ** -0.5, 0.21875),
        "b_query": normal_values(splits[10], (D,), 0.3, 1.8, (), jnp.float32),
        "w_key": normal_values(splits[11], (D, D), D ** -0.5, 0.21875),
        "w_value": normal_values(splits[12], (D, D), D ** -0.5, 0.21875),
        "b_value": normal_values(splits[13], (D,), 0.3, 1.8, (), jnp.float32),
        "w_out": normal_values(splits[14], (D, D), (max(D // 128, 1)) ** -0.5, 2.5),
        "b_out": normal_values(splits[15], (D,), 0.3, 1.8, (), jnp.float32),
        "gain_one": jnp.clip(1.0 + 0.18 * jax.random.normal(splits[16], (D,), jnp.float32), 0.1, 1.9),
        "shift_one": normal_values(splits[17], (D,), 0.3, 1.8, (), jnp.float32),
        "w_up": normal_values(splits[18], (D, FF), D ** -0.5, 0.21875),
        "b_up": normal_values(splits[19], (FF,), 0.3, 1.8, (), jnp.float32),
        "w_down": normal_values(splits[20], (FF, D), FF ** -0.5, 0.109375),
        "b_down": normal_values(splits[21], (D,), 0.3, 1.8, (), jnp.float32),
        "gain_two": jnp.clip(1.0 + 0.18 * jax.random.normal(splits[22], (D,), jnp.float32), 0.1, 1.9),
        "shift_two": normal_values(splits[23], (D,), 0.3, 1.8, (), jnp.float32),
        "cotangent": normal_values(splits[24], (CELLS, LEN, D), 1.0, 6.0, ((0, 16), (1, 2))),
    }


@jax.custom_vjp
def low(v):
    return lax.optimization_barrier(v.astype(jnp.bfloat16)).astype(jnp.float32)

@jax.custom_vjp
def low_back(v):
    return v

def low_keep(v):
    return (low(v), None)

def low_pass(kept, grad):
    return (grad,)

def back_keep(v):
    return (v, None)

def back_low(kept, grad):
    return (low(grad),)
low.defvjp(low_keep, low_pass)
low_back.defvjp(back_keep, back_low)

def layer_norm(value, gain_vec, shift_vec):
    centre = lax.optimization_barrier(jnp.mean(value, axis=-1, keepdims=True))
    centred = value - centre
    variance = lax.optimization_barrier(jnp.mean(centred * centred, axis=-1, keepdims=True))
    return centred * lax.rsqrt(variance + 1e-05) * gain_vec + shift_vec

def matmul(left, right):
    return jnp.dot(left, right, precision=lax.Precision.HIGHEST)

def gelu_exact(value):
    return jax.nn.gelu(value, approximate=False)

def cell_layer(params, cell_ids, cell_know, cell_bins, cell_count):
    gene_table, knowledge_tables, expr_table, w_query, b_query, w_key, w_value, b_value, w_out, b_out, gain_one, shift_one, w_up, b_up, w_down, b_down, gain_two, shift_two = params
    knowledge_term = low(knowledge_tables[0][cell_know] + knowledge_tables[1][cell_know] + knowledge_tables[2][cell_know] + knowledge_tables[3][cell_know])
    embedded = gene_table[cell_ids] + knowledge_term + expr_table[cell_bins]
    x_low = low(embedded)
    query_all = low(low_back(matmul(x_low, w_query) + b_query)).reshape(LEN, HEADS, HEAD_DIM)
    key_all = low(low_back(matmul(x_low, w_key))).reshape(LEN, HEADS, HEAD_DIM)
    value_all = low(low_back(matmul(x_low, w_value) + b_value)).reshape(LEN, HEADS, HEAD_DIM)
    raw_scores = low_back(jnp.einsum('qhd,khd->hqk', query_all, key_all, precision=lax.Precision.HIGHEST))
    scores = raw_scores * HEAD_DIM ** (-0.5)
    valid_keys = jnp.arange(LEN) < cell_count
    scores = jnp.where(valid_keys[None, None, :], scores, -1e+30)
    log_total = jax.nn.logsumexp(scores, axis=-1, keepdims=True)
    attn_probs = jnp.exp(scores - log_total)
    context = jnp.einsum('hqk,khd->qhd', low(attn_probs), value_all, precision=lax.Precision.HIGHEST)
    context_low = low(low_back(context.reshape(LEN, D)))
    attn_out = low_back(matmul(context_low, w_out) + b_out)
    normed_one = layer_norm(embedded + attn_out, gain_one, shift_one)
    normed_low = low(normed_one)
    pre_ffn = low_back(matmul(normed_low, w_up) + b_up)
    activated = low(gelu_exact(pre_ffn))
    ffn_out = low_back(matmul(activated, w_down) + b_down)
    return layer_norm(normed_one + ffn_out, gain_two, shift_two)

def reference(gene_ids, homolog_ids, knowledge_ids, expr_bins, species, cell_lengths, gene_table, knowledge_tables, expr_table, w_query, b_query, w_key, w_value, b_value, w_out, b_out, gain_one, shift_one, w_up, b_up, w_down, b_down, gain_two, shift_two, cotangent):
    chosen_ids = jnp.where(species[:, None] == 1, homolog_ids, gene_ids)
    float_args = tuple((item.astype(jnp.float32) for item in (gene_table, knowledge_tables, expr_table, w_query, b_query, w_key, w_value, b_value, w_out, b_out, gain_one, shift_one, w_up, b_up, w_down, b_down, gain_two, shift_two)))

    def forward(*params):

        def cell_step(carried, cell_data):
            cell_ids, cell_know, cell_bins, cell_count = cell_data
            return (carried, cell_layer(params, cell_ids, cell_know, cell_bins, cell_count))
        unused, outputs = lax.scan(jax.checkpoint(cell_step), 0, (chosen_ids, knowledge_ids, expr_bins, cell_lengths))
        return outputs
    final, pullback = jax.vjp(forward, *float_args)
    gradients = pullback(cotangent.astype(jnp.float32))
    row_counts = jnp.zeros((2, VOCAB), jnp.int32)
    row_counts = row_counts.at[0, chosen_ids.reshape(-1)].add(1)
    row_counts = row_counts.at[1, knowledge_ids.reshape(-1)].add(1)
    return (final.astype(jnp.bfloat16), gradients[0], gradients[1][0], gradients[2], gradients[3], gradients[4], gradients[5], gradients[6], gradients[7], gradients[8], gradients[9], gradients[10], gradients[11], gradients[12], gradients[13], gradients[14], gradients[15], gradients[16], gradients[17], row_counts)
```

```python
import functools

import jax
import jax.numpy as jnp
from jax import lax
from jax.experimental import pallas as pl
from jax.experimental.pallas import tpu as pltpu
from jax.sharding import PartitionSpec as P

HEADS = 12
HEAD_DIM = 64
PAIR = 2 * HEAD_DIM
CHUNK = 256
EVERY = ("dp", "seq")
F32 = jnp.float32
BF16 = jnp.bfloat16
NN = (((1,), (0,)), ((), ()))
NT = (((1,), (1,)), ((), ()))
TN = (((0,), (0,)), ((), ()))


def mm(left, right, dims=NN):
    return lax.dot_general(left, right, dims, preferred_element_type=F32)


def params(mib):
    return pltpu.CompilerParams(vmem_limit_bytes=mib * 2**20)


def route_kernel(rows_dev, capacity, gene_ref, know_ref, req_ref, gene_slot_ref, know_slot_ref):
    tokens = gene_ref.shape[0]
    devices, slots_all = req_ref.shape
    lane = lax.broadcasted_iota(jnp.int32, (tokens, devices), 1)
    earlier = (
        lax.broadcasted_iota(jnp.int32, (tokens, tokens), 0)
        > lax.broadcasted_iota(jnp.int32, (tokens, tokens), 1)
    ).astype(F32).astype(BF16)
    rank_lane = lax.broadcasted_iota(jnp.int32, (tokens, capacity), 1)
    asked = []
    for which, (ids_ref, slot_ref) in enumerate(((gene_ref, gene_slot_ref), (know_ref, know_slot_ref))):
        row = ids_ref[...] - lane * rows_dev
        hit = (row >= 0) & (row < rows_dev)
        before = mm(earlier, hit.astype(F32).astype(BF16))
        rank = jnp.sum(jnp.where(hit, before, 0.0), axis=1, keepdims=True)
        owner = jnp.sum(jnp.where(hit, lane, 0).astype(F32), axis=1, keepdims=True)
        slot_ref[...] = (owner * slots_all + rank).astype(jnp.int32) + which * capacity
        rank_hit = (rank_lane == rank.astype(jnp.int32)).astype(F32).astype(BF16)
        coded = jnp.where(hit, row + 1, 0)
        high = (coded >> 4).astype(F32).astype(BF16)
        low = (coded & 15).astype(F32).astype(BF16)
        wanted = (mm(high, rank_hit, TN) * 16.0 + mm(low, rank_hit, TN)).astype(jnp.int32)
        asked.append(jnp.where(wanted > 0, wanted - 1 + which * rows_dev, -1))
    req_ref[:, :capacity] = asked[0]
    req_ref[:, capacity:] = asked[1]


def route(gene_ids, know_ids, rows_dev, capacity, devices):
    tokens = gene_ids.shape[0]
    return pl.pallas_call(
        functools.partial(route_kernel, rows_dev, capacity),
        out_shape=(
            jax.ShapeDtypeStruct((devices, 2 * capacity), jnp.int32),
            jax.ShapeDtypeStruct((tokens, 1), jnp.int32),
            jax.ShapeDtypeStruct((tokens, 1), jnp.int32),
        ),
        compiler_params=params(32),
        name="route",
    )(gene_ids[:, None], know_ids[:, None])


def head_mask(rows, head):
    lanes = lax.broadcasted_iota(jnp.int32, (rows, PAIR), 1)
    return (lanes >= head * HEAD_DIM) & (lanes < (head + 1) * HEAD_DIM)


def masked_scores(scores, first_key, count):
    at = lax.broadcasted_iota(jnp.int32, scores.shape, 0) + first_key
    return jnp.where(at < count, scores, -1e30)


def fold_rows(value, how):
    return how(value.reshape(value.shape[0] // 8, 8, value.shape[1]), axis=0)


def attend_kernel(
    where_ref, q_ref, ka_ref, kb_ref, va_ref, vb_ref, out_ref, lse_ref, vt_ref, score_ref
):
    half = ka_ref.shape[0]
    chunks = half // CHUNK
    vt_ref[:, :half] = va_ref[...].T
    vt_ref[:, half:] = vb_ref[...].T

    def block(at, carry):
        rows = pl.ds(pl.multiple_of(at * CHUNK, CHUNK), CHUNK)
        query = q_ref[rows, :]
        outs = []
        for head in range(2):
            q_head = jnp.where(head_mask(CHUNK, head), query, jnp.zeros_like(query))
            top = None
            for c in range(2 * chunks):
                part, inner = divmod(c, chunks)
                key = (ka_ref, kb_ref)[part][inner * CHUNK : (inner + 1) * CHUNK, :]
                scores = masked_scores(
                    mm(key, q_head, NT), where_ref[part] + inner * CHUNK, where_ref[2]
                )
                score_ref[head, c * CHUNK : (c + 1) * CHUNK, :] = scores
                high = fold_rows(scores, jnp.max)
                top = high if top is None else jnp.maximum(top, high)
            top = jnp.max(top, axis=0, keepdims=True)
            total = None
            acc = None
            for c in range(2 * chunks):
                probs = jnp.exp(score_ref[head, c * CHUNK : (c + 1) * CHUNK, :] - top)
                part_sum = fold_rows(probs, jnp.sum)
                total = part_sum if total is None else total + part_sum
                part_out = mm(
                    vt_ref[head * HEAD_DIM : (head + 1) * HEAD_DIM, c * CHUNK : (c + 1) * CHUNK],
                    probs.astype(BF16),
                )
                acc = part_out if acc is None else acc + part_out
            total = jnp.sum(total, axis=0, keepdims=True)
            outs.append(acc / total)
            lse_ref[0, head : head + 1, rows] = top + jnp.log(total)
        out_ref[rows, :] = jnp.concatenate(outs, axis=0).T
        return carry

    lax.fori_loop(0, q_ref.shape[0] // CHUNK, block, 0)


def attend(where, query, key_a, key_b, value_a, value_b):
    tokens, width = query.shape
    half = key_a.shape[0]
    pairs = width // PAIR
    column = lambda rows: pl.BlockSpec((rows, PAIR), lambda p, w: (0, p))
    return pl.pallas_call(
        attend_kernel,
        grid_spec=pltpu.PrefetchScalarGridSpec(
            num_scalar_prefetch=1,
            grid=(pairs,),
            in_specs=[column(tokens)] + [column(half)] * 4,
            out_specs=[column(tokens), pl.BlockSpec((1, 2, tokens), lambda p, w: (p, 0, 0))],
            scratch_shapes=[
                pltpu.VMEM((PAIR, 2 * half), BF16),
                pltpu.VMEM((2, 2 * half, CHUNK), F32),
            ],
        ),
        out_shape=(
            jax.ShapeDtypeStruct((tokens, width), F32),
            jax.ShapeDtypeStruct((pairs, 2, tokens), F32),
        ),
        compiler_params=params(48),
        name="attend",
    )(where, query, key_a, key_b, value_a, value_b)


def attend_back_kernel(
    where_ref, q_ref, g_ref, o_ref, lse_ref, k_ref, v_ref, *rest
):
    if len(rest) == 7:
        dq_in_ref, dq_ref, dk_ref, dv_ref, kt_ref, dk_acc, dv_acc = rest
    else:
        dq_in_ref = None
        dq_ref, dk_ref, dv_ref, kt_ref, dk_acc, dv_acc = rest
    keys = k_ref.shape[0]
    kt_ref[...] = k_ref[...].T
    dk_acc[...] = jnp.zeros_like(dk_acc)
    dv_acc[...] = jnp.zeros_like(dv_acc)
    picks = (
        lax.broadcasted_iota(jnp.int32, (8, PAIR), 1) // HEAD_DIM
        == lax.broadcasted_iota(jnp.int32, (8, PAIR), 0)
    ).astype(F32)

    def block(at, carry):
        rows = pl.ds(pl.multiple_of(at * CHUNK, CHUNK), CHUNK)
        query = q_ref[rows, :]
        grad = g_ref[rows, :]
        inner = lax.dot_general(
            picks,
            grad.astype(F32) * o_ref[rows, :],
            NT,
            precision=lax.Precision.HIGHEST,
            preferred_element_type=F32,
        )
        masks = [head_mask(CHUNK, head) for head in range(2)]
        q_heads = [jnp.where(m, query, jnp.zeros_like(query)) for m in masks]
        g_heads = [jnp.where(m, grad, jnp.zeros_like(grad)) for m in masks]
        dqs = [None, None]
        for c in range(keys // CHUNK):
            span = slice(c * CHUNK, (c + 1) * CHUNK)
            key = k_ref[span, :]
            value = v_ref[span, :]
            dk = None
            dv = None
            for head in range(2):
                scores = masked_scores(
                    mm(key, q_heads[head], NT), where_ref[0] + c * CHUNK, where_ref[1]
                )
                probs = jnp.exp(scores - lse_ref[0, head : head + 1, rows])
                grad_probs = mm(value, g_heads[head], NT)
                grad_scores = (probs * (grad_probs - inner[head : head + 1, :])).astype(BF16)
                dv_head = mm(probs.astype(BF16), g_heads[head])
                dk_head = mm(grad_scores, q_heads[head])
                dv = dv_head if dv is None else dv + dv_head
                dk = dk_head if dk is None else dk + dk_head
                dq = mm(kt_ref[head * HEAD_DIM : (head + 1) * HEAD_DIM, span], grad_scores)
                dqs[head] = dq if dqs[head] is None else dqs[head] + dq
            dk_acc[span, :] += dk
            dv_acc[span, :] += dv
        dq = jnp.concatenate(dqs, axis=0).T * HEAD_DIM ** (-0.5)
        if dq_in_ref is not None:
            dq = dq + dq_in_ref[rows, :]
        dq_ref[rows, :] = dq.astype(dq_ref.dtype)
        return carry

    lax.fori_loop(0, q_ref.shape[0] // CHUNK, block, 0)
    dk_ref[...] = dk_acc[...].astype(BF16)
    dv_ref[...] = dv_acc[...].astype(BF16)


def attend_back(where, query, grad, out, lse, key, value, dq_in=None):
    tokens, width = query.shape
    keys = key.shape[0]
    pairs = width // PAIR
    column = lambda rows: pl.BlockSpec((rows, PAIR), lambda p, w: (0, p))
    more = [] if dq_in is None else [dq_in]
    return pl.pallas_call(
        attend_back_kernel,
        grid_spec=pltpu.PrefetchScalarGridSpec(
            num_scalar_prefetch=1,
            grid=(pairs,),
            in_specs=[column(tokens)] * 3
            + [pl.BlockSpec((1, 2, tokens), lambda p, w: (p, 0, 0))]
            + [column(keys)] * 2
            + [column(tokens)] * len(more),
            out_specs=[column(tokens), column(keys), column(keys)],
            scratch_shapes=[
                pltpu.VMEM((PAIR, keys), BF16),
                pltpu.VMEM((keys, PAIR), F32),
                pltpu.VMEM((keys, PAIR), F32),
            ],
        ),
        out_shape=(
            jax.ShapeDtypeStruct((tokens, width), F32 if dq_in is None else BF16),
            jax.ShapeDtypeStruct((keys, width), BF16),
            jax.ShapeDtypeStruct((keys, width), BF16),
        ),
        compiler_params=params(48),
        name="attend_back" if dq_in is None else "attend_back_last",
    )(where, query, grad, out, lse, key, value, *more)


def norm_parts(value):
    centre = jnp.mean(value, axis=-1, keepdims=True)
    centred = value - centre
    variance = jnp.mean(centred * centred, axis=-1, keepdims=True)
    inverse = lax.rsqrt(variance + 1e-05)
    return centred * inverse, inverse


def norm_back(grad, unit, inverse, gain):
    grad_unit = grad * gain
    return inverse * (
        grad_unit
        - jnp.mean(grad_unit, axis=-1, keepdims=True)
        - unit * jnp.mean(grad_unit * unit, axis=-1, keepdims=True)
    )


def middle_kernel(
    ctx_ref,
    emb_ref,
    cot_ref,
    w_out_ref,
    w_up_ref,
    w_down_ref,
    small_ref,
    b_up_ref,
    out_ref,
    ctx_low_ref,
    normed_ref,
    act_ref,
    gffn_ref,
    gpre_ref,
    gattn_ref,
    gone_ref,
    gctx_ref,
    sums_ref,
    up_sums_ref,
    slope_ref,
):
    step = pl.program_id(0)
    width = emb_ref.shape[1]
    wide = w_up_ref.shape[1]

    @pl.when(step == 0)
    def _():
        sums_ref[...] = jnp.zeros_like(sums_ref)
        up_sums_ref[...] = jnp.zeros_like(up_sums_ref)

    b_out, gain_one, shift_one, b_down, gain_two, shift_two = (
        small_ref[i : i + 1, :] for i in range(6)
    )
    ctx_low = ctx_ref[...].astype(BF16)
    ctx_low_ref[...] = ctx_low
    unit_one, inv_one = norm_parts(emb_ref[...] + mm(ctx_low, w_out_ref[...]) + b_out)
    normed = unit_one * gain_one + shift_one
    normed_low = normed.astype(BF16)
    normed_ref[...] = normed_low
    ffn = None
    for c in range(wide // width):
        span = slice(c * width, (c + 1) * width)
        pre = mm(normed_low, w_up_ref[:, span]) + b_up_ref[:, span]
        below = 0.5 * (1.0 + lax.erf(pre * 0.7071067811865476))
        act = (pre * below).astype(BF16)
        act_ref[:, span] = act
        slope_ref[:, span] = below + pre * (0.3989422804014327 * jnp.exp(-0.5 * pre * pre))
        part = mm(act, w_down_ref[span, :])
        ffn = part if ffn is None else ffn + part
    unit_two, inv_two = norm_parts(normed + ffn + b_down)
    out_ref[...] = (unit_two * gain_two + shift_two).astype(BF16)
    grad = cot_ref[...].astype(F32)
    sums_ref[0:8, :] += fold_rows(grad * unit_two, jnp.sum)
    sums_ref[8:16, :] += fold_rows(grad, jnp.sum)
    grad_two = norm_back(grad, unit_two, inv_two, gain_two)
    gffn = grad_two.astype(BF16)
    gffn_ref[...] = gffn
    sums_ref[16:24, :] += fold_rows(gffn.astype(F32), jnp.sum)
    grad_normed = grad_two
    for c in range(wide // width):
        span = slice(c * width, (c + 1) * width)
        gpre = (mm(gffn, w_down_ref[span, :], NT) * slope_ref[:, span]).astype(BF16)
        gpre_ref[:, span] = gpre
        up_sums_ref[:, span] += fold_rows(gpre.astype(F32), jnp.sum)
        grad_normed = grad_normed + mm(gpre, w_up_ref[:, span], NT)
    sums_ref[24:32, :] += fold_rows(grad_normed * unit_one, jnp.sum)
    sums_ref[32:40, :] += fold_rows(grad_normed, jnp.sum)
    grad_one = norm_back(grad_normed, unit_one, inv_one, gain_one)
    gone_ref[...] = grad_one
    gattn = grad_one.astype(BF16)
    gattn_ref[...] = gattn
    sums_ref[40:48, :] += fold_rows(gattn.astype(F32), jnp.sum)
    gctx_ref[...] = mm(gattn, w_out_ref[...], NT).astype(BF16)


def middle(ctx, embedded, cotangent, w_out, w_up, w_down, small, b_up, block=256):
    tokens, width = embedded.shape
    wide = w_up.shape[1]
    whole = lambda a: pl.BlockSpec(a.shape, lambda i: (0, 0), pipeline_mode=pl.Buffered(1))
    rows = lambda n: pl.BlockSpec((block, n), lambda i: (i, 0))
    fixed = lambda r, n: pl.BlockSpec((r, n), lambda i: (0, 0))
    shape = lambda n, dtype: jax.ShapeDtypeStruct((tokens, n), dtype)
    return pl.pallas_call(
        middle_kernel,
        grid=(tokens // block,),
        in_specs=[rows(width)] * 3 + [whole(w_out), whole(w_up), whole(w_down), whole(small), whole(b_up)],
        out_specs=[
            rows(width),
            rows(width),
            rows(width),
            rows(wide),
            rows(width),
            rows(wide),
            rows(width),
            rows(width),
            rows(width),
            fixed(48, width),
            fixed(8, wide),
        ],
        out_shape=[
            shape(width, BF16),
            shape(width, BF16),
            shape(width, BF16),
            shape(wide, BF16),
            shape(width, BF16),
            shape(wide, BF16),
            shape(width, BF16),
            shape(width, F32),
            shape(width, BF16),
            jax.ShapeDtypeStruct((48, width), F32),
            jax.ShapeDtypeStruct((8, wide), F32),
        ],
        scratch_shapes=[pltpu.VMEM((block, wide), F32)],
        compiler_params=params(60),
        name="middle",
    )(ctx, embedded, cotangent, w_out, w_up, w_down, small, b_up)


def local(
    gene_ids,
    homolog_ids,
    knowledge_ids,
    expr_bins,
    species,
    cell_lengths,
    gene_table,
    knowledge_tables,
    expr_table,
    w_query,
    b_query,
    w_key,
    w_value,
    b_value,
    w_out,
    b_out,
    gain_one,
    shift_one,
    w_up,
    b_up,
    w_down,
    b_down,
    gain_two,
    shift_two,
    cotangent,
):
    tokens = gene_ids.shape[1]
    rows_dev, width = gene_table.shape
    devices = lax.axis_size(EVERY)
    capacity = 2 * tokens // devices
    slots_all = 2 * capacity
    slots = devices * slots_all
    bins = expr_table.shape[0]
    me = lax.axis_index("seq")

    chosen = jnp.where(species[0] == 1, homolog_ids, gene_ids).reshape(-1)
    requests, gene_slot, know_slot = route(
        chosen, knowledge_ids.reshape(-1), rows_dev, capacity, devices
    )
    received = lax.all_to_all(requests, EVERY, split_axis=0, concat_axis=0, tiled=True)
    know_sum = jnp.sum(knowledge_tables.astype(F32), axis=0).astype(BF16)
    combined = jnp.concatenate([gene_table, know_sum], axis=0)
    asked = received.reshape(-1)
    asked_hot = (asked[:, None] == jnp.arange(2 * rows_dev)[None, :]).astype(BF16)
    found = mm(asked_hot, combined).astype(BF16).reshape(devices, slots_all, width)
    fetched = lax.all_to_all(found, EVERY, split_axis=0, concat_axis=0, tiled=True)
    slot_at = jnp.arange(slots)[None, :]
    slot_hot = ((slot_at == gene_slot) | (slot_at == know_slot)).astype(BF16)
    bin_hot = (expr_bins.reshape(-1)[:, None] == jnp.arange(bins)[None, :]).astype(BF16)
    embedded = mm(slot_hot, fetched.reshape(slots, width)) + mm(bin_hot, expr_table)
    x_low = embedded.astype(BF16)

    x_other = lax.ppermute(x_low, "seq", [(0, 1), (1, 0)])
    query = ((mm(x_low, w_query) + b_query).astype(BF16) * HEAD_DIM ** (-0.5)).astype(BF16)
    key, key_other = (mm(x, w_key).astype(BF16) for x in (x_low, x_other))
    value, value_other = ((mm(x, w_value) + b_value).astype(BF16) for x in (x_low, x_other))
    where = jnp.stack([me * tokens, (1 - me) * tokens, cell_lengths[0]]).astype(jnp.int32)
    context, lse = attend(where, query, key, key_other, value, value_other)

    small = jnp.stack([b_out, gain_one, shift_one, b_down, gain_two, shift_two])
    (
        layer_output,
        ctx_low,
        normed_low,
        activated,
        grad_ffn,
        grad_pre,
        grad_attn,
        grad_one,
        grad_ctx,
        sums,
        up_sums,
    ) = middle(
        context, embedded, cotangent.reshape(tokens, width), w_out, w_up, w_down, small, b_up[None, :]
    )
    w_down_grad = mm(activated, grad_ffn, TN)
    w_up_grad = mm(normed_low, grad_pre, TN)
    w_out_grad = mm(ctx_low, grad_attn, TN)
    early = lax.psum(
        (
            w_down_grad.astype(BF16),
            w_up_grad.astype(BF16),
            w_out_grad.astype(BF16),
        ),
        EVERY,
    )
    w_down_grad, w_up_grad, w_out_grad = (g.astype(F32) for g in early)

    dq_part, dk_other, dv_other = attend_back(
        where[1:], query, grad_ctx, context, lse, key_other, value_other
    )
    dx_other = (mm(dk_other, w_key, NT) + mm(dv_other, w_value, NT)).astype(BF16)
    dx_from_other = lax.ppermute(dx_other, "seq", [(0, 1), (1, 0)])
    dq, dk, dv = attend_back(
        where[0::2], query, grad_ctx, context, lse, key, value, dq_part
    )
    grad_embedded = (
        grad_one
        + mm(dq, w_query, NT)
        + mm(dk, w_key, NT)
        + mm(dv, w_value, NT)
        + dx_from_other.astype(F32)
    )
    w_query_grad = mm(x_low, dq, TN)
    w_key_grad = mm(x_low, dk, TN) + mm(x_other, dk_other, TN)
    w_value_grad = mm(x_low, dv, TN) + mm(x_other, dv_other, TN)
    b_query_grad = jnp.sum(dq.astype(F32), axis=0)
    b_value_grad = jnp.sum(dv.astype(F32), axis=0) + jnp.sum(dv_other.astype(F32), axis=0)

    grad_low = grad_embedded.astype(BF16)
    grad_rest = (grad_embedded - grad_low.astype(F32)).astype(BF16)
    expr_grad = mm(bin_hot, grad_low, TN) + mm(bin_hot, grad_rest, TN)
    outgoing = mm(slot_hot, grad_low, TN).astype(BF16).reshape(devices, slots_all, width)
    returned = lax.all_to_all(outgoing, EVERY, split_axis=0, concat_axis=0, tiled=True)
    owned = jnp.arange(2 * rows_dev)[:, None] == asked[None, :]
    table_grads = mm(owned.astype(BF16), returned.reshape(slots, width))
    row_counts = jnp.sum(owned.astype(jnp.int32), axis=1).reshape(2, rows_dev)

    late = lax.psum(
        (
            expr_grad,
            w_query_grad,
            w_key_grad,
            w_value_grad,
            b_query_grad,
            b_value_grad,
            jnp.sum(sums.reshape(6, 8, width), axis=1),
            jnp.sum(up_sums, axis=0),
        ),
        EVERY,
    )
    expr_grad, w_query_grad, w_key_grad, w_value_grad, b_query_grad, b_value_grad, sums, b_up_grad = late
    gain_two_grad, shift_two_grad, b_down_grad, gain_one_grad, shift_one_grad, b_out_grad = (
        sums[i] for i in range(6)
    )
    return (
        layer_output.reshape(1, tokens, width),
        table_grads[:rows_dev],
        table_grads[rows_dev:],
        expr_grad,
        w_query_grad,
        b_query_grad,
        w_key_grad,
        w_value_grad,
        b_value_grad,
        w_out_grad,
        b_out_grad,
        gain_one_grad,
        shift_one_grad,
        w_up_grad,
        b_up_grad,
        w_down_grad,
        b_down_grad,
        gain_two_grad,
        shift_two_grad,
        row_counts,
    )


def solution(mesh):
    whole = P()
    placed = (
        (P("dp", "seq"),) * 4
        + (P("dp"),) * 2
        + (P(EVERY, None), P(None, EVERY, None))
        + (whole,) * 16
        + (P("dp", "seq", None),)
    )
    given = (
        (P("dp", "seq", None),)
        + (P(EVERY, None),) * 2
        + (whole,) * 16
        + (P(None, EVERY),)
    )
    return jax.shard_map(local, mesh=mesh, in_specs=placed, out_specs=given, check_vma=False)
```

```python
import functools

import jax
import jax.numpy as jnp
from jax import lax
from jax.experimental import pallas as pl
from jax.experimental.pallas import tpu as pltpu
from jax.sharding import Mesh, PartitionSpec as P

HEADS = 12
HEAD_DIM = 64
PAIR = 2 * HEAD_DIM
KEY_CHUNK = 512
LOG2E = 1.4426950408889634
SWAP = [(0, 1), (1, 0)]
F32 = jnp.float32
BF16 = jnp.bfloat16
NN = (((1,), (0,)), ((), ()))
NT = (((1,), (1,)), ((), ()))
TN = (((0,), (0,)), ((), ()))


def mm(left, right, dims=NN):
    return lax.dot_general(left, right, dims, preferred_element_type=F32)


def params(mib):
    return pltpu.CompilerParams(vmem_limit_bytes=mib * 2**20)


def cost(flops, moved):
    return pl.CostEstimate(flops=flops, bytes_accessed=moved, transcendentals=0)


def hot(left, right):
    return (left == right).astype(BF16)


def route_kernel(
    rows_dev, capacity, top_ref, gene_ref, know_ref, req_ref, gene_slot_ref, know_slot_ref
):
    tokens = gene_ref.shape[0]
    devices, slots_all = req_ref.shape
    group = devices // 2
    lane = lax.broadcasted_iota(jnp.int32, (tokens, devices), 1)
    mine = lane < group
    top = top_ref[0]
    first = jnp.where(mine, lane + top * group, lane - top * group) * rows_dev
    earlier = (
        lax.broadcasted_iota(jnp.int32, (tokens, tokens), 0)
        > lax.broadcasted_iota(jnp.int32, (tokens, tokens), 1)
    ).astype(F32).astype(BF16)
    rank_lane = lax.broadcasted_iota(jnp.int32, (tokens, capacity), 1)
    asked = []
    for which, (ids_ref, slot_ref) in enumerate(((gene_ref, gene_slot_ref), (know_ref, know_slot_ref))):
        row = ids_ref[...] - first
        hit = (row >= 0) & (row < rows_dev)
        before = mm(earlier, hit.astype(F32).astype(BF16))
        rank = jnp.sum(jnp.where(hit, before, 0.0), axis=1, keepdims=True)
        owner = jnp.sum(jnp.where(hit, lane, 0).astype(F32), axis=1, keepdims=True)
        slot_ref[...] = (owner * slots_all + rank).astype(jnp.int32) + which * capacity
        rank_hit = (rank_lane == rank.astype(jnp.int32)).astype(F32).astype(BF16)
        coded = jnp.where(hit, row + 1, 0)
        high = (coded >> 4).astype(F32).astype(BF16)
        low = (coded & 15).astype(F32).astype(BF16)
        wanted = (mm(high, rank_hit, TN) * 16.0 + mm(low, rank_hit, TN)).astype(jnp.int32)
        asked.append(jnp.where(wanted > 0, wanted - 1 + which * rows_dev, -1))
    req_ref[:, :capacity] = asked[0]
    req_ref[:, capacity:] = asked[1]


def route(top, gene_ids, know_ids, rows_dev, capacity, devices):
    tokens = gene_ids.shape[0]
    return pl.pallas_call(
        functools.partial(route_kernel, rows_dev, capacity),
        in_specs=[pl.BlockSpec(memory_space=pltpu.SMEM)] + [pl.BlockSpec(memory_space=pltpu.VMEM)] * 2,
        out_shape=(
            jax.ShapeDtypeStruct((devices, 2 * capacity), jnp.int32),
            jax.ShapeDtypeStruct((tokens, 1), jnp.int32),
            jax.ShapeDtypeStruct((tokens, 1), jnp.int32),
        ),
        compiler_params=params(32),
        name="route",
    )(top.reshape(1), gene_ids[:, None], know_ids[:, None])


def fill_keys(aug_ref, key, first_key, count):
    lanes = lax.broadcasted_iota(jnp.int32, key.shape, 1)
    at = lax.broadcasted_iota(jnp.int32, key.shape, 0) + first_key
    bias = jnp.where(at < count, 0.0, -1e30).astype(BF16)
    none = jnp.zeros_like(key)
    aug_ref[:, :PAIR] = jnp.where(lanes < HEAD_DIM, key, jnp.where(lanes == HEAD_DIM, bias, none))
    aug_ref[:, PAIR : 2 * PAIR] = key
    aug_ref[:, 2 * PAIR :] = jnp.where(lanes >= HEAD_DIM, key, jnp.where(lanes == 0, bias, none))


def head_mask(shape, head):
    lanes = lax.broadcasted_iota(jnp.int32, shape, 1)
    return (lanes >= head * HEAD_DIM) & (lanes < (head + 1) * HEAD_DIM)


def spread_query(query, head):
    lanes = lax.broadcasted_iota(jnp.int32, query.shape, 1)
    scaled = query.astype(F32) * (HEAD_DIM ** (-0.5) * LOG2E)
    scaled = jnp.where(head_mask(query.shape, head), scaled, 0.0)
    high = scaled.astype(BF16)
    low = scaled - high.astype(F32)
    low = jnp.where(lanes == (1 - head) * HEAD_DIM, 1.0, low).astype(BF16)
    return jnp.concatenate([low, high] if head == 0 else [high, low], axis=1)


def fold_rows(value, how):
    return how(value.reshape(value.shape[0] // 8, 8, value.shape[1]), axis=0)


def attend_kernel(merge, where_ref, q_ref, k_ref, v_ref, *rest):
    if merge:
        out_in_ref, lse_in_ref, out_ref, lse_ref, aug_ref, vt_ref, score_ref = rest
    else:
        out_ref, lse_ref, aug_ref, vt_ref, score_ref = rest
    spans = [slice(c, c + KEY_CHUNK) for c in range(0, k_ref.shape[0], KEY_CHUNK)]
    fill_keys(aug_ref, k_ref[...], where_ref[0], where_ref[1])
    vt_ref[...] = v_ref[...].T
    outs = []
    for head in range(2):
        own = slice(head * HEAD_DIM, (head + 1) * HEAD_DIM)
        query = spread_query(q_ref[...], head)
        top = None
        for span in spans:
            scores = mm(aug_ref[span, head * PAIR : (head + 2) * PAIR], query, NT)
            score_ref[head, span, :] = scores
            high = fold_rows(scores, jnp.max)
            top = high if top is None else jnp.maximum(top, high)
        top = jnp.max(top, axis=0, keepdims=True)
        total = None
        acc = None
        for span in spans:
            probs = jnp.exp2(score_ref[head, span, :] - top)
            part = fold_rows(probs, jnp.sum)
            total = part if total is None else total + part
            part = mm(vt_ref[own, span], probs.astype(BF16))
            acc = part if acc is None else acc + part
        total = jnp.sum(total, axis=0, keepdims=True)
        lse = top + jnp.log2(total)
        if merge:
            before = lse_in_ref[0, head : head + 1, :]
            both = jnp.maximum(lse, before)
            both = both + jnp.log2(jnp.exp2(lse - both) + jnp.exp2(before - both))
            acc = acc * (jnp.exp2(lse - both) / total)
            acc = acc + out_in_ref[own, :] * jnp.exp2(before - both)
            lse = both
        else:
            acc = acc / total
        lse_ref[0, head : head + 1, :] = lse
        outs.append(acc)
    out = jnp.concatenate(outs, axis=0)
    out_ref[...] = out.T if merge else out


def attend(where, query, key, value, before=()):
    tokens, width = query.shape
    keys = key.shape[0]
    pairs = width // PAIR
    column = lambda rows: pl.BlockSpec((rows, PAIR), lambda p, w: (0, p))
    upright = pl.BlockSpec((PAIR, tokens), lambda p, w: (p, 0))
    stats = pl.BlockSpec((1, 2, tokens), lambda p, w: (p, 0, 0))
    merge = len(before) > 0
    return pl.pallas_call(
        functools.partial(attend_kernel, merge),
        grid_spec=pltpu.PrefetchScalarGridSpec(
            num_scalar_prefetch=1,
            grid=(pairs,),
            in_specs=[column(tokens), column(keys), column(keys)] + ([upright, stats] if merge else []),
            out_specs=[column(tokens) if merge else upright, stats],
            scratch_shapes=[
                pltpu.VMEM((keys, 3 * PAIR), BF16),
                pltpu.VMEM((PAIR, keys), BF16),
                pltpu.VMEM((2, keys, tokens), F32),
            ],
        ),
        out_shape=(
            jax.ShapeDtypeStruct((tokens, width) if merge else (width, tokens), F32),
            jax.ShapeDtypeStruct((pairs, 2, tokens), F32),
        ),
        compiler_params=params(48),
        cost_estimate=cost(16 * tokens * keys * width, 2 * tokens * width * 10),
        name="attend_more" if merge else "attend",
    )(where, query, key, value, *before)


def attend_back_kernel(
    add, untouched, where_ref, q_ref, g_ref, o_ref, lse_ref, k_ref, v_ref, *rest
):
    dq_in_ref = rest[0] if add else None
    dq_ref, dk_ref, dv_ref, aug_ref, kt_ref = rest[int(add) + untouched :]
    fill_keys(aug_ref, k_ref[...], where_ref[0], where_ref[1])
    kt_ref[...] = k_ref[...].T
    grad = g_ref[...]
    picks = (
        lax.broadcasted_iota(jnp.int32, (8, PAIR), 1) // HEAD_DIM
        == lax.broadcasted_iota(jnp.int32, (8, PAIR), 0)
    ).astype(F32)
    inner = lax.dot_general(
        picks,
        grad.astype(F32) * o_ref[...],
        NT,
        precision=lax.Precision.HIGHEST,
        preferred_element_type=F32,
    )
    scaled = q_ref[...] * jnp.asarray(HEAD_DIM ** (-0.5), BF16)
    none = jnp.zeros_like(grad)
    masks = [head_mask(grad.shape, head) for head in range(2)]
    queries = [spread_query(q_ref[...], head) for head in range(2)]
    q_heads = [jnp.where(m, scaled, none) for m in masks]
    g_heads = [jnp.where(m, grad, none) for m in masks]
    dqs = [None, None]
    for first in range(0, k_ref.shape[0], KEY_CHUNK):
        span = slice(first, first + KEY_CHUNK)
        dk = None
        dv = None
        for head in range(2):
            own = slice(head * HEAD_DIM, (head + 1) * HEAD_DIM)
            scores = mm(aug_ref[span, head * PAIR : (head + 2) * PAIR], queries[head], NT)
            probs = jnp.exp2(scores - lse_ref[0, head : head + 1, :])
            grad_probs = mm(v_ref[span, :], g_heads[head], NT)
            grad_scores = (probs * (grad_probs - inner[head : head + 1, :])).astype(BF16)
            part = mm(kt_ref[own, span], grad_scores)
            dqs[head] = part if dqs[head] is None else dqs[head] + part
            part = mm(probs.astype(BF16), g_heads[head])
            dv = part if dv is None else dv + part
            part = mm(grad_scores, q_heads[head])
            dk = part if dk is None else dk + part
        dk_ref[span, :] = dk.astype(BF16)
        dv_ref[span, :] = dv.astype(BF16)
    dq = jnp.concatenate(dqs, axis=0).T * HEAD_DIM ** (-0.5)
    if add:
        dq = dq + dq_in_ref[...]
    dq_ref[...] = dq.astype(dq_ref.dtype)


def attend_back(where, query, grad, out, lse, key, value, first, count, before, into):
    tokens, width = query.shape
    keys = key.shape[0]
    column = lambda rows: pl.BlockSpec((rows, PAIR), lambda p, w: (0, p + first))
    untouched = pl.BlockSpec(memory_space=pl.ANY)
    add = len(before) > 0
    given = 7 + len(before)
    return pl.pallas_call(
        functools.partial(attend_back_kernel, add, len(into)),
        grid_spec=pltpu.PrefetchScalarGridSpec(
            num_scalar_prefetch=1,
            grid=(count,),
            in_specs=[column(tokens)] * 3
            + [pl.BlockSpec((1, 2, tokens), lambda p, w: (p + first, 0, 0))]
            + [column(keys)] * 2
            + [column(tokens)] * len(before)
            + [untouched] * len(into),
            out_specs=[column(tokens), column(keys), column(keys)],
            scratch_shapes=[
                pltpu.VMEM((keys, 3 * PAIR), BF16),
                pltpu.VMEM((PAIR, keys), BF16),
            ],
        ),
        out_shape=(
            jax.ShapeDtypeStruct((tokens, width), BF16 if add else F32),
            jax.ShapeDtypeStruct((keys, width), BF16),
            jax.ShapeDtypeStruct((keys, width), BF16),
        ),
        input_output_aliases={given + i: i for i in range(len(into))},
        compiler_params=params(56),
        cost_estimate=cost(40 * tokens * keys * PAIR * count, 2 * tokens * PAIR * count * 12),
        name=("attend_back_more" if add else "attend_back") + str(first),
    )(where, query, grad, out, lse, key, value, *before, *into)


def norm_parts(value):
    centre = jnp.mean(value, axis=-1, keepdims=True)
    centred = value - centre
    variance = jnp.mean(centred * centred, axis=-1, keepdims=True)
    inverse = lax.rsqrt(variance + 1e-05)
    return centred * inverse, inverse


def norm_back(grad, unit, inverse, gain):
    grad_unit = grad * gain
    return inverse * (
        grad_unit
        - jnp.mean(grad_unit, axis=-1, keepdims=True)
        - unit * jnp.mean(grad_unit * unit, axis=-1, keepdims=True)
    )


def middle_kernel(
    ctx_ref,
    emb_ref,
    cot_ref,
    w_out_ref,
    w_up_ref,
    w_down_ref,
    small_ref,
    b_up_ref,
    out_ref,
    ctx_low_ref,
    normed_ref,
    act_ref,
    gffn_ref,
    gpre_ref,
    gattn_ref,
    gone_ref,
    gctx_ref,
    sums_ref,
    up_sums_ref,
    slope_ref,
):
    step = pl.program_id(0)
    width = emb_ref.shape[1]
    wide = w_up_ref.shape[1]

    @pl.when(step == 0)
    def _():
        sums_ref[...] = jnp.zeros_like(sums_ref)
        up_sums_ref[...] = jnp.zeros_like(up_sums_ref)

    b_out, gain_one, shift_one, b_down, gain_two, shift_two = (
        small_ref[i : i + 1, :] for i in range(6)
    )
    ctx_low = ctx_ref[...].astype(BF16)
    ctx_low_ref[...] = ctx_low
    unit_one, inv_one = norm_parts(emb_ref[...] + mm(ctx_low, w_out_ref[...]) + b_out)
    normed = unit_one * gain_one + shift_one
    normed_low = normed.astype(BF16)
    normed_ref[...] = normed_low
    ffn = None
    for c in range(wide // width):
        span = slice(c * width, (c + 1) * width)
        pre = mm(normed_low, w_up_ref[:, span]) + b_up_ref[:, span]
        below = 0.5 * (1.0 + lax.erf(pre * 0.7071067811865476))
        act = (pre * below).astype(BF16)
        act_ref[:, span] = act
        slope_ref[:, span] = below + pre * (0.3989422804014327 * jnp.exp(-0.5 * pre * pre))
        part = mm(act, w_down_ref[span, :])
        ffn = part if ffn is None else ffn + part
    unit_two, inv_two = norm_parts(normed + ffn + b_down)
    out_ref[...] = (unit_two * gain_two + shift_two).astype(BF16)
    grad = cot_ref[...].astype(F32)
    sums_ref[0:8, :] += fold_rows(grad * unit_two, jnp.sum)
    sums_ref[8:16, :] += fold_rows(grad, jnp.sum)
    grad_two = norm_back(grad, unit_two, inv_two, gain_two)
    gffn = grad_two.astype(BF16)
    gffn_ref[...] = gffn
    sums_ref[16:24, :] += fold_rows(gffn.astype(F32), jnp.sum)
    grad_normed = grad_two
    for c in range(wide // width):
        span = slice(c * width, (c + 1) * width)
        gpre = (mm(gffn, w_down_ref[span, :], NT) * slope_ref[:, span]).astype(BF16)
        gpre_ref[:, span] = gpre
        up_sums_ref[:, span] += fold_rows(gpre.astype(F32), jnp.sum)
        grad_normed = grad_normed + mm(gpre, w_up_ref[:, span], NT)
    sums_ref[24:32, :] += fold_rows(grad_normed * unit_one, jnp.sum)
    sums_ref[32:40, :] += fold_rows(grad_normed, jnp.sum)
    grad_one = norm_back(grad_normed, unit_one, inv_one, gain_one)
    gone_ref[...] = grad_one
    gattn = grad_one.astype(BF16)
    gattn_ref[...] = gattn
    sums_ref[40:48, :] += fold_rows(gattn.astype(F32), jnp.sum)
    gctx_ref[...] = mm(gattn, w_out_ref[...], NT).astype(BF16)


def middle(ctx, embedded, cotangent, w_out, w_up, w_down, small, b_up, block=256):
    tokens, width = embedded.shape
    wide = w_up.shape[1]
    whole = lambda a: pl.BlockSpec(a.shape, lambda i: (0, 0), pipeline_mode=pl.Buffered(1))
    rows = lambda n: pl.BlockSpec((block, n), lambda i: (i, 0))
    fixed = lambda r, n: pl.BlockSpec((r, n), lambda i: (0, 0))
    shape = lambda n, dtype: jax.ShapeDtypeStruct((tokens, n), dtype)
    return pl.pallas_call(
        middle_kernel,
        grid=(tokens // block,),
        in_specs=[rows(width)] * 3 + [whole(w_out), whole(w_up), whole(w_down), whole(small), whole(b_up)],
        out_specs=[
            rows(width),
            rows(width),
            rows(width),
            rows(wide),
            rows(width),
            rows(wide),
            rows(width),
            rows(width),
            rows(width),
            fixed(48, width),
            fixed(8, wide),
        ],
        out_shape=[
            shape(width, BF16),
            shape(width, BF16),
            shape(width, BF16),
            shape(wide, BF16),
            shape(width, BF16),
            shape(wide, BF16),
            shape(width, BF16),
            shape(width, F32),
            shape(width, BF16),
            jax.ShapeDtypeStruct((48, width), F32),
            jax.ShapeDtypeStruct((8, wide), F32),
        ],
        scratch_shapes=[pltpu.VMEM((block, wide), F32)],
        compiler_params=params(60),
        cost_estimate=cost(tokens * width * (8 * wide + 4 * width) * 2, 2 * tokens * (2 * wide + 14 * width)),
        name="middle",
    )(ctx, embedded, cotangent, w_out, w_up, w_down, small, b_up)


def cut(value, axis):
    rows = value.shape[0] // 2
    me = lax.axis_index(axis)
    keep = lax.dynamic_slice_in_dim(value, me * rows, rows, 0)
    return keep, lax.dynamic_slice_in_dim(value, (1 - me) * rows, rows, 0)


def halve(value, axis):
    keep, send = cut(value, axis)
    return keep + lax.ppermute(send, axis, SWAP)


def double(value, axis):
    first = lax.axis_index(axis) == 0
    other = lax.ppermute(value, axis, SWAP)
    return jnp.concatenate([jnp.where(first, value, other), jnp.where(first, other, value)], axis=0)


def orders_of(dp_axes):
    core, near, far = dp_axes[-1], dp_axes[-2], dp_axes[-3::-1]
    return (core, near, "seq", *far), (core, "seq", near, *far)


def doubled(pieces, orders):
    for step in reversed(range(len(orders[0]))):
        pieces = [double(p, order[step]) for p, order in zip(pieces, orders)]
    return pieces


def sum_everywhere(value, orders):
    pieces = jnp.split(halve(value, orders[0][0]), 2, axis=0)
    for step in range(1, len(orders[0])):
        pieces = [halve(p, order[step]) for p, order in zip(pieces, orders)]
    pieces = doubled(pieces, [order[1:] for order in orders])
    return double(jnp.concatenate(pieces, axis=0), orders[0][0])


def local(
    dp_axes,
    gene_ids,
    homolog_ids,
    knowledge_ids,
    expr_bins,
    species,
    cell_lengths,
    gene_table,
    knowledge_tables,
    expr_table,
    w_query,
    b_query,
    w_key,
    w_value,
    b_value,
    w_out,
    b_out,
    gain_one,
    shift_one,
    w_up,
    b_up,
    w_down,
    b_down,
    gain_two,
    shift_two,
    cotangent,
):
    tokens = gene_ids.shape[1]
    rows_dev, width = gene_table.shape
    wide = w_up.shape[1]
    every = (*dp_axes, "seq")
    top_axis, group_axes = dp_axes[0], (*dp_axes[1:], "seq")
    devices = lax.axis_size(every)
    group = devices // 2
    capacity = 2 * tokens // devices
    slots_all = 2 * capacity
    slots = group * slots_all
    bins = expr_table.shape[0]
    me = lax.axis_index("seq")

    def exchange(value, axis):
        return lax.all_to_all(value, group_axes, split_axis=axis, concat_axis=axis, tiled=True)

    gene_table, knowledge_tables = lax.optimization_barrier((gene_table, knowledge_tables))
    gene_other = lax.ppermute(gene_table, top_axis, SWAP)
    know_sum = jnp.sum(knowledge_tables.astype(F32), axis=0).astype(BF16)
    chosen = jnp.where(species[0] == 1, homolog_ids, gene_ids).reshape(-1)
    requests, gene_slot, know_slot = route(
        lax.axis_index(top_axis), chosen, knowledge_ids.reshape(-1), rows_dev, capacity, devices
    )
    asked = exchange(requests.reshape(2, group, slots_all), 1).reshape(2, slots)
    asked, gene_other, know_sum = lax.optimization_barrier((asked, gene_other, know_sum))
    know_other = lax.ppermute(know_sum, top_axis, SWAP)
    tables = [
        jnp.concatenate([gene_table, know_sum], axis=0),
        jnp.concatenate([gene_other, know_other], axis=0),
    ]
    row_at = jnp.arange(2 * rows_dev)
    slot_at = jnp.arange(slots)
    bin_hot = hot(expr_bins.reshape(-1)[:, None], jnp.arange(bins)[None, :])
    embedded = mm(bin_hot, expr_table)
    slot_hots = []
    for part in range(2):
        found = mm(hot(asked[part][:, None], row_at[None, :]), tables[part]).astype(BF16)
        fetched = exchange(found.reshape(group, slots_all, width), 0).reshape(slots, width)
        at = slot_at[None, :] + part * slots
        slot_hots.append(((at == gene_slot) | (at == know_slot)).astype(BF16))
        embedded = embedded + mm(slot_hots[part], fetched)
    x_low = embedded.astype(BF16)

    x_other = lax.ppermute(x_low, "seq", SWAP)
    query = (mm(x_low, w_query) + b_query).astype(BF16)
    key, key_other = (mm(x, w_key).astype(BF16) for x in (x_low, x_other))
    value, value_other = ((mm(x, w_value) + b_value).astype(BF16) for x in (x_low, x_other))
    mine = jnp.stack([me * tokens, cell_lengths[0]]).astype(jnp.int32)
    others = jnp.stack([(1 - me) * tokens, cell_lengths[0]]).astype(jnp.int32)
    context, lse = attend(
        others, query, key_other, value_other, attend(mine, query, key, value)
    )

    small = jnp.stack([b_out, gain_one, shift_one, b_down, gain_two, shift_two])
    (
        layer_output,
        ctx_low,
        normed_low,
        activated,
        grad_ffn,
        grad_pre,
        grad_attn,
        grad_one,
        grad_ctx,
        sums,
        up_sums,
    ) = middle(
        context, embedded, cotangent.reshape(tokens, width), w_out, w_up, w_down, small, b_up[None, :]
    )

    orders = orders_of(dp_axes)
    step = 0
    ffn_grads = [mm(activated, grad_ffn, TN).astype(BF16), mm(normed_low, grad_pre, TN).astype(BF16)]
    ffn_grads, grad_ctx = lax.optimization_barrier((ffn_grads, grad_ctx))
    w_out_grad = mm(ctx_low, grad_attn, TN)
    ffn_grads = [halve(g, order[0]) for g, order in zip(ffn_grads, orders)]
    pairs = width // PAIR
    sides = ((others, key_other, value_other), (mine, key, value))
    grads = []
    before = ()
    dx_from_other = None
    for side, (place, keys, values) in enumerate(sides):
        into = ()
        for part in range(2):
            step += 1
            cuts = [cut(g, order[step]) for g, order in zip(ffn_grads, orders)]
            cuts, grad_ctx, into, before = lax.optimization_barrier((cuts, grad_ctx, into, before))
            arrived = [lax.ppermute(c[1], order[step], SWAP) for c, order in zip(cuts, orders)]
            into = attend_back(
                place,
                query,
                grad_ctx,
                context,
                lse,
                keys,
                values,
                part * pairs // 2,
                pairs // 2,
                before,
                into,
            )
            arrived, into = lax.optimization_barrier((arrived, into))
            ffn_grads = [c[0] + a for c, a in zip(cuts, arrived)]
        grads.append(into)
        if side == 0:
            before = into[:1]
            dx_other = (mm(into[1], w_key, NT) + mm(into[2], w_value, NT)).astype(BF16)
            dx_other, before = lax.optimization_barrier((dx_other, before))
            dx_from_other = lax.ppermute(dx_other, "seq", SWAP)
    for order_step in range(step + 1, len(orders[0])):
        ffn_grads = [halve(g, order[order_step]) for g, order in zip(ffn_grads, orders)]
    (_, dk_other, dv_other), (dq, dk, dv) = grads
    dq, dk, dv, dx_from_other = lax.optimization_barrier((dq, dk, dv, dx_from_other))
    grad_embedded = (
        grad_one
        + mm(dq, w_query, NT)
        + mm(dk, w_key, NT)
        + mm(dv, w_value, NT)
        + dx_from_other.astype(F32)
    )
    grad_low = grad_embedded.astype(BF16)

    owned = [row_at[:, None] == asked[part][None, :] for part in range(2)]
    counts = [jnp.sum(o.astype(jnp.int32), axis=1) for o in owned]
    row_counts = counts[0] + lax.ppermute(counts[1], top_axis, SWAP)
    table_parts = [None, None]
    outgoing = [mm(hots, grad_low, TN).astype(BF16) for hots in slot_hots]
    outgoing, ffn_grads, dq, dk, dv = lax.optimization_barrier((outgoing, ffn_grads, dq, dk, dv))
    for part in (1, 0):
        returned = exchange(outgoing[part].reshape(group, slots_all, width), 0).reshape(slots, width)
        table_parts[part] = mm(owned[part].astype(BF16), returned)
    table_grads = table_parts[0] + lax.ppermute(
        table_parts[1].astype(BF16), top_axis, SWAP
    ).astype(F32)

    w_query_grad = mm(x_low, dq, TN)
    w_key_grad = mm(x_low, dk, TN) + mm(x_other, dk_other, TN)
    w_value_grad = mm(x_low, dv, TN) + mm(x_other, dv_other, TN)
    b_query_grad = jnp.sum(dq.astype(F32), axis=0)
    b_value_grad = jnp.sum(dv.astype(F32), axis=0) + jnp.sum(dv_other.astype(F32), axis=0)
    grad_rest = (grad_embedded - grad_low.astype(F32)).astype(BF16)
    expr_grad = mm(bin_hot, grad_low, TN) + mm(bin_hot, grad_rest, TN)
    late = [
        w_query_grad,
        w_key_grad,
        w_value_grad,
        w_out_grad,
        expr_grad,
        b_query_grad[None, :],
        b_value_grad[None, :],
        jnp.sum(sums.reshape(6, 8, width), axis=1),
        jnp.sum(up_sums, axis=0).reshape(wide // width, width),
    ]
    heights = [item.shape[0] for item in late]
    late.append(jnp.zeros((-sum(heights) % 512, width), F32))
    late = sum_everywhere(jnp.concatenate([item.astype(BF16) for item in late], axis=0), orders)
    w_down_grad, w_up_grad = (g.astype(F32) for g in doubled(ffn_grads, orders))
    taken = []
    for height in heights:
        at = sum(item.shape[0] for item in taken)
        taken.append(late[at : at + height].astype(F32))
    w_query_grad, w_key_grad, w_value_grad, w_out_grad, *taken = taken
    expr_grad, b_query_grad, b_value_grad, sums, b_up_grad = taken
    gain_two_grad, shift_two_grad, b_down_grad, gain_one_grad, shift_one_grad, b_out_grad = (
        sums[i] for i in range(6)
    )
    return (
        layer_output.reshape(1, tokens, width),
        table_grads[:rows_dev],
        table_grads[rows_dev:],
        expr_grad,
        w_query_grad,
        b_query_grad[0],
        w_key_grad,
        w_value_grad,
        b_value_grad[0],
        w_out_grad,
        b_out_grad,
        gain_one_grad,
        shift_one_grad,
        w_up_grad,
        b_up_grad.reshape(wide),
        w_down_grad,
        b_down_grad,
        gain_two_grad,
        shift_two_grad,
        row_counts.reshape(2, rows_dev),
    )


def solution(mesh):
    bits = mesh.shape["dp"].bit_length() - 1
    dp_axes = tuple(f"dp{i}" for i in range(bits))
    fine = Mesh(mesh.devices.reshape((2,) * bits + (mesh.shape["seq"],)), (*dp_axes, "seq"))
    every = (*dp_axes, "seq")
    whole = P()
    placed = (
        (P(dp_axes, "seq"),) * 4
        + (P(dp_axes),) * 2
        + (P(every, None), P(None, every, None))
        + (whole,) * 16
        + (P(dp_axes, "seq", None),)
    )
    given = (
        (P(dp_axes, "seq", None),)
        + (P(every, None),) * 2
        + (whole,) * 16
        + (P(None, every),)
    )
    return jax.shard_map(
        functools.partial(local, dp_axes), mesh=fine, in_specs=placed, out_specs=given, check_vma=False
    )
```

```python
import functools

import jax
import jax.numpy as jnp
from jax import lax
from jax.experimental import pallas as pl
from jax.experimental.pallas import tpu as pltpu
from jax.sharding import Mesh, PartitionSpec as P

HEADS = 12
HEAD_DIM = 64
PAIR = 2 * HEAD_DIM
KEY_CHUNK = 512
LOG2E = 1.4426950408889634
SWAP = [(0, 1), (1, 0)]
F32 = jnp.float32
BF16 = jnp.bfloat16
NN = (((1,), (0,)), ((), ()))
NT = (((1,), (1,)), ((), ()))
TN = (((0,), (0,)), ((), ()))


def mm(left, right, dims=NN):
    return lax.dot_general(left, right, dims, preferred_element_type=F32)


def params(mib):
    return pltpu.CompilerParams(vmem_limit_bytes=mib * 2**20)


def cost(flops, moved):
    return pl.CostEstimate(flops=flops, bytes_accessed=moved, transcendentals=0)


def hot(left, right):
    return (left == right).astype(BF16)


def route_kernel(
    rows_dev, capacity, top_ref, gene_ref, know_ref, req_ref, gene_slot_ref, know_slot_ref
):
    tokens = gene_ref.shape[0]
    devices, slots_all = req_ref.shape
    group = devices // 2
    lane = lax.broadcasted_iota(jnp.int32, (tokens, devices), 1)
    mine = lane < group
    top = top_ref[0]
    first = jnp.where(mine, lane + top * group, lane - top * group) * rows_dev
    earlier = (
        lax.broadcasted_iota(jnp.int32, (tokens, tokens), 0)
        > lax.broadcasted_iota(jnp.int32, (tokens, tokens), 1)
    ).astype(F32).astype(BF16)
    rank_lane = lax.broadcasted_iota(jnp.int32, (tokens, capacity), 1)
    asked = []
    for which, (ids_ref, slot_ref) in enumerate(((gene_ref, gene_slot_ref), (know_ref, know_slot_ref))):
        row = ids_ref[...] - first
        hit = (row >= 0) & (row < rows_dev)
        before = mm(earlier, hit.astype(F32).astype(BF16))
        rank = jnp.sum(jnp.where(hit, before, 0.0), axis=1, keepdims=True)
        owner = jnp.sum(jnp.where(hit, lane, 0).astype(F32), axis=1, keepdims=True)
        slot_ref[...] = (owner * slots_all + rank).astype(jnp.int32) + which * capacity
        rank_hit = (rank_lane == rank.astype(jnp.int32)).astype(F32).astype(BF16)
        coded = jnp.where(hit, row + 1, 0)
        high = (coded >> 4).astype(F32).astype(BF16)
        low = (coded & 15).astype(F32).astype(BF16)
        wanted = (mm(high, rank_hit, TN) * 16.0 + mm(low, rank_hit, TN)).astype(jnp.int32)
        asked.append(jnp.where(wanted > 0, wanted - 1 + which * rows_dev, -1))
    req_ref[:, :capacity] = asked[0]
    req_ref[:, capacity:] = asked[1]


def route(top, gene_ids, know_ids, rows_dev, capacity, devices):
    tokens = gene_ids.shape[0]
    return pl.pallas_call(
        functools.partial(route_kernel, rows_dev, capacity),
        in_specs=[pl.BlockSpec(memory_space=pltpu.SMEM)] + [pl.BlockSpec(memory_space=pltpu.VMEM)] * 2,
        out_shape=(
            jax.ShapeDtypeStruct((devices, 2 * capacity), jnp.int32),
            jax.ShapeDtypeStruct((tokens, 1), jnp.int32),
            jax.ShapeDtypeStruct((tokens, 1), jnp.int32),
        ),
        compiler_params=params(32),
        name="route",
    )(top.reshape(1), gene_ids[:, None], know_ids[:, None])


def fill_keys(aug_ref, key, first_key, count):
    lanes = lax.broadcasted_iota(jnp.int32, key.shape, 1)
    at = lax.broadcasted_iota(jnp.int32, key.shape, 0) + first_key
    bias = jnp.where(at < count, 0.0, -1e30).astype(BF16)
    none = jnp.zeros_like(key)
    aug_ref[:, :PAIR] = jnp.where(lanes < HEAD_DIM, key, jnp.where(lanes == HEAD_DIM, bias, none))
    aug_ref[:, PAIR : 2 * PAIR] = key
    aug_ref[:, 2 * PAIR :] = jnp.where(lanes >= HEAD_DIM, key, jnp.where(lanes == 0, bias, none))


def head_mask(shape, head):
    lanes = lax.broadcasted_iota(jnp.int32, shape, 1)
    return (lanes >= head * HEAD_DIM) & (lanes < (head + 1) * HEAD_DIM)


def spread_query(query, head):
    lanes = lax.broadcasted_iota(jnp.int32, query.shape, 1)
    scaled = query.astype(F32) * (HEAD_DIM ** (-0.5) * LOG2E)
    scaled = jnp.where(head_mask(query.shape, head), scaled, 0.0)
    high = scaled.astype(BF16)
    low = scaled - high.astype(F32)
    low = jnp.where(lanes == (1 - head) * HEAD_DIM, 1.0, low).astype(BF16)
    return jnp.concatenate([low, high] if head == 0 else [high, low], axis=1)


def fold_rows(value, how):
    return how(value.reshape(value.shape[0] // 8, 8, value.shape[1]), axis=0)


def attend_kernel(merge, where_ref, q_ref, k_ref, v_ref, *rest):
    if merge:
        out_in_ref, lse_in_ref, out_ref, lse_ref, aug_ref, vt_ref, score_ref = rest
    else:
        out_ref, lse_ref, aug_ref, vt_ref, score_ref = rest
    spans = [slice(c, c + KEY_CHUNK) for c in range(0, k_ref.shape[0], KEY_CHUNK)]
    fill_keys(aug_ref, k_ref[...], where_ref[0], where_ref[1])
    vt_ref[...] = v_ref[...].T
    outs = []
    for head in range(2):
        own = slice(head * HEAD_DIM, (head + 1) * HEAD_DIM)
        query = spread_query(q_ref[...], head)
        top = None
        for span in spans:
            scores = mm(aug_ref[span, head * PAIR : (head + 2) * PAIR], query, NT)
            score_ref[head, span, :] = scores
            high = fold_rows(scores, jnp.max)
            top = high if top is None else jnp.maximum(top, high)
        top = jnp.max(top, axis=0, keepdims=True)
        total = None
        acc = None
        for span in spans:
            probs = jnp.exp2(score_ref[head, span, :] - top)
            part = fold_rows(probs, jnp.sum)
            total = part if total is None else total + part
            part = mm(vt_ref[own, span], probs.astype(BF16))
            acc = part if acc is None else acc + part
        total = jnp.sum(total, axis=0, keepdims=True)
        lse = top + jnp.log2(total)
        if merge:
            before = lse_in_ref[0, head : head + 1, :]
            both = jnp.maximum(lse, before)
            both = both + jnp.log2(jnp.exp2(lse - both) + jnp.exp2(before - both))
            acc = acc * (jnp.exp2(lse - both) / total)
            acc = acc + out_in_ref[own, :] * jnp.exp2(before - both)
            lse = both
        else:
            acc = acc / total
        lse_ref[0, head : head + 1, :] = lse
        outs.append(acc)
    out = jnp.concatenate(outs, axis=0)
    out_ref[...] = out.T if merge else out


def attend(where, query, key, value, before=()):
    tokens, width = query.shape
    keys = key.shape[0]
    pairs = width // PAIR
    column = lambda rows: pl.BlockSpec((rows, PAIR), lambda p, w: (0, p))
    upright = pl.BlockSpec((PAIR, tokens), lambda p, w: (p, 0))
    stats = pl.BlockSpec((1, 2, tokens), lambda p, w: (p, 0, 0))
    merge = len(before) > 0
    return pl.pallas_call(
        functools.partial(attend_kernel, merge),
        grid_spec=pltpu.PrefetchScalarGridSpec(
            num_scalar_prefetch=1,
            grid=(pairs,),
            in_specs=[column(tokens), column(keys), column(keys)] + ([upright, stats] if merge else []),
            out_specs=[column(tokens) if merge else upright, stats],
            scratch_shapes=[
                pltpu.VMEM((keys, 3 * PAIR), BF16),
                pltpu.VMEM((PAIR, keys), BF16),
                pltpu.VMEM((2, keys, tokens), F32),
            ],
        ),
        out_shape=(
            jax.ShapeDtypeStruct((tokens, width) if merge else (width, tokens), F32),
            jax.ShapeDtypeStruct((pairs, 2, tokens), F32),
        ),
        compiler_params=params(48),
        cost_estimate=cost(16 * tokens * keys * width, 2 * tokens * width * 10),
        name="attend_more" if merge else "attend",
    )(where, query, key, value, *before)


def attend_back_kernel(
    add, untouched, where_ref, q_ref, g_ref, o_ref, lse_ref, k_ref, v_ref, *rest
):
    dq_in_ref = rest[0] if add else None
    dq_ref, dk_ref, dv_ref, aug_ref, kt_ref = rest[int(add) + untouched :]
    fill_keys(aug_ref, k_ref[...], where_ref[0], where_ref[1])
    kt_ref[...] = k_ref[...].T
    grad = g_ref[...]
    picks = (
        lax.broadcasted_iota(jnp.int32, (8, PAIR), 1) // HEAD_DIM
        == lax.broadcasted_iota(jnp.int32, (8, PAIR), 0)
    ).astype(F32)
    inner = lax.dot_general(
        picks,
        grad.astype(F32) * o_ref[...],
        NT,
        precision=lax.Precision.HIGHEST,
        preferred_element_type=F32,
    )
    scaled = q_ref[...] * jnp.asarray(HEAD_DIM ** (-0.5), BF16)
    none = jnp.zeros_like(grad)
    masks = [head_mask(grad.shape, head) for head in range(2)]
    queries = [spread_query(q_ref[...], head) for head in range(2)]
    q_heads = [jnp.where(m, scaled, none) for m in masks]
    g_heads = [jnp.where(m, grad, none) for m in masks]
    dqs = [None, None]
    for first in range(0, k_ref.shape[0], KEY_CHUNK):
        span = slice(first, first + KEY_CHUNK)
        dk = None
        dv = None
        for head in range(2):
            own = slice(head * HEAD_DIM, (head + 1) * HEAD_DIM)
            scores = mm(aug_ref[span, head * PAIR : (head + 2) * PAIR], queries[head], NT)
            probs = jnp.exp2(scores - lse_ref[0, head : head + 1, :])
            grad_probs = mm(v_ref[span, :], g_heads[head], NT)
            grad_scores = (probs * (grad_probs - inner[head : head + 1, :])).astype(BF16)
            part = mm(kt_ref[own, span], grad_scores)
            dqs[head] = part if dqs[head] is None else dqs[head] + part
            part = mm(probs.astype(BF16), g_heads[head])
            dv = part if dv is None else dv + part
            part = mm(grad_scores, q_heads[head])
            dk = part if dk is None else dk + part
        dk_ref[span, :] = dk.astype(BF16)
        dv_ref[span, :] = dv.astype(BF16)
    dq = jnp.concatenate(dqs, axis=0).T * HEAD_DIM ** (-0.5)
    if add:
        dq = dq + dq_in_ref[...]
    dq_ref[...] = dq.astype(dq_ref.dtype)


def attend_back(where, query, grad, out, lse, key, value, first, count, before, into):
    tokens, width = query.shape
    keys = key.shape[0]
    column = lambda rows: pl.BlockSpec((rows, PAIR), lambda p, w: (0, p + first))
    untouched = pl.BlockSpec(memory_space=pl.ANY)
    add = len(before) > 0
    given = 7 + len(before)
    return pl.pallas_call(
        functools.partial(attend_back_kernel, add, len(into)),
        grid_spec=pltpu.PrefetchScalarGridSpec(
            num_scalar_prefetch=1,
            grid=(count,),
            in_specs=[column(tokens)] * 3
            + [pl.BlockSpec((1, 2, tokens), lambda p, w: (p + first, 0, 0))]
            + [column(keys)] * 2
            + [column(tokens)] * len(before)
            + [untouched] * len(into),
            out_specs=[column(tokens), column(keys), column(keys)],
            scratch_shapes=[
                pltpu.VMEM((keys, 3 * PAIR), BF16),
                pltpu.VMEM((PAIR, keys), BF16),
            ],
        ),
        out_shape=(
            jax.ShapeDtypeStruct((tokens, width), BF16 if add else F32),
            jax.ShapeDtypeStruct((keys, width), BF16),
            jax.ShapeDtypeStruct((keys, width), BF16),
        ),
        input_output_aliases={given + i: i for i in range(len(into))},
        compiler_params=params(56),
        cost_estimate=cost(40 * tokens * keys * PAIR * count, 2 * tokens * PAIR * count * 12),
        name=("attend_back_more" if add else "attend_back") + str(first),
    )(where, query, grad, out, lse, key, value, *before, *into)


def norm_parts(value):
    centre = jnp.mean(value, axis=-1, keepdims=True)
    centred = value - centre
    variance = jnp.mean(centred * centred, axis=-1, keepdims=True)
    inverse = lax.rsqrt(variance + 1e-05)
    return centred * inverse, inverse


def norm_back(grad, unit, inverse, gain):
    grad_unit = grad * gain
    return inverse * (
        grad_unit
        - jnp.mean(grad_unit, axis=-1, keepdims=True)
        - unit * jnp.mean(grad_unit * unit, axis=-1, keepdims=True)
    )


def middle_kernel(
    ctx_ref,
    emb_ref,
    cot_ref,
    w_out_ref,
    w_up_ref,
    w_down_ref,
    small_ref,
    b_up_ref,
    out_ref,
    ctx_low_ref,
    normed_ref,
    act_ref,
    gffn_ref,
    gpre_ref,
    gattn_ref,
    gone_ref,
    gctx_ref,
    sums_ref,
    up_sums_ref,
    slope_ref,
):
    step = pl.program_id(0)
    width = emb_ref.shape[1]
    wide = w_up_ref.shape[1]

    @pl.when(step == 0)
    def _():
        sums_ref[...] = jnp.zeros_like(sums_ref)
        up_sums_ref[...] = jnp.zeros_like(up_sums_ref)

    b_out, gain_one, shift_one, b_down, gain_two, shift_two = (
        small_ref[i : i + 1, :] for i in range(6)
    )
    ctx_low = ctx_ref[...].astype(BF16)
    ctx_low_ref[...] = ctx_low
    unit_one, inv_one = norm_parts(emb_ref[...] + mm(ctx_low, w_out_ref[...]) + b_out)
    normed = unit_one * gain_one + shift_one
    normed_low = normed.astype(BF16)
    normed_ref[...] = normed_low
    ffn = None
    for c in range(wide // width):
        span = slice(c * width, (c + 1) * width)
        pre = mm(normed_low, w_up_ref[:, span]) + b_up_ref[:, span]
        below = 0.5 * (1.0 + lax.erf(pre * 0.7071067811865476))
        act = (pre * below).astype(BF16)
        act_ref[:, span] = act
        slope_ref[:, span] = below + pre * (0.3989422804014327 * jnp.exp(-0.5 * pre * pre))
        part = mm(act, w_down_ref[span, :])
        ffn = part if ffn is None else ffn + part
    unit_two, inv_two = norm_parts(normed + ffn + b_down)
    out_ref[...] = (unit_two * gain_two + shift_two).astype(BF16)
    grad = cot_ref[...].astype(F32)
    sums_ref[0:8, :] += fold_rows(grad * unit_two, jnp.sum)
    sums_ref[8:16, :] += fold_rows(grad, jnp.sum)
    grad_two = norm_back(grad, unit_two, inv_two, gain_two)
    gffn = grad_two.astype(BF16)
    gffn_ref[...] = gffn
    sums_ref[16:24, :] += fold_rows(gffn.astype(F32), jnp.sum)
    grad_normed = grad_two
    for c in range(wide // width):
        span = slice(c * width, (c + 1) * width)
        gpre = (mm(gffn, w_down_ref[span, :], NT) * slope_ref[:, span]).astype(BF16)
        gpre_ref[:, span] = gpre
        up_sums_ref[:, span] += fold_rows(gpre.astype(F32), jnp.sum)
        grad_normed = grad_normed + mm(gpre, w_up_ref[:, span], NT)
    sums_ref[24:32, :] += fold_rows(grad_normed * unit_one, jnp.sum)
    sums_ref[32:40, :] += fold_rows(grad_normed, jnp.sum)
    grad_one = norm_back(grad_normed, unit_one, inv_one, gain_one)
    gone_ref[...] = grad_one
    gattn = grad_one.astype(BF16)
    gattn_ref[...] = gattn
    sums_ref[40:48, :] += fold_rows(gattn.astype(F32), jnp.sum)
    gctx_ref[...] = mm(gattn, w_out_ref[...], NT).astype(BF16)


def middle(ctx, embedded, cotangent, w_out, w_up, w_down, small, b_up, block=256):
    tokens, width = embedded.shape
    wide = w_up.shape[1]
    whole = lambda a: pl.BlockSpec(a.shape, lambda i: (0, 0), pipeline_mode=pl.Buffered(1))
    rows = lambda n: pl.BlockSpec((block, n), lambda i: (i, 0))
    fixed = lambda r, n: pl.BlockSpec((r, n), lambda i: (0, 0))
    shape = lambda n, dtype: jax.ShapeDtypeStruct((tokens, n), dtype)
    return pl.pallas_call(
        middle_kernel,
        grid=(tokens // block,),
        in_specs=[rows(width)] * 3 + [whole(w_out), whole(w_up), whole(w_down), whole(small), whole(b_up)],
        out_specs=[
            rows(width),
            rows(width),
            rows(width),
            rows(wide),
            rows(width),
            rows(wide),
            rows(width),
            rows(width),
            rows(width),
            fixed(48, width),
            fixed(8, wide),
        ],
        out_shape=[
            shape(width, BF16),
            shape(width, BF16),
            shape(width, BF16),
            shape(wide, BF16),
            shape(width, BF16),
            shape(wide, BF16),
            shape(width, BF16),
            shape(width, F32),
            shape(width, BF16),
            jax.ShapeDtypeStruct((48, width), F32),
            jax.ShapeDtypeStruct((8, wide), F32),
        ],
        scratch_shapes=[pltpu.VMEM((block, wide), F32)],
        compiler_params=params(60),
        cost_estimate=cost(tokens * width * (8 * wide + 4 * width) * 2, 2 * tokens * (2 * wide + 14 * width)),
        name="middle",
    )(ctx, embedded, cotangent, w_out, w_up, w_down, small, b_up)


def cut(value, axis):
    rows = value.shape[0] // 2
    me = lax.axis_index(axis)
    keep = lax.dynamic_slice_in_dim(value, me * rows, rows, 0)
    return keep, lax.dynamic_slice_in_dim(value, (1 - me) * rows, rows, 0)


def halve(value, axis):
    keep, send = cut(value, axis)
    return keep + lax.ppermute(send, axis, SWAP)


def double(value, axis):
    first = lax.axis_index(axis) == 0
    other = lax.ppermute(value, axis, SWAP)
    return jnp.concatenate([jnp.where(first, value, other), jnp.where(first, other, value)], axis=0)


def orders_of(dp_axes):
    core, near, far = dp_axes[-1], dp_axes[-2], dp_axes[-3::-1]
    return (core, near, "seq", *far), (core, "seq", near, *far)


def doubled(pieces, orders):
    for step in reversed(range(len(orders[0]))):
        pieces = [double(p, order[step]) for p, order in zip(pieces, orders)]
    return pieces


def sum_everywhere(value, orders):
    pieces = jnp.split(halve(value, orders[0][0]), 2, axis=0)
    for step in range(1, len(orders[0])):
        pieces = [halve(p, order[step]) for p, order in zip(pieces, orders)]
    pieces = doubled(pieces, [order[1:] for order in orders])
    return double(jnp.concatenate(pieces, axis=0), orders[0][0])


def local(
    dp_axes,
    gene_ids,
    homolog_ids,
    knowledge_ids,
    expr_bins,
    species,
    cell_lengths,
    gene_table,
    knowledge_tables,
    expr_table,
    w_query,
    b_query,
    w_key,
    w_value,
    b_value,
    w_out,
    b_out,
    gain_one,
    shift_one,
    w_up,
    b_up,
    w_down,
    b_down,
    gain_two,
    shift_two,
    cotangent,
):
    tokens = gene_ids.shape[1]
    rows_dev, width = gene_table.shape
    wide = w_up.shape[1]
    every = (*dp_axes, "seq")
    top_axis, group_axes = dp_axes[0], (*dp_axes[1:], "seq")
    devices = lax.axis_size(every)
    group = devices // 2
    capacity = 2 * tokens // devices
    slots_all = 2 * capacity
    slots = group * slots_all
    bins = expr_table.shape[0]
    me = lax.axis_index("seq")

    def exchange(value, axis):
        return lax.all_to_all(value, group_axes, split_axis=axis, concat_axis=axis, tiled=True)

    gene_table, knowledge_tables = lax.optimization_barrier((gene_table, knowledge_tables))
    gene_other = lax.ppermute(gene_table, top_axis, SWAP)
    know_sum = jnp.sum(knowledge_tables.astype(F32), axis=0).astype(BF16)
    chosen = jnp.where(species[0] == 1, homolog_ids, gene_ids).reshape(-1)
    requests, gene_slot, know_slot = route(
        lax.axis_index(top_axis), chosen, knowledge_ids.reshape(-1), rows_dev, capacity, devices
    )
    asked = exchange(requests.reshape(2, group, slots_all), 1).reshape(2, slots)
    know_other = lax.ppermute(know_sum, top_axis, SWAP)
    asked, gene_other, know_other = lax.optimization_barrier((asked, gene_other, know_other))
    tables = [
        jnp.concatenate([gene_table, know_sum], axis=0),
        jnp.concatenate([gene_other, know_other], axis=0),
    ]
    row_at = jnp.arange(2 * rows_dev)
    slot_at = jnp.arange(slots)
    bin_hot = hot(expr_bins.reshape(-1)[:, None], jnp.arange(bins)[None, :])
    embedded = mm(bin_hot, expr_table)
    slot_hots = []
    for part in range(2):
        found = mm(hot(asked[part][:, None], row_at[None, :]), tables[part]).astype(BF16)
        fetched = exchange(found.reshape(group, slots_all, width), 0).reshape(slots, width)
        at = slot_at[None, :] + part * slots
        slot_hots.append(((at == gene_slot) | (at == know_slot)).astype(BF16))
        embedded = embedded + mm(slot_hots[part], fetched)
    x_low = embedded.astype(BF16)

    x_other = lax.ppermute(x_low, "seq", SWAP)
    query = (mm(x_low, w_query) + b_query).astype(BF16)
    key, key_other = (mm(x, w_key).astype(BF16) for x in (x_low, x_other))
    value, value_other = ((mm(x, w_value) + b_value).astype(BF16) for x in (x_low, x_other))
    mine = jnp.stack([me * tokens, cell_lengths[0]]).astype(jnp.int32)
    others = jnp.stack([(1 - me) * tokens, cell_lengths[0]]).astype(jnp.int32)
    context, lse = attend(
        others, query, key_other, value_other, attend(mine, query, key, value)
    )

    small = jnp.stack([b_out, gain_one, shift_one, b_down, gain_two, shift_two])
    (
        layer_output,
        ctx_low,
        normed_low,
        activated,
        grad_ffn,
        grad_pre,
        grad_attn,
        grad_one,
        grad_ctx,
        sums,
        up_sums,
    ) = middle(
        context, embedded, cotangent.reshape(tokens, width), w_out, w_up, w_down, small, b_up[None, :]
    )

    orders = orders_of(dp_axes)
    step = 0
    ffn_grads = [mm(activated, grad_ffn, TN).astype(BF16), mm(normed_low, grad_pre, TN).astype(BF16)]
    ffn_grads, grad_ctx = lax.optimization_barrier((ffn_grads, grad_ctx))
    w_out_grad = mm(ctx_low, grad_attn, TN)
    ffn_grads = [halve(g, order[0]) for g, order in zip(ffn_grads, orders)]
    pairs = width // PAIR
    sides = ((others, key_other, value_other), (mine, key, value))
    grads = []
    before = ()
    dx_from_other = None
    for side, (place, keys, values) in enumerate(sides):
        into = ()
        for part in range(2):
            step += 1
            cuts = [cut(g, order[step]) for g, order in zip(ffn_grads, orders)]
            cuts, grad_ctx, into, before = lax.optimization_barrier((cuts, grad_ctx, into, before))
            arrived = [lax.ppermute(c[1], order[step], SWAP) for c, order in zip(cuts, orders)]
            into = attend_back(
                place,
                query,
                grad_ctx,
                context,
                lse,
                keys,
                values,
                part * pairs // 2,
                pairs // 2,
                before,
                into,
            )
            arrived, into = lax.optimization_barrier((arrived, into))
            ffn_grads = [c[0] + a for c, a in zip(cuts, arrived)]
        grads.append(into)
        if side == 0:
            before = into[:1]
            dx_other = (mm(into[1], w_key, NT) + mm(into[2], w_value, NT)).astype(BF16)
            dx_other, before = lax.optimization_barrier((dx_other, before))
            dx_from_other = lax.ppermute(dx_other, "seq", SWAP)
    for order_step in range(step + 1, len(orders[0])):
        ffn_grads = [halve(g, order[order_step]) for g, order in zip(ffn_grads, orders)]
    (_, dk_other, dv_other), (dq, dk, dv) = grads
    dq, dk, dv, dx_from_other = lax.optimization_barrier((dq, dk, dv, dx_from_other))
    grad_embedded = (
        grad_one
        + mm(dq, w_query, NT)
        + mm(dk, w_key, NT)
        + mm(dv, w_value, NT)
        + dx_from_other.astype(F32)
    )
    grad_low = grad_embedded.astype(BF16)

    owned = [row_at[:, None] == asked[part][None, :] for part in range(2)]
    counts = [jnp.sum(o.astype(jnp.int32), axis=1) for o in owned]
    row_counts = counts[0] + lax.ppermute(counts[1], top_axis, SWAP)
    outgoing = [mm(hots, grad_low, TN).astype(BF16) for hots in slot_hots]
    outgoing, dq, dk, dv = lax.optimization_barrier((outgoing, dq, dk, dv))
    returned = [
        exchange(rows.reshape(group, slots_all, width), 0).reshape(slots, width)
        for rows in outgoing[::-1]
    ][::-1]

    w_query_grad = mm(x_low, dq, TN)
    w_key_grad = mm(x_low, dk, TN) + mm(x_other, dk_other, TN)
    w_value_grad = mm(x_low, dv, TN) + mm(x_other, dv_other, TN)
    b_query_grad = jnp.sum(dq.astype(F32), axis=0)
    b_value_grad = jnp.sum(dv.astype(F32), axis=0) + jnp.sum(dv_other.astype(F32), axis=0)
    grad_rest = (grad_embedded - grad_low.astype(F32)).astype(BF16)
    expr_grad = mm(bin_hot, grad_low, TN) + mm(bin_hot, grad_rest, TN)
    short = jnp.concatenate(
        [
            jnp.sum(sums.reshape(6, 8, width), axis=1),
            jnp.sum(up_sums, axis=0).reshape(wide // width, width),
            b_query_grad[None, :],
            b_value_grad[None, :],
        ],
        axis=0,
    )
    short = jnp.pad(short, ((0, -short.shape[0] % 16), (0, 0)))
    late = [w_query_grad, w_key_grad, w_value_grad, w_out_grad, expr_grad, short]
    heights = [item.shape[0] for item in late]
    late.append(jnp.zeros((-sum(heights) % 512, width), F32))
    late = jnp.concatenate([item.astype(BF16) for item in late], axis=0)
    returned, late, ffn_grads = lax.optimization_barrier((returned, late, ffn_grads))
    table_parts = [mm(owned[part].astype(BF16), returned[part]) for part in range(2)]
    table_grads = table_parts[0] + lax.ppermute(
        table_parts[1].astype(BF16), top_axis, SWAP
    ).astype(F32)
    late = sum_everywhere(late, orders)
    w_down_grad, w_up_grad = (g.astype(F32) for g in doubled(ffn_grads, orders))
    taken = []
    for height in heights:
        at = sum(item.shape[0] for item in taken)
        taken.append(late[at : at + height].astype(F32))
    w_query_grad, w_key_grad, w_value_grad, w_out_grad, expr_grad, short = taken
    gain_two_grad, shift_two_grad, b_down_grad, gain_one_grad, shift_one_grad, b_out_grad = (
        short[i] for i in range(6)
    )
    b_up_grad = short[6 : 6 + wide // width].reshape(wide)
    b_query_grad, b_value_grad = short[6 + wide // width], short[7 + wide // width]
    return (
        layer_output.reshape(1, tokens, width),
        table_grads[:rows_dev],
        table_grads[rows_dev:],
        expr_grad,
        w_query_grad,
        b_query_grad,
        w_key_grad,
        w_value_grad,
        b_value_grad,
        w_out_grad,
        b_out_grad,
        gain_one_grad,
        shift_one_grad,
        w_up_grad,
        b_up_grad,
        w_down_grad,
        b_down_grad,
        gain_two_grad,
        shift_two_grad,
        row_counts.reshape(2, rows_dev),
    )


def solution(mesh):
    bits = mesh.shape["dp"].bit_length() - 1
    dp_axes = tuple(f"dp{i}" for i in range(bits))
    fine = Mesh(mesh.devices.reshape((2,) * bits + (mesh.shape["seq"],)), (*dp_axes, "seq"))
    every = (*dp_axes, "seq")
    whole = P()
    placed = (
        (P(dp_axes, "seq"),) * 4
        + (P(dp_axes),) * 2
        + (P(every, None), P(None, every, None))
        + (whole,) * 16
        + (P(dp_axes, "seq", None),)
    )
    given = (
        (P(dp_axes, "seq", None),)
        + (P(every, None),) * 2
        + (whole,) * 16
        + (P(None, every),)
    )
    return jax.shard_map(
        functools.partial(local, dp_axes), mesh=fine, in_specs=placed, out_specs=given, check_vma=False
    )
```

```python
import functools

import jax
import jax.numpy as jnp
from jax import lax
from jax.experimental import pallas as pl
from jax.experimental.pallas import tpu as pltpu
from jax.sharding import Mesh, PartitionSpec as P

HEADS = 12
HEAD_DIM = 64
PAIR = 2 * HEAD_DIM
KEY_CHUNK = 512
LOG2E = 1.4426950408889634
SWAP = [(0, 1), (1, 0)]
F32 = jnp.float32
BF16 = jnp.bfloat16
NN = (((1,), (0,)), ((), ()))
NT = (((1,), (1,)), ((), ()))
TN = (((0,), (0,)), ((), ()))


def mm(left, right, dims=NN):
    return lax.dot_general(left, right, dims, preferred_element_type=F32)


def params(mib):
    return pltpu.CompilerParams(vmem_limit_bytes=mib * 2**20)


def cost(flops, moved):
    return pl.CostEstimate(flops=flops, bytes_accessed=moved, transcendentals=0)


def hot(left, right):
    return (left == right).astype(BF16)


def route_kernel(
    rows_dev, capacity, top_ref, gene_ref, know_ref, req_ref, gene_slot_ref, know_slot_ref
):
    tokens = gene_ref.shape[0]
    devices, slots_all = req_ref.shape
    group = devices // 2
    lane = lax.broadcasted_iota(jnp.int32, (tokens, devices), 1)
    mine = lane < group
    top = top_ref[0]
    first = jnp.where(mine, lane + top * group, lane - top * group) * rows_dev
    earlier = (
        lax.broadcasted_iota(jnp.int32, (tokens, tokens), 0)
        > lax.broadcasted_iota(jnp.int32, (tokens, tokens), 1)
    ).astype(F32).astype(BF16)
    rank_lane = lax.broadcasted_iota(jnp.int32, (tokens, capacity), 1)
    asked = []
    for which, (ids_ref, slot_ref) in enumerate(((gene_ref, gene_slot_ref), (know_ref, know_slot_ref))):
        row = ids_ref[...] - first
        hit = (row >= 0) & (row < rows_dev)
        before = mm(earlier, hit.astype(F32).astype(BF16))
        rank = jnp.sum(jnp.where(hit, before, 0.0), axis=1, keepdims=True)
        owner = jnp.sum(jnp.where(hit, lane, 0).astype(F32), axis=1, keepdims=True)
        slot_ref[...] = (owner * slots_all + rank).astype(jnp.int32) + which * capacity
        rank_hit = (rank_lane == rank.astype(jnp.int32)).astype(F32).astype(BF16)
        coded = jnp.where(hit, row + 1, 0)
        high = (coded >> 4).astype(F32).astype(BF16)
        low = (coded & 15).astype(F32).astype(BF16)
        wanted = (mm(high, rank_hit, TN) * 16.0 + mm(low, rank_hit, TN)).astype(jnp.int32)
        asked.append(jnp.where(wanted > 0, wanted - 1 + which * rows_dev, -1))
    req_ref[:, :capacity] = asked[0]
    req_ref[:, capacity:] = asked[1]


def route(top, gene_ids, know_ids, rows_dev, capacity, devices):
    tokens = gene_ids.shape[0]
    return pl.pallas_call(
        functools.partial(route_kernel, rows_dev, capacity),
        in_specs=[pl.BlockSpec(memory_space=pltpu.SMEM)] + [pl.BlockSpec(memory_space=pltpu.VMEM)] * 2,
        out_shape=(
            jax.ShapeDtypeStruct((devices, 2 * capacity), jnp.int32),
            jax.ShapeDtypeStruct((tokens, 1), jnp.int32),
            jax.ShapeDtypeStruct((tokens, 1), jnp.int32),
        ),
        compiler_params=params(32),
        name="route",
    )(top.reshape(1), gene_ids[:, None], know_ids[:, None])


def fill_keys(aug_ref, key, first_key, count):
    lanes = lax.broadcasted_iota(jnp.int32, key.shape, 1)
    at = lax.broadcasted_iota(jnp.int32, key.shape, 0) + first_key
    bias = jnp.where(at < count, 0.0, -1e30).astype(BF16)
    none = jnp.zeros_like(key)
    aug_ref[:, :PAIR] = jnp.where(lanes < HEAD_DIM, key, jnp.where(lanes == HEAD_DIM, bias, none))
    aug_ref[:, PAIR : 2 * PAIR] = key
    aug_ref[:, 2 * PAIR :] = jnp.where(lanes >= HEAD_DIM, key, jnp.where(lanes == 0, bias, none))


def head_mask(shape, head):
    lanes = lax.broadcasted_iota(jnp.int32, shape, 1)
    return (lanes >= head * HEAD_DIM) & (lanes < (head + 1) * HEAD_DIM)


def spread_query(query, head):
    lanes = lax.broadcasted_iota(jnp.int32, query.shape, 1)
    scaled = query.astype(F32) * (HEAD_DIM ** (-0.5) * LOG2E)
    scaled = jnp.where(head_mask(query.shape, head), scaled, 0.0)
    high = scaled.astype(BF16)
    low = scaled - high.astype(F32)
    low = jnp.where(lanes == (1 - head) * HEAD_DIM, 1.0, low).astype(BF16)
    return jnp.concatenate([low, high] if head == 0 else [high, low], axis=1)


def fold_rows(value, how):
    return how(value.reshape(value.shape[0] // 8, 8, value.shape[1]), axis=0)


def attend_kernel(merge, where_ref, q_ref, k_ref, v_ref, *rest):
    if merge:
        out_in_ref, lse_in_ref, out_ref, lse_ref, aug_ref, vt_ref, score_ref = rest
    else:
        out_ref, lse_ref, aug_ref, vt_ref, score_ref = rest
    spans = [slice(c, c + KEY_CHUNK) for c in range(0, k_ref.shape[0], KEY_CHUNK)]
    fill_keys(aug_ref, k_ref[...], where_ref[0], where_ref[1])
    vt_ref[...] = v_ref[...].T
    outs = []
    for head in range(2):
        own = slice(head * HEAD_DIM, (head + 1) * HEAD_DIM)
        query = spread_query(q_ref[...], head)
        top = None
        for span in spans:
            scores = mm(aug_ref[span, head * PAIR : (head + 2) * PAIR], query, NT)
            score_ref[head, span, :] = scores
            high = fold_rows(scores, jnp.max)
            top = high if top is None else jnp.maximum(top, high)
        top = jnp.max(top, axis=0, keepdims=True)
        total = None
        acc = None
        for span in spans:
            probs = jnp.exp2(score_ref[head, span, :] - top)
            part = fold_rows(probs, jnp.sum)
            total = part if total is None else total + part
            part = mm(vt_ref[own, span], probs.astype(BF16))
            acc = part if acc is None else acc + part
        total = jnp.sum(total, axis=0, keepdims=True)
        lse = top + jnp.log2(total)
        if merge:
            before = lse_in_ref[0, head : head + 1, :]
            both = jnp.maximum(lse, before)
            both = both + jnp.log2(jnp.exp2(lse - both) + jnp.exp2(before - both))
            acc = acc * (jnp.exp2(lse - both) / total)
            acc = acc + out_in_ref[own, :] * jnp.exp2(before - both)
            lse = both
        else:
            acc = acc / total
        lse_ref[0, head : head + 1, :] = lse
        outs.append(acc)
    out = jnp.concatenate(outs, axis=0)
    out_ref[...] = out.T if merge else out


def attend(where, query, key, value, before=()):
    tokens, width = query.shape
    keys = key.shape[0]
    pairs = width // PAIR
    column = lambda rows: pl.BlockSpec((rows, PAIR), lambda p, w: (0, p))
    upright = pl.BlockSpec((PAIR, tokens), lambda p, w: (p, 0))
    stats = pl.BlockSpec((1, 2, tokens), lambda p, w: (p, 0, 0))
    merge = len(before) > 0
    return pl.pallas_call(
        functools.partial(attend_kernel, merge),
        grid_spec=pltpu.PrefetchScalarGridSpec(
            num_scalar_prefetch=1,
            grid=(pairs,),
            in_specs=[column(tokens), column(keys), column(keys)] + ([upright, stats] if merge else []),
            out_specs=[column(tokens) if merge else upright, stats],
            scratch_shapes=[
                pltpu.VMEM((keys, 3 * PAIR), BF16),
                pltpu.VMEM((PAIR, keys), BF16),
                pltpu.VMEM((2, keys, tokens), F32),
            ],
        ),
        out_shape=(
            jax.ShapeDtypeStruct((tokens, width) if merge else (width, tokens), F32),
            jax.ShapeDtypeStruct((pairs, 2, tokens), F32),
        ),
        compiler_params=params(48),
        cost_estimate=cost(16 * tokens * keys * width, 2 * tokens * width * 10),
        name="attend_more" if merge else "attend",
    )(where, query, key, value, *before)


def attend_back_kernel(
    add, untouched, where_ref, q_ref, g_ref, o_ref, lse_ref, k_ref, v_ref, *rest
):
    dq_in_ref = rest[0] if add else None
    dq_ref, dk_ref, dv_ref, aug_ref, kt_ref = rest[int(add) + untouched :]
    fill_keys(aug_ref, k_ref[...], where_ref[0], where_ref[1])
    kt_ref[...] = k_ref[...].T
    grad = g_ref[...]
    picks = (
        lax.broadcasted_iota(jnp.int32, (8, PAIR), 1) // HEAD_DIM
        == lax.broadcasted_iota(jnp.int32, (8, PAIR), 0)
    ).astype(F32)
    inner = lax.dot_general(
        picks,
        grad.astype(F32) * o_ref[...],
        NT,
        precision=lax.Precision.HIGHEST,
        preferred_element_type=F32,
    )
    scaled = q_ref[...] * jnp.asarray(HEAD_DIM ** (-0.5), BF16)
    none = jnp.zeros_like(grad)
    masks = [head_mask(grad.shape, head) for head in range(2)]
    queries = [spread_query(q_ref[...], head) for head in range(2)]
    q_heads = [jnp.where(m, scaled, none) for m in masks]
    g_heads = [jnp.where(m, grad, none) for m in masks]
    dqs = [None, None]
    for first in range(0, k_ref.shape[0], KEY_CHUNK):
        span = slice(first, first + KEY_CHUNK)
        dk = None
        dv = None
        for head in range(2):
            own = slice(head * HEAD_DIM, (head + 1) * HEAD_DIM)
            scores = mm(aug_ref[span, head * PAIR : (head + 2) * PAIR], queries[head], NT)
            probs = jnp.exp2(scores - lse_ref[0, head : head + 1, :])
            grad_probs = mm(v_ref[span, :], g_heads[head], NT)
            grad_scores = (probs * (grad_probs - inner[head : head + 1, :])).astype(BF16)
            part = mm(kt_ref[own, span], grad_scores)
            dqs[head] = part if dqs[head] is None else dqs[head] + part
            part = mm(probs.astype(BF16), g_heads[head])
            dv = part if dv is None else dv + part
            part = mm(grad_scores, q_heads[head])
            dk = part if dk is None else dk + part
        dk_ref[span, :] = dk.astype(BF16)
        dv_ref[span, :] = dv.astype(BF16)
    dq = jnp.concatenate(dqs, axis=0).T * HEAD_DIM ** (-0.5)
    if add:
        dq = dq + dq_in_ref[...]
    dq_ref[...] = dq.astype(dq_ref.dtype)


def attend_back(where, query, grad, out, lse, key, value, first, count, before, into):
    tokens, width = query.shape
    keys = key.shape[0]
    column = lambda rows: pl.BlockSpec((rows, PAIR), lambda p, w: (0, p + first))
    untouched = pl.BlockSpec(memory_space=pl.ANY)
    add = len(before) > 0
    given = 7 + len(before)
    return pl.pallas_call(
        functools.partial(attend_back_kernel, add, len(into)),
        grid_spec=pltpu.PrefetchScalarGridSpec(
            num_scalar_prefetch=1,
            grid=(count,),
            in_specs=[column(tokens)] * 3
            + [pl.BlockSpec((1, 2, tokens), lambda p, w: (p + first, 0, 0))]
            + [column(keys)] * 2
            + [column(tokens)] * len(before)
            + [untouched] * len(into),
            out_specs=[column(tokens), column(keys), column(keys)],
            scratch_shapes=[
                pltpu.VMEM((keys, 3 * PAIR), BF16),
                pltpu.VMEM((PAIR, keys), BF16),
            ],
        ),
        out_shape=(
            jax.ShapeDtypeStruct((tokens, width), BF16 if add else F32),
            jax.ShapeDtypeStruct((keys, width), BF16),
            jax.ShapeDtypeStruct((keys, width), BF16),
        ),
        input_output_aliases={given + i: i for i in range(len(into))},
        compiler_params=params(56),
        cost_estimate=cost(40 * tokens * keys * PAIR * count, 2 * tokens * PAIR * count * 12),
        name=("attend_back_more" if add else "attend_back") + str(first),
    )(where, query, grad, out, lse, key, value, *before, *into)


def norm_parts(value):
    centre = jnp.mean(value, axis=-1, keepdims=True)
    centred = value - centre
    variance = jnp.mean(centred * centred, axis=-1, keepdims=True)
    inverse = lax.rsqrt(variance + 1e-05)
    return centred * inverse, inverse


def norm_back(grad, unit, inverse, gain):
    grad_unit = grad * gain
    return inverse * (
        grad_unit
        - jnp.mean(grad_unit, axis=-1, keepdims=True)
        - unit * jnp.mean(grad_unit * unit, axis=-1, keepdims=True)
    )


def middle_kernel(
    ctx_ref,
    emb_ref,
    cot_ref,
    w_out_ref,
    w_up_ref,
    w_down_ref,
    small_ref,
    b_up_ref,
    out_ref,
    ctx_low_ref,
    normed_ref,
    act_ref,
    gffn_ref,
    gpre_ref,
    gattn_ref,
    gone_ref,
    gctx_ref,
    sums_ref,
    up_sums_ref,
    slope_ref,
):
    step = pl.program_id(0)
    width = emb_ref.shape[1]
    wide = w_up_ref.shape[1]

    @pl.when(step == 0)
    def _():
        sums_ref[...] = jnp.zeros_like(sums_ref)
        up_sums_ref[...] = jnp.zeros_like(up_sums_ref)

    b_out, gain_one, shift_one, b_down, gain_two, shift_two = (
        small_ref[i : i + 1, :] for i in range(6)
    )
    ctx_low = ctx_ref[...].astype(BF16)
    ctx_low_ref[...] = ctx_low
    unit_one, inv_one = norm_parts(emb_ref[...] + mm(ctx_low, w_out_ref[...]) + b_out)
    normed = unit_one * gain_one + shift_one
    normed_low = normed.astype(BF16)
    normed_ref[...] = normed_low
    ffn = None
    for c in range(wide // width):
        span = slice(c * width, (c + 1) * width)
        pre = mm(normed_low, w_up_ref[:, span]) + b_up_ref[:, span]
        below = 0.5 * (1.0 + lax.erf(pre * 0.7071067811865476))
        act = (pre * below).astype(BF16)
        act_ref[:, span] = act
        slope_ref[:, span] = below + pre * (0.3989422804014327 * jnp.exp(-0.5 * pre * pre))
        part = mm(act, w_down_ref[span, :])
        ffn = part if ffn is None else ffn + part
    unit_two, inv_two = norm_parts(normed + ffn + b_down)
    out_ref[...] = (unit_two * gain_two + shift_two).astype(BF16)
    grad = cot_ref[...].astype(F32)
    sums_ref[0:8, :] += fold_rows(grad * unit_two, jnp.sum)
    sums_ref[8:16, :] += fold_rows(grad, jnp.sum)
    grad_two = norm_back(grad, unit_two, inv_two, gain_two)
    gffn = grad_two.astype(BF16)
    gffn_ref[...] = gffn
    sums_ref[16:24, :] += fold_rows(gffn.astype(F32), jnp.sum)
    grad_normed = grad_two
    for c in range(wide // width):
        span = slice(c * width, (c + 1) * width)
        gpre = (mm(gffn, w_down_ref[span, :], NT) * slope_ref[:, span]).astype(BF16)
        gpre_ref[:, span] = gpre
        up_sums_ref[:, span] += fold_rows(gpre.astype(F32), jnp.sum)
        grad_normed = grad_normed + mm(gpre, w_up_ref[:, span], NT)
    sums_ref[24:32, :] += fold_rows(grad_normed * unit_one, jnp.sum)
    sums_ref[32:40, :] += fold_rows(grad_normed, jnp.sum)
    grad_one = norm_back(grad_normed, unit_one, inv_one, gain_one)
    gone_ref[...] = grad_one
    gattn = grad_one.astype(BF16)
    gattn_ref[...] = gattn
    sums_ref[40:48, :] += fold_rows(gattn.astype(F32), jnp.sum)
    gctx_ref[...] = mm(gattn, w_out_ref[...], NT).astype(BF16)


def middle(ctx, embedded, cotangent, w_out, w_up, w_down, small, b_up, block=256):
    tokens, width = embedded.shape
    wide = w_up.shape[1]
    whole = lambda a: pl.BlockSpec(a.shape, lambda i: (0, 0), pipeline_mode=pl.Buffered(1))
    rows = lambda n: pl.BlockSpec((block, n), lambda i: (i, 0))
    fixed = lambda r, n: pl.BlockSpec((r, n), lambda i: (0, 0))
    shape = lambda n, dtype: jax.ShapeDtypeStruct((tokens, n), dtype)
    return pl.pallas_call(
        middle_kernel,
        grid=(tokens // block,),
        in_specs=[rows(width)] * 3 + [whole(w_out), whole(w_up), whole(w_down), whole(small), whole(b_up)],
        out_specs=[
            rows(width),
            rows(width),
            rows(width),
            rows(wide),
            rows(width),
            rows(wide),
            rows(width),
            rows(width),
            rows(width),
            fixed(48, width),
            fixed(8, wide),
        ],
        out_shape=[
            shape(width, BF16),
            shape(width, BF16),
            shape(width, BF16),
            shape(wide, BF16),
            shape(width, BF16),
            shape(wide, BF16),
            shape(width, BF16),
            shape(width, F32),
            shape(width, BF16),
            jax.ShapeDtypeStruct((48, width), F32),
            jax.ShapeDtypeStruct((8, wide), F32),
        ],
        scratch_shapes=[pltpu.VMEM((block, wide), F32)],
        compiler_params=params(60),
        cost_estimate=cost(tokens * width * (8 * wide + 4 * width) * 2, 2 * tokens * (2 * wide + 14 * width)),
        name="middle",
    )(ctx, embedded, cotangent, w_out, w_up, w_down, small, b_up)


def weight_sums_kernel(counts, half_ref, act_ref, gffn_ref, gpre_ref, norm_ref, ctx_ref, gattn_ref, out_ref):
    at = pl.program_id(0) + half_ref[0] * pl.num_programs(0)
    first = 0
    for count, left, right in zip(counts, (act_ref, gpre_ref, ctx_ref), (gffn_ref, norm_ref, gattn_ref)):
        @pl.when((at >= first) & (at < first + count))
        def _(left=left, right=right):
            out_ref[...] = mm(left[...], right[...], TN).astype(BF16)
        first += count


def weight_sums(half, activated, grad_ffn, grad_pre, normed, ctx, grad_attn, block=384):
    tokens, width = grad_ffn.shape
    lefts = (activated, grad_pre, ctx)
    counts = [left.shape[1] // block for left in lefts]
    steps = sum(counts) // 2
    specs = []
    first = 0
    for left, right, count in zip(lefts, (grad_ffn, normed, grad_attn), counts):
        specs.append(
            pl.BlockSpec(
                (tokens, block),
                lambda i, h, first=first, count=count: (0, jnp.clip(i + h[0] * steps - first, 0, count - 1)),
            )
        )
        specs.append(pl.BlockSpec((tokens, width), lambda i, h: (0, 0), pipeline_mode=pl.Buffered(1)))
        first += count
    return pl.pallas_call(
        functools.partial(weight_sums_kernel, counts),
        grid_spec=pltpu.PrefetchScalarGridSpec(
            num_scalar_prefetch=1,
            grid=(steps,),
            in_specs=specs,
            out_specs=pl.BlockSpec((block, width), lambda i, h: (i, 0)),
        ),
        out_shape=jax.ShapeDtypeStruct((steps * block, width), BF16),
        compiler_params=params(40),
        cost_estimate=cost(2 * tokens * width * block * steps, 2 * steps * block * (tokens + width)),
        name="weight_sums",
    )(half.reshape(1), activated, grad_ffn, grad_pre, normed, ctx, grad_attn)


def cut(value, axis):
    rows = value.shape[0] // 2
    me = lax.axis_index(axis)
    keep = lax.dynamic_slice_in_dim(value, me * rows, rows, 0)
    return keep, lax.dynamic_slice_in_dim(value, (1 - me) * rows, rows, 0)


def swap(value, axis):
    return lax.ppermute(value, axis, SWAP)


def join(value, other, axis):
    first = lax.axis_index(axis) == 0
    return jnp.concatenate([jnp.where(first, value, other), jnp.where(first, other, value)], axis=0)


def stages_of(dp_axes):
    near, far = dp_axes[-2], dp_axes[-3::-1]
    down = [((near, "seq"), True), (("seq", near), True)] + [((axis,), True) for axis in far]
    return down + [(axes, False) for axes, _ in down[::-1]]


def begin(pieces, stage):
    axes, halves = stage
    if len(pieces) < len(axes):
        pieces = jnp.split(pieces[0], 2, axis=0)
    if len(pieces) > len(axes):
        pieces = [jnp.concatenate(pieces, axis=0)]
    if halves:
        keeps, sends = zip(*(cut(p, axis) for p, axis in zip(pieces, axes)))
        return list(keeps), list(sends)
    return list(pieces), list(pieces)


def travel(sends, stage):
    return [swap(s, axis) for s, axis in zip(sends, stage[0])]


def end(keeps, arrived, stage):
    axes, halves = stage
    if halves:
        return [k + a for k, a in zip(keeps, arrived)]
    return [join(k, a, axis) for k, a, axis in zip(keeps, arrived, axes)]


def run_stages(pieces, stages):
    for stage in stages:
        keeps, sends = begin(pieces, stage)
        pieces = end(keeps, travel(sends, stage), stage)
    return pieces


def local(
    dp_axes,
    gene_ids,
    homolog_ids,
    knowledge_ids,
    expr_bins,
    species,
    cell_lengths,
    gene_table,
    knowledge_tables,
    expr_table,
    w_query,
    b_query,
    w_key,
    w_value,
    b_value,
    w_out,
    b_out,
    gain_one,
    shift_one,
    w_up,
    b_up,
    w_down,
    b_down,
    gain_two,
    shift_two,
    cotangent,
):
    tokens = gene_ids.shape[1]
    rows_dev, width = gene_table.shape
    wide = w_up.shape[1]
    every = (*dp_axes, "seq")
    top_axis, group_axes = dp_axes[0], (*dp_axes[1:], "seq")
    devices = lax.axis_size(every)
    group = devices // 2
    capacity = 2 * tokens // devices
    slots_all = 2 * capacity
    slots = group * slots_all
    bins = expr_table.shape[0]
    me = lax.axis_index("seq")

    def exchange(value, axis):
        return lax.all_to_all(value, group_axes, split_axis=axis, concat_axis=axis, tiled=True)

    gene_table, knowledge_tables = lax.optimization_barrier((gene_table, knowledge_tables))
    gene_other = lax.ppermute(gene_table, top_axis, SWAP)
    know_sum = jnp.sum(knowledge_tables.astype(F32), axis=0).astype(BF16)
    chosen = jnp.where(species[0] == 1, homolog_ids, gene_ids).reshape(-1)
    requests, gene_slot, know_slot = route(
        lax.axis_index(top_axis), chosen, knowledge_ids.reshape(-1), rows_dev, capacity, devices
    )
    asked = exchange(requests.reshape(2, group, slots_all), 1).reshape(2, slots)
    know_other = lax.ppermute(know_sum, top_axis, SWAP)
    asked, gene_other, know_other = lax.optimization_barrier((asked, gene_other, know_other))
    tables = [
        jnp.concatenate([gene_table, know_sum], axis=0),
        jnp.concatenate([gene_other, know_other], axis=0),
    ]
    row_at = jnp.arange(2 * rows_dev)
    slot_at = jnp.arange(slots)
    bin_hot = hot(expr_bins.reshape(-1)[:, None], jnp.arange(bins)[None, :])
    embedded = mm(bin_hot, expr_table)
    slot_hots = []
    for part in range(2):
        found = mm(hot(asked[part][:, None], row_at[None, :]), tables[part]).astype(BF16)
        fetched = exchange(found.reshape(group, slots_all, width), 0).reshape(slots, width)
        at = slot_at[None, :] + part * slots
        slot_hots.append(((at == gene_slot) | (at == know_slot)).astype(BF16))
        embedded = embedded + mm(slot_hots[part], fetched)
    x_low = embedded.astype(BF16)

    x_other = lax.ppermute(x_low, "seq", SWAP)
    query = (mm(x_low, w_query) + b_query).astype(BF16)
    key, key_other = (mm(x, w_key).astype(BF16) for x in (x_low, x_other))
    value, value_other = ((mm(x, w_value) + b_value).astype(BF16) for x in (x_low, x_other))
    mine = jnp.stack([me * tokens, cell_lengths[0]]).astype(jnp.int32)
    others = jnp.stack([(1 - me) * tokens, cell_lengths[0]]).astype(jnp.int32)
    owned = [row_at[:, None] == asked[part][None, :] for part in range(2)]
    counts = [jnp.sum(o.astype(jnp.int32), axis=1) for o in owned]
    counts_back = lax.ppermute(counts[1], top_axis, SWAP)
    first_part = attend(mine, query, key, value)
    first_part, counts_back = lax.optimization_barrier((first_part, counts_back))
    row_counts = counts[0] + counts_back
    context, lse = attend(others, query, key_other, value_other, first_part)

    small = jnp.stack([b_out, gain_one, shift_one, b_down, gain_two, shift_two])
    (
        layer_output,
        ctx_low,
        normed_low,
        activated,
        grad_ffn,
        grad_pre,
        grad_attn,
        grad_one,
        grad_ctx,
        sums,
        up_sums,
    ) = middle(
        context, embedded, cotangent.reshape(tokens, width), w_out, w_up, w_down, small, b_up[None, :]
    )

    core = dp_axes[-1]
    stages = stages_of(dp_axes)
    my_core = lax.axis_index(core)
    lefts_rights = (activated, grad_ffn, grad_pre, normed_low, ctx_low, grad_attn)
    sent = weight_sums(1 - my_core, *lefts_rights)
    sent, lefts_rights = lax.optimization_barrier((sent, lefts_rights))
    arrived = swap(sent, core)
    kept = weight_sums(my_core, *lefts_rights)
    kept, arrived, grad_ctx = lax.optimization_barrier((kept, arrived, grad_ctx))
    early = jnp.split(kept + arrived, 2, axis=0)
    pairs = width // PAIR
    third = pairs // 3
    sides = ((others, key_other, value_other), (mine, key, value))
    parts = (((0, 2 * third), (2 * third, third)), ((0, third), (third, third), (2 * third, third)))
    done = 0
    grads = []
    before = ()
    for side, (place, keys, values) in enumerate(sides):
        into = ()
        for first, count in parts[side]:
            keeps, sends = begin(early, stages[done])
            keeps, sends, grad_ctx, into, before = lax.optimization_barrier(
                (keeps, sends, grad_ctx, into, before)
            )
            came = travel(sends, stages[done])
            into = attend_back(
                place, query, grad_ctx, context, lse, keys, values, first, count, before, into
            )
            came, into = lax.optimization_barrier((came, into))
            early = end(keeps, came, stages[done])
            done += 1
        grads.append(into)
        if side == 0:
            before = into[:1]
            dx_other = (mm(into[1], w_key, NT) + mm(into[2], w_value, NT)).astype(BF16)
            dx_other, before = lax.optimization_barrier((dx_other, before))
            dx_from_other = swap(dx_other, "seq")
    (_, dk_other, dv_other), (dq, dk, dv) = grads
    keeps, sends = begin(early, stages[done])
    keeps, sends, dq, dk, dv, dx_from_other = lax.optimization_barrier(
        (keeps, sends, dq, dk, dv, dx_from_other)
    )
    came = travel(sends, stages[done])
    grad_embedded = (
        grad_one
        + mm(dq, w_query, NT)
        + mm(dk, w_key, NT)
        + mm(dv, w_value, NT)
        + dx_from_other.astype(F32)
    )
    grad_low = grad_embedded.astype(BF16)

    outgoing = [mm(hots, grad_low, TN).astype(BF16) for hots in slot_hots]
    outgoing, dq, dk, dv, came = lax.optimization_barrier((outgoing, dq, dk, dv, came))
    early = end(keeps, came, stages[done])
    done += 1

    def give_back(rows):
        return exchange(rows.reshape(group, slots_all, width), 0).reshape(slots, width)

    returned_other = give_back(outgoing[1])
    w_query_grad = mm(x_low, dq, TN)
    w_key_grad = mm(x_low, dk, TN) + mm(x_other, dk_other, TN)
    w_value_grad = mm(x_low, dv, TN) + mm(x_other, dv_other, TN)
    b_query_grad = jnp.sum(dq.astype(F32), axis=0)
    b_value_grad = jnp.sum(dv.astype(F32), axis=0) + jnp.sum(dv_other.astype(F32), axis=0)
    grad_rest = (grad_embedded - grad_low.astype(F32)).astype(BF16)
    expr_grad = mm(bin_hot, grad_low, TN) + mm(bin_hot, grad_rest, TN)
    short = jnp.concatenate(
        [
            jnp.sum(sums.reshape(6, 8, width), axis=1),
            jnp.sum(up_sums, axis=0).reshape(wide // width, width),
            b_query_grad[None, :],
            b_value_grad[None, :],
        ],
        axis=0,
    )
    short = jnp.pad(short, ((0, -short.shape[0] % 16), (0, 0)))
    late = [w_query_grad, w_key_grad, w_value_grad, expr_grad, short]
    heights = [item.shape[0] for item in late]
    late.append(jnp.zeros((-sum(heights) % 512, width), F32))
    late = jnp.concatenate([item.astype(BF16) for item in late], axis=0)
    keep, send = cut(late, core)
    keep, send, outgoing, returned_other = lax.optimization_barrier(
        (keep, send, outgoing, returned_other)
    )
    returned = give_back(outgoing[0])
    from_other = swap(mm(owned[1].astype(BF16), returned_other).astype(BF16), top_axis)
    late = jnp.split(keep + swap(send, core), 2, axis=0)
    returned, late, early, from_other = lax.optimization_barrier((returned, late, early, from_other))
    table_grads = mm(owned[0].astype(BF16), returned) + from_other.astype(F32)
    early = run_stages(early, stages[done:])
    early = jnp.concatenate(early, axis=0)
    early = join(early, swap(early, core), core)
    w_down_grad = early[:wide].astype(F32)
    w_up_grad = early[wide : 2 * wide].T.astype(F32)
    w_out_grad = early[2 * wide :].astype(F32)
    late = run_stages(late, stages[:-2])
    late, w_down_grad, w_up_grad, w_out_grad = lax.optimization_barrier(
        (late, w_down_grad, w_up_grad, w_out_grad)
    )
    late = jnp.concatenate(run_stages(late, stages[-2:]), axis=0)
    late = join(late, swap(late, core), core)
    taken = []
    for height in heights:
        at = sum(item.shape[0] for item in taken)
        taken.append(late[at : at + height].astype(F32))
    w_query_grad, w_key_grad, w_value_grad, expr_grad, short = taken
    gain_two_grad, shift_two_grad, b_down_grad, gain_one_grad, shift_one_grad, b_out_grad = (
        short[i] for i in range(6)
    )
    b_up_grad = short[6 : 6 + wide // width].reshape(wide)
    b_query_grad, b_value_grad = short[6 + wide // width], short[7 + wide // width]
    return (
        layer_output.reshape(1, tokens, width),
        table_grads[:rows_dev],
        table_grads[rows_dev:],
        expr_grad,
        w_query_grad,
        b_query_grad,
        w_key_grad,
        w_value_grad,
        b_value_grad,
        w_out_grad,
        b_out_grad,
        gain_one_grad,
        shift_one_grad,
        w_up_grad,
        b_up_grad,
        w_down_grad,
        b_down_grad,
        gain_two_grad,
        shift_two_grad,
        row_counts.reshape(2, rows_dev),
    )


def solution(mesh):
    bits = mesh.shape["dp"].bit_length() - 1
    dp_axes = tuple(f"dp{i}" for i in range(bits))
    fine = Mesh(mesh.devices.reshape((2,) * bits + (mesh.shape["seq"],)), (*dp_axes, "seq"))
    every = (*dp_axes, "seq")
    whole = P()
    placed = (
        (P(dp_axes, "seq"),) * 4
        + (P(dp_axes),) * 2
        + (P(every, None), P(None, every, None))
        + (whole,) * 16
        + (P(dp_axes, "seq", None),)
    )
    given = (
        (P(dp_axes, "seq", None),)
        + (P(every, None),) * 2
        + (whole,) * 16
        + (P(None, every),)
    )
    return jax.shard_map(
        functools.partial(local, dp_axes), mesh=fine, in_specs=placed, out_specs=given, check_vma=False
    )
```

```python
import functools

import jax
import jax.numpy as jnp
from jax import lax
from jax.experimental import pallas as pl
from jax.experimental.pallas import tpu as pltpu
from jax.sharding import Mesh, PartitionSpec as P

HEADS = 12
HEAD_DIM = 64
PAIR = 2 * HEAD_DIM
KEY_CHUNK = 512
LOG2E = 1.4426950408889634
SWAP = [(0, 1), (1, 0)]
F32 = jnp.float32
BF16 = jnp.bfloat16
NN = (((1,), (0,)), ((), ()))
NT = (((1,), (1,)), ((), ()))
TN = (((0,), (0,)), ((), ()))


def mm(left, right, dims=NN):
    return lax.dot_general(left, right, dims, preferred_element_type=F32)


def params(mib):
    return pltpu.CompilerParams(vmem_limit_bytes=mib * 2**20)


def cost(flops, moved):
    return pl.CostEstimate(flops=flops, bytes_accessed=moved, transcendentals=0)


def hot(left, right):
    return (left == right).astype(BF16)


def route_kernel(
    rows_dev, capacity, top_ref, gene_ref, know_ref, req_ref, gene_slot_ref, know_slot_ref
):
    tokens = gene_ref.shape[0]
    devices, slots_all = req_ref.shape
    group = devices // 2
    lane = lax.broadcasted_iota(jnp.int32, (tokens, devices), 1)
    mine = lane < group
    top = top_ref[0]
    first = jnp.where(mine, lane + top * group, lane - top * group) * rows_dev
    earlier = (
        lax.broadcasted_iota(jnp.int32, (tokens, tokens), 0)
        > lax.broadcasted_iota(jnp.int32, (tokens, tokens), 1)
    ).astype(F32).astype(BF16)
    rank_lane = lax.broadcasted_iota(jnp.int32, (tokens, capacity), 1)
    asked = []
    for which, (ids_ref, slot_ref) in enumerate(((gene_ref, gene_slot_ref), (know_ref, know_slot_ref))):
        row = ids_ref[...] - first
        hit = (row >= 0) & (row < rows_dev)
        before = mm(earlier, hit.astype(F32).astype(BF16))
        rank = jnp.sum(jnp.where(hit, before, 0.0), axis=1, keepdims=True)
        owner = jnp.sum(jnp.where(hit, lane, 0).astype(F32), axis=1, keepdims=True)
        slot_ref[...] = (owner * slots_all + rank).astype(jnp.int32) + which * capacity
        rank_hit = (rank_lane == rank.astype(jnp.int32)).astype(F32).astype(BF16)
        coded = jnp.where(hit, row + 1, 0)
        high = (coded >> 4).astype(F32).astype(BF16)
        low = (coded & 15).astype(F32).astype(BF16)
        wanted = (mm(high, rank_hit, TN) * 16.0 + mm(low, rank_hit, TN)).astype(jnp.int32)
        asked.append(jnp.where(wanted > 0, wanted - 1 + which * rows_dev, -1))
    req_ref[:, :capacity] = asked[0]
    req_ref[:, capacity:] = asked[1]


def route(top, gene_ids, know_ids, rows_dev, capacity, devices):
    tokens = gene_ids.shape[0]
    return pl.pallas_call(
        functools.partial(route_kernel, rows_dev, capacity),
        in_specs=[pl.BlockSpec(memory_space=pltpu.SMEM)] + [pl.BlockSpec(memory_space=pltpu.VMEM)] * 2,
        out_shape=(
            jax.ShapeDtypeStruct((devices, 2 * capacity), jnp.int32),
            jax.ShapeDtypeStruct((tokens, 1), jnp.int32),
            jax.ShapeDtypeStruct((tokens, 1), jnp.int32),
        ),
        compiler_params=params(32),
        name="route",
    )(top.reshape(1), gene_ids[:, None], know_ids[:, None])


def fill_keys(aug_ref, key, first_key, count):
    lanes = lax.broadcasted_iota(jnp.int32, key.shape, 1)
    at = lax.broadcasted_iota(jnp.int32, key.shape, 0) + first_key
    bias = jnp.where(at < count, 0.0, -1e30).astype(BF16)
    none = jnp.zeros_like(key)
    aug_ref[:, :PAIR] = jnp.where(lanes < HEAD_DIM, key, jnp.where(lanes == HEAD_DIM, bias, none))
    aug_ref[:, PAIR : 2 * PAIR] = key
    aug_ref[:, 2 * PAIR :] = jnp.where(lanes >= HEAD_DIM, key, jnp.where(lanes == 0, bias, none))


def head_mask(shape, head):
    lanes = lax.broadcasted_iota(jnp.int32, shape, 1)
    return (lanes >= head * HEAD_DIM) & (lanes < (head + 1) * HEAD_DIM)


def spread_query(query, head):
    lanes = lax.broadcasted_iota(jnp.int32, query.shape, 1)
    scaled = query.astype(F32) * (HEAD_DIM ** (-0.5) * LOG2E)
    scaled = jnp.where(head_mask(query.shape, head), scaled, 0.0)
    high = scaled.astype(BF16)
    low = scaled - high.astype(F32)
    low = jnp.where(lanes == (1 - head) * HEAD_DIM, 1.0, low).astype(BF16)
    return jnp.concatenate([low, high] if head == 0 else [high, low], axis=1)


def fold_rows(value, how):
    return how(value.reshape(value.shape[0] // 8, 8, value.shape[1]), axis=0)


def attend_kernel(merge, where_ref, q_ref, k_ref, v_ref, *rest):
    if merge:
        out_in_ref, lse_in_ref, out_ref, lse_ref, aug_ref, vt_ref, score_ref = rest
    else:
        out_ref, lse_ref, aug_ref, vt_ref, score_ref = rest
    spans = [slice(c, c + KEY_CHUNK) for c in range(0, k_ref.shape[0], KEY_CHUNK)]
    fill_keys(aug_ref, k_ref[...], where_ref[0], where_ref[1])
    vt_ref[...] = v_ref[...].T
    outs = []
    for head in range(2):
        own = slice(head * HEAD_DIM, (head + 1) * HEAD_DIM)
        query = spread_query(q_ref[...], head)
        top = None
        for span in spans:
            scores = mm(aug_ref[span, head * PAIR : (head + 2) * PAIR], query, NT)
            score_ref[head, span, :] = scores
            high = fold_rows(scores, jnp.max)
            top = high if top is None else jnp.maximum(top, high)
        top = jnp.max(top, axis=0, keepdims=True)
        total = None
        acc = None
        for span in spans:
            probs = jnp.exp2(score_ref[head, span, :] - top)
            part = fold_rows(probs, jnp.sum)
            total = part if total is None else total + part
            part = mm(vt_ref[own, span], probs.astype(BF16))
            acc = part if acc is None else acc + part
        total = jnp.sum(total, axis=0, keepdims=True)
        lse = top + jnp.log2(total)
        if merge:
            before = lse_in_ref[0, head : head + 1, :]
            both = jnp.maximum(lse, before)
            both = both + jnp.log2(jnp.exp2(lse - both) + jnp.exp2(before - both))
            acc = acc * (jnp.exp2(lse - both) / total)
            acc = acc + out_in_ref[own, :] * jnp.exp2(before - both)
            lse = both
        else:
            acc = acc / total
        lse_ref[0, head : head + 1, :] = lse
        outs.append(acc)
    out = jnp.concatenate(outs, axis=0)
    out_ref[...] = out.T if merge else out


def attend(where, query, key, value, before=()):
    tokens, width = query.shape
    keys = key.shape[0]
    pairs = width // PAIR
    column = lambda rows: pl.BlockSpec((rows, PAIR), lambda p, w: (0, p))
    upright = pl.BlockSpec((PAIR, tokens), lambda p, w: (p, 0))
    stats = pl.BlockSpec((1, 2, tokens), lambda p, w: (p, 0, 0))
    merge = len(before) > 0
    return pl.pallas_call(
        functools.partial(attend_kernel, merge),
        grid_spec=pltpu.PrefetchScalarGridSpec(
            num_scalar_prefetch=1,
            grid=(pairs,),
            in_specs=[column(tokens), column(keys), column(keys)] + ([upright, stats] if merge else []),
            out_specs=[column(tokens) if merge else upright, stats],
            scratch_shapes=[
                pltpu.VMEM((keys, 3 * PAIR), BF16),
                pltpu.VMEM((PAIR, keys), BF16),
                pltpu.VMEM((2, keys, tokens), F32),
            ],
        ),
        out_shape=(
            jax.ShapeDtypeStruct((tokens, width) if merge else (width, tokens), F32),
            jax.ShapeDtypeStruct((pairs, 2, tokens), F32),
        ),
        compiler_params=params(48),
        cost_estimate=cost(16 * tokens * keys * width, 2 * tokens * width * 10),
        name="attend_more" if merge else "attend",
    )(where, query, key, value, *before)


def attend_back_kernel(
    add, untouched, where_ref, q_ref, g_ref, o_ref, lse_ref, k_ref, v_ref, *rest
):
    dq_in_ref = rest[0] if add else None
    dq_ref, dk_ref, dv_ref, aug_ref, kt_ref = rest[int(add) + untouched :]
    fill_keys(aug_ref, k_ref[...], where_ref[0], where_ref[1])
    kt_ref[...] = k_ref[...].T
    grad = g_ref[...]
    picks = (
        lax.broadcasted_iota(jnp.int32, (8, PAIR), 1) // HEAD_DIM
        == lax.broadcasted_iota(jnp.int32, (8, PAIR), 0)
    ).astype(F32)
    inner = lax.dot_general(
        picks,
        grad.astype(F32) * o_ref[...],
        NT,
        precision=lax.Precision.HIGHEST,
        preferred_element_type=F32,
    )
    scaled = q_ref[...] * jnp.asarray(HEAD_DIM ** (-0.5), BF16)
    none = jnp.zeros_like(grad)
    masks = [head_mask(grad.shape, head) for head in range(2)]
    queries = [spread_query(q_ref[...], head) for head in range(2)]
    q_heads = [jnp.where(m, scaled, none) for m in masks]
    g_heads = [jnp.where(m, grad, none) for m in masks]
    dqs = [None, None]
    for first in range(0, k_ref.shape[0], KEY_CHUNK):
        span = slice(first, first + KEY_CHUNK)
        dk = None
        dv = None
        for head in range(2):
            own = slice(head * HEAD_DIM, (head + 1) * HEAD_DIM)
            scores = mm(aug_ref[span, head * PAIR : (head + 2) * PAIR], queries[head], NT)
            probs = jnp.exp2(scores - lse_ref[0, head : head + 1, :])
            grad_probs = mm(v_ref[span, :], g_heads[head], NT)
            grad_scores = (probs * (grad_probs - inner[head : head + 1, :])).astype(BF16)
            part = mm(kt_ref[own, span], grad_scores)
            dqs[head] = part if dqs[head] is None else dqs[head] + part
            part = mm(probs.astype(BF16), g_heads[head])
            dv = part if dv is None else dv + part
            part = mm(grad_scores, q_heads[head])
            dk = part if dk is None else dk + part
        dk_ref[span, :] = dk.astype(BF16)
        dv_ref[span, :] = dv.astype(BF16)
    dq = jnp.concatenate(dqs, axis=0).T * HEAD_DIM ** (-0.5)
    if add:
        dq = dq + dq_in_ref[...]
    dq_ref[...] = dq.astype(dq_ref.dtype)


def attend_back(where, query, grad, out, lse, key, value, first, count, before, into):
    tokens, width = query.shape
    keys = key.shape[0]
    column = lambda rows: pl.BlockSpec((rows, PAIR), lambda p, w: (0, p + first))
    untouched = pl.BlockSpec(memory_space=pl.ANY)
    add = len(before) > 0
    given = 7 + len(before)
    return pl.pallas_call(
        functools.partial(attend_back_kernel, add, len(into)),
        grid_spec=pltpu.PrefetchScalarGridSpec(
            num_scalar_prefetch=1,
            grid=(count,),
            in_specs=[column(tokens)] * 3
            + [pl.BlockSpec((1, 2, tokens), lambda p, w: (p + first, 0, 0))]
            + [column(keys)] * 2
            + [column(tokens)] * len(before)
            + [untouched] * len(into),
            out_specs=[column(tokens), column(keys), column(keys)],
            scratch_shapes=[
                pltpu.VMEM((keys, 3 * PAIR), BF16),
                pltpu.VMEM((PAIR, keys), BF16),
            ],
        ),
        out_shape=(
            jax.ShapeDtypeStruct((tokens, width), BF16 if add else F32),
            jax.ShapeDtypeStruct((keys, width), BF16),
            jax.ShapeDtypeStruct((keys, width), BF16),
        ),
        input_output_aliases={given + i: i for i in range(len(into))},
        compiler_params=params(56),
        cost_estimate=cost(40 * tokens * keys * PAIR * count, 2 * tokens * PAIR * count * 12),
        name=("attend_back_more" if add else "attend_back") + str(first),
    )(where, query, grad, out, lse, key, value, *before, *into)


def norm_parts(value):
    centre = jnp.mean(value, axis=-1, keepdims=True)
    centred = value - centre
    variance = jnp.mean(centred * centred, axis=-1, keepdims=True)
    inverse = lax.rsqrt(variance + 1e-05)
    return centred * inverse, inverse


def norm_back(grad, unit, inverse, gain):
    grad_unit = grad * gain
    return inverse * (
        grad_unit
        - jnp.mean(grad_unit, axis=-1, keepdims=True)
        - unit * jnp.mean(grad_unit * unit, axis=-1, keepdims=True)
    )


def middle_kernel(
    ctx_ref,
    emb_ref,
    cot_ref,
    w_out_ref,
    w_up_ref,
    w_down_ref,
    small_ref,
    b_up_ref,
    out_ref,
    ctx_low_ref,
    normed_ref,
    act_ref,
    gffn_ref,
    gpre_ref,
    gattn_ref,
    gone_ref,
    gctx_ref,
    sums_ref,
    up_sums_ref,
    slope_ref,
):
    step = pl.program_id(0)
    width = emb_ref.shape[1]
    wide = w_up_ref.shape[1]

    @pl.when(step == 0)
    def _():
        sums_ref[...] = jnp.zeros_like(sums_ref)
        up_sums_ref[...] = jnp.zeros_like(up_sums_ref)

    b_out, gain_one, shift_one, b_down, gain_two, shift_two = (
        small_ref[i : i + 1, :] for i in range(6)
    )
    ctx_low = ctx_ref[...].astype(BF16)
    ctx_low_ref[...] = ctx_low
    unit_one, inv_one = norm_parts(emb_ref[...] + mm(ctx_low, w_out_ref[...]) + b_out)
    normed = unit_one * gain_one + shift_one
    normed_low = normed.astype(BF16)
    normed_ref[...] = normed_low
    ffn = None
    for c in range(wide // width):
        span = slice(c * width, (c + 1) * width)
        pre = mm(normed_low, w_up_ref[:, span]) + b_up_ref[:, span]
        below = 0.5 * (1.0 + lax.erf(pre * 0.7071067811865476))
        act = (pre * below).astype(BF16)
        act_ref[:, span] = act
        slope_ref[:, span] = below + pre * (0.3989422804014327 * jnp.exp(-0.5 * pre * pre))
        part = mm(act, w_down_ref[span, :])
        ffn = part if ffn is None else ffn + part
    unit_two, inv_two = norm_parts(normed + ffn + b_down)
    out_ref[...] = (unit_two * gain_two + shift_two).astype(BF16)
    grad = cot_ref[...].astype(F32)
    sums_ref[0:8, :] += fold_rows(grad * unit_two, jnp.sum)
    sums_ref[8:16, :] += fold_rows(grad, jnp.sum)
    grad_two = norm_back(grad, unit_two, inv_two, gain_two)
    gffn = grad_two.astype(BF16)
    gffn_ref[...] = gffn
    sums_ref[16:24, :] += fold_rows(gffn.astype(F32), jnp.sum)
    grad_normed = grad_two
    for c in range(wide // width):
        span = slice(c * width, (c + 1) * width)
        gpre = (mm(gffn, w_down_ref[span, :], NT) * slope_ref[:, span]).astype(BF16)
        gpre_ref[:, span] = gpre
        up_sums_ref[:, span] += fold_rows(gpre.astype(F32), jnp.sum)
        grad_normed = grad_normed + mm(gpre, w_up_ref[:, span], NT)
    sums_ref[24:32, :] += fold_rows(grad_normed * unit_one, jnp.sum)
    sums_ref[32:40, :] += fold_rows(grad_normed, jnp.sum)
    grad_one = norm_back(grad_normed, unit_one, inv_one, gain_one)
    gone_ref[...] = grad_one
    gattn = grad_one.astype(BF16)
    gattn_ref[...] = gattn
    sums_ref[40:48, :] += fold_rows(gattn.astype(F32), jnp.sum)
    gctx_ref[...] = mm(gattn, w_out_ref[...], NT).astype(BF16)


def middle(ctx, embedded, cotangent, w_out, w_up, w_down, small, b_up, block=256):
    tokens, width = embedded.shape
    wide = w_up.shape[1]
    whole = lambda a: pl.BlockSpec(a.shape, lambda i: (0, 0), pipeline_mode=pl.Buffered(1))
    rows = lambda n: pl.BlockSpec((block, n), lambda i: (i, 0))
    fixed = lambda r, n: pl.BlockSpec((r, n), lambda i: (0, 0))
    shape = lambda n, dtype: jax.ShapeDtypeStruct((tokens, n), dtype)
    return pl.pallas_call(
        middle_kernel,
        grid=(tokens // block,),
        in_specs=[rows(width)] * 3 + [whole(w_out), whole(w_up), whole(w_down), whole(small), whole(b_up)],
        out_specs=[
            rows(width),
            rows(width),
            rows(width),
            rows(wide),
            rows(width),
            rows(wide),
            rows(width),
            rows(width),
            rows(width),
            fixed(48, width),
            fixed(8, wide),
        ],
        out_shape=[
            shape(width, BF16),
            shape(width, BF16),
            shape(width, BF16),
            shape(wide, BF16),
            shape(width, BF16),
            shape(wide, BF16),
            shape(width, BF16),
            shape(width, F32),
            shape(width, BF16),
            jax.ShapeDtypeStruct((48, width), F32),
            jax.ShapeDtypeStruct((8, wide), F32),
        ],
        scratch_shapes=[pltpu.VMEM((block, wide), F32)],
        compiler_params=params(60),
        cost_estimate=cost(tokens * width * (8 * wide + 4 * width) * 2, 2 * tokens * (2 * wide + 14 * width)),
        name="middle",
    )(ctx, embedded, cotangent, w_out, w_up, w_down, small, b_up)


def weight_sums_kernel(counts, half_ref, act_ref, gffn_ref, gpre_ref, norm_ref, ctx_ref, gattn_ref, out_ref):
    at = pl.program_id(0) + half_ref[0] * pl.num_programs(0)
    first = 0
    for count, left, right in zip(counts, (act_ref, gpre_ref, ctx_ref), (gffn_ref, norm_ref, gattn_ref)):
        @pl.when((at >= first) & (at < first + count))
        def _(left=left, right=right):
            out_ref[...] = mm(left[...], right[...], TN).astype(BF16)
        first += count


def weight_sums(half, activated, grad_ffn, grad_pre, normed, ctx, grad_attn, block=384):
    tokens, width = grad_ffn.shape
    lefts = (activated, grad_pre, ctx)
    counts = [left.shape[1] // block for left in lefts]
    steps = sum(counts) // 2
    specs = []
    first = 0
    for left, right, count in zip(lefts, (grad_ffn, normed, grad_attn), counts):
        specs.append(
            pl.BlockSpec(
                (tokens, block),
                lambda i, h, first=first, count=count: (0, jnp.clip(i + h[0] * steps - first, 0, count - 1)),
            )
        )
        specs.append(pl.BlockSpec((tokens, width), lambda i, h: (0, 0), pipeline_mode=pl.Buffered(1)))
        first += count
    return pl.pallas_call(
        functools.partial(weight_sums_kernel, counts),
        grid_spec=pltpu.PrefetchScalarGridSpec(
            num_scalar_prefetch=1,
            grid=(steps,),
            in_specs=specs,
            out_specs=pl.BlockSpec((block, width), lambda i, h: (i, 0)),
        ),
        out_shape=jax.ShapeDtypeStruct((steps * block, width), BF16),
        compiler_params=params(60),
        cost_estimate=cost(2 * tokens * width * block * steps, 2 * steps * block * (tokens + width)),
        name="weight_sums",
    )(half.reshape(1), activated, grad_ffn, grad_pre, normed, ctx, grad_attn)


def unpack_kernel(counts, upright, core_ref, own_ref, other_ref, *out_refs):
    at = pl.program_id(0)
    half = pl.num_programs(0) // 2
    mine = jnp.where(at < half, 0, 1) == core_ref[0]
    rows = jnp.where(mine, own_ref[...], other_ref[...]).astype(F32)
    first = 0
    for count, turn, out_ref in zip(counts, upright, out_refs):

        @pl.when((at >= first) & (at < first + count))
        def _(turn=turn, out_ref=out_ref):
            out_ref[...] = rows.T if turn else rows

        first += count


def unpack(core, own, other, heights, upright, block):
    half, width = own.shape
    steps = 2 * half // block
    counts = [height // block for height in heights]
    source = pl.BlockSpec((block, width), lambda i, c: (i % (steps // 2), 0))
    specs, shapes = [], []
    first = 0
    for height, count, turn in zip(heights, counts, upright):
        place = lambda i, first=first, count=count: jnp.clip(i - first, 0, count - 1)
        if turn:
            specs.append(pl.BlockSpec((width, block), lambda i, c, place=place: (0, place(i))))
            shapes.append(jax.ShapeDtypeStruct((width, height), F32))
        else:
            specs.append(pl.BlockSpec((block, width), lambda i, c, place=place: (place(i), 0)))
            shapes.append(jax.ShapeDtypeStruct((height, width), F32))
        first += count
    return pl.pallas_call(
        functools.partial(unpack_kernel, counts, upright),
        grid_spec=pltpu.PrefetchScalarGridSpec(
            num_scalar_prefetch=1, grid=(steps,), in_specs=[source, source], out_specs=specs
        ),
        out_shape=shapes,
        compiler_params=params(60),
        cost_estimate=cost(2 * half * width, 2 * half * width * 8),
        name="unpack",
    )(core.reshape(1), own, other)


def cut(value, axis):
    rows = value.shape[0] // 2
    me = lax.axis_index(axis)
    keep = lax.dynamic_slice_in_dim(value, me * rows, rows, 0)
    return keep, lax.dynamic_slice_in_dim(value, (1 - me) * rows, rows, 0)


def swap(value, axis):
    return lax.ppermute(value, axis, SWAP)


def join(value, other, axis):
    first = lax.axis_index(axis) == 0
    return jnp.concatenate([jnp.where(first, value, other), jnp.where(first, other, value)], axis=0)


def stages_of(dp_axes):
    near, far = dp_axes[-2], dp_axes[-3::-1]
    down = [((near, "seq"), True), (("seq", near), True)] + [((axis,), True) for axis in far]
    return down + [(axes, False) for axes, _ in down[::-1]]


def begin(pieces, stage):
    axes, halves = stage
    if len(pieces) < len(axes):
        pieces = jnp.split(pieces[0], 2, axis=0)
    if len(pieces) > len(axes):
        pieces = [jnp.concatenate(pieces, axis=0)]
    if halves:
        keeps, sends = zip(*(cut(p, axis) for p, axis in zip(pieces, axes)))
        return list(keeps), list(sends)
    return list(pieces), list(pieces)


def travel(sends, stage):
    return [swap(s, axis) for s, axis in zip(sends, stage[0])]


def end(keeps, arrived, stage):
    axes, halves = stage
    if halves:
        return [k + a for k, a in zip(keeps, arrived)]
    return [join(k, a, axis) for k, a, axis in zip(keeps, arrived, axes)]


def run_stages(pieces, stages):
    for stage in stages:
        keeps, sends = begin(pieces, stage)
        pieces = end(keeps, travel(sends, stage), stage)
    return pieces


def local(
    dp_axes,
    gene_ids,
    homolog_ids,
    knowledge_ids,
    expr_bins,
    species,
    cell_lengths,
    gene_table,
    knowledge_tables,
    expr_table,
    w_query,
    b_query,
    w_key,
    w_value,
    b_value,
    w_out,
    b_out,
    gain_one,
    shift_one,
    w_up,
    b_up,
    w_down,
    b_down,
    gain_two,
    shift_two,
    cotangent,
):
    tokens = gene_ids.shape[1]
    rows_dev, width = gene_table.shape
    wide = w_up.shape[1]
    every = (*dp_axes, "seq")
    top_axis, group_axes = dp_axes[0], (*dp_axes[1:], "seq")
    devices = lax.axis_size(every)
    group = devices // 2
    capacity = 2 * tokens // devices
    slots_all = 2 * capacity
    slots = group * slots_all
    bins = expr_table.shape[0]
    me = lax.axis_index("seq")

    def exchange(value, axis):
        return lax.all_to_all(value, group_axes, split_axis=axis, concat_axis=axis, tiled=True)

    gene_table, knowledge_tables = lax.optimization_barrier((gene_table, knowledge_tables))
    gene_other = lax.ppermute(gene_table, top_axis, SWAP)
    know_sum = jnp.sum(knowledge_tables.astype(F32), axis=0).astype(BF16)
    chosen = jnp.where(species[0] == 1, homolog_ids, gene_ids).reshape(-1)
    requests, gene_slot, know_slot = route(
        lax.axis_index(top_axis), chosen, knowledge_ids.reshape(-1), rows_dev, capacity, devices
    )
    asked = exchange(requests.reshape(2, group, slots_all), 1).reshape(2, slots)
    asked, gene_other, know_sum = lax.optimization_barrier((asked, gene_other, know_sum))
    know_other = lax.ppermute(know_sum, top_axis, SWAP)
    tables = [
        jnp.concatenate([gene_table, know_sum], axis=0),
        jnp.concatenate([gene_other, know_other], axis=0),
    ]
    row_at = jnp.arange(2 * rows_dev)
    slot_at = jnp.arange(slots)
    bin_hot = hot(expr_bins.reshape(-1)[:, None], jnp.arange(bins)[None, :])
    embedded = mm(bin_hot, expr_table)
    slot_hots = []
    for part in range(2):
        found = mm(hot(asked[part][:, None], row_at[None, :]), tables[part]).astype(BF16)
        fetched = exchange(found.reshape(group, slots_all, width), 0).reshape(slots, width)
        at = slot_at[None, :] + part * slots
        slot_hots.append(((at == gene_slot) | (at == know_slot)).astype(BF16))
        embedded = embedded + mm(slot_hots[part], fetched)
    x_low = embedded.astype(BF16)

    x_other = lax.ppermute(x_low, "seq", SWAP)
    query = (mm(x_low, w_query) + b_query).astype(BF16)
    key, key_other = (mm(x, w_key).astype(BF16) for x in (x_low, x_other))
    value, value_other = ((mm(x, w_value) + b_value).astype(BF16) for x in (x_low, x_other))
    mine = jnp.stack([me * tokens, cell_lengths[0]]).astype(jnp.int32)
    others = jnp.stack([(1 - me) * tokens, cell_lengths[0]]).astype(jnp.int32)
    owned = [row_at[:, None] == asked[part][None, :] for part in range(2)]
    counts = [jnp.sum(o.astype(jnp.int32), axis=1) for o in owned]
    counts_back = lax.ppermute(counts[1], top_axis, SWAP)
    first_part = attend(mine, query, key, value)
    first_part, counts_back = lax.optimization_barrier((first_part, counts_back))
    row_counts = counts[0] + counts_back
    context, lse = attend(others, query, key_other, value_other, first_part)

    small = jnp.stack([b_out, gain_one, shift_one, b_down, gain_two, shift_two])
    (
        layer_output,
        ctx_low,
        normed_low,
        activated,
        grad_ffn,
        grad_pre,
        grad_attn,
        grad_one,
        grad_ctx,
        sums,
        up_sums,
    ) = middle(
        context, embedded, cotangent.reshape(tokens, width), w_out, w_up, w_down, small, b_up[None, :]
    )

    core = dp_axes[-1]
    stages = stages_of(dp_axes)
    my_core = lax.axis_index(core)
    lefts_rights = (activated, grad_ffn, grad_pre, normed_low, ctx_low, grad_attn)
    sent = weight_sums(1 - my_core, *lefts_rights)
    sent, lefts_rights = lax.optimization_barrier((sent, lefts_rights))
    arrived = swap(sent, core)
    kept = weight_sums(my_core, *lefts_rights)
    kept, arrived, grad_ctx = lax.optimization_barrier((kept, arrived, grad_ctx))
    early = jnp.split(kept + arrived, 2, axis=0)
    pairs = width // PAIR
    third = pairs // 3
    sides = ((others, key_other, value_other), (mine, key, value))
    parts = (((0, 2 * third), (2 * third, third)), ((0, third), (third, third), (2 * third, third)))
    done = 0
    grads = []
    before = ()
    for side, (place, keys, values) in enumerate(sides):
        into = ()
        for first, count in parts[side]:
            keeps, sends = begin(early, stages[done])
            keeps, sends, grad_ctx, into, before = lax.optimization_barrier(
                (keeps, sends, grad_ctx, into, before)
            )
            came = travel(sends, stages[done])
            into = attend_back(
                place, query, grad_ctx, context, lse, keys, values, first, count, before, into
            )
            came, into = lax.optimization_barrier((came, into))
            early = end(keeps, came, stages[done])
            done += 1
        grads.append(into)
        if side == 0:
            before = into[:1]
            dx_other = (mm(into[1], w_key, NT) + mm(into[2], w_value, NT)).astype(BF16)
            dx_other, before = lax.optimization_barrier((dx_other, before))
            dx_from_other = swap(dx_other, "seq")
    (_, dk_other, dv_other), (dq, dk, dv) = grads
    keeps, sends = begin(early, stages[done])
    keeps, sends, dq, dk, dv, dx_from_other = lax.optimization_barrier(
        (keeps, sends, dq, dk, dv, dx_from_other)
    )
    came = travel(sends, stages[done])
    grad_embedded = (
        grad_one
        + mm(dq, w_query, NT)
        + mm(dk, w_key, NT)
        + mm(dv, w_value, NT)
        + dx_from_other.astype(F32)
    )
    grad_low = grad_embedded.astype(BF16)
    grad_low, came = lax.optimization_barrier((grad_low, came))
    keeps, sends = begin(end(keeps, came, stages[done]), stages[done + 1])
    done += 1
    keeps, sends, grad_low = lax.optimization_barrier((keeps, sends, grad_low))
    came = travel(sends, stages[done])

    outgoing = [mm(hots, grad_low, TN).astype(BF16) for hots in slot_hots]
    outgoing, dq, dk, dv, came = lax.optimization_barrier((outgoing, dq, dk, dv, came))
    early = end(keeps, came, stages[done])
    done += 1

    def give_back(rows):
        return exchange(rows.reshape(group, slots_all, width), 0).reshape(slots, width)

    returned_other = give_back(outgoing[1])
    w_query_grad = mm(x_low, dq, TN)
    w_key_grad = mm(x_low, dk, TN) + mm(x_other, dk_other, TN)
    w_value_grad = mm(x_low, dv, TN) + mm(x_other, dv_other, TN)
    b_query_grad = jnp.sum(dq.astype(F32), axis=0)
    b_value_grad = jnp.sum(dv.astype(F32), axis=0) + jnp.sum(dv_other.astype(F32), axis=0)
    grad_rest = (grad_embedded - grad_low.astype(F32)).astype(BF16)
    expr_grad = mm(bin_hot, grad_low, TN) + mm(bin_hot, grad_rest, TN)
    short = jnp.concatenate(
        [
            jnp.sum(sums.reshape(6, 8, width), axis=1),
            jnp.sum(up_sums, axis=0).reshape(wide // width, width),
            b_query_grad[None, :],
            b_value_grad[None, :],
        ],
        axis=0,
    )
    block = 128
    short = jnp.pad(short, ((0, -short.shape[0] % block), (0, 0)))
    late = [w_query_grad, w_key_grad, w_value_grad, expr_grad, short]
    heights = [item.shape[0] for item in late]
    late = jnp.concatenate([item.astype(BF16) for item in late], axis=0)
    keep, send = cut(late, core)
    keep, send, outgoing, returned_other = lax.optimization_barrier(
        (keep, send, outgoing, returned_other)
    )
    returned = give_back(outgoing[0])
    from_other = swap(mm(owned[1].astype(BF16), returned_other).astype(BF16), top_axis)
    late = jnp.split(keep + swap(send, core), 2, axis=0)
    returned, late, early, from_other = lax.optimization_barrier((returned, late, early, from_other))
    table_grads = mm(owned[0].astype(BF16), returned) + from_other.astype(F32)
    late = run_stages(late, stages[:2])
    late, early = lax.optimization_barrier((late, early))
    early_step = begin(early, stages[done])
    last = len(stages) - 1
    for at, stage in enumerate(stages[2:], start=2):
        keeps, sends = begin(late, stage)
        if at in (2, last):
            keeps, sends, early_step = lax.optimization_barrier((keeps, sends, early_step))
        came = travel(sends, stage)
        if at == 2:
            early_came = travel(early_step[1], stages[done])
        if at == last:
            early = unpack(
                my_core, *early_step, (wide, wide, width), (False, True, False), 384
            )
            came, early = lax.optimization_barrier((came, early))
        late = end(keeps, came, stage)
        if at == last - 2:
            late, early_came = lax.optimization_barrier((late, early_came))
            early = end(early_step[0], early_came, stages[done])
            early = jnp.concatenate(run_stages(early, stages[done + 1 :]), axis=0)
            early_step = (early, swap(early, core))
    w_down_grad, w_up_grad, w_out_grad = early
    late = jnp.concatenate(late, axis=0)
    late_other = swap(late, core)
    w_query_grad, w_key_grad, w_value_grad, expr_grad, short = unpack(
        my_core, late, late_other, heights, (False,) * 5, block
    )
    gain_two_grad, shift_two_grad, b_down_grad, gain_one_grad, shift_one_grad, b_out_grad = (
        short[i] for i in range(6)
    )
    b_up_grad = short[6 : 6 + wide // width].reshape(wide)
    b_query_grad, b_value_grad = short[6 + wide // width], short[7 + wide // width]
    return (
        layer_output.reshape(1, tokens, width),
        table_grads[:rows_dev],
        table_grads[rows_dev:],
        expr_grad,
        w_query_grad,
        b_query_grad,
        w_key_grad,
        w_value_grad,
        b_value_grad,
        w_out_grad,
        b_out_grad,
        gain_one_grad,
        shift_one_grad,
        w_up_grad,
        b_up_grad,
        w_down_grad,
        b_down_grad,
        gain_two_grad,
        shift_two_grad,
        row_counts.reshape(2, rows_dev),
    )


def solution(mesh):
    bits = mesh.shape["dp"].bit_length() - 1
    dp_axes = tuple(f"dp{i}" for i in range(bits))
    fine = Mesh(mesh.devices.reshape((2,) * bits + (mesh.shape["seq"],)), (*dp_axes, "seq"))
    every = (*dp_axes, "seq")
    whole = P()
    placed = (
        (P(dp_axes, "seq"),) * 4
        + (P(dp_axes),) * 2
        + (P(every, None), P(None, every, None))
        + (whole,) * 16
        + (P(dp_axes, "seq", None),)
    )
    given = (
        (P(dp_axes, "seq", None),)
        + (P(every, None),) * 2
        + (whole,) * 16
        + (P(None, every),)
    )
    return jax.shard_map(
        functools.partial(local, dp_axes), mesh=fine, in_specs=placed, out_specs=given, check_vma=False
    )
```

```python
import functools

import jax
import jax.numpy as jnp
from jax import lax
from jax.experimental import pallas as pl
from jax.experimental.pallas import tpu as pltpu
from jax.sharding import Mesh, PartitionSpec as P

HEADS = 12
HEAD_DIM = 64
PAIR = 2 * HEAD_DIM
KEY_CHUNK = 512
LOG2E = 1.4426950408889634
SWAP = [(0, 1), (1, 0)]
F32 = jnp.float32
BF16 = jnp.bfloat16
NN = (((1,), (0,)), ((), ()))
NT = (((1,), (1,)), ((), ()))
TN = (((0,), (0,)), ((), ()))


def mm(left, right, dims=NN):
    return lax.dot_general(left, right, dims, preferred_element_type=F32)


def params(mib):
    return pltpu.CompilerParams(vmem_limit_bytes=mib * 2**20)


def cost(flops, moved):
    return pl.CostEstimate(flops=flops, bytes_accessed=moved, transcendentals=0)


def hot(left, right):
    return (left == right).astype(BF16)


def route_kernel(
    rows_dev, capacity, top_ref, gene_ref, know_ref, req_ref, gene_slot_ref, know_slot_ref
):
    tokens = gene_ref.shape[0]
    devices, slots_all = req_ref.shape
    group = devices // 2
    lane = lax.broadcasted_iota(jnp.int32, (tokens, devices), 1)
    mine = lane < group
    top = top_ref[0]
    first = jnp.where(mine, lane + top * group, lane - top * group) * rows_dev
    earlier = (
        lax.broadcasted_iota(jnp.int32, (tokens, tokens), 0)
        > lax.broadcasted_iota(jnp.int32, (tokens, tokens), 1)
    ).astype(F32).astype(BF16)
    rank_lane = lax.broadcasted_iota(jnp.int32, (tokens, capacity), 1)
    asked = []
    for which, (ids_ref, slot_ref) in enumerate(((gene_ref, gene_slot_ref), (know_ref, know_slot_ref))):
        row = ids_ref[...] - first
        hit = (row >= 0) & (row < rows_dev)
        before = mm(earlier, hit.astype(F32).astype(BF16))
        rank = jnp.sum(jnp.where(hit, before, 0.0), axis=1, keepdims=True)
        owner = jnp.sum(jnp.where(hit, lane, 0).astype(F32), axis=1, keepdims=True)
        slot_ref[...] = (owner * slots_all + rank).astype(jnp.int32) + which * capacity
        rank_hit = (rank_lane == rank.astype(jnp.int32)).astype(F32).astype(BF16)
        coded = jnp.where(hit, row + 1, 0)
        high = (coded >> 4).astype(F32).astype(BF16)
        low = (coded & 15).astype(F32).astype(BF16)
        wanted = (mm(high, rank_hit, TN) * 16.0 + mm(low, rank_hit, TN)).astype(jnp.int32)
        asked.append(jnp.where(wanted > 0, wanted - 1 + which * rows_dev, -1))
    req_ref[:, :capacity] = asked[0]
    req_ref[:, capacity:] = asked[1]


def route(top, gene_ids, know_ids, rows_dev, capacity, devices):
    tokens = gene_ids.shape[0]
    return pl.pallas_call(
        functools.partial(route_kernel, rows_dev, capacity),
        in_specs=[pl.BlockSpec(memory_space=pltpu.SMEM)] + [pl.BlockSpec(memory_space=pltpu.VMEM)] * 2,
        out_shape=(
            jax.ShapeDtypeStruct((devices, 2 * capacity), jnp.int32),
            jax.ShapeDtypeStruct((tokens, 1), jnp.int32),
            jax.ShapeDtypeStruct((tokens, 1), jnp.int32),
        ),
        compiler_params=params(32),
        name="route",
    )(top.reshape(1), gene_ids[:, None], know_ids[:, None])


def fill_keys(aug_ref, key, first_key, count):
    lanes = lax.broadcasted_iota(jnp.int32, key.shape, 1)
    at = lax.broadcasted_iota(jnp.int32, key.shape, 0) + first_key
    bias = jnp.where(at < count, 0.0, -1e30).astype(BF16)
    none = jnp.zeros_like(key)
    aug_ref[:, :PAIR] = jnp.where(lanes < HEAD_DIM, key, jnp.where(lanes == HEAD_DIM, bias, none))
    aug_ref[:, PAIR : 2 * PAIR] = key
    aug_ref[:, 2 * PAIR :] = jnp.where(lanes >= HEAD_DIM, key, jnp.where(lanes == 0, bias, none))


def head_mask(shape, head):
    lanes = lax.broadcasted_iota(jnp.int32, shape, 1)
    return (lanes >= head * HEAD_DIM) & (lanes < (head + 1) * HEAD_DIM)


def spread_query(query, head):
    lanes = lax.broadcasted_iota(jnp.int32, query.shape, 1)
    scaled = query.astype(F32) * (HEAD_DIM ** (-0.5) * LOG2E)
    scaled = jnp.where(head_mask(query.shape, head), scaled, 0.0)
    high = scaled.astype(BF16)
    low = scaled - high.astype(F32)
    low = jnp.where(lanes == (1 - head) * HEAD_DIM, 1.0, low).astype(BF16)
    return jnp.concatenate([low, high] if head == 0 else [high, low], axis=1)


def fold_rows(value, how):
    return how(value.reshape(value.shape[0] // 8, 8, value.shape[1]), axis=0)


def attend_kernel(merge, where_ref, q_ref, k_ref, v_ref, *rest):
    if merge:
        out_in_ref, lse_in_ref, out_ref, lse_ref, aug_ref, vt_ref, score_ref = rest
    else:
        out_ref, lse_ref, aug_ref, vt_ref, score_ref = rest
    spans = [slice(c, c + KEY_CHUNK) for c in range(0, k_ref.shape[0], KEY_CHUNK)]
    fill_keys(aug_ref, k_ref[...], where_ref[0], where_ref[1])
    vt_ref[...] = v_ref[...].T
    outs = []
    for head in range(2):
        own = slice(head * HEAD_DIM, (head + 1) * HEAD_DIM)
        query = spread_query(q_ref[...], head)
        top = None
        for span in spans:
            scores = mm(aug_ref[span, head * PAIR : (head + 2) * PAIR], query, NT)
            score_ref[head, span, :] = scores
            high = fold_rows(scores, jnp.max)
            top = high if top is None else jnp.maximum(top, high)
        top = jnp.max(top, axis=0, keepdims=True)
        total = None
        acc = None
        for span in spans:
            probs = jnp.exp2(score_ref[head, span, :] - top)
            part = fold_rows(probs, jnp.sum)
            total = part if total is None else total + part
            part = mm(vt_ref[own, span], probs.astype(BF16))
            acc = part if acc is None else acc + part
        total = jnp.sum(total, axis=0, keepdims=True)
        lse = top + jnp.log2(total)
        if merge:
            before = lse_in_ref[0, head : head + 1, :]
            both = jnp.maximum(lse, before)
            both = both + jnp.log2(jnp.exp2(lse - both) + jnp.exp2(before - both))
            acc = acc * (jnp.exp2(lse - both) / total)
            acc = acc + out_in_ref[own, :] * jnp.exp2(before - both)
            lse = both
        else:
            acc = acc / total
        lse_ref[0, head : head + 1, :] = lse
        outs.append(acc)
    out = jnp.concatenate(outs, axis=0)
    out_ref[...] = out.T if merge else out


def attend(where, query, key, value, before=()):
    tokens, width = query.shape
    keys = key.shape[0]
    pairs = width // PAIR
    column = lambda rows: pl.BlockSpec((rows, PAIR), lambda p, w: (0, p))
    upright = pl.BlockSpec((PAIR, tokens), lambda p, w: (p, 0))
    stats = pl.BlockSpec((1, 2, tokens), lambda p, w: (p, 0, 0))
    merge = len(before) > 0
    return pl.pallas_call(
        functools.partial(attend_kernel, merge),
        grid_spec=pltpu.PrefetchScalarGridSpec(
            num_scalar_prefetch=1,
            grid=(pairs,),
            in_specs=[column(tokens), column(keys), column(keys)] + ([upright, stats] if merge else []),
            out_specs=[column(tokens) if merge else upright, stats],
            scratch_shapes=[
                pltpu.VMEM((keys, 3 * PAIR), BF16),
                pltpu.VMEM((PAIR, keys), BF16),
                pltpu.VMEM((2, keys, tokens), F32),
            ],
        ),
        out_shape=(
            jax.ShapeDtypeStruct((tokens, width) if merge else (width, tokens), F32),
            jax.ShapeDtypeStruct((pairs, 2, tokens), F32),
        ),
        compiler_params=params(48),
        cost_estimate=cost(16 * tokens * keys * width, 2 * tokens * width * 10),
        name="attend_more" if merge else "attend",
    )(where, query, key, value, *before)


def attend_back_kernel(
    add, untouched, where_ref, q_ref, g_ref, o_ref, lse_ref, k_ref, v_ref, *rest
):
    dq_in_ref = rest[0] if add else None
    dq_ref, dk_ref, dv_ref, aug_ref, kt_ref = rest[int(add) + untouched :]
    fill_keys(aug_ref, k_ref[...], where_ref[0], where_ref[1])
    kt_ref[...] = k_ref[...].T
    grad = g_ref[...]
    picks = (
        lax.broadcasted_iota(jnp.int32, (8, PAIR), 1) // HEAD_DIM
        == lax.broadcasted_iota(jnp.int32, (8, PAIR), 0)
    ).astype(F32)
    inner = lax.dot_general(
        picks,
        grad.astype(F32) * o_ref[...],
        NT,
        precision=lax.Precision.HIGHEST,
        preferred_element_type=F32,
    )
    scaled = q_ref[...] * jnp.asarray(HEAD_DIM ** (-0.5), BF16)
    none = jnp.zeros_like(grad)
    masks = [head_mask(grad.shape, head) for head in range(2)]
    queries = [spread_query(q_ref[...], head) for head in range(2)]
    q_heads = [jnp.where(m, scaled, none) for m in masks]
    g_heads = [jnp.where(m, grad, none) for m in masks]
    dqs = [None, None]
    for first in range(0, k_ref.shape[0], KEY_CHUNK):
        span = slice(first, first + KEY_CHUNK)
        dk = None
        dv = None
        for head in range(2):
            own = slice(head * HEAD_DIM, (head + 1) * HEAD_DIM)
            scores = mm(aug_ref[span, head * PAIR : (head + 2) * PAIR], queries[head], NT)
            probs = jnp.exp2(scores - lse_ref[0, head : head + 1, :])
            grad_probs = mm(v_ref[span, :], g_heads[head], NT)
            grad_scores = (probs * (grad_probs - inner[head : head + 1, :])).astype(BF16)
            part = mm(kt_ref[own, span], grad_scores)
            dqs[head] = part if dqs[head] is None else dqs[head] + part
            part = mm(probs.astype(BF16), g_heads[head])
            dv = part if dv is None else dv + part
            part = mm(grad_scores, q_heads[head])
            dk = part if dk is None else dk + part
        dk_ref[span, :] = dk.astype(BF16)
        dv_ref[span, :] = dv.astype(BF16)
    dq = jnp.concatenate(dqs, axis=0).T * HEAD_DIM ** (-0.5)
    if add:
        dq = dq + dq_in_ref[...]
    dq_ref[...] = dq.astype(dq_ref.dtype)


def attend_back(where, query, grad, out, lse, key, value, first, count, before, into):
    tokens, width = query.shape
    keys = key.shape[0]
    column = lambda rows: pl.BlockSpec((rows, PAIR), lambda p, w: (0, p + first))
    untouched = pl.BlockSpec(memory_space=pl.ANY)
    add = len(before) > 0
    given = 7 + len(before)
    return pl.pallas_call(
        functools.partial(attend_back_kernel, add, len(into)),
        grid_spec=pltpu.PrefetchScalarGridSpec(
            num_scalar_prefetch=1,
            grid=(count,),
            in_specs=[column(tokens)] * 3
            + [pl.BlockSpec((1, 2, tokens), lambda p, w: (p + first, 0, 0))]
            + [column(keys)] * 2
            + [column(tokens)] * len(before)
            + [untouched] * len(into),
            out_specs=[column(tokens), column(keys), column(keys)],
            scratch_shapes=[
                pltpu.VMEM((keys, 3 * PAIR), BF16),
                pltpu.VMEM((PAIR, keys), BF16),
            ],
        ),
        out_shape=(
            jax.ShapeDtypeStruct((tokens, width), BF16 if add else F32),
            jax.ShapeDtypeStruct((keys, width), BF16),
            jax.ShapeDtypeStruct((keys, width), BF16),
        ),
        input_output_aliases={given + i: i for i in range(len(into))},
        compiler_params=params(56),
        cost_estimate=cost(40 * tokens * keys * PAIR * count, 2 * tokens * PAIR * count * 12),
        name=("attend_back_more" if add else "attend_back") + str(first),
    )(where, query, grad, out, lse, key, value, *before, *into)


def norm_parts(value):
    centre = jnp.mean(value, axis=-1, keepdims=True)
    centred = value - centre
    variance = jnp.mean(centred * centred, axis=-1, keepdims=True)
    inverse = lax.rsqrt(variance + 1e-05)
    return centred * inverse, inverse


def norm_back(grad, unit, inverse, gain):
    grad_unit = grad * gain
    return inverse * (
        grad_unit
        - jnp.mean(grad_unit, axis=-1, keepdims=True)
        - unit * jnp.mean(grad_unit * unit, axis=-1, keepdims=True)
    )


def middle_kernel(
    ctx_ref,
    emb_ref,
    cot_ref,
    w_out_ref,
    w_up_ref,
    w_down_ref,
    small_ref,
    b_up_ref,
    out_ref,
    ctx_low_ref,
    normed_ref,
    act_ref,
    gffn_ref,
    gpre_ref,
    gattn_ref,
    gone_ref,
    gctx_ref,
    sums_ref,
    up_sums_ref,
    slope_ref,
):
    step = pl.program_id(0)
    width = emb_ref.shape[1]
    wide = w_up_ref.shape[1]

    @pl.when(step == 0)
    def _():
        sums_ref[...] = jnp.zeros_like(sums_ref)
        up_sums_ref[...] = jnp.zeros_like(up_sums_ref)

    b_out, gain_one, shift_one, b_down, gain_two, shift_two = (
        small_ref[i : i + 1, :] for i in range(6)
    )
    ctx_low = ctx_ref[...].astype(BF16)
    ctx_low_ref[...] = ctx_low
    unit_one, inv_one = norm_parts(emb_ref[...] + mm(ctx_low, w_out_ref[...]) + b_out)
    normed = unit_one * gain_one + shift_one
    normed_low = normed.astype(BF16)
    normed_ref[...] = normed_low
    ffn = None
    for c in range(wide // width):
        span = slice(c * width, (c + 1) * width)
        pre = mm(normed_low, w_up_ref[:, span]) + b_up_ref[:, span]
        below = 0.5 * (1.0 + lax.erf(pre * 0.7071067811865476))
        act = (pre * below).astype(BF16)
        act_ref[:, span] = act
        slope_ref[:, span] = below + pre * (0.3989422804014327 * jnp.exp(-0.5 * pre * pre))
        part = mm(act, w_down_ref[span, :])
        ffn = part if ffn is None else ffn + part
    unit_two, inv_two = norm_parts(normed + ffn + b_down)
    out_ref[...] = (unit_two * gain_two + shift_two).astype(BF16)
    grad = cot_ref[...].astype(F32)
    sums_ref[0:8, :] += fold_rows(grad * unit_two, jnp.sum)
    sums_ref[8:16, :] += fold_rows(grad, jnp.sum)
    grad_two = norm_back(grad, unit_two, inv_two, gain_two)
    gffn = grad_two.astype(BF16)
    gffn_ref[...] = gffn
    sums_ref[16:24, :] += fold_rows(gffn.astype(F32), jnp.sum)
    grad_normed = grad_two
    for c in range(wide // width):
        span = slice(c * width, (c + 1) * width)
        gpre = (mm(gffn, w_down_ref[span, :], NT) * slope_ref[:, span]).astype(BF16)
        gpre_ref[:, span] = gpre
        up_sums_ref[:, span] += fold_rows(gpre.astype(F32), jnp.sum)
        grad_normed = grad_normed + mm(gpre, w_up_ref[:, span], NT)
    sums_ref[24:32, :] += fold_rows(grad_normed * unit_one, jnp.sum)
    sums_ref[32:40, :] += fold_rows(grad_normed, jnp.sum)
    grad_one = norm_back(grad_normed, unit_one, inv_one, gain_one)
    gone_ref[...] = grad_one
    gattn = grad_one.astype(BF16)
    gattn_ref[...] = gattn
    sums_ref[40:48, :] += fold_rows(gattn.astype(F32), jnp.sum)
    gctx_ref[...] = mm(gattn, w_out_ref[...], NT).astype(BF16)


def middle(ctx, embedded, cotangent, w_out, w_up, w_down, small, b_up, block=256):
    tokens, width = embedded.shape
    wide = w_up.shape[1]
    whole = lambda a: pl.BlockSpec(a.shape, lambda i: (0, 0), pipeline_mode=pl.Buffered(1))
    rows = lambda n: pl.BlockSpec((block, n), lambda i: (i, 0))
    fixed = lambda r, n: pl.BlockSpec((r, n), lambda i: (0, 0))
    shape = lambda n, dtype: jax.ShapeDtypeStruct((tokens, n), dtype)
    return pl.pallas_call(
        middle_kernel,
        grid=(tokens // block,),
        in_specs=[rows(width)] * 3 + [whole(w_out), whole(w_up), whole(w_down), whole(small), whole(b_up)],
        out_specs=[
            rows(width),
            rows(width),
            rows(width),
            rows(wide),
            rows(width),
            rows(wide),
            rows(width),
            rows(width),
            rows(width),
            fixed(48, width),
            fixed(8, wide),
        ],
        out_shape=[
            shape(width, BF16),
            shape(width, BF16),
            shape(width, BF16),
            shape(wide, BF16),
            shape(width, BF16),
            shape(wide, BF16),
            shape(width, BF16),
            shape(width, F32),
            shape(width, BF16),
            jax.ShapeDtypeStruct((48, width), F32),
            jax.ShapeDtypeStruct((8, wide), F32),
        ],
        scratch_shapes=[pltpu.VMEM((block, wide), F32)],
        compiler_params=params(60),
        cost_estimate=cost(tokens * width * (8 * wide + 4 * width) * 2, 2 * tokens * (2 * wide + 14 * width)),
        name="middle",
    )(ctx, embedded, cotangent, w_out, w_up, w_down, small, b_up)


def weight_sums_kernel(counts, half_ref, act_ref, gffn_ref, gpre_ref, norm_ref, ctx_ref, gattn_ref, out_ref):
    at = pl.program_id(0) + half_ref[0] * pl.num_programs(0)
    first = 0
    for count, left, right in zip(counts, (act_ref, gpre_ref, ctx_ref), (gffn_ref, norm_ref, gattn_ref)):
        @pl.when((at >= first) & (at < first + count))
        def _(left=left, right=right):
            out_ref[...] = mm(left[...], right[...], TN).astype(BF16)
        first += count


def weight_sums(half, activated, grad_ffn, grad_pre, normed, ctx, grad_attn, block=384):
    tokens, width = grad_ffn.shape
    lefts = (activated, grad_pre, ctx)
    counts = [left.shape[1] // block for left in lefts]
    steps = sum(counts) // 2
    specs = []
    first = 0
    for left, right, count in zip(lefts, (grad_ffn, normed, grad_attn), counts):
        specs.append(
            pl.BlockSpec(
                (tokens, block),
                lambda i, h, first=first, count=count: (0, jnp.clip(i + h[0] * steps - first, 0, count - 1)),
            )
        )
        specs.append(pl.BlockSpec((tokens, width), lambda i, h: (0, 0), pipeline_mode=pl.Buffered(1)))
        first += count
    return pl.pallas_call(
        functools.partial(weight_sums_kernel, counts),
        grid_spec=pltpu.PrefetchScalarGridSpec(
            num_scalar_prefetch=1,
            grid=(steps,),
            in_specs=specs,
            out_specs=pl.BlockSpec((block, width), lambda i, h: (i, 0)),
        ),
        out_shape=jax.ShapeDtypeStruct((steps * block, width), BF16),
        compiler_params=params(60),
        cost_estimate=cost(2 * tokens * width * block * steps, 2 * steps * block * (tokens + width)),
        name="weight_sums",
    )(half.reshape(1), activated, grad_ffn, grad_pre, normed, ctx, grad_attn)


def unpack_kernel(counts, upright, core_ref, own_ref, other_ref, *out_refs):
    at = pl.program_id(0)
    half = pl.num_programs(0) // 2
    mine = jnp.where(at < half, 0, 1) == core_ref[0]
    rows = jnp.where(mine, own_ref[...], other_ref[...]).astype(F32)
    first = 0
    for count, turn, out_ref in zip(counts, upright, out_refs):

        @pl.when((at >= first) & (at < first + count))
        def _(turn=turn, out_ref=out_ref):
            out_ref[...] = rows.T if turn else rows

        first += count


def unpack(core, own, other, heights, upright, block):
    half, width = own.shape
    steps = 2 * half // block
    counts = [height // block for height in heights]
    last = steps // 2 - 1
    source = lambda turn: pl.BlockSpec(
        (block, width),
        lambda i, c: (jnp.clip(i - (c[0] if turn == 0 else 1 - c[0]) * (last + 1), 0, last), 0),
    )
    specs, shapes = [], []
    first = 0
    for height, count, turn in zip(heights, counts, upright):
        place = lambda i, first=first, count=count: jnp.clip(i - first, 0, count - 1)
        if turn:
            specs.append(pl.BlockSpec((width, block), lambda i, c, place=place: (0, place(i))))
            shapes.append(jax.ShapeDtypeStruct((width, height), F32))
        else:
            specs.append(pl.BlockSpec((block, width), lambda i, c, place=place: (place(i), 0)))
            shapes.append(jax.ShapeDtypeStruct((height, width), F32))
        first += count
    return pl.pallas_call(
        functools.partial(unpack_kernel, counts, upright),
        grid_spec=pltpu.PrefetchScalarGridSpec(
            num_scalar_prefetch=1, grid=(steps,), in_specs=[source(0), source(1)], out_specs=specs
        ),
        out_shape=shapes,
        compiler_params=params(60),
        cost_estimate=cost(2 * half * width, 2 * half * width * 8),
        name="unpack",
    )(core.reshape(1), own, other)


def unpack_whole_kernel(heights, core_ref, own_ref, other_ref, *out_refs):
    half = own_ref.shape[0]
    lower = core_ref[0] == 0
    first = 0
    for height, out_ref in zip(heights, out_refs):
        for part in range(2):
            start, stop = max(first, part * half), min(first + height, (part + 1) * half)
            if start < stop:
                span = slice(start - part * half, stop - part * half)
                near, far = (own_ref, other_ref) if part == 0 else (other_ref, own_ref)
                rows = jnp.where(lower, near[span, :], far[span, :])
                out_ref[start - first : stop - first, :] = rows.astype(F32)
        first += height


def unpack_whole(core, own, other, heights):
    width = own.shape[1]
    vmem = pl.BlockSpec(memory_space=pltpu.VMEM)
    return pl.pallas_call(
        functools.partial(unpack_whole_kernel, heights),
        in_specs=[pl.BlockSpec(memory_space=pltpu.SMEM), vmem, vmem],
        out_specs=[vmem] * len(heights),
        out_shape=[jax.ShapeDtypeStruct((height, width), F32) for height in heights],
        compiler_params=params(60),
        name="unpack_whole",
    )(core.reshape(1), own, other)


def cut(value, axis):
    rows = value.shape[0] // 2
    me = lax.axis_index(axis)
    keep = lax.dynamic_slice_in_dim(value, me * rows, rows, 0)
    return keep, lax.dynamic_slice_in_dim(value, (1 - me) * rows, rows, 0)


def swap(value, axis):
    return lax.ppermute(value, axis, SWAP)


def join(value, other, axis):
    first = lax.axis_index(axis) == 0
    return jnp.concatenate([jnp.where(first, value, other), jnp.where(first, other, value)], axis=0)


def stages_of(dp_axes):
    near, far = dp_axes[-2], dp_axes[-3::-1]
    down = [((near, "seq"), True), (("seq", near), True)] + [((axis,), True) for axis in far]
    return down + [(axes, False) for axes, _ in down[::-1]]


def begin(pieces, stage):
    axes, halves = stage
    if len(pieces) < len(axes):
        pieces = jnp.split(pieces[0], 2, axis=0)
    if len(pieces) > len(axes):
        pieces = [jnp.concatenate(pieces, axis=0)]
    if halves:
        keeps, sends = zip(*(cut(p, axis) for p, axis in zip(pieces, axes)))
        return list(keeps), list(sends)
    return list(pieces), list(pieces)


def travel(sends, stage):
    return [swap(s, axis) for s, axis in zip(sends, stage[0])]


def end(keeps, arrived, stage):
    axes, halves = stage
    if halves:
        return [k + a for k, a in zip(keeps, arrived)]
    return [join(k, a, axis) for k, a, axis in zip(keeps, arrived, axes)]


def run_stages(pieces, stages):
    for stage in stages:
        keeps, sends = begin(pieces, stage)
        pieces = end(keeps, travel(sends, stage), stage)
    return pieces


def local(
    dp_axes,
    gene_ids,
    homolog_ids,
    knowledge_ids,
    expr_bins,
    species,
    cell_lengths,
    gene_table,
    knowledge_tables,
    expr_table,
    w_query,
    b_query,
    w_key,
    w_value,
    b_value,
    w_out,
    b_out,
    gain_one,
    shift_one,
    w_up,
    b_up,
    w_down,
    b_down,
    gain_two,
    shift_two,
    cotangent,
):
    tokens = gene_ids.shape[1]
    rows_dev, width = gene_table.shape
    wide = w_up.shape[1]
    every = (*dp_axes, "seq")
    top_axis, group_axes = dp_axes[0], (*dp_axes[1:], "seq")
    devices = lax.axis_size(every)
    group = devices // 2
    capacity = 2 * tokens // devices
    slots_all = 2 * capacity
    slots = group * slots_all
    bins = expr_table.shape[0]
    me = lax.axis_index("seq")

    def exchange(value, axis):
        return lax.all_to_all(value, group_axes, split_axis=axis, concat_axis=axis, tiled=True)

    gene_table, knowledge_tables = lax.optimization_barrier((gene_table, knowledge_tables))
    gene_other = lax.ppermute(gene_table, top_axis, SWAP)
    know_sum = jnp.sum(knowledge_tables.astype(F32), axis=0).astype(BF16)
    chosen = jnp.where(species[0] == 1, homolog_ids, gene_ids).reshape(-1)
    requests, gene_slot, know_slot = route(
        lax.axis_index(top_axis), chosen, knowledge_ids.reshape(-1), rows_dev, capacity, devices
    )
    asked = exchange(requests.reshape(2, group, slots_all), 1).reshape(2, slots)
    asked, gene_other, know_sum = lax.optimization_barrier((asked, gene_other, know_sum))
    know_other = lax.ppermute(know_sum, top_axis, SWAP)
    tables = [
        jnp.concatenate([gene_table, know_sum], axis=0),
        jnp.concatenate([gene_other, know_other], axis=0),
    ]
    row_at = jnp.arange(2 * rows_dev)
    slot_at = jnp.arange(slots)
    bin_hot = hot(expr_bins.reshape(-1)[:, None], jnp.arange(bins)[None, :])
    embedded = mm(bin_hot, expr_table)
    slot_hots = []
    for part in range(2):
        found = mm(hot(asked[part][:, None], row_at[None, :]), tables[part]).astype(BF16)
        fetched = exchange(found.reshape(group, slots_all, width), 0).reshape(slots, width)
        at = slot_at[None, :] + part * slots
        slot_hots.append(((at == gene_slot) | (at == know_slot)).astype(BF16))
        embedded = embedded + mm(slot_hots[part], fetched)
    x_low = embedded.astype(BF16)

    x_other = lax.ppermute(x_low, "seq", SWAP)
    query = (mm(x_low, w_query) + b_query).astype(BF16)
    key, key_other = (mm(x, w_key).astype(BF16) for x in (x_low, x_other))
    value, value_other = ((mm(x, w_value) + b_value).astype(BF16) for x in (x_low, x_other))
    mine = jnp.stack([me * tokens, cell_lengths[0]]).astype(jnp.int32)
    others = jnp.stack([(1 - me) * tokens, cell_lengths[0]]).astype(jnp.int32)
    owned = [row_at[:, None] == asked[part][None, :] for part in range(2)]
    counts = [jnp.sum(o.astype(jnp.int32), axis=1) for o in owned]
    counts_back = lax.ppermute(counts[1], top_axis, SWAP)
    first_part = attend(mine, query, key, value)
    first_part, counts_back = lax.optimization_barrier((first_part, counts_back))
    row_counts = counts[0] + counts_back
    context, lse = attend(others, query, key_other, value_other, first_part)

    small = jnp.stack([b_out, gain_one, shift_one, b_down, gain_two, shift_two])
    (
        layer_output,
        ctx_low,
        normed_low,
        activated,
        grad_ffn,
        grad_pre,
        grad_attn,
        grad_one,
        grad_ctx,
        sums,
        up_sums,
    ) = middle(
        context, embedded, cotangent.reshape(tokens, width), w_out, w_up, w_down, small, b_up[None, :]
    )

    core = dp_axes[-1]
    stages = stages_of(dp_axes)
    my_core = lax.axis_index(core)
    lefts_rights = (activated, grad_ffn, grad_pre, normed_low, ctx_low, grad_attn)
    sent = weight_sums(1 - my_core, *lefts_rights)
    sent, lefts_rights = lax.optimization_barrier((sent, lefts_rights))
    arrived = swap(sent, core)
    kept = weight_sums(my_core, *lefts_rights)
    kept, arrived, grad_ctx = lax.optimization_barrier((kept, arrived, grad_ctx))
    early = jnp.split(kept + arrived, 2, axis=0)
    pairs = width // PAIR
    third = pairs // 3
    sides = ((others, key_other, value_other), (mine, key, value))
    parts = (((0, 2 * third), (2 * third, third)), ((0, third), (third, third), (2 * third, third)))
    done = 0
    grads = []
    before = ()
    for side, (place, keys, values) in enumerate(sides):
        into = ()
        for first, count in parts[side]:
            keeps, sends = begin(early, stages[done])
            keeps, sends, grad_ctx, into, before = lax.optimization_barrier(
                (keeps, sends, grad_ctx, into, before)
            )
            came = travel(sends, stages[done])
            into = attend_back(
                place, query, grad_ctx, context, lse, keys, values, first, count, before, into
            )
            came, into = lax.optimization_barrier((came, into))
            early = end(keeps, came, stages[done])
            done += 1
        grads.append(into)
        if side == 0:
            before = into[:1]
            dx_other = (mm(into[1], w_key, NT) + mm(into[2], w_value, NT)).astype(BF16)
            dx_other, before = lax.optimization_barrier((dx_other, before))
            dx_from_other = swap(dx_other, "seq")
    (_, dk_other, dv_other), (dq, dk, dv) = grads
    keeps, sends = begin(early, stages[done])
    keeps, sends, dq, dk, dv, dx_from_other = lax.optimization_barrier(
        (keeps, sends, dq, dk, dv, dx_from_other)
    )
    came = travel(sends, stages[done])
    grad_embedded = (
        grad_one
        + mm(dq, w_query, NT)
        + mm(dk, w_key, NT)
        + mm(dv, w_value, NT)
        + dx_from_other.astype(F32)
    )
    grad_low = grad_embedded.astype(BF16)
    grad_low, came = lax.optimization_barrier((grad_low, came))
    keeps, sends = begin(end(keeps, came, stages[done]), stages[done + 1])
    done += 1
    keeps, sends, grad_low = lax.optimization_barrier((keeps, sends, grad_low))
    came = travel(sends, stages[done])

    outgoing = [mm(hots, grad_low, TN).astype(BF16) for hots in slot_hots]
    outgoing, dq, dk, dv, came = lax.optimization_barrier((outgoing, dq, dk, dv, came))
    early = end(keeps, came, stages[done])
    done += 1

    def give_back(rows):
        return exchange(rows.reshape(group, slots_all, width), 0).reshape(slots, width)

    returned_other = give_back(outgoing[1])
    w_query_grad = mm(x_low, dq, TN)
    w_key_grad = mm(x_low, dk, TN) + mm(x_other, dk_other, TN)
    w_value_grad = mm(x_low, dv, TN) + mm(x_other, dv_other, TN)
    b_query_grad = jnp.sum(dq.astype(F32), axis=0)
    b_value_grad = jnp.sum(dv.astype(F32), axis=0) + jnp.sum(dv_other.astype(F32), axis=0)
    grad_rest = (grad_embedded - grad_low.astype(F32)).astype(BF16)
    expr_grad = mm(bin_hot, grad_low, TN) + mm(bin_hot, grad_rest, TN)
    short = jnp.concatenate(
        [
            jnp.sum(sums.reshape(6, 8, width), axis=1),
            jnp.sum(up_sums, axis=0).reshape(wide // width, width),
            b_query_grad[None, :],
            b_value_grad[None, :],
        ],
        axis=0,
    )
    block = 128
    short = jnp.pad(short, ((0, -short.shape[0] % block), (0, 0)))
    late = [w_query_grad, w_key_grad, w_value_grad, expr_grad, short]
    heights = [item.shape[0] for item in late]
    late = jnp.concatenate([item.astype(BF16) for item in late], axis=0)
    keep, send = cut(late, core)
    keep, send, outgoing, returned_other = lax.optimization_barrier(
        (keep, send, outgoing, returned_other)
    )
    returned = give_back(outgoing[0])
    from_other = swap(mm(owned[1].astype(BF16), returned_other).astype(BF16), top_axis)
    late = jnp.split(keep + swap(send, core), 2, axis=0)
    returned, late, early, from_other = lax.optimization_barrier((returned, late, early, from_other))
    table_grads = mm(owned[0].astype(BF16), returned) + from_other.astype(F32)
    late = run_stages(late, stages[:2])
    late, early = lax.optimization_barrier((late, early))
    early_step = begin(early, stages[done])
    last = len(stages) - 1
    for at, stage in enumerate(stages[2:], start=2):
        keeps, sends = begin(late, stage)
        if at == 2:
            keeps, sends, early_step = lax.optimization_barrier((keeps, sends, early_step))
        came = travel(sends, stage)
        if at == 2:
            early_came = travel(early_step[1], stages[done])
        if at == 4:
            came, table_grads = lax.optimization_barrier((came, table_grads))
        late = end(keeps, came, stage)
        if at == last - 1:
            late, early_came = lax.optimization_barrier((late, early_came))
            early = end(early_step[0], early_came, stages[done])
            early = jnp.concatenate(run_stages(early, stages[done + 1 :]), axis=0)
            early_step = (early, swap(early, core))
    late = jnp.concatenate(late, axis=0)
    late_other = swap(late, core)
    late, early_step = lax.optimization_barrier((late, early_step))
    early = unpack(my_core, *early_step, (wide, wide, width), (False, True, False), 384)
    late_other, early = lax.optimization_barrier((late_other, early))
    w_down_grad, w_up_grad, w_out_grad = early
    w_query_grad, w_key_grad, w_value_grad, expr_grad, short = unpack_whole(
        my_core, late, late_other, heights
    )
    gain_two_grad, shift_two_grad, b_down_grad, gain_one_grad, shift_one_grad, b_out_grad = (
        short[i] for i in range(6)
    )
    b_up_grad = short[6 : 6 + wide // width].reshape(wide)
    b_query_grad, b_value_grad = short[6 + wide // width], short[7 + wide // width]
    return (
        layer_output.reshape(1, tokens, width),
        table_grads[:rows_dev],
        table_grads[rows_dev:],
        expr_grad,
        w_query_grad,
        b_query_grad,
        w_key_grad,
        w_value_grad,
        b_value_grad,
        w_out_grad,
        b_out_grad,
        gain_one_grad,
        shift_one_grad,
        w_up_grad,
        b_up_grad,
        w_down_grad,
        b_down_grad,
        gain_two_grad,
        shift_two_grad,
        row_counts.reshape(2, rows_dev),
    )


def solution(mesh):
    bits = mesh.shape["dp"].bit_length() - 1
    dp_axes = tuple(f"dp{i}" for i in range(bits))
    fine = Mesh(mesh.devices.reshape((2,) * bits + (mesh.shape["seq"],)), (*dp_axes, "seq"))
    every = (*dp_axes, "seq")
    whole = P()
    placed = (
        (P(dp_axes, "seq"),) * 4
        + (P(dp_axes),) * 2
        + (P(every, None), P(None, every, None))
        + (whole,) * 16
        + (P(dp_axes, "seq", None),)
    )
    given = (
        (P(dp_axes, "seq", None),)
        + (P(every, None),) * 2
        + (whole,) * 16
        + (P(None, every),)
    )
    return jax.shard_map(
        functools.partial(local, dp_axes), mesh=fine, in_specs=placed, out_specs=given, check_vma=False
    )
```

```python
import functools

import jax
import jax.numpy as jnp
from jax import lax
from jax.experimental import pallas as pl
from jax.experimental.pallas import tpu as pltpu
from jax.sharding import Mesh, PartitionSpec as P

HEADS = 12
HEAD_DIM = 64
PAIR = 2 * HEAD_DIM
KEY_CHUNK = 512
LOG2E = 1.4426950408889634
SWAP = [(0, 1), (1, 0)]
F32 = jnp.float32
BF16 = jnp.bfloat16
NN = (((1,), (0,)), ((), ()))
NT = (((1,), (1,)), ((), ()))
TN = (((0,), (0,)), ((), ()))


def mm(left, right, dims=NN):
    return lax.dot_general(left, right, dims, preferred_element_type=F32)


def params(mib):
    return pltpu.CompilerParams(vmem_limit_bytes=mib * 2**20)


def cost(flops, moved):
    return pl.CostEstimate(flops=flops, bytes_accessed=moved, transcendentals=0)


def hot(left, right):
    return (left == right).astype(BF16)


def route_kernel(
    rows_dev, capacity, top_ref, gene_ref, know_ref, req_ref, gene_slot_ref, know_slot_ref
):
    tokens = gene_ref.shape[0]
    devices, slots_all = req_ref.shape
    group = devices // 2
    lane = lax.broadcasted_iota(jnp.int32, (tokens, devices), 1)
    mine = lane < group
    top = top_ref[0]
    first = jnp.where(mine, lane + top * group, lane - top * group) * rows_dev
    earlier = (
        lax.broadcasted_iota(jnp.int32, (tokens, tokens), 0)
        > lax.broadcasted_iota(jnp.int32, (tokens, tokens), 1)
    ).astype(F32).astype(BF16)
    rank_lane = lax.broadcasted_iota(jnp.int32, (tokens, capacity), 1)
    asked = []
    for which, (ids_ref, slot_ref) in enumerate(((gene_ref, gene_slot_ref), (know_ref, know_slot_ref))):
        row = ids_ref[...] - first
        hit = (row >= 0) & (row < rows_dev)
        before = mm(earlier, hit.astype(F32).astype(BF16))
        rank = jnp.sum(jnp.where(hit, before, 0.0), axis=1, keepdims=True)
        owner = jnp.sum(jnp.where(hit, lane, 0).astype(F32), axis=1, keepdims=True)
        slot_ref[...] = (owner * slots_all + rank).astype(jnp.int32) + which * capacity
        rank_hit = (rank_lane == rank.astype(jnp.int32)).astype(F32).astype(BF16)
        coded = jnp.where(hit, row + 1, 0)
        high = (coded >> 4).astype(F32).astype(BF16)
        low = (coded & 15).astype(F32).astype(BF16)
        wanted = (mm(high, rank_hit, TN) * 16.0 + mm(low, rank_hit, TN)).astype(jnp.int32)
        asked.append(jnp.where(wanted > 0, wanted - 1 + which * rows_dev, -1))
    req_ref[:, :capacity] = asked[0]
    req_ref[:, capacity:] = asked[1]


def route(top, gene_ids, know_ids, rows_dev, capacity, devices):
    tokens = gene_ids.shape[0]
    return pl.pallas_call(
        functools.partial(route_kernel, rows_dev, capacity),
        in_specs=[pl.BlockSpec(memory_space=pltpu.SMEM)] + [pl.BlockSpec(memory_space=pltpu.VMEM)] * 2,
        out_shape=(
            jax.ShapeDtypeStruct((devices, 2 * capacity), jnp.int32),
            jax.ShapeDtypeStruct((tokens, 1), jnp.int32),
            jax.ShapeDtypeStruct((tokens, 1), jnp.int32),
        ),
        compiler_params=params(32),
        name="route",
    )(top.reshape(1), gene_ids[:, None], know_ids[:, None])


def fill_keys(aug_ref, key, first_key, count):
    lanes = lax.broadcasted_iota(jnp.int32, key.shape, 1)
    at = lax.broadcasted_iota(jnp.int32, key.shape, 0) + first_key
    bias = jnp.where(at < count, 0.0, -1e30).astype(BF16)
    none = jnp.zeros_like(key)
    aug_ref[:, :PAIR] = jnp.where(lanes < HEAD_DIM, key, jnp.where(lanes == HEAD_DIM, bias, none))
    aug_ref[:, PAIR : 2 * PAIR] = key
    aug_ref[:, 2 * PAIR :] = jnp.where(lanes >= HEAD_DIM, key, jnp.where(lanes == 0, bias, none))


def head_mask(shape, head):
    lanes = lax.broadcasted_iota(jnp.int32, shape, 1)
    return (lanes >= head * HEAD_DIM) & (lanes < (head + 1) * HEAD_DIM)


def spread_query(query, head):
    lanes = lax.broadcasted_iota(jnp.int32, query.shape, 1)
    scaled = query.astype(F32) * (HEAD_DIM ** (-0.5) * LOG2E)
    scaled = jnp.where(head_mask(query.shape, head), scaled, 0.0)
    high = scaled.astype(BF16)
    low = scaled - high.astype(F32)
    low = jnp.where(lanes == (1 - head) * HEAD_DIM, 1.0, low).astype(BF16)
    return jnp.concatenate([low, high] if head == 0 else [high, low], axis=1)


def fold_rows(value, how):
    return how(value.reshape(value.shape[0] // 8, 8, value.shape[1]), axis=0)


def attend_kernel(merge, where_ref, q_ref, k_ref, v_ref, *rest):
    if merge:
        out_in_ref, lse_in_ref, out_ref, lse_ref, aug_ref, vt_ref, score_ref = rest
    else:
        out_ref, lse_ref, aug_ref, vt_ref, score_ref = rest
    spans = [slice(c, c + KEY_CHUNK) for c in range(0, k_ref.shape[0], KEY_CHUNK)]
    fill_keys(aug_ref, k_ref[...], where_ref[0], where_ref[1])
    vt_ref[...] = v_ref[...].T
    outs = []
    for head in range(2):
        own = slice(head * HEAD_DIM, (head + 1) * HEAD_DIM)
        query = spread_query(q_ref[...], head)
        top = None
        for span in spans:
            scores = mm(aug_ref[span, head * PAIR : (head + 2) * PAIR], query, NT)
            score_ref[head, span, :] = scores
            high = fold_rows(scores, jnp.max)
            top = high if top is None else jnp.maximum(top, high)
        top = jnp.max(top, axis=0, keepdims=True)
        total = None
        acc = None
        for span in spans:
            probs = jnp.exp2(score_ref[head, span, :] - top)
            part = fold_rows(probs, jnp.sum)
            total = part if total is None else total + part
            part = mm(vt_ref[own, span], probs.astype(BF16))
            acc = part if acc is None else acc + part
        total = jnp.sum(total, axis=0, keepdims=True)
        lse = top + jnp.log2(total)
        if merge:
            before = lse_in_ref[0, head : head + 1, :]
            both = jnp.maximum(lse, before)
            both = both + jnp.log2(jnp.exp2(lse - both) + jnp.exp2(before - both))
            acc = acc * (jnp.exp2(lse - both) / total)
            acc = acc + out_in_ref[own, :] * jnp.exp2(before - both)
            lse = both
        else:
            acc = acc / total
        lse_ref[0, head : head + 1, :] = lse
        outs.append(acc)
    out = jnp.concatenate(outs, axis=0)
    out_ref[...] = out.T if merge else out


def attend(where, query, key, value, before=()):
    tokens, width = query.shape
    keys = key.shape[0]
    pairs = width // PAIR
    column = lambda rows: pl.BlockSpec((rows, PAIR), lambda p, w: (0, p))
    upright = pl.BlockSpec((PAIR, tokens), lambda p, w: (p, 0))
    stats = pl.BlockSpec((1, 2, tokens), lambda p, w: (p, 0, 0))
    merge = len(before) > 0
    return pl.pallas_call(
        functools.partial(attend_kernel, merge),
        grid_spec=pltpu.PrefetchScalarGridSpec(
            num_scalar_prefetch=1,
            grid=(pairs,),
            in_specs=[column(tokens), column(keys), column(keys)] + ([upright, stats] if merge else []),
            out_specs=[column(tokens) if merge else upright, stats],
            scratch_shapes=[
                pltpu.VMEM((keys, 3 * PAIR), BF16),
                pltpu.VMEM((PAIR, keys), BF16),
                pltpu.VMEM((2, keys, tokens), F32),
            ],
        ),
        out_shape=(
            jax.ShapeDtypeStruct((tokens, width) if merge else (width, tokens), F32),
            jax.ShapeDtypeStruct((pairs, 2, tokens), F32),
        ),
        compiler_params=params(48),
        cost_estimate=cost(16 * tokens * keys * width, 2 * tokens * width * 10),
        name="attend_more" if merge else "attend",
    )(where, query, key, value, *before)


def attend_back_kernel(
    add, untouched, where_ref, q_ref, g_ref, o_ref, lse_ref, k_ref, v_ref, *rest
):
    dq_in_ref = rest[0] if add else None
    dq_ref, dk_ref, dv_ref, aug_ref, kt_ref = rest[int(add) + untouched :]
    fill_keys(aug_ref, k_ref[...], where_ref[0], where_ref[1])
    kt_ref[...] = k_ref[...].T
    grad = g_ref[...]
    picks = (
        lax.broadcasted_iota(jnp.int32, (8, PAIR), 1) // HEAD_DIM
        == lax.broadcasted_iota(jnp.int32, (8, PAIR), 0)
    ).astype(F32)
    inner = lax.dot_general(
        picks,
        grad.astype(F32) * o_ref[...],
        NT,
        precision=lax.Precision.HIGHEST,
        preferred_element_type=F32,
    )
    scaled = q_ref[...] * jnp.asarray(HEAD_DIM ** (-0.5), BF16)
    none = jnp.zeros_like(grad)
    masks = [head_mask(grad.shape, head) for head in range(2)]
    queries = [spread_query(q_ref[...], head) for head in range(2)]
    q_heads = [jnp.where(m, scaled, none) for m in masks]
    g_heads = [jnp.where(m, grad, none) for m in masks]
    dqs = [None, None]
    for first in range(0, k_ref.shape[0], KEY_CHUNK):
        span = slice(first, first + KEY_CHUNK)
        dk = None
        dv = None
        for head in range(2):
            own = slice(head * HEAD_DIM, (head + 1) * HEAD_DIM)
            scores = mm(aug_ref[span, head * PAIR : (head + 2) * PAIR], queries[head], NT)
            probs = jnp.exp2(scores - lse_ref[0, head : head + 1, :])
            grad_probs = mm(v_ref[span, :], g_heads[head], NT)
            grad_scores = (probs * (grad_probs - inner[head : head + 1, :])).astype(BF16)
            part = mm(kt_ref[own, span], grad_scores)
            dqs[head] = part if dqs[head] is None else dqs[head] + part
            part = mm(probs.astype(BF16), g_heads[head])
            dv = part if dv is None else dv + part
            part = mm(grad_scores, q_heads[head])
            dk = part if dk is None else dk + part
        dk_ref[span, :] = dk.astype(BF16)
        dv_ref[span, :] = dv.astype(BF16)
    dq = jnp.concatenate(dqs, axis=0).T * HEAD_DIM ** (-0.5)
    if add:
        dq = dq + dq_in_ref[...]
    dq_ref[...] = dq.astype(dq_ref.dtype)


def attend_back(where, query, grad, out, lse, key, value, first, count, before, into):
    tokens, width = query.shape
    keys = key.shape[0]
    column = lambda rows: pl.BlockSpec((rows, PAIR), lambda p, w: (0, p + first))
    untouched = pl.BlockSpec(memory_space=pl.ANY)
    add = len(before) > 0
    given = 7 + len(before)
    return pl.pallas_call(
        functools.partial(attend_back_kernel, add, len(into)),
        grid_spec=pltpu.PrefetchScalarGridSpec(
            num_scalar_prefetch=1,
            grid=(count,),
            in_specs=[column(tokens)] * 3
            + [pl.BlockSpec((1, 2, tokens), lambda p, w: (p + first, 0, 0))]
            + [column(keys)] * 2
            + [column(tokens)] * len(before)
            + [untouched] * len(into),
            out_specs=[column(tokens), column(keys), column(keys)],
            scratch_shapes=[
                pltpu.VMEM((keys, 3 * PAIR), BF16),
                pltpu.VMEM((PAIR, keys), BF16),
            ],
        ),
        out_shape=(
            jax.ShapeDtypeStruct((tokens, width), BF16 if add else F32),
            jax.ShapeDtypeStruct((keys, width), BF16),
            jax.ShapeDtypeStruct((keys, width), BF16),
        ),
        input_output_aliases={given + i: i for i in range(len(into))},
        compiler_params=params(56),
        cost_estimate=cost(40 * tokens * keys * PAIR * count, 2 * tokens * PAIR * count * 12),
        name=("attend_back_more" if add else "attend_back") + str(first),
    )(where, query, grad, out, lse, key, value, *before, *into)


def norm_parts(value):
    centre = jnp.mean(value, axis=-1, keepdims=True)
    centred = value - centre
    variance = jnp.mean(centred * centred, axis=-1, keepdims=True)
    inverse = lax.rsqrt(variance + 1e-05)
    return centred * inverse, inverse


def norm_back(grad, unit, inverse, gain):
    grad_unit = grad * gain
    return inverse * (
        grad_unit
        - jnp.mean(grad_unit, axis=-1, keepdims=True)
        - unit * jnp.mean(grad_unit * unit, axis=-1, keepdims=True)
    )


def middle_kernel(
    ctx_ref,
    emb_ref,
    cot_ref,
    w_out_ref,
    w_up_ref,
    w_down_ref,
    small_ref,
    b_up_ref,
    out_ref,
    ctx_low_ref,
    normed_ref,
    act_ref,
    gffn_ref,
    gpre_ref,
    gattn_ref,
    gone_ref,
    gctx_ref,
    sums_ref,
    up_sums_ref,
    slope_ref,
):
    step = pl.program_id(0)
    width = emb_ref.shape[1]
    wide = w_up_ref.shape[1]

    @pl.when(step == 0)
    def _():
        sums_ref[...] = jnp.zeros_like(sums_ref)
        up_sums_ref[...] = jnp.zeros_like(up_sums_ref)

    b_out, gain_one, shift_one, b_down, gain_two, shift_two = (
        small_ref[i : i + 1, :] for i in range(6)
    )
    ctx_low = ctx_ref[...].astype(BF16)
    ctx_low_ref[...] = ctx_low
    unit_one, inv_one = norm_parts(emb_ref[...] + mm(ctx_low, w_out_ref[...]) + b_out)
    normed = unit_one * gain_one + shift_one
    normed_low = normed.astype(BF16)
    normed_ref[...] = normed_low
    ffn = None
    for c in range(wide // width):
        span = slice(c * width, (c + 1) * width)
        pre = mm(normed_low, w_up_ref[:, span]) + b_up_ref[:, span]
        below = 0.5 * (1.0 + lax.erf(pre * 0.7071067811865476))
        act = (pre * below).astype(BF16)
        act_ref[:, span] = act
        slope_ref[:, span] = below + pre * (0.3989422804014327 * jnp.exp(-0.5 * pre * pre))
        part = mm(act, w_down_ref[span, :])
        ffn = part if ffn is None else ffn + part
    unit_two, inv_two = norm_parts(normed + ffn + b_down)
    out_ref[...] = (unit_two * gain_two + shift_two).astype(BF16)
    grad = cot_ref[...].astype(F32)
    sums_ref[0:8, :] += fold_rows(grad * unit_two, jnp.sum)
    sums_ref[8:16, :] += fold_rows(grad, jnp.sum)
    grad_two = norm_back(grad, unit_two, inv_two, gain_two)
    gffn = grad_two.astype(BF16)
    gffn_ref[...] = gffn
    sums_ref[16:24, :] += fold_rows(gffn.astype(F32), jnp.sum)
    grad_normed = grad_two
    for c in range(wide // width):
        span = slice(c * width, (c + 1) * width)
        gpre = (mm(gffn, w_down_ref[span, :], NT) * slope_ref[:, span]).astype(BF16)
        gpre_ref[:, span] = gpre
        up_sums_ref[:, span] += fold_rows(gpre.astype(F32), jnp.sum)
        grad_normed = grad_normed + mm(gpre, w_up_ref[:, span], NT)
    sums_ref[24:32, :] += fold_rows(grad_normed * unit_one, jnp.sum)
    sums_ref[32:40, :] += fold_rows(grad_normed, jnp.sum)
    grad_one = norm_back(grad_normed, unit_one, inv_one, gain_one)
    gone_ref[...] = grad_one
    gattn = grad_one.astype(BF16)
    gattn_ref[...] = gattn
    sums_ref[40:48, :] += fold_rows(gattn.astype(F32), jnp.sum)
    gctx_ref[...] = mm(gattn, w_out_ref[...], NT).astype(BF16)


def middle(ctx, embedded, cotangent, w_out, w_up, w_down, small, b_up, block=256):
    tokens, width = embedded.shape
    wide = w_up.shape[1]
    whole = lambda a: pl.BlockSpec(a.shape, lambda i: (0, 0), pipeline_mode=pl.Buffered(1))
    rows = lambda n: pl.BlockSpec((block, n), lambda i: (i, 0))
    fixed = lambda r, n: pl.BlockSpec((r, n), lambda i: (0, 0))
    shape = lambda n, dtype: jax.ShapeDtypeStruct((tokens, n), dtype)
    return pl.pallas_call(
        middle_kernel,
        grid=(tokens // block,),
        in_specs=[rows(width)] * 3 + [whole(w_out), whole(w_up), whole(w_down), whole(small), whole(b_up)],
        out_specs=[
            rows(width),
            rows(width),
            rows(width),
            rows(wide),
            rows(width),
            rows(wide),
            rows(width),
            rows(width),
            rows(width),
            fixed(48, width),
            fixed(8, wide),
        ],
        out_shape=[
            shape(width, BF16),
            shape(width, BF16),
            shape(width, BF16),
            shape(wide, BF16),
            shape(width, BF16),
            shape(wide, BF16),
            shape(width, BF16),
            shape(width, F32),
            shape(width, BF16),
            jax.ShapeDtypeStruct((48, width), F32),
            jax.ShapeDtypeStruct((8, wide), F32),
        ],
        scratch_shapes=[pltpu.VMEM((block, wide), F32)],
        compiler_params=params(60),
        cost_estimate=cost(tokens * width * (8 * wide + 4 * width) * 2, 2 * tokens * (2 * wide + 14 * width)),
        name="middle",
    )(ctx, embedded, cotangent, w_out, w_up, w_down, small, b_up)


def weight_sums_kernel(counts, half_ref, act_ref, gffn_ref, gpre_ref, norm_ref, ctx_ref, gattn_ref, out_ref):
    at = pl.program_id(0) + half_ref[0] * pl.num_programs(0)
    first = 0
    for count, left, right in zip(counts, (act_ref, gpre_ref, ctx_ref), (gffn_ref, norm_ref, gattn_ref)):
        @pl.when((at >= first) & (at < first + count))
        def _(left=left, right=right):
            out_ref[...] = mm(left[...], right[...], TN).astype(BF16)
        first += count


def weight_sums(half, activated, grad_ffn, grad_pre, normed, ctx, grad_attn, block=384):
    tokens, width = grad_ffn.shape
    lefts = (activated, grad_pre, ctx)
    counts = [left.shape[1] // block for left in lefts]
    steps = sum(counts) // 2
    specs = []
    first = 0
    for left, right, count in zip(lefts, (grad_ffn, normed, grad_attn), counts):
        specs.append(
            pl.BlockSpec(
                (tokens, block),
                lambda i, h, first=first, count=count: (0, jnp.clip(i + h[0] * steps - first, 0, count - 1)),
            )
        )
        specs.append(pl.BlockSpec((tokens, width), lambda i, h: (0, 0), pipeline_mode=pl.Buffered(1)))
        first += count
    return pl.pallas_call(
        functools.partial(weight_sums_kernel, counts),
        grid_spec=pltpu.PrefetchScalarGridSpec(
            num_scalar_prefetch=1,
            grid=(steps,),
            in_specs=specs,
            out_specs=pl.BlockSpec((block, width), lambda i, h: (i, 0)),
        ),
        out_shape=jax.ShapeDtypeStruct((steps * block, width), BF16),
        compiler_params=params(60),
        cost_estimate=cost(2 * tokens * width * block * steps, 2 * steps * block * (tokens + width)),
        name="weight_sums",
    )(half.reshape(1), activated, grad_ffn, grad_pre, normed, ctx, grad_attn)


def unpack_early_kernel(upper, core_ref, *refs):
    (down_own, down_other, up_own, up_other, out_own, out_other, down_ref, up_ref, out_ref) = refs
    at = pl.program_id(0)
    low = core_ref[0] == 0
    down_ref[...] = jnp.where(low, down_own[...], down_other[...]).astype(F32)
    mine = jnp.where(at < upper, low, jnp.logical_not(low))
    up_ref[...] = jnp.where(mine, up_own[...], up_other[...]).astype(F32).T

    @pl.when(at < out_ref.shape[0])
    def _():
        out_ref[at] = jnp.where(low, out_other[...], out_own[...]).astype(F32)


def unpack_early(core, own, other, wide, block=384):
    half, width = own.shape
    steps, blocks = wide // block, half // block
    upper = blocks - steps
    outs = width // block
    last = blocks - 1
    pick = lambda use, place: jnp.where(use, place, last)

    def pair(place, in_low):
        return [
            pl.BlockSpec(
                (block, width),
                lambda i, c, turn=turn: (pick(in_low(i) == (c[0] == turn), place(i)), 0),
            )
            for turn in range(2)
        ]

    sources = (
        pair(lambda i: i, lambda i: i >= 0)
        + pair(lambda i: jnp.where(i < upper, steps + i, i - upper), lambda i: i < upper)
        + pair(lambda i: blocks - outs + jnp.minimum(i, outs - 1), lambda i: i < 0)
    )
    down, up, out = pl.pallas_call(
        functools.partial(unpack_early_kernel, upper),
        grid_spec=pltpu.PrefetchScalarGridSpec(
            num_scalar_prefetch=1,
            grid=(steps,),
            in_specs=sources,
            out_specs=[
                pl.BlockSpec((block, width), lambda i, c: (i, 0)),
                pl.BlockSpec((width, block), lambda i, c: (0, i)),
                pl.BlockSpec((outs, block, width), lambda i, c: (0, 0, 0)),
            ],
        ),
        out_shape=[
            jax.ShapeDtypeStruct((wide, width), F32),
            jax.ShapeDtypeStruct((width, wide), F32),
            jax.ShapeDtypeStruct((outs, block, width), F32),
        ],
        compiler_params=params(60),
        cost_estimate=cost(2 * half * width, 2 * half * width * 6),
        name="unpack_early",
    )(core.reshape(1), *(own, other) * 3)
    return down, up, out.reshape(width, width)


def unpack_whole_kernel(heights, core_ref, own_ref, other_ref, *out_refs):
    half = own_ref.shape[0]
    lower = core_ref[0] == 0
    first = 0
    for height, out_ref in zip(heights, out_refs):
        for part in range(2):
            start, stop = max(first, part * half), min(first + height, (part + 1) * half)
            if start < stop:
                span = slice(start - part * half, stop - part * half)
                near, far = (own_ref, other_ref) if part == 0 else (other_ref, own_ref)
                rows = jnp.where(lower, near[span, :], far[span, :])
                out_ref[start - first : stop - first, :] = rows.astype(F32)
        first += height


def unpack_whole(core, own, other, heights):
    width = own.shape[1]
    vmem = pl.BlockSpec(memory_space=pltpu.VMEM)
    return pl.pallas_call(
        functools.partial(unpack_whole_kernel, heights),
        in_specs=[pl.BlockSpec(memory_space=pltpu.SMEM), vmem, vmem],
        out_specs=[vmem] * len(heights),
        out_shape=[jax.ShapeDtypeStruct((height, width), F32) for height in heights],
        compiler_params=params(60),
        name="unpack_whole",
    )(core.reshape(1), own, other)


def cut(value, axis):
    rows = value.shape[0] // 2
    me = lax.axis_index(axis)
    keep = lax.dynamic_slice_in_dim(value, me * rows, rows, 0)
    return keep, lax.dynamic_slice_in_dim(value, (1 - me) * rows, rows, 0)


def swap(value, axis):
    return lax.ppermute(value, axis, SWAP)


def join(value, other, axis):
    first = lax.axis_index(axis) == 0
    return jnp.concatenate([jnp.where(first, value, other), jnp.where(first, other, value)], axis=0)


def stages_of(dp_axes):
    near, far = dp_axes[-2], dp_axes[-3::-1]
    down = [((near, "seq"), True), (("seq", near), True)] + [((axis,), True) for axis in far]
    return down + [(axes, False) for axes, _ in down[::-1]]


def begin(pieces, stage):
    axes, halves = stage
    if len(pieces) < len(axes):
        pieces = jnp.split(pieces[0], 2, axis=0)
    if len(pieces) > len(axes):
        pieces = [jnp.concatenate(pieces, axis=0)]
    if halves:
        keeps, sends = zip(*(cut(p, axis) for p, axis in zip(pieces, axes)))
        return list(keeps), list(sends)
    return list(pieces), list(pieces)


def travel(sends, stage):
    return [swap(s, axis) for s, axis in zip(sends, stage[0])]


def end(keeps, arrived, stage):
    axes, halves = stage
    if halves:
        return [k + a for k, a in zip(keeps, arrived)]
    return [join(k, a, axis) for k, a, axis in zip(keeps, arrived, axes)]


def run_stages(pieces, stages):
    for stage in stages:
        keeps, sends = begin(pieces, stage)
        pieces = end(keeps, travel(sends, stage), stage)
    return pieces


def local(
    dp_axes,
    gene_ids,
    homolog_ids,
    knowledge_ids,
    expr_bins,
    species,
    cell_lengths,
    gene_table,
    knowledge_tables,
    expr_table,
    w_query,
    b_query,
    w_key,
    w_value,
    b_value,
    w_out,
    b_out,
    gain_one,
    shift_one,
    w_up,
    b_up,
    w_down,
    b_down,
    gain_two,
    shift_two,
    cotangent,
):
    tokens = gene_ids.shape[1]
    rows_dev, width = gene_table.shape
    wide = w_up.shape[1]
    every = (*dp_axes, "seq")
    top_axis, group_axes = dp_axes[0], (*dp_axes[1:], "seq")
    devices = lax.axis_size(every)
    group = devices // 2
    capacity = 2 * tokens // devices
    slots_all = 2 * capacity
    slots = group * slots_all
    bins = expr_table.shape[0]
    me = lax.axis_index("seq")

    def exchange(value, axis):
        return lax.all_to_all(value, group_axes, split_axis=axis, concat_axis=axis, tiled=True)

    gene_table, knowledge_tables = lax.optimization_barrier((gene_table, knowledge_tables))
    gene_other = lax.ppermute(gene_table, top_axis, SWAP)
    know_sum = jnp.sum(knowledge_tables.astype(F32), axis=0).astype(BF16)
    chosen = jnp.where(species[0] == 1, homolog_ids, gene_ids).reshape(-1)
    requests, gene_slot, know_slot = route(
        lax.axis_index(top_axis), chosen, knowledge_ids.reshape(-1), rows_dev, capacity, devices
    )
    asked = exchange(requests.reshape(2, group, slots_all), 1).reshape(2, slots)
    asked, gene_other, know_sum = lax.optimization_barrier((asked, gene_other, know_sum))
    know_other = lax.ppermute(know_sum, top_axis, SWAP)
    tables = [
        jnp.concatenate([gene_table, know_sum], axis=0),
        jnp.concatenate([gene_other, know_other], axis=0),
    ]
    row_at = jnp.arange(2 * rows_dev)
    slot_at = jnp.arange(slots)
    bin_hot = hot(expr_bins.reshape(-1)[:, None], jnp.arange(bins)[None, :])
    embedded = mm(bin_hot, expr_table)
    slot_hots = []
    for part in range(2):
        found = mm(hot(asked[part][:, None], row_at[None, :]), tables[part]).astype(BF16)
        fetched = exchange(found.reshape(group, slots_all, width), 0).reshape(slots, width)
        at = slot_at[None, :] + part * slots
        slot_hots.append(((at == gene_slot) | (at == know_slot)).astype(BF16))
        embedded = embedded + mm(slot_hots[part], fetched)
    x_low = embedded.astype(BF16)

    x_other = lax.ppermute(x_low, "seq", SWAP)
    query = (mm(x_low, w_query) + b_query).astype(BF16)
    key, key_other = (mm(x, w_key).astype(BF16) for x in (x_low, x_other))
    value, value_other = ((mm(x, w_value) + b_value).astype(BF16) for x in (x_low, x_other))
    mine = jnp.stack([me * tokens, cell_lengths[0]]).astype(jnp.int32)
    others = jnp.stack([(1 - me) * tokens, cell_lengths[0]]).astype(jnp.int32)
    owned = [row_at[:, None] == asked[part][None, :] for part in range(2)]
    counts = [jnp.sum(o.astype(jnp.int32), axis=1) for o in owned]
    counts_back = lax.ppermute(counts[1], top_axis, SWAP)
    first_part = attend(mine, query, key, value)
    first_part, counts_back = lax.optimization_barrier((first_part, counts_back))
    row_counts = counts[0] + counts_back
    context, lse = attend(others, query, key_other, value_other, first_part)

    small = jnp.stack([b_out, gain_one, shift_one, b_down, gain_two, shift_two])
    (
        layer_output,
        ctx_low,
        normed_low,
        activated,
        grad_ffn,
        grad_pre,
        grad_attn,
        grad_one,
        grad_ctx,
        sums,
        up_sums,
    ) = middle(
        context, embedded, cotangent.reshape(tokens, width), w_out, w_up, w_down, small, b_up[None, :]
    )

    core = dp_axes[-1]
    stages = stages_of(dp_axes)
    my_core = lax.axis_index(core)
    lefts_rights = (activated, grad_ffn, grad_pre, normed_low, ctx_low, grad_attn)
    sent = weight_sums(1 - my_core, *lefts_rights)
    sent, lefts_rights = lax.optimization_barrier((sent, lefts_rights))
    arrived = swap(sent, core)
    kept = weight_sums(my_core, *lefts_rights)
    kept, arrived, grad_ctx = lax.optimization_barrier((kept, arrived, grad_ctx))
    early = jnp.split(kept + arrived, 2, axis=0)
    pairs = width // PAIR
    third = pairs // 3
    sides = ((others, key_other, value_other), (mine, key, value))
    parts = (((0, 2 * third), (2 * third, third)), ((0, third), (third, third), (2 * third, third)))
    done = 0
    grads = []
    before = ()
    for side, (place, keys, values) in enumerate(sides):
        into = ()
        for first, count in parts[side]:
            keeps, sends = begin(early, stages[done])
            keeps, sends, grad_ctx, into, before = lax.optimization_barrier(
                (keeps, sends, grad_ctx, into, before)
            )
            came = travel(sends, stages[done])
            into = attend_back(
                place, query, grad_ctx, context, lse, keys, values, first, count, before, into
            )
            came, into = lax.optimization_barrier((came, into))
            early = end(keeps, came, stages[done])
            done += 1
        grads.append(into)
        if side == 0:
            before = into[:1]
            dx_other = (mm(into[1], w_key, NT) + mm(into[2], w_value, NT)).astype(BF16)
            dx_other, before = lax.optimization_barrier((dx_other, before))
            dx_from_other = swap(dx_other, "seq")
    (_, dk_other, dv_other), (dq, dk, dv) = grads
    keeps, sends = begin(early, stages[done])
    keeps, sends, dq, dk, dv, dx_from_other = lax.optimization_barrier(
        (keeps, sends, dq, dk, dv, dx_from_other)
    )
    came = travel(sends, stages[done])
    grad_embedded = (
        grad_one
        + mm(dq, w_query, NT)
        + mm(dk, w_key, NT)
        + mm(dv, w_value, NT)
        + dx_from_other.astype(F32)
    )
    grad_low = grad_embedded.astype(BF16)
    grad_low, came = lax.optimization_barrier((grad_low, came))
    keeps, sends = begin(end(keeps, came, stages[done]), stages[done + 1])
    done += 1
    keeps, sends, grad_low = lax.optimization_barrier((keeps, sends, grad_low))
    came = travel(sends, stages[done])

    outgoing = [mm(hots, grad_low, TN).astype(BF16) for hots in slot_hots]
    outgoing, dq, dk, dv, came = lax.optimization_barrier((outgoing, dq, dk, dv, came))
    early = end(keeps, came, stages[done])
    done += 1

    def give_back(rows):
        return exchange(rows.reshape(group, slots_all, width), 0).reshape(slots, width)

    returned_other = give_back(outgoing[1])
    w_query_grad = mm(x_low, dq, TN)
    w_key_grad = mm(x_low, dk, TN) + mm(x_other, dk_other, TN)
    w_value_grad = mm(x_low, dv, TN) + mm(x_other, dv_other, TN)
    b_query_grad = jnp.sum(dq.astype(F32), axis=0)
    b_value_grad = jnp.sum(dv.astype(F32), axis=0) + jnp.sum(dv_other.astype(F32), axis=0)
    grad_rest = (grad_embedded - grad_low.astype(F32)).astype(BF16)
    expr_grad = mm(bin_hot, grad_low, TN) + mm(bin_hot, grad_rest, TN)
    short = jnp.concatenate(
        [
            jnp.sum(sums.reshape(6, 8, width), axis=1),
            jnp.sum(up_sums, axis=0).reshape(wide // width, width),
            b_query_grad[None, :],
            b_value_grad[None, :],
        ],
        axis=0,
    )
    block = 128
    short = jnp.pad(short, ((0, -short.shape[0] % block), (0, 0)))
    late = [w_query_grad, w_key_grad, w_value_grad, expr_grad, short]
    heights = [item.shape[0] for item in late]
    late = jnp.concatenate([item.astype(BF16) for item in late], axis=0)
    keep, send = cut(late, core)
    keep, send, outgoing, returned_other = lax.optimization_barrier(
        (keep, send, outgoing, returned_other)
    )
    returned = give_back(outgoing[0])
    for_other = mm(owned[1].astype(BF16), returned_other).astype(BF16)
    late = jnp.split(keep + swap(send, core), 2, axis=0)
    returned, late, early, for_other = lax.optimization_barrier((returned, late, early, for_other))
    table_own = mm(owned[0].astype(BF16), returned)
    from_other = swap(for_other, top_axis)
    last = len(stages) - 1
    early_step = begin(early, stages[done])
    for at, stage in enumerate(stages):
        keeps, sends = begin(late, stage)
        if at == 1:
            keeps, sends, early_step = lax.optimization_barrier((keeps, sends, early_step))
            early_came = travel(early_step[1], stages[done])
        if at == 2:
            keeps, sends, from_other = lax.optimization_barrier((keeps, sends, from_other))
        if at == 3:
            keeps, sends, early_came = lax.optimization_barrier((keeps, sends, early_came))
            early = end(early_step[0], early_came, stages[done])
            early = jnp.concatenate(run_stages(early, stages[done + 1 :]), axis=0)
            early_step = (early, swap(early, core))
        if at == last - 2:
            keeps, sends, early_step = lax.optimization_barrier((keeps, sends, early_step))
        came = travel(sends, stage)
        if at == 4:
            table_grads = table_own + from_other.astype(F32)
            came, table_grads = lax.optimization_barrier((came, table_grads))
        if at == last - 2:
            early = unpack_early(my_core, *early_step, wide)
            came, early = lax.optimization_barrier((came, early))
        late = end(keeps, came, stage)
    late = jnp.concatenate(late, axis=0)
    late_other = swap(late, core)
    w_down_grad, w_up_grad, w_out_grad = early
    w_query_grad, w_key_grad, w_value_grad, expr_grad, short = unpack_whole(
        my_core, late, late_other, heights
    )
    gain_two_grad, shift_two_grad, b_down_grad, gain_one_grad, shift_one_grad, b_out_grad = (
        short[i] for i in range(6)
    )
    b_up_grad = short[6 : 6 + wide // width].reshape(wide)
    b_query_grad, b_value_grad = short[6 + wide // width], short[7 + wide // width]
    return (
        layer_output.reshape(1, tokens, width),
        table_grads[:rows_dev],
        table_grads[rows_dev:],
        expr_grad,
        w_query_grad,
        b_query_grad,
        w_key_grad,
        w_value_grad,
        b_value_grad,
        w_out_grad,
        b_out_grad,
        gain_one_grad,
        shift_one_grad,
        w_up_grad,
        b_up_grad,
        w_down_grad,
        b_down_grad,
        gain_two_grad,
        shift_two_grad,
        row_counts.reshape(2, rows_dev),
    )


def solution(mesh):
    bits = mesh.shape["dp"].bit_length() - 1
    dp_axes = tuple(f"dp{i}" for i in range(bits))
    fine = Mesh(mesh.devices.reshape((2,) * bits + (mesh.shape["seq"],)), (*dp_axes, "seq"))
    every = (*dp_axes, "seq")
    whole = P()
    placed = (
        (P(dp_axes, "seq"),) * 4
        + (P(dp_axes),) * 2
        + (P(every, None), P(None, every, None))
        + (whole,) * 16
        + (P(dp_axes, "seq", None),)
    )
    given = (
        (P(dp_axes, "seq", None),)
        + (P(every, None),) * 2
        + (whole,) * 16
        + (P(None, every),)
    )
    return jax.shard_map(
        functools.partial(local, dp_axes), mesh=fine, in_specs=placed, out_specs=given, check_vma=False
    )
```

```python
import functools

import jax
import jax.numpy as jnp
from jax import lax
from jax.experimental import pallas as pl
from jax.experimental.pallas import tpu as pltpu
from jax.sharding import Mesh, PartitionSpec as P

HEADS = 12
HEAD_DIM = 64
PAIR = 2 * HEAD_DIM
KEY_CHUNK = 512
LOG2E = 1.4426950408889634
SWAP = [(0, 1), (1, 0)]
F32 = jnp.float32
BF16 = jnp.bfloat16
NN = (((1,), (0,)), ((), ()))
NT = (((1,), (1,)), ((), ()))
TN = (((0,), (0,)), ((), ()))


def mm(left, right, dims=NN):
    return lax.dot_general(left, right, dims, preferred_element_type=F32)


def params(mib):
    return pltpu.CompilerParams(vmem_limit_bytes=mib * 2**20)


def cost(flops, moved):
    return pl.CostEstimate(flops=flops, bytes_accessed=moved, transcendentals=0)


def hot(left, right):
    return (left == right).astype(BF16)


def route_kernel(
    rows_dev, capacity, top_ref, gene_ref, know_ref, req_ref, gene_slot_ref, know_slot_ref
):
    tokens = gene_ref.shape[0]
    devices, slots_all = req_ref.shape
    lane = lax.broadcasted_iota(jnp.int32, (tokens, devices), 1)
    top = top_ref[0]
    half = jnp.where((lane & 1) == 0, top, 1 - top)
    first = (half * (devices // 2) + (lane >> 1)) * rows_dev
    earlier = (
        lax.broadcasted_iota(jnp.int32, (tokens, tokens), 0)
        > lax.broadcasted_iota(jnp.int32, (tokens, tokens), 1)
    ).astype(F32).astype(BF16)
    rank_lane = lax.broadcasted_iota(jnp.int32, (tokens, capacity), 1)
    asked = []
    for which, (ids_ref, slot_ref) in enumerate(((gene_ref, gene_slot_ref), (know_ref, know_slot_ref))):
        row = ids_ref[...] - first
        hit = (row >= 0) & (row < rows_dev)
        before = mm(earlier, hit.astype(F32).astype(BF16))
        rank = jnp.sum(jnp.where(hit, before, 0.0), axis=1, keepdims=True)
        owner = jnp.sum(jnp.where(hit, lane, 0).astype(F32), axis=1, keepdims=True)
        slot_ref[...] = (owner * slots_all + rank).astype(jnp.int32) + which * capacity
        rank_hit = (rank_lane == rank.astype(jnp.int32)).astype(F32).astype(BF16)
        coded = jnp.where(hit, row + 1, 0)
        high = (coded >> 4).astype(F32).astype(BF16)
        low = (coded & 15).astype(F32).astype(BF16)
        wanted = (mm(high, rank_hit, TN) * 16.0 + mm(low, rank_hit, TN)).astype(jnp.int32)
        asked.append(jnp.where(wanted > 0, wanted - 1 + which * rows_dev, -1))
    req_ref[:, :capacity] = asked[0]
    req_ref[:, capacity:] = asked[1]


def route(top, gene_ids, know_ids, rows_dev, capacity, devices):
    tokens = gene_ids.shape[0]
    return pl.pallas_call(
        functools.partial(route_kernel, rows_dev, capacity),
        in_specs=[pl.BlockSpec(memory_space=pltpu.SMEM)] + [pl.BlockSpec(memory_space=pltpu.VMEM)] * 2,
        out_shape=(
            jax.ShapeDtypeStruct((devices, 2 * capacity), jnp.int32),
            jax.ShapeDtypeStruct((tokens, 1), jnp.int32),
            jax.ShapeDtypeStruct((tokens, 1), jnp.int32),
        ),
        compiler_params=params(32),
        name="route",
    )(top.reshape(1), gene_ids[:, None], know_ids[:, None])


def fill_keys(aug_ref, key, first_key, count):
    lanes = lax.broadcasted_iota(jnp.int32, key.shape, 1)
    at = lax.broadcasted_iota(jnp.int32, key.shape, 0) + first_key
    bias = jnp.where(at < count, 0.0, -1e30).astype(BF16)
    none = jnp.zeros_like(key)
    aug_ref[:, :PAIR] = jnp.where(lanes < HEAD_DIM, key, jnp.where(lanes == HEAD_DIM, bias, none))
    aug_ref[:, PAIR : 2 * PAIR] = key
    aug_ref[:, 2 * PAIR :] = jnp.where(lanes >= HEAD_DIM, key, jnp.where(lanes == 0, bias, none))


def head_mask(shape, head):
    lanes = lax.broadcasted_iota(jnp.int32, shape, 1)
    return (lanes >= head * HEAD_DIM) & (lanes < (head + 1) * HEAD_DIM)


def spread_query(query, head):
    lanes = lax.broadcasted_iota(jnp.int32, query.shape, 1)
    scaled = query.astype(F32) * (HEAD_DIM ** (-0.5) * LOG2E)
    scaled = jnp.where(head_mask(query.shape, head), scaled, 0.0)
    high = scaled.astype(BF16)
    low = scaled - high.astype(F32)
    low = jnp.where(lanes == (1 - head) * HEAD_DIM, 1.0, low).astype(BF16)
    return jnp.concatenate([low, high] if head == 0 else [high, low], axis=1)


def fold_rows(value, how):
    return how(value.reshape(value.shape[0] // 8, 8, value.shape[1]), axis=0)


def attend_kernel(merge, where_ref, q_ref, k_ref, v_ref, *rest):
    if merge:
        out_in_ref, lse_in_ref, out_ref, lse_ref, aug_ref, vt_ref, score_ref = rest
    else:
        out_ref, lse_ref, aug_ref, vt_ref, score_ref = rest
    spans = [slice(c, c + KEY_CHUNK) for c in range(0, k_ref.shape[0], KEY_CHUNK)]
    fill_keys(aug_ref, k_ref[...], where_ref[0], where_ref[1])
    vt_ref[...] = v_ref[...].T
    outs = []
    for head in range(2):
        own = slice(head * HEAD_DIM, (head + 1) * HEAD_DIM)
        query = spread_query(q_ref[...], head)
        top = None
        for span in spans:
            scores = mm(aug_ref[span, head * PAIR : (head + 2) * PAIR], query, NT)
            score_ref[head, span, :] = scores
            high = fold_rows(scores, jnp.max)
            top = high if top is None else jnp.maximum(top, high)
        top = jnp.max(top, axis=0, keepdims=True)
        total = None
        acc = None
        for span in spans:
            probs = jnp.exp2(score_ref[head, span, :] - top)
            part = fold_rows(probs, jnp.sum)
            total = part if total is None else total + part
            part = mm(vt_ref[own, span], probs.astype(BF16))
            acc = part if acc is None else acc + part
        total = jnp.sum(total, axis=0, keepdims=True)
        lse = top + jnp.log2(total)
        if merge:
            before = lse_in_ref[0, head : head + 1, :]
            both = jnp.maximum(lse, before)
            both = both + jnp.log2(jnp.exp2(lse - both) + jnp.exp2(before - both))
            acc = acc * (jnp.exp2(lse - both) / total)
            acc = acc + out_in_ref[own, :] * jnp.exp2(before - both)
            lse = both
        else:
            acc = acc / total
        lse_ref[0, head : head + 1, :] = lse
        outs.append(acc)
    out = jnp.concatenate(outs, axis=0)
    out_ref[...] = out.T if merge else out


def attend(where, query, key, value, before=()):
    tokens, width = query.shape
    keys = key.shape[0]
    pairs = width // PAIR
    column = lambda rows: pl.BlockSpec((rows, PAIR), lambda p, w: (0, p))
    upright = pl.BlockSpec((PAIR, tokens), lambda p, w: (p, 0))
    stats = pl.BlockSpec((1, 2, tokens), lambda p, w: (p, 0, 0))
    merge = len(before) > 0
    return pl.pallas_call(
        functools.partial(attend_kernel, merge),
        grid_spec=pltpu.PrefetchScalarGridSpec(
            num_scalar_prefetch=1,
            grid=(pairs,),
            in_specs=[column(tokens), column(keys), column(keys)] + ([upright, stats] if merge else []),
            out_specs=[column(tokens) if merge else upright, stats],
            scratch_shapes=[
                pltpu.VMEM((keys, 3 * PAIR), BF16),
                pltpu.VMEM((PAIR, keys), BF16),
                pltpu.VMEM((2, keys, tokens), F32),
            ],
        ),
        out_shape=(
            jax.ShapeDtypeStruct((tokens, width) if merge else (width, tokens), F32),
            jax.ShapeDtypeStruct((pairs, 2, tokens), F32),
        ),
        compiler_params=params(48),
        cost_estimate=cost(16 * tokens * keys * width, 2 * tokens * width * 10),
        name="attend_more" if merge else "attend",
    )(where, query, key, value, *before)


def attend_back_kernel(
    add, untouched, where_ref, q_ref, g_ref, o_ref, lse_ref, k_ref, v_ref, *rest
):
    dq_in_ref = rest[0] if add else None
    dq_ref, dk_ref, dv_ref, aug_ref, kt_ref = rest[int(add) + untouched :]
    fill_keys(aug_ref, k_ref[...], where_ref[0], where_ref[1])
    kt_ref[...] = k_ref[...].T
    grad = g_ref[...]
    picks = (
        lax.broadcasted_iota(jnp.int32, (8, PAIR), 1) // HEAD_DIM
        == lax.broadcasted_iota(jnp.int32, (8, PAIR), 0)
    ).astype(F32)
    inner = lax.dot_general(
        picks,
        grad.astype(F32) * o_ref[...],
        NT,
        precision=lax.Precision.HIGHEST,
        preferred_element_type=F32,
    )
    scaled = q_ref[...] * jnp.asarray(HEAD_DIM ** (-0.5), BF16)
    none = jnp.zeros_like(grad)
    masks = [head_mask(grad.shape, head) for head in range(2)]
    queries = [spread_query(q_ref[...], head) for head in range(2)]
    q_heads = [jnp.where(m, scaled, none) for m in masks]
    g_heads = [jnp.where(m, grad, none) for m in masks]
    dqs = [None, None]
    for first in range(0, k_ref.shape[0], KEY_CHUNK):
        span = slice(first, first + KEY_CHUNK)
        dk = None
        dv = None
        for head in range(2):
            own = slice(head * HEAD_DIM, (head + 1) * HEAD_DIM)
            scores = mm(aug_ref[span, head * PAIR : (head + 2) * PAIR], queries[head], NT)
            probs = jnp.exp2(scores - lse_ref[0, head : head + 1, :])
            grad_probs = mm(v_ref[span, :], g_heads[head], NT)
            grad_scores = (probs * (grad_probs - inner[head : head + 1, :])).astype(BF16)
            part = mm(kt_ref[own, span], grad_scores)
            dqs[head] = part if dqs[head] is None else dqs[head] + part
            part = mm(probs.astype(BF16), g_heads[head])
            dv = part if dv is None else dv + part
            part = mm(grad_scores, q_heads[head])
            dk = part if dk is None else dk + part
        dk_ref[span, :] = dk.astype(BF16)
        dv_ref[span, :] = dv.astype(BF16)
    dq = jnp.concatenate(dqs, axis=0).T * HEAD_DIM ** (-0.5)
    if add:
        dq = dq + dq_in_ref[...]
    dq_ref[...] = dq.astype(dq_ref.dtype)


def attend_back(where, query, grad, out, lse, key, value, first, count, before, into):
    tokens, width = query.shape
    keys = key.shape[0]
    column = lambda rows: pl.BlockSpec((rows, PAIR), lambda p, w: (0, p + first))
    untouched = pl.BlockSpec(memory_space=pl.ANY)
    add = len(before) > 0
    given = 7 + len(before)
    return pl.pallas_call(
        functools.partial(attend_back_kernel, add, len(into)),
        grid_spec=pltpu.PrefetchScalarGridSpec(
            num_scalar_prefetch=1,
            grid=(count,),
            in_specs=[column(tokens)] * 3
            + [pl.BlockSpec((1, 2, tokens), lambda p, w: (p + first, 0, 0))]
            + [column(keys)] * 2
            + [column(tokens)] * len(before)
            + [untouched] * len(into),
            out_specs=[column(tokens), column(keys), column(keys)],
            scratch_shapes=[
                pltpu.VMEM((keys, 3 * PAIR), BF16),
                pltpu.VMEM((PAIR, keys), BF16),
            ],
        ),
        out_shape=(
            jax.ShapeDtypeStruct((tokens, width), BF16 if add else F32),
            jax.ShapeDtypeStruct((keys, width), BF16),
            jax.ShapeDtypeStruct((keys, width), BF16),
        ),
        input_output_aliases={given + i: i for i in range(len(into))},
        compiler_params=params(56),
        cost_estimate=cost(40 * tokens * keys * PAIR * count, 2 * tokens * PAIR * count * 12),
        name=("attend_back_more" if add else "attend_back") + str(first),
    )(where, query, grad, out, lse, key, value, *before, *into)


def norm_parts(value):
    centre = jnp.mean(value, axis=-1, keepdims=True)
    centred = value - centre
    variance = jnp.mean(centred * centred, axis=-1, keepdims=True)
    inverse = lax.rsqrt(variance + 1e-05)
    return centred * inverse, inverse


def norm_back(grad, unit, inverse, gain):
    grad_unit = grad * gain
    return inverse * (
        grad_unit
        - jnp.mean(grad_unit, axis=-1, keepdims=True)
        - unit * jnp.mean(grad_unit * unit, axis=-1, keepdims=True)
    )


def middle_kernel(
    ctx_ref,
    emb_ref,
    cot_ref,
    w_out_ref,
    w_up_ref,
    w_down_ref,
    small_ref,
    b_up_ref,
    out_ref,
    ctx_low_ref,
    normed_ref,
    act_ref,
    gffn_ref,
    gpre_ref,
    gattn_ref,
    gone_ref,
    gctx_ref,
    sums_ref,
    up_sums_ref,
    slope_ref,
):
    step = pl.program_id(0)
    width = emb_ref.shape[1]
    wide = w_up_ref.shape[1]

    @pl.when(step == 0)
    def _():
        sums_ref[...] = jnp.zeros_like(sums_ref)
        up_sums_ref[...] = jnp.zeros_like(up_sums_ref)

    b_out, gain_one, shift_one, b_down, gain_two, shift_two = (
        small_ref[i : i + 1, :] for i in range(6)
    )
    ctx_low = ctx_ref[...].astype(BF16)
    ctx_low_ref[...] = ctx_low
    unit_one, inv_one = norm_parts(emb_ref[...] + mm(ctx_low, w_out_ref[...]) + b_out)
    normed = unit_one * gain_one + shift_one
    normed_low = normed.astype(BF16)
    normed_ref[...] = normed_low
    ffn = None
    for c in range(wide // width):
        span = slice(c * width, (c + 1) * width)
        pre = mm(normed_low, w_up_ref[:, span]) + b_up_ref[:, span]
        below = 0.5 * (1.0 + lax.erf(pre * 0.7071067811865476))
        act = (pre * below).astype(BF16)
        act_ref[:, span] = act
        slope_ref[:, span] = below + pre * (0.3989422804014327 * jnp.exp(-0.5 * pre * pre))
        part = mm(act, w_down_ref[span, :])
        ffn = part if ffn is None else ffn + part
    unit_two, inv_two = norm_parts(normed + ffn + b_down)
    out_ref[...] = (unit_two * gain_two + shift_two).astype(BF16)
    grad = cot_ref[...].astype(F32)
    sums_ref[0:8, :] += fold_rows(grad * unit_two, jnp.sum)
    sums_ref[8:16, :] += fold_rows(grad, jnp.sum)
    grad_two = norm_back(grad, unit_two, inv_two, gain_two)
    gffn = grad_two.astype(BF16)
    gffn_ref[...] = gffn
    sums_ref[16:24, :] += fold_rows(gffn.astype(F32), jnp.sum)
    grad_normed = grad_two
    for c in range(wide // width):
        span = slice(c * width, (c + 1) * width)
        gpre = (mm(gffn, w_down_ref[span, :], NT) * slope_ref[:, span]).astype(BF16)
        gpre_ref[:, span] = gpre
        up_sums_ref[:, span] += fold_rows(gpre.astype(F32), jnp.sum)
        grad_normed = grad_normed + mm(gpre, w_up_ref[:, span], NT)
    sums_ref[24:32, :] += fold_rows(grad_normed * unit_one, jnp.sum)
    sums_ref[32:40, :] += fold_rows(grad_normed, jnp.sum)
    grad_one = norm_back(grad_normed, unit_one, inv_one, gain_one)
    gone_ref[...] = grad_one
    gattn = grad_one.astype(BF16)
    gattn_ref[...] = gattn
    sums_ref[40:48, :] += fold_rows(gattn.astype(F32), jnp.sum)
    gctx_ref[...] = mm(gattn, w_out_ref[...], NT).astype(BF16)


def middle(ctx, embedded, cotangent, w_out, w_up, w_down, small, b_up, block=256):
    tokens, width = embedded.shape
    wide = w_up.shape[1]
    whole = lambda a: pl.BlockSpec(a.shape, lambda i: (0, 0), pipeline_mode=pl.Buffered(1))
    rows = lambda n: pl.BlockSpec((block, n), lambda i: (i, 0))
    fixed = lambda r, n: pl.BlockSpec((r, n), lambda i: (0, 0))
    shape = lambda n, dtype: jax.ShapeDtypeStruct((tokens, n), dtype)
    return pl.pallas_call(
        middle_kernel,
        grid=(tokens // block,),
        in_specs=[rows(width)] * 3 + [whole(w_out), whole(w_up), whole(w_down), whole(small), whole(b_up)],
        out_specs=[
            rows(width),
            rows(width),
            rows(width),
            rows(wide),
            rows(width),
            rows(wide),
            rows(width),
            rows(width),
            rows(width),
            fixed(48, width),
            fixed(8, wide),
        ],
        out_shape=[
            shape(width, BF16),
            shape(width, BF16),
            shape(width, BF16),
            shape(wide, BF16),
            shape(width, BF16),
            shape(wide, BF16),
            shape(width, BF16),
            shape(width, F32),
            shape(width, BF16),
            jax.ShapeDtypeStruct((48, width), F32),
            jax.ShapeDtypeStruct((8, wide), F32),
        ],
        scratch_shapes=[pltpu.VMEM((block, wide), F32)],
        compiler_params=params(60),
        cost_estimate=cost(tokens * width * (8 * wide + 4 * width) * 2, 2 * tokens * (2 * wide + 14 * width)),
        name="middle",
    )(ctx, embedded, cotangent, w_out, w_up, w_down, small, b_up)


def weight_sums_kernel(counts, half_ref, act_ref, gffn_ref, gpre_ref, norm_ref, ctx_ref, gattn_ref, out_ref):
    at = pl.program_id(0) + half_ref[0] * pl.num_programs(0)
    first = 0
    for count, left, right in zip(counts, (act_ref, gpre_ref, ctx_ref), (gffn_ref, norm_ref, gattn_ref)):
        @pl.when((at >= first) & (at < first + count))
        def _(left=left, right=right):
            out_ref[...] = mm(left[...], right[...], TN).astype(BF16)
        first += count


def weight_sums(half, activated, grad_ffn, grad_pre, normed, ctx, grad_attn, block=384):
    tokens, width = grad_ffn.shape
    lefts = (activated, grad_pre, ctx)
    counts = [left.shape[1] // block for left in lefts]
    steps = sum(counts) // 2
    specs = []
    first = 0
    for left, right, count in zip(lefts, (grad_ffn, normed, grad_attn), counts):
        specs.append(
            pl.BlockSpec(
                (tokens, block),
                lambda i, h, first=first, count=count: (0, jnp.clip(i + h[0] * steps - first, 0, count - 1)),
            )
        )
        specs.append(pl.BlockSpec((tokens, width), lambda i, h: (0, 0), pipeline_mode=pl.Buffered(1)))
        first += count
    return pl.pallas_call(
        functools.partial(weight_sums_kernel, counts),
        grid_spec=pltpu.PrefetchScalarGridSpec(
            num_scalar_prefetch=1,
            grid=(steps,),
            in_specs=specs,
            out_specs=pl.BlockSpec((block, width), lambda i, h: (i, 0)),
        ),
        out_shape=jax.ShapeDtypeStruct((steps * block, width), BF16),
        compiler_params=params(60),
        cost_estimate=cost(2 * tokens * width * block * steps, 2 * steps * block * (tokens + width)),
        name="weight_sums",
    )(half.reshape(1), activated, grad_ffn, grad_pre, normed, ctx, grad_attn)


def unpack_kernel(first, half, turn, core_ref, own_ref, other_ref, out_ref):
    at = pl.program_id(0) + first
    mine = (at >= half) == (core_ref[0] == 1)
    rows = jnp.where(mine, own_ref[...], other_ref[...]).astype(F32)
    out_ref[...] = rows.T if turn else rows


def unpack(core, own, other, first, rows, turn, block=384):
    half, width = own.shape[0] // block, own.shape[1]
    first, steps = first // block, rows // block

    def place(i, c, owner):
        at = i + first
        inside = (at >= half) == (c[0] == owner)
        return jnp.where(inside, at % half, half - 1), 0

    return pl.pallas_call(
        functools.partial(unpack_kernel, first, half, turn),
        grid_spec=pltpu.PrefetchScalarGridSpec(
            num_scalar_prefetch=1,
            grid=(steps,),
            in_specs=[
                pl.BlockSpec((block, width), functools.partial(place, owner=1)),
                pl.BlockSpec((block, width), functools.partial(place, owner=0)),
            ],
            out_specs=pl.BlockSpec((width, block), lambda i, c: (0, i))
            if turn
            else pl.BlockSpec((block, width), lambda i, c: (i, 0)),
        ),
        out_shape=jax.ShapeDtypeStruct((width, rows) if turn else (rows, width), F32),
        compiler_params=params(60),
        cost_estimate=cost(rows * width, rows * width * 6),
        name="unpack" + str(first),
    )(core.reshape(1), own, other)


def unpack_whole_kernel(heights, core_ref, own_ref, other_ref, *out_refs):
    half = own_ref.shape[0]
    lower = core_ref[0] == 0
    first = 0
    for height, out_ref in zip(heights, out_refs):
        for part in range(2):
            start, stop = max(first, part * half), min(first + height, (part + 1) * half)
            if start < stop:
                span = slice(start - part * half, stop - part * half)
                near, far = (own_ref, other_ref) if part == 0 else (other_ref, own_ref)
                rows = jnp.where(lower, near[span, :], far[span, :])
                out_ref[start - first : stop - first, :] = rows.astype(F32)
        first += height


def unpack_whole(core, own, other, heights):
    width = own.shape[1]
    vmem = pl.BlockSpec(memory_space=pltpu.VMEM)
    return pl.pallas_call(
        functools.partial(unpack_whole_kernel, heights),
        in_specs=[pl.BlockSpec(memory_space=pltpu.SMEM), vmem, vmem],
        out_specs=[vmem] * len(heights),
        out_shape=[jax.ShapeDtypeStruct((height, width), F32) for height in heights],
        compiler_params=params(60),
        name="unpack_whole",
    )(core.reshape(1), own, other)


def cut(value, axis):
    rows = value.shape[0] // 2
    me = lax.axis_index(axis)
    keep = lax.dynamic_slice_in_dim(value, me * rows, rows, 0)
    return keep, lax.dynamic_slice_in_dim(value, (1 - me) * rows, rows, 0)


def swap(value, axis):
    return lax.ppermute(value, axis, SWAP)


def join(value, other, axis):
    first = lax.axis_index(axis) == 0
    return jnp.concatenate([jnp.where(first, value, other), jnp.where(first, other, value)], axis=0)


def stages_of(dp_axes):
    near, far = dp_axes[-2], dp_axes[-3::-1]
    down = [((near, "seq"), True), (("seq", near), True)] + [((axis,), True) for axis in far]
    return down + [(axes, False) for axes, _ in down[::-1]]


def begin(pieces, stage):
    axes, halves = stage
    if len(pieces) < len(axes):
        pieces = jnp.split(pieces[0], 2, axis=0)
    if len(pieces) > len(axes):
        pieces = [jnp.concatenate(pieces, axis=0)]
    if halves:
        keeps, sends = zip(*(cut(p, axis) for p, axis in zip(pieces, axes)))
        return list(keeps), list(sends)
    return list(pieces), list(pieces)


def travel(sends, stage):
    return [swap(s, axis) for s, axis in zip(sends, stage[0])]


def end(keeps, arrived, stage):
    axes, halves = stage
    if halves:
        return [k + a for k, a in zip(keeps, arrived)]
    return [join(k, a, axis) for k, a, axis in zip(keeps, arrived, axes)]


def run_stages(pieces, stages):
    for stage in stages:
        keeps, sends = begin(pieces, stage)
        pieces = end(keeps, travel(sends, stage), stage)
    return pieces


def local(
    dp_axes,
    gene_ids,
    homolog_ids,
    knowledge_ids,
    expr_bins,
    species,
    cell_lengths,
    gene_table,
    knowledge_tables,
    expr_table,
    w_query,
    b_query,
    w_key,
    w_value,
    b_value,
    w_out,
    b_out,
    gain_one,
    shift_one,
    w_up,
    b_up,
    w_down,
    b_down,
    gain_two,
    shift_two,
    cotangent,
):
    tokens = gene_ids.shape[1]
    rows_dev, width = gene_table.shape
    wide = w_up.shape[1]
    every = (*dp_axes, "seq")
    top_axis, group_axes = dp_axes[0], (*dp_axes[1:], "seq")
    devices = lax.axis_size(every)
    group = devices // 2
    capacity = 2 * tokens // devices
    slots_all = 2 * capacity
    slots = devices * slots_all
    bins = expr_table.shape[0]
    me = lax.axis_index("seq")

    def exchange(value):
        return lax.all_to_all(value, group_axes, split_axis=0, concat_axis=0, tiled=True)

    gene_table, knowledge_tables = lax.optimization_barrier((gene_table, knowledge_tables))
    gene_other = lax.ppermute(gene_table, top_axis, SWAP)
    know_sum = jnp.sum(knowledge_tables.astype(F32), axis=0).astype(BF16)
    chosen = jnp.where(species[0] == 1, homolog_ids, gene_ids).reshape(-1)
    requests, gene_slot, know_slot = route(
        lax.axis_index(top_axis), chosen, knowledge_ids.reshape(-1), rows_dev, capacity, devices
    )
    asked = exchange(requests.reshape(group, 2 * slots_all))
    know_other = lax.ppermute(know_sum, top_axis, SWAP)
    asked, gene_other, know_other = lax.optimization_barrier((asked, gene_other, know_other))
    asked = asked.reshape(group, 2, slots_all)
    shift = jnp.arange(2)[None, :, None] * (2 * rows_dev)
    asked = jnp.where(asked >= 0, asked + shift, -1).reshape(slots)
    tables = jnp.concatenate([gene_table, know_sum, gene_other, know_other], axis=0)
    row_at = jnp.arange(4 * rows_dev)
    bin_hot = hot(expr_bins.reshape(-1)[:, None], jnp.arange(bins)[None, :])
    found = mm(hot(asked[:, None], row_at[None, :]), tables).astype(BF16)
    fetched = exchange(found.reshape(group, 2 * slots_all, width)).reshape(slots, width)
    slot_at = jnp.arange(slots)[None, :]
    slot_hot = ((slot_at == gene_slot) | (slot_at == know_slot)).astype(BF16)
    embedded = mm(slot_hot, fetched) + mm(bin_hot, expr_table)
    x_low = embedded.astype(BF16)

    x_other = lax.ppermute(x_low, "seq", SWAP)
    query = (mm(x_low, w_query) + b_query).astype(BF16)
    key, key_other = (mm(x, w_key).astype(BF16) for x in (x_low, x_other))
    value, value_other = ((mm(x, w_value) + b_value).astype(BF16) for x in (x_low, x_other))
    mine = jnp.stack([me * tokens, cell_lengths[0]]).astype(jnp.int32)
    others = jnp.stack([(1 - me) * tokens, cell_lengths[0]]).astype(jnp.int32)
    block_rows = 2 * rows_dev
    owned = [row_at[at : at + block_rows, None] == asked[None, :] for at in (0, block_rows)]
    counts = [jnp.sum(o.astype(jnp.int32), axis=1) for o in owned]
    counts_back = lax.ppermute(counts[1], top_axis, SWAP)
    first_part = attend(mine, query, key, value)
    first_part, counts_back = lax.optimization_barrier((first_part, counts_back))
    row_counts = counts[0] + counts_back
    context, lse = attend(others, query, key_other, value_other, first_part)

    small = jnp.stack([b_out, gain_one, shift_one, b_down, gain_two, shift_two])
    (
        layer_output,
        ctx_low,
        normed_low,
        activated,
        grad_ffn,
        grad_pre,
        grad_attn,
        grad_one,
        grad_ctx,
        sums,
        up_sums,
    ) = middle(
        context, embedded, cotangent.reshape(tokens, width), w_out, w_up, w_down, small, b_up[None, :]
    )

    core = dp_axes[-1]
    stages = stages_of(dp_axes)
    my_core = lax.axis_index(core)
    lefts_rights = (activated, grad_ffn, grad_pre, normed_low, ctx_low, grad_attn)
    sent = weight_sums(1 - my_core, *lefts_rights)
    sent, lefts_rights = lax.optimization_barrier((sent, lefts_rights))
    arrived = swap(sent, core)
    kept = weight_sums(my_core, *lefts_rights)
    kept, arrived, grad_ctx = lax.optimization_barrier((kept, arrived, grad_ctx))
    early = jnp.split(kept + arrived, 2, axis=0)
    pairs = width // PAIR
    third = pairs // 3
    sides = ((others, key_other, value_other), (mine, key, value))
    parts = (((0, 2 * third), (2 * third, third)), ((0, third), (third, third), (2 * third, third)))
    done = 0
    grads = []
    before = ()
    for side, (place, keys, values) in enumerate(sides):
        into = ()
        for first, count in parts[side]:
            keeps, sends = begin(early, stages[done])
            keeps, sends, grad_ctx, into, before = lax.optimization_barrier(
                (keeps, sends, grad_ctx, into, before)
            )
            came = travel(sends, stages[done])
            into = attend_back(
                place, query, grad_ctx, context, lse, keys, values, first, count, before, into
            )
            came, into = lax.optimization_barrier((came, into))
            early = end(keeps, came, stages[done])
            done += 1
        grads.append(into)
        if side == 0:
            before = into[:1]
            dx_other = (mm(into[1], w_key, NT) + mm(into[2], w_value, NT)).astype(BF16)
            dx_other, before = lax.optimization_barrier((dx_other, before))
            dx_from_other = swap(dx_other, "seq")
    (_, dk_other, dv_other), (dq, dk, dv) = grads
    keeps, sends = begin(early, stages[done])
    keeps, sends, dq, dk, dv, dx_from_other = lax.optimization_barrier(
        (keeps, sends, dq, dk, dv, dx_from_other)
    )
    came = travel(sends, stages[done])
    grad_embedded = (
        grad_one
        + mm(dq, w_query, NT)
        + mm(dk, w_key, NT)
        + mm(dv, w_value, NT)
        + dx_from_other.astype(F32)
    )
    grad_low = grad_embedded.astype(BF16)
    grad_low, came = lax.optimization_barrier((grad_low, came))
    keeps, sends = begin(end(keeps, came, stages[done]), stages[done + 1])
    done += 1
    keeps, sends, grad_low = lax.optimization_barrier((keeps, sends, grad_low))
    came = travel(sends, stages[done])

    outgoing = mm(slot_hot, grad_low, TN).astype(BF16)
    outgoing, dq, dk, dv, came = lax.optimization_barrier((outgoing, dq, dk, dv, came))
    early = end(keeps, came, stages[done])
    done += 1
    returned = exchange(outgoing.reshape(group, 2 * slots_all, width)).reshape(slots, width)
    w_query_grad = mm(x_low, dq, TN)
    w_key_grad = mm(x_low, dk, TN) + mm(x_other, dk_other, TN)
    w_value_grad = mm(x_low, dv, TN) + mm(x_other, dv_other, TN)
    b_query_grad = jnp.sum(dq.astype(F32), axis=0)
    b_value_grad = jnp.sum(dv.astype(F32), axis=0) + jnp.sum(dv_other.astype(F32), axis=0)
    grad_rest = (grad_embedded - grad_low.astype(F32)).astype(BF16)
    expr_grad = mm(bin_hot, grad_low, TN) + mm(bin_hot, grad_rest, TN)
    short = jnp.concatenate(
        [
            jnp.sum(sums.reshape(6, 8, width), axis=1),
            jnp.sum(up_sums, axis=0).reshape(wide // width, width),
            b_query_grad[None, :],
            b_value_grad[None, :],
        ],
        axis=0,
    )
    block = 128
    short = jnp.pad(short, ((0, -short.shape[0] % block), (0, 0)))
    late = [w_query_grad, w_key_grad, w_value_grad, expr_grad, short]
    heights = [item.shape[0] for item in late]
    late = jnp.concatenate([item.astype(BF16) for item in late], axis=0)
    keep, send = cut(late, core)
    late = jnp.split(keep + swap(send, core), 2, axis=0)
    returned, late, early = lax.optimization_barrier((returned, late, early))
    from_other = swap(mm(owned[1].astype(BF16), returned).astype(BF16), top_axis)
    table_own = mm(owned[0].astype(BF16), returned)
    last = len(stages) - 1
    early_parts = []
    early_step = begin(early, stages[done])
    for at, stage in enumerate(stages):
        keeps, sends = begin(late, stage)
        if at == 1:
            keeps, sends, early_step = lax.optimization_barrier((keeps, sends, early_step))
            early_came = travel(early_step[1], stages[done])
        if at == 3:
            keeps, sends, early_came = lax.optimization_barrier((keeps, sends, early_came))
            early = end(early_step[0], early_came, stages[done])
            early = jnp.concatenate(run_stages(early, stages[done + 1 :]), axis=0)
            early_step = (early, swap(early, core))
        if at == last - 2:
            keeps, sends, early_step = lax.optimization_barrier((keeps, sends, early_step))
        came = travel(sends, stage)
        if at == 1:
            came, from_other, table_own = lax.optimization_barrier((came, from_other, table_own))
        if at == 4:
            table_grads = table_own + from_other.astype(F32)
            came, table_grads = lax.optimization_barrier((came, table_grads))
        if at >= last - 2:
            part = at - last + 2
            early_parts.append(
                unpack(
                    my_core,
                    *early_step,
                    part * wide,
                    (wide, wide, width)[part],
                    part == 1,
                )
            )
            came, early_parts = lax.optimization_barrier((came, early_parts))
        late = end(keeps, came, stage)
    late = jnp.concatenate(late, axis=0)
    late_other = swap(late, core)
    w_down_grad, w_up_grad, w_out_grad = early_parts
    w_query_grad, w_key_grad, w_value_grad, expr_grad, short = unpack_whole(
        my_core, late, late_other, heights
    )
    gain_two_grad, shift_two_grad, b_down_grad, gain_one_grad, shift_one_grad, b_out_grad = (
        short[i] for i in range(6)
    )
    b_up_grad = short[6 : 6 + wide // width].reshape(wide)
    b_query_grad, b_value_grad = short[6 + wide // width], short[7 + wide // width]
    return (
        layer_output.reshape(1, tokens, width),
        table_grads[:rows_dev],
        table_grads[rows_dev:],
        expr_grad,
        w_query_grad,
        b_query_grad,
        w_key_grad,
        w_value_grad,
        b_value_grad,
        w_out_grad,
        b_out_grad,
        gain_one_grad,
        shift_one_grad,
        w_up_grad,
        b_up_grad,
        w_down_grad,
        b_down_grad,
        gain_two_grad,
        shift_two_grad,
        row_counts.reshape(2, rows_dev),
    )


def solution(mesh):
    bits = mesh.shape["dp"].bit_length() - 1
    dp_axes = tuple(f"dp{i}" for i in range(bits))
    fine = Mesh(mesh.devices.reshape((2,) * bits + (mesh.shape["seq"],)), (*dp_axes, "seq"))
    every = (*dp_axes, "seq")
    whole = P()
    placed = (
        (P(dp_axes, "seq"),) * 4
        + (P(dp_axes),) * 2
        + (P(every, None), P(None, every, None))
        + (whole,) * 16
        + (P(dp_axes, "seq", None),)
    )
    given = (
        (P(dp_axes, "seq", None),)
        + (P(every, None),) * 2
        + (whole,) * 16
        + (P(None, every),)
    )
    return jax.shard_map(
        functools.partial(local, dp_axes), mesh=fine, in_specs=placed, out_specs=given, check_vma=False
    )
```

```python
import functools

import jax
import jax.numpy as jnp
from jax import lax
from jax.experimental import pallas as pl
from jax.experimental.pallas import tpu as pltpu
from jax.sharding import Mesh, PartitionSpec as P

HEADS = 12
HEAD_DIM = 64
PAIR = 2 * HEAD_DIM
KEY_CHUNK = 512
LOG2E = 1.4426950408889634
SWAP = [(0, 1), (1, 0)]
F32 = jnp.float32
BF16 = jnp.bfloat16
NN = (((1,), (0,)), ((), ()))
NT = (((1,), (1,)), ((), ()))
TN = (((0,), (0,)), ((), ()))


def mm(left, right, dims=NN):
    return lax.dot_general(left, right, dims, preferred_element_type=F32)


def params(mib):
    return pltpu.CompilerParams(vmem_limit_bytes=mib * 2**20)


def cost(flops, moved):
    return pl.CostEstimate(flops=flops, bytes_accessed=moved, transcendentals=0)


def hot(left, right):
    return (left == right).astype(BF16)


def route_kernel(
    rows_dev, capacity, top_ref, gene_ref, know_ref, req_ref, gene_slot_ref, know_slot_ref
):
    tokens = gene_ref.shape[0]
    devices, slots_all = req_ref.shape
    lane = lax.broadcasted_iota(jnp.int32, (tokens, devices), 1)
    top = top_ref[0]
    half = jnp.where((lane & 1) == 0, top, 1 - top)
    first = (half * (devices // 2) + (lane >> 1)) * rows_dev
    earlier = (
        lax.broadcasted_iota(jnp.int32, (tokens, tokens), 0)
        > lax.broadcasted_iota(jnp.int32, (tokens, tokens), 1)
    ).astype(F32).astype(BF16)
    rank_lane = lax.broadcasted_iota(jnp.int32, (tokens, capacity), 1)
    asked = []
    for which, (ids_ref, slot_ref) in enumerate(((gene_ref, gene_slot_ref), (know_ref, know_slot_ref))):
        row = ids_ref[...] - first
        hit = (row >= 0) & (row < rows_dev)
        before = mm(earlier, hit.astype(F32).astype(BF16))
        rank = jnp.sum(jnp.where(hit, before, 0.0), axis=1, keepdims=True)
        owner = jnp.sum(jnp.where(hit, lane, 0).astype(F32), axis=1, keepdims=True)
        slot_ref[...] = (owner * slots_all + rank).astype(jnp.int32) + which * capacity
        rank_hit = (rank_lane == rank.astype(jnp.int32)).astype(F32).astype(BF16)
        coded = jnp.where(hit, row + 1, 0)
        high = (coded >> 4).astype(F32).astype(BF16)
        low = (coded & 15).astype(F32).astype(BF16)
        wanted = (mm(high, rank_hit, TN) * 16.0 + mm(low, rank_hit, TN)).astype(jnp.int32)
        asked.append(jnp.where(wanted > 0, wanted - 1 + which * rows_dev, -1))
    req_ref[:, :capacity] = asked[0]
    req_ref[:, capacity:] = asked[1]


def route(top, gene_ids, know_ids, rows_dev, capacity, devices):
    tokens = gene_ids.shape[0]
    return pl.pallas_call(
        functools.partial(route_kernel, rows_dev, capacity),
        in_specs=[pl.BlockSpec(memory_space=pltpu.SMEM)] + [pl.BlockSpec(memory_space=pltpu.VMEM)] * 2,
        out_shape=(
            jax.ShapeDtypeStruct((devices, 2 * capacity), jnp.int32),
            jax.ShapeDtypeStruct((tokens, 1), jnp.int32),
            jax.ShapeDtypeStruct((tokens, 1), jnp.int32),
        ),
        compiler_params=params(32),
        name="route",
    )(top.reshape(1), gene_ids[:, None], know_ids[:, None])


def fill_keys(aug_ref, key, first_key, count):
    lanes = lax.broadcasted_iota(jnp.int32, key.shape, 1)
    at = lax.broadcasted_iota(jnp.int32, key.shape, 0) + first_key
    bias = jnp.where(at < count, 0.0, -1e30).astype(BF16)
    none = jnp.zeros_like(key)
    aug_ref[:, :PAIR] = jnp.where(lanes < HEAD_DIM, key, jnp.where(lanes == HEAD_DIM, bias, none))
    aug_ref[:, PAIR : 2 * PAIR] = key
    aug_ref[:, 2 * PAIR :] = jnp.where(lanes >= HEAD_DIM, key, jnp.where(lanes == 0, bias, none))


def head_mask(shape, head):
    lanes = lax.broadcasted_iota(jnp.int32, shape, 1)
    return (lanes >= head * HEAD_DIM) & (lanes < (head + 1) * HEAD_DIM)


def spread_query(query, head):
    lanes = lax.broadcasted_iota(jnp.int32, query.shape, 1)
    scaled = query.astype(F32) * (HEAD_DIM ** (-0.5) * LOG2E)
    scaled = jnp.where(head_mask(query.shape, head), scaled, 0.0)
    high = scaled.astype(BF16)
    low = scaled - high.astype(F32)
    low = jnp.where(lanes == (1 - head) * HEAD_DIM, 1.0, low).astype(BF16)
    return jnp.concatenate([low, high] if head == 0 else [high, low], axis=1)


def fold_rows(value, how):
    return how(value.reshape(value.shape[0] // 8, 8, value.shape[1]), axis=0)


def attend_kernel(merge, where_ref, q_ref, k_ref, v_ref, *rest):
    if merge:
        out_in_ref, lse_in_ref, out_ref, lse_ref, aug_ref, vt_ref, score_ref = rest
    else:
        out_ref, lse_ref, aug_ref, vt_ref, score_ref = rest
    spans = [slice(c, c + KEY_CHUNK) for c in range(0, k_ref.shape[0], KEY_CHUNK)]
    fill_keys(aug_ref, k_ref[...], where_ref[0], where_ref[1])
    vt_ref[...] = v_ref[...].T
    outs = []
    for head in range(2):
        own = slice(head * HEAD_DIM, (head + 1) * HEAD_DIM)
        query = spread_query(q_ref[...], head)
        top = None
        for span in spans:
            scores = mm(aug_ref[span, head * PAIR : (head + 2) * PAIR], query, NT)
            score_ref[head, span, :] = scores
            high = fold_rows(scores, jnp.max)
            top = high if top is None else jnp.maximum(top, high)
        top = jnp.max(top, axis=0, keepdims=True)
        total = None
        acc = None
        for span in spans:
            probs = jnp.exp2(score_ref[head, span, :] - top)
            part = fold_rows(probs, jnp.sum)
            total = part if total is None else total + part
            part = mm(vt_ref[own, span], probs.astype(BF16))
            acc = part if acc is None else acc + part
        total = jnp.sum(total, axis=0, keepdims=True)
        lse = top + jnp.log2(total)
        if merge:
            before = lse_in_ref[0, head : head + 1, :]
            both = jnp.maximum(lse, before)
            both = both + jnp.log2(jnp.exp2(lse - both) + jnp.exp2(before - both))
            acc = acc * (jnp.exp2(lse - both) / total)
            acc = acc + out_in_ref[own, :] * jnp.exp2(before - both)
            lse = both
        else:
            acc = acc / total
        lse_ref[0, head : head + 1, :] = lse
        outs.append(acc)
    out = jnp.concatenate(outs, axis=0)
    out_ref[...] = out.T if merge else out


def attend(where, query, key, value, before=()):
    tokens, width = query.shape
    keys = key.shape[0]
    pairs = width // PAIR
    column = lambda rows: pl.BlockSpec((rows, PAIR), lambda p, w: (0, p))
    upright = pl.BlockSpec((PAIR, tokens), lambda p, w: (p, 0))
    stats = pl.BlockSpec((1, 2, tokens), lambda p, w: (p, 0, 0))
    merge = len(before) > 0
    return pl.pallas_call(
        functools.partial(attend_kernel, merge),
        grid_spec=pltpu.PrefetchScalarGridSpec(
            num_scalar_prefetch=1,
            grid=(pairs,),
            in_specs=[column(tokens), column(keys), column(keys)] + ([upright, stats] if merge else []),
            out_specs=[column(tokens) if merge else upright, stats],
            scratch_shapes=[
                pltpu.VMEM((keys, 3 * PAIR), BF16),
                pltpu.VMEM((PAIR, keys), BF16),
                pltpu.VMEM((2, keys, tokens), F32),
            ],
        ),
        out_shape=(
            jax.ShapeDtypeStruct((tokens, width) if merge else (width, tokens), F32),
            jax.ShapeDtypeStruct((pairs, 2, tokens), F32),
        ),
        compiler_params=params(48),
        cost_estimate=cost(16 * tokens * keys * width, 2 * tokens * width * 10),
        name="attend_more" if merge else "attend",
    )(where, query, key, value, *before)


def attend_back_kernel(
    add, untouched, where_ref, q_ref, g_ref, o_ref, lse_ref, k_ref, v_ref, *rest
):
    dq_in_ref = rest[0] if add else None
    dq_ref, dk_ref, dv_ref, aug_ref, kt_ref = rest[int(add) + untouched :]
    fill_keys(aug_ref, k_ref[...], where_ref[0], where_ref[1])
    kt_ref[...] = k_ref[...].T
    grad = g_ref[...]
    picks = (
        lax.broadcasted_iota(jnp.int32, (8, PAIR), 1) // HEAD_DIM
        == lax.broadcasted_iota(jnp.int32, (8, PAIR), 0)
    ).astype(F32)
    inner = lax.dot_general(
        picks,
        grad.astype(F32) * o_ref[...],
        NT,
        precision=lax.Precision.HIGHEST,
        preferred_element_type=F32,
    )
    scaled = q_ref[...] * jnp.asarray(HEAD_DIM ** (-0.5), BF16)
    none = jnp.zeros_like(grad)
    masks = [head_mask(grad.shape, head) for head in range(2)]
    queries = [spread_query(q_ref[...], head) for head in range(2)]
    q_heads = [jnp.where(m, scaled, none) for m in masks]
    g_heads = [jnp.where(m, grad, none) for m in masks]
    dqs = [None, None]
    for first in range(0, k_ref.shape[0], KEY_CHUNK):
        span = slice(first, first + KEY_CHUNK)
        dk = None
        dv = None
        for head in range(2):
            own = slice(head * HEAD_DIM, (head + 1) * HEAD_DIM)
            scores = mm(aug_ref[span, head * PAIR : (head + 2) * PAIR], queries[head], NT)
            probs = jnp.exp2(scores - lse_ref[0, head : head + 1, :])
            grad_probs = mm(v_ref[span, :], g_heads[head], NT)
            grad_scores = (probs * (grad_probs - inner[head : head + 1, :])).astype(BF16)
            part = mm(kt_ref[own, span], grad_scores)
            dqs[head] = part if dqs[head] is None else dqs[head] + part
            part = mm(probs.astype(BF16), g_heads[head])
            dv = part if dv is None else dv + part
            part = mm(grad_scores, q_heads[head])
            dk = part if dk is None else dk + part
        dk_ref[span, :] = dk.astype(BF16)
        dv_ref[span, :] = dv.astype(BF16)
    dq = jnp.concatenate(dqs, axis=0).T * HEAD_DIM ** (-0.5)
    if add:
        dq = dq + dq_in_ref[...]
    dq_ref[...] = dq.astype(dq_ref.dtype)


def attend_back(where, query, grad, out, lse, key, value, first, count, before, into):
    tokens, width = query.shape
    keys = key.shape[0]
    column = lambda rows: pl.BlockSpec((rows, PAIR), lambda p, w: (0, p + first))
    untouched = pl.BlockSpec(memory_space=pl.ANY)
    add = len(before) > 0
    given = 7 + len(before)
    return pl.pallas_call(
        functools.partial(attend_back_kernel, add, len(into)),
        grid_spec=pltpu.PrefetchScalarGridSpec(
            num_scalar_prefetch=1,
            grid=(count,),
            in_specs=[column(tokens)] * 3
            + [pl.BlockSpec((1, 2, tokens), lambda p, w: (p + first, 0, 0))]
            + [column(keys)] * 2
            + [column(tokens)] * len(before)
            + [untouched] * len(into),
            out_specs=[column(tokens), column(keys), column(keys)],
            scratch_shapes=[
                pltpu.VMEM((keys, 3 * PAIR), BF16),
                pltpu.VMEM((PAIR, keys), BF16),
            ],
        ),
        out_shape=(
            jax.ShapeDtypeStruct((tokens, width), BF16 if add else F32),
            jax.ShapeDtypeStruct((keys, width), BF16),
            jax.ShapeDtypeStruct((keys, width), BF16),
        ),
        input_output_aliases={given + i: i for i in range(len(into))},
        compiler_params=params(56),
        cost_estimate=cost(40 * tokens * keys * PAIR * count, 2 * tokens * PAIR * count * 12),
        name=("attend_back_more" if add else "attend_back") + str(first),
    )(where, query, grad, out, lse, key, value, *before, *into)


def norm_parts(value):
    centre = jnp.mean(value, axis=-1, keepdims=True)
    centred = value - centre
    variance = jnp.mean(centred * centred, axis=-1, keepdims=True)
    inverse = lax.rsqrt(variance + 1e-05)
    return centred * inverse, inverse


def norm_back(grad, unit, inverse, gain):
    grad_unit = grad * gain
    return inverse * (
        grad_unit
        - jnp.mean(grad_unit, axis=-1, keepdims=True)
        - unit * jnp.mean(grad_unit * unit, axis=-1, keepdims=True)
    )


def middle_kernel(
    ctx_ref,
    emb_ref,
    cot_ref,
    w_out_ref,
    w_up_ref,
    w_down_ref,
    small_ref,
    b_up_ref,
    out_ref,
    ctx_low_ref,
    normed_ref,
    act_ref,
    gffn_ref,
    gpre_ref,
    gattn_ref,
    gone_ref,
    gctx_ref,
    sums_ref,
    up_sums_ref,
    slope_ref,
):
    step = pl.program_id(0)
    width = emb_ref.shape[1]
    wide = w_up_ref.shape[1]

    @pl.when(step == 0)
    def _():
        sums_ref[...] = jnp.zeros_like(sums_ref)
        up_sums_ref[...] = jnp.zeros_like(up_sums_ref)

    b_out, gain_one, shift_one, b_down, gain_two, shift_two = (
        small_ref[i : i + 1, :] for i in range(6)
    )
    ctx_low = ctx_ref[...].astype(BF16)
    ctx_low_ref[...] = ctx_low
    unit_one, inv_one = norm_parts(emb_ref[...] + mm(ctx_low, w_out_ref[...]) + b_out)
    normed = unit_one * gain_one + shift_one
    normed_low = normed.astype(BF16)
    normed_ref[...] = normed_low
    ffn = None
    for c in range(wide // width):
        span = slice(c * width, (c + 1) * width)
        pre = mm(normed_low, w_up_ref[:, span]) + b_up_ref[:, span]
        below = 0.5 * (1.0 + lax.erf(pre * 0.7071067811865476))
        act = (pre * below).astype(BF16)
        act_ref[:, span] = act
        slope_ref[:, span] = below + pre * (0.3989422804014327 * jnp.exp(-0.5 * pre * pre))
        part = mm(act, w_down_ref[span, :])
        ffn = part if ffn is None else ffn + part
    unit_two, inv_two = norm_parts(normed + ffn + b_down)
    out_ref[...] = (unit_two * gain_two + shift_two).astype(BF16)
    grad = cot_ref[...].astype(F32)
    sums_ref[0:8, :] += fold_rows(grad * unit_two, jnp.sum)
    sums_ref[8:16, :] += fold_rows(grad, jnp.sum)
    grad_two = norm_back(grad, unit_two, inv_two, gain_two)
    gffn = grad_two.astype(BF16)
    gffn_ref[...] = gffn
    sums_ref[16:24, :] += fold_rows(gffn.astype(F32), jnp.sum)
    grad_normed = grad_two
    for c in range(wide // width):
        span = slice(c * width, (c + 1) * width)
        gpre = (mm(gffn, w_down_ref[span, :], NT) * slope_ref[:, span]).astype(BF16)
        gpre_ref[:, span] = gpre
        up_sums_ref[:, span] += fold_rows(gpre.astype(F32), jnp.sum)
        grad_normed = grad_normed + mm(gpre, w_up_ref[:, span], NT)
    sums_ref[24:32, :] += fold_rows(grad_normed * unit_one, jnp.sum)
    sums_ref[32:40, :] += fold_rows(grad_normed, jnp.sum)
    grad_one = norm_back(grad_normed, unit_one, inv_one, gain_one)
    gone_ref[...] = grad_one
    gattn = grad_one.astype(BF16)
    gattn_ref[...] = gattn
    sums_ref[40:48, :] += fold_rows(gattn.astype(F32), jnp.sum)
    gctx_ref[...] = mm(gattn, w_out_ref[...], NT).astype(BF16)


def middle(ctx, embedded, cotangent, w_out, w_up, w_down, small, b_up, block=256):
    tokens, width = embedded.shape
    wide = w_up.shape[1]
    whole = lambda a: pl.BlockSpec(a.shape, lambda i: (0, 0), pipeline_mode=pl.Buffered(1))
    rows = lambda n: pl.BlockSpec((block, n), lambda i: (i, 0))
    fixed = lambda r, n: pl.BlockSpec((r, n), lambda i: (0, 0))
    shape = lambda n, dtype: jax.ShapeDtypeStruct((tokens, n), dtype)
    return pl.pallas_call(
        middle_kernel,
        grid=(tokens // block,),
        in_specs=[rows(width)] * 3 + [whole(w_out), whole(w_up), whole(w_down), whole(small), whole(b_up)],
        out_specs=[
            rows(width),
            rows(width),
            rows(width),
            rows(wide),
            rows(width),
            rows(wide),
            rows(width),
            rows(width),
            rows(width),
            fixed(48, width),
            fixed(8, wide),
        ],
        out_shape=[
            shape(width, BF16),
            shape(width, BF16),
            shape(width, BF16),
            shape(wide, BF16),
            shape(width, BF16),
            shape(wide, BF16),
            shape(width, BF16),
            shape(width, F32),
            shape(width, BF16),
            jax.ShapeDtypeStruct((48, width), F32),
            jax.ShapeDtypeStruct((8, wide), F32),
        ],
        scratch_shapes=[pltpu.VMEM((block, wide), F32)],
        compiler_params=params(60),
        cost_estimate=cost(tokens * width * (8 * wide + 4 * width) * 2, 2 * tokens * (2 * wide + 14 * width)),
        name="middle",
    )(ctx, embedded, cotangent, w_out, w_up, w_down, small, b_up)


def weight_sums_kernel(counts, half_ref, act_ref, gffn_ref, gpre_ref, norm_ref, ctx_ref, gattn_ref, out_ref):
    at = pl.program_id(0) + half_ref[0] * pl.num_programs(0)
    first = 0
    for count, left, right in zip(counts, (act_ref, gpre_ref, ctx_ref), (gffn_ref, norm_ref, gattn_ref)):
        @pl.when((at >= first) & (at < first + count))
        def _(left=left, right=right):
            out_ref[...] = mm(left[...], right[...], TN).astype(BF16)
        first += count


def weight_sums(half, activated, grad_ffn, grad_pre, normed, ctx, grad_attn, block=384):
    tokens, width = grad_ffn.shape
    lefts = (activated, grad_pre, ctx)
    counts = [left.shape[1] // block for left in lefts]
    steps = sum(counts) // 2
    specs = []
    first = 0
    for left, right, count in zip(lefts, (grad_ffn, normed, grad_attn), counts):
        specs.append(
            pl.BlockSpec(
                (tokens, block),
                lambda i, h, first=first, count=count: (0, jnp.clip(i + h[0] * steps - first, 0, count - 1)),
            )
        )
        specs.append(pl.BlockSpec((tokens, width), lambda i, h: (0, 0), pipeline_mode=pl.Buffered(1)))
        first += count
    return pl.pallas_call(
        functools.partial(weight_sums_kernel, counts),
        grid_spec=pltpu.PrefetchScalarGridSpec(
            num_scalar_prefetch=1,
            grid=(steps,),
            in_specs=specs,
            out_specs=pl.BlockSpec((block, width), lambda i, h: (i, 0)),
        ),
        out_shape=jax.ShapeDtypeStruct((steps * block, width), BF16),
        compiler_params=params(60),
        cost_estimate=cost(2 * tokens * width * block * steps, 2 * steps * block * (tokens + width)),
        name="weight_sums",
    )(half.reshape(1), activated, grad_ffn, grad_pre, normed, ctx, grad_attn)


def unpack_kernel(first, half, turn, core_ref, own_ref, other_ref, out_ref):
    at = pl.program_id(0) + first
    mine = (at >= half) == (core_ref[0] == 1)
    rows = jnp.where(mine, own_ref[...], other_ref[...]).astype(F32)
    out_ref[...] = rows.T if turn else rows


def unpack(core, own, other, first, rows, turn, block=384):
    half, width = own.shape[0] // block, own.shape[1]
    first, steps = first // block, rows // block

    def place(i, c, owner):
        at = i + first
        inside = (at >= half) == (c[0] == owner)
        return jnp.where(inside, at % half, half - 1), 0

    return pl.pallas_call(
        functools.partial(unpack_kernel, first, half, turn),
        grid_spec=pltpu.PrefetchScalarGridSpec(
            num_scalar_prefetch=1,
            grid=(steps,),
            in_specs=[
                pl.BlockSpec((block, width), functools.partial(place, owner=1)),
                pl.BlockSpec((block, width), functools.partial(place, owner=0)),
            ],
            out_specs=pl.BlockSpec((width, block), lambda i, c: (0, i))
            if turn
            else pl.BlockSpec((block, width), lambda i, c: (i, 0)),
        ),
        out_shape=jax.ShapeDtypeStruct((width, rows) if turn else (rows, width), F32),
        compiler_params=params(60),
        cost_estimate=cost(rows * width, rows * width * 6),
        name="unpack" + str(first),
    )(core.reshape(1), own, other)


def unpack_whole_kernel(heights, core_ref, own_ref, other_ref, *out_refs):
    half = own_ref.shape[0]
    lower = core_ref[0] == 0
    first = 0
    for height, out_ref in zip(heights, out_refs):
        for part in range(2):
            start, stop = max(first, part * half), min(first + height, (part + 1) * half)
            if start < stop:
                span = slice(start - part * half, stop - part * half)
                near, far = (own_ref, other_ref) if part == 0 else (other_ref, own_ref)
                rows = jnp.where(lower, near[span, :], far[span, :])
                out_ref[start - first : stop - first, :] = rows.astype(F32)
        first += height


def unpack_whole(core, own, other, heights):
    width = own.shape[1]
    vmem = pl.BlockSpec(memory_space=pltpu.VMEM)
    return pl.pallas_call(
        functools.partial(unpack_whole_kernel, heights),
        in_specs=[pl.BlockSpec(memory_space=pltpu.SMEM), vmem, vmem],
        out_specs=[vmem] * len(heights),
        out_shape=[jax.ShapeDtypeStruct((height, width), F32) for height in heights],
        compiler_params=params(60),
        name="unpack_whole",
    )(core.reshape(1), own, other)


def cut(value, axis):
    rows = value.shape[0] // 2
    me = lax.axis_index(axis)
    keep = lax.dynamic_slice_in_dim(value, me * rows, rows, 0)
    return keep, lax.dynamic_slice_in_dim(value, (1 - me) * rows, rows, 0)


def swap(value, axis):
    return lax.ppermute(value, axis, SWAP)


def join(value, other, axis):
    first = lax.axis_index(axis) == 0
    return jnp.concatenate([jnp.where(first, value, other), jnp.where(first, other, value)], axis=0)


def stages_of(dp_axes):
    near, far = dp_axes[-2], dp_axes[-3::-1]
    down = [((near, "seq"), True), (("seq", near), True)] + [((axis,), True) for axis in far]
    return down + [(axes, False) for axes, _ in down[::-1]]


def begin(pieces, stage):
    axes, halves = stage
    if len(pieces) < len(axes):
        pieces = jnp.split(pieces[0], 2, axis=0)
    if len(pieces) > len(axes):
        pieces = [jnp.concatenate(pieces, axis=0)]
    if halves:
        keeps, sends = zip(*(cut(p, axis) for p, axis in zip(pieces, axes)))
        return list(keeps), list(sends)
    return list(pieces), list(pieces)


def travel(sends, stage):
    return [swap(s, axis) for s, axis in zip(sends, stage[0])]


def end(keeps, arrived, stage):
    axes, halves = stage
    if halves:
        return [k + a for k, a in zip(keeps, arrived)]
    return [join(k, a, axis) for k, a, axis in zip(keeps, arrived, axes)]


def run_stages(pieces, stages):
    for stage in stages:
        keeps, sends = begin(pieces, stage)
        pieces = end(keeps, travel(sends, stage), stage)
    return pieces


def local(
    dp_axes,
    gene_ids,
    homolog_ids,
    knowledge_ids,
    expr_bins,
    species,
    cell_lengths,
    gene_table,
    knowledge_tables,
    expr_table,
    w_query,
    b_query,
    w_key,
    w_value,
    b_value,
    w_out,
    b_out,
    gain_one,
    shift_one,
    w_up,
    b_up,
    w_down,
    b_down,
    gain_two,
    shift_two,
    cotangent,
):
    tokens = gene_ids.shape[1]
    rows_dev, width = gene_table.shape
    wide = w_up.shape[1]
    every = (*dp_axes, "seq")
    top_axis, group_axes = dp_axes[0], (*dp_axes[1:], "seq")
    devices = lax.axis_size(every)
    group = devices // 2
    capacity = 2 * tokens // devices
    slots_all = 2 * capacity
    slots = devices * slots_all
    bins = expr_table.shape[0]
    me = lax.axis_index("seq")

    def exchange(value):
        return lax.all_to_all(value, group_axes, split_axis=0, concat_axis=0, tiled=True)

    gene_table, knowledge_tables = lax.optimization_barrier((gene_table, knowledge_tables))
    gene_other = lax.ppermute(gene_table, top_axis, SWAP)
    know_sum = jnp.sum(knowledge_tables.astype(F32), axis=0).astype(BF16)
    chosen = jnp.where(species[0] == 1, homolog_ids, gene_ids).reshape(-1)
    requests, gene_slot, know_slot = route(
        lax.axis_index(top_axis), chosen, knowledge_ids.reshape(-1), rows_dev, capacity, devices
    )
    asked = exchange(requests.reshape(group, 2 * slots_all))
    asked, gene_other, know_sum = lax.optimization_barrier((asked, gene_other, know_sum))
    know_other = lax.ppermute(know_sum, top_axis, SWAP)
    asked = asked.reshape(group, 2, slots_all)
    shift = jnp.arange(2)[None, :, None] * (2 * rows_dev)
    asked = jnp.where(asked >= 0, asked + shift, -1).reshape(group, 2 * slots_all)
    row_at = jnp.arange(4 * rows_dev)
    slot_at = jnp.arange(slots).reshape(group, 2 * slots_all)
    bin_hot = hot(expr_bins.reshape(-1)[:, None], jnp.arange(bins)[None, :])
    embedded = mm(bin_hot, expr_table)
    fetched = gene_other
    tables = jnp.concatenate([gene_table, know_sum, gene_other], axis=0)
    late_rows = slice(slots_all + capacity, 2 * slots_all)
    early_rows = slice(0, slots_all + capacity)
    for columns, rows, table in (
        (early_rows, row_at[: 3 * rows_dev], tables),
        (late_rows, row_at[3 * rows_dev :], know_other),
    ):
        wanted = asked[:, columns].reshape(-1)
        found = mm(hot(wanted[:, None], rows[None, :]), table).astype(BF16)
        found, _ = lax.optimization_barrier((found, fetched))
        fetched = exchange(found.reshape(group, -1, width)).reshape(-1, width)
        at = slot_at[:, columns].reshape(1, -1)
        embedded = embedded + mm(((at == gene_slot) | (at == know_slot)).astype(BF16), fetched)
    asked = asked.reshape(slots)
    slot_at = slot_at.reshape(1, slots)
    slot_hot = ((slot_at == gene_slot) | (slot_at == know_slot)).astype(BF16)
    x_low = embedded.astype(BF16)

    x_other = lax.ppermute(x_low, "seq", SWAP)
    query = (mm(x_low, w_query) + b_query).astype(BF16)
    key, key_other = (mm(x, w_key).astype(BF16) for x in (x_low, x_other))
    value, value_other = ((mm(x, w_value) + b_value).astype(BF16) for x in (x_low, x_other))
    mine = jnp.stack([me * tokens, cell_lengths[0]]).astype(jnp.int32)
    others = jnp.stack([(1 - me) * tokens, cell_lengths[0]]).astype(jnp.int32)
    block_rows = 2 * rows_dev
    owned = [row_at[at : at + block_rows, None] == asked[None, :] for at in (0, block_rows)]
    counts = [jnp.sum(o.astype(jnp.int32), axis=1) for o in owned]
    counts_back = lax.ppermute(counts[1], top_axis, SWAP)
    first_part = attend(mine, query, key, value)
    first_part, counts_back = lax.optimization_barrier((first_part, counts_back))
    row_counts = counts[0] + counts_back
    context, lse = attend(others, query, key_other, value_other, first_part)

    small = jnp.stack([b_out, gain_one, shift_one, b_down, gain_two, shift_two])
    (
        layer_output,
        ctx_low,
        normed_low,
        activated,
        grad_ffn,
        grad_pre,
        grad_attn,
        grad_one,
        grad_ctx,
        sums,
        up_sums,
    ) = middle(
        context, embedded, cotangent.reshape(tokens, width), w_out, w_up, w_down, small, b_up[None, :]
    )

    core = dp_axes[-1]
    stages = stages_of(dp_axes)
    my_core = lax.axis_index(core)
    lefts_rights = (activated, grad_ffn, grad_pre, normed_low, ctx_low, grad_attn)
    sent = weight_sums(1 - my_core, *lefts_rights)
    sent, lefts_rights = lax.optimization_barrier((sent, lefts_rights))
    arrived = swap(sent, core)
    kept = weight_sums(my_core, *lefts_rights)
    kept, arrived, grad_ctx = lax.optimization_barrier((kept, arrived, grad_ctx))
    early = jnp.split(kept + arrived, 2, axis=0)
    pairs = width // PAIR
    third = pairs // 3
    sides = ((others, key_other, value_other), (mine, key, value))
    parts = (((0, 2 * third), (2 * third, third)), ((0, third), (third, third), (2 * third, third)))
    done = 0
    grads = []
    before = ()
    for side, (place, keys, values) in enumerate(sides):
        into = ()
        for first, count in parts[side]:
            keeps, sends = begin(early, stages[done])
            keeps, sends, grad_ctx, into, before = lax.optimization_barrier(
                (keeps, sends, grad_ctx, into, before)
            )
            came = travel(sends, stages[done])
            into = attend_back(
                place, query, grad_ctx, context, lse, keys, values, first, count, before, into
            )
            came, into = lax.optimization_barrier((came, into))
            early = end(keeps, came, stages[done])
            done += 1
        grads.append(into)
        if side == 0:
            before = into[:1]
            dx_other = (mm(into[1], w_key, NT) + mm(into[2], w_value, NT)).astype(BF16)
            dx_other, before = lax.optimization_barrier((dx_other, before))
            dx_from_other = swap(dx_other, "seq")
    (_, dk_other, dv_other), (dq, dk, dv) = grads
    keeps, sends = begin(early, stages[done])
    keeps, sends, dq, dk, dv, dx_from_other = lax.optimization_barrier(
        (keeps, sends, dq, dk, dv, dx_from_other)
    )
    came = travel(sends, stages[done])
    grad_embedded = (
        grad_one
        + mm(dq, w_query, NT)
        + mm(dk, w_key, NT)
        + mm(dv, w_value, NT)
        + dx_from_other.astype(F32)
    )
    grad_low = grad_embedded.astype(BF16)
    grad_low, came = lax.optimization_barrier((grad_low, came))
    keeps, sends = begin(end(keeps, came, stages[done]), stages[done + 1])
    done += 1
    keeps, sends, grad_low = lax.optimization_barrier((keeps, sends, grad_low))
    came = travel(sends, stages[done])

    outgoing = mm(slot_hot, grad_low, TN).astype(BF16)
    outgoing, dq, dk, dv, came = lax.optimization_barrier((outgoing, dq, dk, dv, came))
    early = end(keeps, came, stages[done])
    done += 1
    returned = exchange(outgoing.reshape(group, 2 * slots_all, width)).reshape(slots, width)
    w_query_grad = mm(x_low, dq, TN)
    w_key_grad = mm(x_low, dk, TN) + mm(x_other, dk_other, TN)
    w_value_grad = mm(x_low, dv, TN) + mm(x_other, dv_other, TN)
    b_query_grad = jnp.sum(dq.astype(F32), axis=0)
    b_value_grad = jnp.sum(dv.astype(F32), axis=0) + jnp.sum(dv_other.astype(F32), axis=0)
    grad_rest = (grad_embedded - grad_low.astype(F32)).astype(BF16)
    expr_grad = mm(bin_hot, grad_low, TN) + mm(bin_hot, grad_rest, TN)
    short = jnp.concatenate(
        [
            jnp.sum(sums.reshape(6, 8, width), axis=1),
            jnp.sum(up_sums, axis=0).reshape(wide // width, width),
            b_query_grad[None, :],
            b_value_grad[None, :],
        ],
        axis=0,
    )
    block = 128
    short = jnp.pad(short, ((0, -short.shape[0] % block), (0, 0)))
    late = [w_query_grad, w_key_grad, w_value_grad, expr_grad, short]
    heights = [item.shape[0] for item in late]
    late = jnp.concatenate([item.astype(BF16) for item in late], axis=0)
    keep, send = cut(late, core)
    late = jnp.split(keep + swap(send, core), 2, axis=0)
    keeps, sends = begin(late, stages[0])
    came = travel(sends, stages[0])
    returned, keeps, came, early = lax.optimization_barrier((returned, keeps, came, early))
    late = end(keeps, came, stages[0])
    from_other = swap(mm(owned[1].astype(BF16), returned).astype(BF16), top_axis)
    table_own = mm(owned[0].astype(BF16), returned)
    last = len(stages) - 1
    early_parts = []
    early_step = begin(early, stages[done])
    for at, stage in enumerate(stages[1:], start=1):
        keeps, sends = begin(late, stage)
        if at == 1:
            keeps, sends, early_step = lax.optimization_barrier((keeps, sends, early_step))
            early_came = travel(early_step[1], stages[done])
        if at == 3:
            keeps, sends, early_came = lax.optimization_barrier((keeps, sends, early_came))
            early = end(early_step[0], early_came, stages[done])
            early = jnp.concatenate(run_stages(early, stages[done + 1 :]), axis=0)
            early_step = (early, swap(early, core))
        if at == last - 2:
            keeps, sends, early_step = lax.optimization_barrier((keeps, sends, early_step))
        came = travel(sends, stage)
        if at == 1:
            came, from_other, table_own = lax.optimization_barrier((came, from_other, table_own))
        if at == 4:
            table_grads = table_own + from_other.astype(F32)
            came, table_grads = lax.optimization_barrier((came, table_grads))
        if at >= last - 2:
            part = at - last + 2
            early_parts.append(
                unpack(
                    my_core,
                    *early_step,
                    part * wide,
                    (wide, wide, width)[part],
                    part == 1,
                )
            )
            came, early_parts = lax.optimization_barrier((came, early_parts))
        late = end(keeps, came, stage)
    late = jnp.concatenate(late, axis=0)
    late_other = swap(late, core)
    w_down_grad, w_up_grad, w_out_grad = early_parts
    w_query_grad, w_key_grad, w_value_grad, expr_grad, short = unpack_whole(
        my_core, late, late_other, heights
    )
    gain_two_grad, shift_two_grad, b_down_grad, gain_one_grad, shift_one_grad, b_out_grad = (
        short[i] for i in range(6)
    )
    b_up_grad = short[6 : 6 + wide // width].reshape(wide)
    b_query_grad, b_value_grad = short[6 + wide // width], short[7 + wide // width]
    return (
        layer_output.reshape(1, tokens, width),
        table_grads[:rows_dev],
        table_grads[rows_dev:],
        expr_grad,
        w_query_grad,
        b_query_grad,
        w_key_grad,
        w_value_grad,
        b_value_grad,
        w_out_grad,
        b_out_grad,
        gain_one_grad,
        shift_one_grad,
        w_up_grad,
        b_up_grad,
        w_down_grad,
        b_down_grad,
        gain_two_grad,
        shift_two_grad,
        row_counts.reshape(2, rows_dev),
    )


def solution(mesh):
    bits = mesh.shape["dp"].bit_length() - 1
    dp_axes = tuple(f"dp{i}" for i in range(bits))
    fine = Mesh(mesh.devices.reshape((2,) * bits + (mesh.shape["seq"],)), (*dp_axes, "seq"))
    every = (*dp_axes, "seq")
    whole = P()
    placed = (
        (P(dp_axes, "seq"),) * 4
        + (P(dp_axes),) * 2
        + (P(every, None), P(None, every, None))
        + (whole,) * 16
        + (P(dp_axes, "seq", None),)
    )
    given = (
        (P(dp_axes, "seq", None),)
        + (P(every, None),) * 2
        + (whole,) * 16
        + (P(None, every),)
    )
    return jax.shard_map(
        functools.partial(local, dp_axes), mesh=fine, in_specs=placed, out_specs=given, check_vma=False
    )
```

```python
import functools

import jax
import jax.numpy as jnp
from jax import lax
from jax.experimental import pallas as pl
from jax.experimental.pallas import tpu as pltpu
from jax.sharding import Mesh, PartitionSpec as P

HEADS = 12
HEAD_DIM = 64
PAIR = 2 * HEAD_DIM
KEY_CHUNK = 512
LOG2E = 1.4426950408889634
SWAP = [(0, 1), (1, 0)]
F32 = jnp.float32
BF16 = jnp.bfloat16
NN = (((1,), (0,)), ((), ()))
NT = (((1,), (1,)), ((), ()))
TN = (((0,), (0,)), ((), ()))


def mm(left, right, dims=NN):
    return lax.dot_general(left, right, dims, preferred_element_type=F32)


def params(mib):
    return pltpu.CompilerParams(vmem_limit_bytes=mib * 2**20)


def cost(flops, moved):
    return pl.CostEstimate(flops=flops, bytes_accessed=moved, transcendentals=0)


def hot(left, right):
    return (left == right).astype(BF16)


def route_kernel(
    rows_dev, capacity, top_ref, gene_ref, know_ref, req_ref, gene_slot_ref, know_slot_ref
):
    tokens = gene_ref.shape[0]
    devices, slots_all = req_ref.shape
    lane = lax.broadcasted_iota(jnp.int32, (tokens, devices), 1)
    top = top_ref[0]
    half = jnp.where((lane & 1) == 0, top, 1 - top)
    first = (half * (devices // 2) + (lane >> 1)) * rows_dev
    earlier = (
        lax.broadcasted_iota(jnp.int32, (tokens, tokens), 0)
        > lax.broadcasted_iota(jnp.int32, (tokens, tokens), 1)
    ).astype(F32).astype(BF16)
    rank_lane = lax.broadcasted_iota(jnp.int32, (tokens, capacity), 1)
    asked = []
    for which, (ids_ref, slot_ref) in enumerate(((gene_ref, gene_slot_ref), (know_ref, know_slot_ref))):
        row = ids_ref[...] - first
        hit = (row >= 0) & (row < rows_dev)
        before = mm(earlier, hit.astype(F32).astype(BF16))
        rank = jnp.sum(jnp.where(hit, before, 0.0), axis=1, keepdims=True)
        owner = jnp.sum(jnp.where(hit, lane, 0).astype(F32), axis=1, keepdims=True)
        slot_ref[...] = (owner * slots_all + rank).astype(jnp.int32) + which * capacity
        rank_hit = (rank_lane == rank.astype(jnp.int32)).astype(F32).astype(BF16)
        coded = jnp.where(hit, row + 1, 0)
        high = (coded >> 4).astype(F32).astype(BF16)
        low = (coded & 15).astype(F32).astype(BF16)
        wanted = (mm(high, rank_hit, TN) * 16.0 + mm(low, rank_hit, TN)).astype(jnp.int32)
        asked.append(jnp.where(wanted > 0, wanted - 1 + which * rows_dev, -1))
    req_ref[:, :capacity] = asked[0]
    req_ref[:, capacity:] = asked[1]


def route(top, gene_ids, know_ids, rows_dev, capacity, devices):
    tokens = gene_ids.shape[0]
    return pl.pallas_call(
        functools.partial(route_kernel, rows_dev, capacity),
        in_specs=[pl.BlockSpec(memory_space=pltpu.SMEM)] + [pl.BlockSpec(memory_space=pltpu.VMEM)] * 2,
        out_shape=(
            jax.ShapeDtypeStruct((devices, 2 * capacity), jnp.int32),
            jax.ShapeDtypeStruct((tokens, 1), jnp.int32),
            jax.ShapeDtypeStruct((tokens, 1), jnp.int32),
        ),
        compiler_params=params(32),
        name="route",
    )(top.reshape(1), gene_ids[:, None], know_ids[:, None])


def fill_keys(aug_ref, key, first_key, count):
    lanes = lax.broadcasted_iota(jnp.int32, key.shape, 1)
    at = lax.broadcasted_iota(jnp.int32, key.shape, 0) + first_key
    bias = jnp.where(at < count, 0.0, -1e30).astype(BF16)
    none = jnp.zeros_like(key)
    aug_ref[:, :PAIR] = jnp.where(lanes < HEAD_DIM, key, jnp.where(lanes == HEAD_DIM, bias, none))
    aug_ref[:, PAIR : 2 * PAIR] = key
    aug_ref[:, 2 * PAIR :] = jnp.where(lanes >= HEAD_DIM, key, jnp.where(lanes == 0, bias, none))


def head_mask(shape, head):
    lanes = lax.broadcasted_iota(jnp.int32, shape, 1)
    return (lanes >= head * HEAD_DIM) & (lanes < (head + 1) * HEAD_DIM)


def spread_query(query, head):
    lanes = lax.broadcasted_iota(jnp.int32, query.shape, 1)
    scaled = query.astype(F32) * (HEAD_DIM ** (-0.5) * LOG2E)
    scaled = jnp.where(head_mask(query.shape, head), scaled, 0.0)
    high = scaled.astype(BF16)
    low = scaled - high.astype(F32)
    low = jnp.where(lanes == (1 - head) * HEAD_DIM, 1.0, low).astype(BF16)
    return jnp.concatenate([low, high] if head == 0 else [high, low], axis=1)


def fold_rows(value, how):
    return how(value.reshape(value.shape[0] // 8, 8, value.shape[1]), axis=0)


def attend_kernel(merge, where_ref, q_ref, k_ref, v_ref, *rest):
    if merge:
        out_in_ref, lse_in_ref, out_ref, lse_ref, aug_ref, vt_ref, score_ref = rest
    else:
        out_ref, lse_ref, aug_ref, vt_ref, score_ref = rest
    spans = [slice(c, c + KEY_CHUNK) for c in range(0, k_ref.shape[0], KEY_CHUNK)]
    fill_keys(aug_ref, k_ref[...], where_ref[0], where_ref[1])
    vt_ref[...] = v_ref[...].T
    outs = []
    for head in range(2):
        own = slice(head * HEAD_DIM, (head + 1) * HEAD_DIM)
        query = spread_query(q_ref[...], head)
        top = None
        for span in spans:
            scores = mm(aug_ref[span, head * PAIR : (head + 2) * PAIR], query, NT)
            score_ref[head, span, :] = scores
            high = fold_rows(scores, jnp.max)
            top = high if top is None else jnp.maximum(top, high)
        top = jnp.max(top, axis=0, keepdims=True)
        total = None
        acc = None
        for span in spans:
            probs = jnp.exp2(score_ref[head, span, :] - top)
            part = fold_rows(probs, jnp.sum)
            total = part if total is None else total + part
            part = mm(vt_ref[own, span], probs.astype(BF16))
            acc = part if acc is None else acc + part
        total = jnp.sum(total, axis=0, keepdims=True)
        lse = top + jnp.log2(total)
        if merge:
            before = lse_in_ref[0, head : head + 1, :]
            both = jnp.maximum(lse, before)
            both = both + jnp.log2(jnp.exp2(lse - both) + jnp.exp2(before - both))
            acc = acc * (jnp.exp2(lse - both) / total)
            acc = acc + out_in_ref[own, :] * jnp.exp2(before - both)
            lse = both
        else:
            acc = acc / total
        lse_ref[0, head : head + 1, :] = lse
        outs.append(acc)
    out = jnp.concatenate(outs, axis=0)
    out_ref[...] = out.T if merge else out


def attend(where, query, key, value, before=()):
    tokens, width = query.shape
    keys = key.shape[0]
    pairs = width // PAIR
    column = lambda rows: pl.BlockSpec((rows, PAIR), lambda p, w: (0, p))
    upright = pl.BlockSpec((PAIR, tokens), lambda p, w: (p, 0))
    stats = pl.BlockSpec((1, 2, tokens), lambda p, w: (p, 0, 0))
    merge = len(before) > 0
    return pl.pallas_call(
        functools.partial(attend_kernel, merge),
        grid_spec=pltpu.PrefetchScalarGridSpec(
            num_scalar_prefetch=1,
            grid=(pairs,),
            in_specs=[column(tokens), column(keys), column(keys)] + ([upright, stats] if merge else []),
            out_specs=[column(tokens) if merge else upright, stats],
            scratch_shapes=[
                pltpu.VMEM((keys, 3 * PAIR), BF16),
                pltpu.VMEM((PAIR, keys), BF16),
                pltpu.VMEM((2, keys, tokens), F32),
            ],
        ),
        out_shape=(
            jax.ShapeDtypeStruct((tokens, width) if merge else (width, tokens), F32),
            jax.ShapeDtypeStruct((pairs, 2, tokens), F32),
        ),
        compiler_params=params(48),
        cost_estimate=cost(16 * tokens * keys * width, 2 * tokens * width * 10),
        name="attend_more" if merge else "attend",
    )(where, query, key, value, *before)


def attend_back_kernel(
    add, untouched, where_ref, q_ref, g_ref, o_ref, lse_ref, k_ref, v_ref, *rest
):
    dq_in_ref = rest[0] if add else None
    dq_ref, dk_ref, dv_ref, aug_ref, kt_ref = rest[int(add) + untouched :]
    fill_keys(aug_ref, k_ref[...], where_ref[0], where_ref[1])
    kt_ref[...] = k_ref[...].T
    grad = g_ref[...]
    picks = (
        lax.broadcasted_iota(jnp.int32, (8, PAIR), 1) // HEAD_DIM
        == lax.broadcasted_iota(jnp.int32, (8, PAIR), 0)
    ).astype(F32)
    inner = lax.dot_general(
        picks,
        grad.astype(F32) * o_ref[...],
        NT,
        precision=lax.Precision.HIGHEST,
        preferred_element_type=F32,
    )
    scaled = q_ref[...] * jnp.asarray(HEAD_DIM ** (-0.5), BF16)
    none = jnp.zeros_like(grad)
    masks = [head_mask(grad.shape, head) for head in range(2)]
    queries = [spread_query(q_ref[...], head) for head in range(2)]
    q_heads = [jnp.where(m, scaled, none) for m in masks]
    g_heads = [jnp.where(m, grad, none) for m in masks]
    dqs = [None, None]
    for first in range(0, k_ref.shape[0], KEY_CHUNK):
        span = slice(first, first + KEY_CHUNK)
        dk = None
        dv = None
        for head in range(2):
            own = slice(head * HEAD_DIM, (head + 1) * HEAD_DIM)
            scores = mm(aug_ref[span, head * PAIR : (head + 2) * PAIR], queries[head], NT)
            probs = jnp.exp2(scores - lse_ref[0, head : head + 1, :])
            grad_probs = mm(v_ref[span, :], g_heads[head], NT)
            grad_scores = (probs * (grad_probs - inner[head : head + 1, :])).astype(BF16)
            part = mm(kt_ref[own, span], grad_scores)
            dqs[head] = part if dqs[head] is None else dqs[head] + part
            part = mm(probs.astype(BF16), g_heads[head])
            dv = part if dv is None else dv + part
            part = mm(grad_scores, q_heads[head])
            dk = part if dk is None else dk + part
        dk_ref[span, :] = dk.astype(BF16)
        dv_ref[span, :] = dv.astype(BF16)
    dq = jnp.concatenate(dqs, axis=0).T * HEAD_DIM ** (-0.5)
    if add:
        dq = dq + dq_in_ref[...]
    dq_ref[...] = dq.astype(dq_ref.dtype)


def attend_back(where, query, grad, out, lse, key, value, first, count, before, into):
    tokens, width = query.shape
    keys = key.shape[0]
    column = lambda rows: pl.BlockSpec((rows, PAIR), lambda p, w: (0, p + first))
    untouched = pl.BlockSpec(memory_space=pl.ANY)
    add = len(before) > 0
    given = 7 + len(before)
    return pl.pallas_call(
        functools.partial(attend_back_kernel, add, len(into)),
        grid_spec=pltpu.PrefetchScalarGridSpec(
            num_scalar_prefetch=1,
            grid=(count,),
            in_specs=[column(tokens)] * 3
            + [pl.BlockSpec((1, 2, tokens), lambda p, w: (p + first, 0, 0))]
            + [column(keys)] * 2
            + [column(tokens)] * len(before)
            + [untouched] * len(into),
            out_specs=[column(tokens), column(keys), column(keys)],
            scratch_shapes=[
                pltpu.VMEM((keys, 3 * PAIR), BF16),
                pltpu.VMEM((PAIR, keys), BF16),
            ],
        ),
        out_shape=(
            jax.ShapeDtypeStruct((tokens, width), BF16 if add else F32),
            jax.ShapeDtypeStruct((keys, width), BF16),
            jax.ShapeDtypeStruct((keys, width), BF16),
        ),
        input_output_aliases={given + i: i for i in range(len(into))},
        compiler_params=params(56),
        cost_estimate=cost(40 * tokens * keys * PAIR * count, 2 * tokens * PAIR * count * 12),
        name=("attend_back_more" if add else "attend_back") + str(first),
    )(where, query, grad, out, lse, key, value, *before, *into)


def norm_parts(value):
    centre = jnp.mean(value, axis=-1, keepdims=True)
    centred = value - centre
    variance = jnp.mean(centred * centred, axis=-1, keepdims=True)
    inverse = lax.rsqrt(variance + 1e-05)
    return centred * inverse, inverse


def norm_back(grad, unit, inverse, gain):
    grad_unit = grad * gain
    return inverse * (
        grad_unit
        - jnp.mean(grad_unit, axis=-1, keepdims=True)
        - unit * jnp.mean(grad_unit * unit, axis=-1, keepdims=True)
    )


def middle_kernel(
    ctx_ref,
    emb_ref,
    cot_ref,
    w_out_ref,
    w_up_ref,
    w_down_ref,
    small_ref,
    b_up_ref,
    out_ref,
    ctx_low_ref,
    normed_ref,
    act_ref,
    gffn_ref,
    gpre_ref,
    gattn_ref,
    gone_ref,
    gctx_ref,
    sums_ref,
    up_sums_ref,
    slope_ref,
):
    step = pl.program_id(0)
    width = emb_ref.shape[1]
    wide = w_up_ref.shape[1]

    @pl.when(step == 0)
    def _():
        sums_ref[...] = jnp.zeros_like(sums_ref)
        up_sums_ref[...] = jnp.zeros_like(up_sums_ref)

    b_out, gain_one, shift_one, b_down, gain_two, shift_two = (
        small_ref[i : i + 1, :] for i in range(6)
    )
    ctx_low = ctx_ref[...].astype(BF16)
    ctx_low_ref[...] = ctx_low
    unit_one, inv_one = norm_parts(emb_ref[...] + mm(ctx_low, w_out_ref[...]) + b_out)
    normed = unit_one * gain_one + shift_one
    normed_low = normed.astype(BF16)
    normed_ref[...] = normed_low
    ffn = None
    for c in range(wide // width):
        span = slice(c * width, (c + 1) * width)
        pre = mm(normed_low, w_up_ref[:, span]) + b_up_ref[:, span]
        below = 0.5 * (1.0 + lax.erf(pre * 0.7071067811865476))
        act = (pre * below).astype(BF16)
        act_ref[:, span] = act
        slope_ref[:, span] = below + pre * (0.3989422804014327 * jnp.exp(-0.5 * pre * pre))
        part = mm(act, w_down_ref[span, :])
        ffn = part if ffn is None else ffn + part
    unit_two, inv_two = norm_parts(normed + ffn + b_down)
    out_ref[...] = (unit_two * gain_two + shift_two).astype(BF16)
    grad = cot_ref[...].astype(F32)
    sums_ref[0:8, :] += fold_rows(grad * unit_two, jnp.sum)
    sums_ref[8:16, :] += fold_rows(grad, jnp.sum)
    grad_two = norm_back(grad, unit_two, inv_two, gain_two)
    gffn = grad_two.astype(BF16)
    gffn_ref[...] = gffn
    sums_ref[16:24, :] += fold_rows(gffn.astype(F32), jnp.sum)
    grad_normed = grad_two
    for c in range(wide // width):
        span = slice(c * width, (c + 1) * width)
        gpre = (mm(gffn, w_down_ref[span, :], NT) * slope_ref[:, span]).astype(BF16)
        gpre_ref[:, span] = gpre
        up_sums_ref[:, span] += fold_rows(gpre.astype(F32), jnp.sum)
        grad_normed = grad_normed + mm(gpre, w_up_ref[:, span], NT)
    sums_ref[24:32, :] += fold_rows(grad_normed * unit_one, jnp.sum)
    sums_ref[32:40, :] += fold_rows(grad_normed, jnp.sum)
    grad_one = norm_back(grad_normed, unit_one, inv_one, gain_one)
    gone_ref[...] = grad_one
    gattn = grad_one.astype(BF16)
    gattn_ref[...] = gattn
    sums_ref[40:48, :] += fold_rows(gattn.astype(F32), jnp.sum)
    gctx_ref[...] = mm(gattn, w_out_ref[...], NT).astype(BF16)


def middle(ctx, embedded, cotangent, w_out, w_up, w_down, small, b_up, block=256):
    tokens, width = embedded.shape
    wide = w_up.shape[1]
    whole = lambda a: pl.BlockSpec(a.shape, lambda i: (0, 0), pipeline_mode=pl.Buffered(1))
    rows = lambda n: pl.BlockSpec((block, n), lambda i: (i, 0))
    fixed = lambda r, n: pl.BlockSpec((r, n), lambda i: (0, 0))
    shape = lambda n, dtype: jax.ShapeDtypeStruct((tokens, n), dtype)
    return pl.pallas_call(
        middle_kernel,
        grid=(tokens // block,),
        in_specs=[rows(width)] * 3 + [whole(w_out), whole(w_up), whole(w_down), whole(small), whole(b_up)],
        out_specs=[
            rows(width),
            rows(width),
            rows(width),
            rows(wide),
            rows(width),
            rows(wide),
            rows(width),
            rows(width),
            rows(width),
            fixed(48, width),
            fixed(8, wide),
        ],
        out_shape=[
            shape(width, BF16),
            shape(width, BF16),
            shape(width, BF16),
            shape(wide, BF16),
            shape(width, BF16),
            shape(wide, BF16),
            shape(width, BF16),
            shape(width, F32),
            shape(width, BF16),
            jax.ShapeDtypeStruct((48, width), F32),
            jax.ShapeDtypeStruct((8, wide), F32),
        ],
        scratch_shapes=[pltpu.VMEM((block, wide), F32)],
        compiler_params=params(60),
        cost_estimate=cost(tokens * width * (8 * wide + 4 * width) * 2, 2 * tokens * (2 * wide + 14 * width)),
        name="middle",
    )(ctx, embedded, cotangent, w_out, w_up, w_down, small, b_up)


def weight_sums_kernel(counts, half_ref, act_ref, gffn_ref, gpre_ref, norm_ref, ctx_ref, gattn_ref, out_ref):
    at = pl.program_id(0) + half_ref[0] * pl.num_programs(0)
    first = 0
    for count, left, right in zip(counts, (act_ref, gpre_ref, ctx_ref), (gffn_ref, norm_ref, gattn_ref)):
        @pl.when((at >= first) & (at < first + count))
        def _(left=left, right=right):
            out_ref[...] = mm(left[...], right[...], TN).astype(BF16)
        first += count


def weight_sums(half, activated, grad_ffn, grad_pre, normed, ctx, grad_attn, block=384):
    tokens, width = grad_ffn.shape
    lefts = (activated, grad_pre, ctx)
    counts = [left.shape[1] // block for left in lefts]
    steps = sum(counts) // 2
    specs = []
    first = 0
    for left, right, count in zip(lefts, (grad_ffn, normed, grad_attn), counts):
        specs.append(
            pl.BlockSpec(
                (tokens, block),
                lambda i, h, first=first, count=count: (0, jnp.clip(i + h[0] * steps - first, 0, count - 1)),
            )
        )
        specs.append(pl.BlockSpec((tokens, width), lambda i, h: (0, 0), pipeline_mode=pl.Buffered(1)))
        first += count
    return pl.pallas_call(
        functools.partial(weight_sums_kernel, counts),
        grid_spec=pltpu.PrefetchScalarGridSpec(
            num_scalar_prefetch=1,
            grid=(steps,),
            in_specs=specs,
            out_specs=pl.BlockSpec((block, width), lambda i, h: (i, 0)),
        ),
        out_shape=jax.ShapeDtypeStruct((steps * block, width), BF16),
        compiler_params=params(60),
        cost_estimate=cost(2 * tokens * width * block * steps, 2 * steps * block * (tokens + width)),
        name="weight_sums",
    )(half.reshape(1), activated, grad_ffn, grad_pre, normed, ctx, grad_attn)


def unpack_kernel(first, half, turn, core_ref, own_ref, other_ref, out_ref):
    at = pl.program_id(0) + first
    mine = (at >= half) == (core_ref[0] == 1)
    rows = jnp.where(mine, own_ref[...], other_ref[...]).astype(F32)
    out_ref[...] = rows.T if turn else rows


def unpack(core, own, other, first, rows, turn, block=384):
    half, width = own.shape[0] // block, own.shape[1]
    first, steps = first // block, rows // block

    def place(i, c, owner):
        at = i + first
        inside = (at >= half) == (c[0] == owner)
        return jnp.where(inside, at % half, half - 1), 0

    return pl.pallas_call(
        functools.partial(unpack_kernel, first, half, turn),
        grid_spec=pltpu.PrefetchScalarGridSpec(
            num_scalar_prefetch=1,
            grid=(steps,),
            in_specs=[
                pl.BlockSpec((block, width), functools.partial(place, owner=1)),
                pl.BlockSpec((block, width), functools.partial(place, owner=0)),
            ],
            out_specs=pl.BlockSpec((width, block), lambda i, c: (0, i))
            if turn
            else pl.BlockSpec((block, width), lambda i, c: (i, 0)),
        ),
        out_shape=jax.ShapeDtypeStruct((width, rows) if turn else (rows, width), F32),
        compiler_params=params(60),
        cost_estimate=cost(rows * width, rows * width * 6),
        name="unpack" + str(first),
    )(core.reshape(1), own, other)


def unpack_whole_kernel(heights, core_ref, own_ref, other_ref, *out_refs):
    half = own_ref.shape[0]
    lower = core_ref[0] == 0
    first = 0
    for height, out_ref in zip(heights, out_refs):
        for part in range(2):
            start, stop = max(first, part * half), min(first + height, (part + 1) * half)
            if start < stop:
                span = slice(start - part * half, stop - part * half)
                near, far = (own_ref, other_ref) if part == 0 else (other_ref, own_ref)
                rows = jnp.where(lower, near[span, :], far[span, :])
                out_ref[start - first : stop - first, :] = rows.astype(F32)
        first += height


def unpack_whole(core, own, other, heights):
    width = own.shape[1]
    vmem = pl.BlockSpec(memory_space=pltpu.VMEM)
    return pl.pallas_call(
        functools.partial(unpack_whole_kernel, heights),
        in_specs=[pl.BlockSpec(memory_space=pltpu.SMEM), vmem, vmem],
        out_specs=[vmem] * len(heights),
        out_shape=[jax.ShapeDtypeStruct((height, width), F32) for height in heights],
        compiler_params=params(60),
        name="unpack_whole",
    )(core.reshape(1), own, other)


def cut(value, axis):
    rows = value.shape[0] // 2
    me = lax.axis_index(axis)
    keep = lax.dynamic_slice_in_dim(value, me * rows, rows, 0)
    return keep, lax.dynamic_slice_in_dim(value, (1 - me) * rows, rows, 0)


def swap(value, axis):
    return lax.ppermute(value, axis, SWAP)


def join(value, other, axis):
    first = lax.axis_index(axis) == 0
    return jnp.concatenate([jnp.where(first, value, other), jnp.where(first, other, value)], axis=0)


def stages_of(dp_axes):
    near, far = dp_axes[-2], dp_axes[-3::-1]
    down = [((near, "seq"), True), (("seq", near), True)] + [((axis,), True) for axis in far]
    return down + [(axes, False) for axes, _ in down[::-1]]


def begin(pieces, stage):
    axes, halves = stage
    if len(pieces) < len(axes):
        pieces = jnp.split(pieces[0], 2, axis=0)
    if len(pieces) > len(axes):
        pieces = [jnp.concatenate(pieces, axis=0)]
    if halves:
        keeps, sends = zip(*(cut(p, axis) for p, axis in zip(pieces, axes)))
        return list(keeps), list(sends)
    return list(pieces), list(pieces)


def travel(sends, stage):
    return [swap(s, axis) for s, axis in zip(sends, stage[0])]


def end(keeps, arrived, stage):
    axes, halves = stage
    if halves:
        return [k + a for k, a in zip(keeps, arrived)]
    return [join(k, a, axis) for k, a, axis in zip(keeps, arrived, axes)]


def run_stages(pieces, stages):
    for stage in stages:
        keeps, sends = begin(pieces, stage)
        pieces = end(keeps, travel(sends, stage), stage)
    return pieces


def local(
    dp_axes,
    gene_ids,
    homolog_ids,
    knowledge_ids,
    expr_bins,
    species,
    cell_lengths,
    gene_table,
    knowledge_tables,
    expr_table,
    w_query,
    b_query,
    w_key,
    w_value,
    b_value,
    w_out,
    b_out,
    gain_one,
    shift_one,
    w_up,
    b_up,
    w_down,
    b_down,
    gain_two,
    shift_two,
    cotangent,
):
    tokens = gene_ids.shape[1]
    rows_dev, width = gene_table.shape
    wide = w_up.shape[1]
    every = (*dp_axes, "seq")
    top_axis, group_axes = dp_axes[0], (*dp_axes[1:], "seq")
    devices = lax.axis_size(every)
    group = devices // 2
    capacity = 2 * tokens // devices
    slots_all = 2 * capacity
    slots = devices * slots_all
    bins = expr_table.shape[0]
    me = lax.axis_index("seq")

    def exchange(value):
        return lax.all_to_all(value, group_axes, split_axis=0, concat_axis=0, tiled=True)

    gene_table, knowledge_tables = lax.optimization_barrier((gene_table, knowledge_tables))
    gene_other = lax.ppermute(gene_table, top_axis, SWAP)
    know_sum = jnp.sum(knowledge_tables.astype(F32), axis=0).astype(BF16)
    chosen = jnp.where(species[0] == 1, homolog_ids, gene_ids).reshape(-1)
    requests, gene_slot, know_slot = route(
        lax.axis_index(top_axis), chosen, knowledge_ids.reshape(-1), rows_dev, capacity, devices
    )
    asked = exchange(requests.reshape(group, 2 * slots_all))
    asked, gene_other, know_sum = lax.optimization_barrier((asked, gene_other, know_sum))
    know_other = lax.ppermute(know_sum, top_axis, SWAP)
    asked = asked.reshape(group, 2, slots_all)
    shift = jnp.arange(2)[None, :, None] * (2 * rows_dev)
    asked = jnp.where(asked >= 0, asked + shift, -1).reshape(group, 2 * slots_all)
    row_at = jnp.arange(4 * rows_dev)
    slot_at = jnp.arange(slots).reshape(group, 2 * slots_all)
    bin_hot = hot(expr_bins.reshape(-1)[:, None], jnp.arange(bins)[None, :])
    embedded = mm(bin_hot, expr_table)
    fetched = gene_other
    tables = jnp.concatenate([gene_table, know_sum, gene_other], axis=0)
    late_rows = slice(slots_all + capacity, 2 * slots_all)
    early_rows = slice(0, slots_all + capacity)
    for columns, rows, table in (
        (early_rows, row_at[: 3 * rows_dev], tables),
        (late_rows, row_at[3 * rows_dev :], know_other),
    ):
        wanted = asked[:, columns].reshape(-1)
        found = mm(hot(wanted[:, None], rows[None, :]), table).astype(BF16)
        found, _ = lax.optimization_barrier((found, fetched))
        fetched = exchange(found.reshape(group, -1, width)).reshape(-1, width)
        at = slot_at[:, columns].reshape(1, -1)
        embedded = embedded + mm(((at == gene_slot) | (at == know_slot)).astype(BF16), fetched)
    asked = asked.reshape(slots)
    slot_at = slot_at.reshape(1, slots)
    slot_hot = ((slot_at == gene_slot) | (slot_at == know_slot)).astype(BF16)
    x_low = embedded.astype(BF16)

    x_other = lax.ppermute(x_low, "seq", SWAP)
    query = (mm(x_low, w_query) + b_query).astype(BF16)
    key, key_other = (mm(x, w_key).astype(BF16) for x in (x_low, x_other))
    value, value_other = ((mm(x, w_value) + b_value).astype(BF16) for x in (x_low, x_other))
    mine = jnp.stack([me * tokens, cell_lengths[0]]).astype(jnp.int32)
    others = jnp.stack([(1 - me) * tokens, cell_lengths[0]]).astype(jnp.int32)
    block_rows = 2 * rows_dev
    owned = [row_at[at : at + block_rows, None] == asked[None, :] for at in (0, block_rows)]
    counts = [jnp.sum(o.astype(jnp.int32), axis=1) for o in owned]
    counts_back = lax.ppermute(counts[1], top_axis, SWAP)
    first_part = attend(mine, query, key, value)
    first_part, counts_back = lax.optimization_barrier((first_part, counts_back))
    row_counts = counts[0] + counts_back
    context, lse = attend(others, query, key_other, value_other, first_part)

    small = jnp.stack([b_out, gain_one, shift_one, b_down, gain_two, shift_two])
    (
        layer_output,
        ctx_low,
        normed_low,
        activated,
        grad_ffn,
        grad_pre,
        grad_attn,
        grad_one,
        grad_ctx,
        sums,
        up_sums,
    ) = middle(
        context, embedded, cotangent.reshape(tokens, width), w_out, w_up, w_down, small, b_up[None, :]
    )

    core = dp_axes[-1]
    stages = stages_of(dp_axes)
    my_core = lax.axis_index(core)
    lefts_rights = (activated, grad_ffn, grad_pre, normed_low, ctx_low, grad_attn)
    sent = weight_sums(1 - my_core, *lefts_rights)
    sent, lefts_rights = lax.optimization_barrier((sent, lefts_rights))
    arrived = swap(sent, core)
    kept = weight_sums(my_core, *lefts_rights)
    kept, arrived, grad_ctx = lax.optimization_barrier((kept, arrived, grad_ctx))
    early = jnp.split(kept + arrived, 2, axis=0)
    pairs = width // PAIR
    third = pairs // 3
    sides = ((others, key_other, value_other), (mine, key, value))
    parts = (((0, 2 * third), (2 * third, third)), ((0, third), (third, third), (2 * third, third)))
    done = 0
    grads = []
    before = ()
    for side, (place, keys, values) in enumerate(sides):
        into = ()
        for first, count in parts[side]:
            keeps, sends = begin(early, stages[done])
            keeps, sends, grad_ctx, into, before = lax.optimization_barrier(
                (keeps, sends, grad_ctx, into, before)
            )
            came = travel(sends, stages[done])
            into = attend_back(
                place, query, grad_ctx, context, lse, keys, values, first, count, before, into
            )
            came, into = lax.optimization_barrier((came, into))
            early = end(keeps, came, stages[done])
            done += 1
        grads.append(into)
        if side == 0:
            before = into[:1]
            dx_other = (mm(into[1], w_key, NT) + mm(into[2], w_value, NT)).astype(BF16)
            dx_other, before = lax.optimization_barrier((dx_other, before))
            dx_from_other = swap(dx_other, "seq")
    (_, dk_other, dv_other), (dq, dk, dv) = grads
    keeps, sends = begin(early, stages[done])
    keeps, sends, dq, dk, dv, dx_from_other = lax.optimization_barrier(
        (keeps, sends, dq, dk, dv, dx_from_other)
    )
    came = travel(sends, stages[done])
    grad_embedded = (
        grad_one
        + mm(dq, w_query, NT)
        + mm(dk, w_key, NT)
        + mm(dv, w_value, NT)
        + dx_from_other.astype(F32)
    )
    grad_low = grad_embedded.astype(BF16)
    grad_low, came = lax.optimization_barrier((grad_low, came))
    keeps, sends = begin(end(keeps, came, stages[done]), stages[done + 1])
    done += 1
    keeps, sends, grad_low = lax.optimization_barrier((keeps, sends, grad_low))
    came = travel(sends, stages[done])

    outgoing = mm(slot_hot, grad_low, TN).astype(BF16)
    outgoing, dq, dk, dv, came = lax.optimization_barrier((outgoing, dq, dk, dv, came))
    early = end(keeps, came, stages[done])
    done += 1
    returned = exchange(outgoing.reshape(group, 2 * slots_all, width)).reshape(slots, width)
    w_query_grad = mm(x_low, dq, TN)
    w_key_grad = mm(x_low, dk, TN) + mm(x_other, dk_other, TN)
    w_value_grad = mm(x_low, dv, TN) + mm(x_other, dv_other, TN)
    b_query_grad = jnp.sum(dq.astype(F32), axis=0)
    b_value_grad = jnp.sum(dv.astype(F32), axis=0) + jnp.sum(dv_other.astype(F32), axis=0)
    grad_rest = (grad_embedded - grad_low.astype(F32)).astype(BF16)
    expr_grad = mm(bin_hot, grad_low, TN) + mm(bin_hot, grad_rest, TN)
    short = jnp.concatenate(
        [
            jnp.sum(sums.reshape(6, 8, width), axis=1),
            jnp.sum(up_sums, axis=0).reshape(wide // width, width),
            b_query_grad[None, :],
            b_value_grad[None, :],
        ],
        axis=0,
    )
    block = 128
    short = jnp.pad(short, ((0, -short.shape[0] % block), (0, 0)))
    late = [w_query_grad, w_key_grad, w_value_grad, expr_grad, short]
    heights = [item.shape[0] for item in late]
    late = jnp.concatenate([item.astype(BF16) for item in late], axis=0)
    keep, send = cut(late, core)
    late = jnp.split(keep + swap(send, core), 2, axis=0)
    keeps, sends = begin(late, stages[0])
    came = travel(sends, stages[0])
    returned, keeps, came, early = lax.optimization_barrier((returned, keeps, came, early))
    late = end(keeps, came, stages[0])
    last = len(stages) - 1
    early_parts = []
    early_step = begin(early, stages[done])
    for at, stage in enumerate(stages[1:], start=1):
        keeps, sends = begin(late, stage)
        if at == 1:
            keeps, sends, early_step = lax.optimization_barrier((keeps, sends, early_step))
            early_came = travel(early_step[1], stages[done])
        if at == 4:
            keeps, sends, early_came = lax.optimization_barrier((keeps, sends, early_came))
            early = end(early_step[0], early_came, stages[done])
            early = jnp.concatenate(run_stages(early, stages[done + 1 :]), axis=0)
            early_step = (early, swap(early, core))
        if at == last - 1:
            keeps, sends, early_step, for_other = lax.optimization_barrier(
                (keeps, sends, early_step, for_other)
            )
            from_other = [swap(part, top_axis) for part in jnp.split(for_other, 2, axis=0)]
        if at == last:
            keeps, sends, from_other[0] = lax.optimization_barrier((keeps, sends, from_other[0]))
        came = travel(sends, stage)
        if at == 2:
            table_own = mm(owned[0].astype(BF16), returned)
            came, table_own = lax.optimization_barrier((came, table_own))
        if at == 3:
            for_other = mm(owned[1].astype(BF16), returned).astype(BF16)
            came, for_other = lax.optimization_barrier((came, for_other))
        if at >= last - 1:
            part = at - last + 1
            early_parts.append(
                unpack(my_core, *early_step, part * wide, wide, part == 1)
            )
            came, early_parts = lax.optimization_barrier((came, early_parts))
        if at == last:
            came, from_other[1] = lax.optimization_barrier((came, from_other[1]))
        late = end(keeps, came, stage)
    late = jnp.concatenate(late, axis=0)
    late_other = swap(late, core)
    early_parts.append(unpack(my_core, *early_step, 2 * wide, width, False))
    late_other, early_parts, from_other = lax.optimization_barrier(
        (late_other, early_parts, from_other)
    )
    gene_grad, know_grad = (
        table_own[part * rows_dev : (part + 1) * rows_dev] + from_other[part].astype(F32)
        for part in range(2)
    )
    w_down_grad, w_up_grad, w_out_grad = early_parts
    w_query_grad, w_key_grad, w_value_grad, expr_grad, short = unpack_whole(
        my_core, late, late_other, heights
    )
    gain_two_grad, shift_two_grad, b_down_grad, gain_one_grad, shift_one_grad, b_out_grad = (
        short[i] for i in range(6)
    )
    b_up_grad = short[6 : 6 + wide // width].reshape(wide)
    b_query_grad, b_value_grad = short[6 + wide // width], short[7 + wide // width]
    return (
        layer_output.reshape(1, tokens, width),
        gene_grad,
        know_grad,
        expr_grad,
        w_query_grad,
        b_query_grad,
        w_key_grad,
        w_value_grad,
        b_value_grad,
        w_out_grad,
        b_out_grad,
        gain_one_grad,
        shift_one_grad,
        w_up_grad,
        b_up_grad,
        w_down_grad,
        b_down_grad,
        gain_two_grad,
        shift_two_grad,
        row_counts.reshape(2, rows_dev),
    )


def solution(mesh):
    bits = mesh.shape["dp"].bit_length() - 1
    dp_axes = tuple(f"dp{i}" for i in range(bits))
    fine = Mesh(mesh.devices.reshape((2,) * bits + (mesh.shape["seq"],)), (*dp_axes, "seq"))
    every = (*dp_axes, "seq")
    whole = P()
    placed = (
        (P(dp_axes, "seq"),) * 4
        + (P(dp_axes),) * 2
        + (P(every, None), P(None, every, None))
        + (whole,) * 16
        + (P(dp_axes, "seq", None),)
    )
    given = (
        (P(dp_axes, "seq", None),)
        + (P(every, None),) * 2
        + (whole,) * 16
        + (P(None, every),)
    )
    return jax.shard_map(
        functools.partial(local, dp_axes), mesh=fine, in_specs=placed, out_specs=given, check_vma=False
    )
```

```python
import functools

import jax
import jax.numpy as jnp
from jax import lax
from jax.experimental import pallas as pl
from jax.experimental.pallas import tpu as pltpu
from jax.sharding import Mesh, PartitionSpec as P

HEADS = 12
HEAD_DIM = 64
PAIR = 2 * HEAD_DIM
KEY_CHUNK = 512
LOG2E = 1.4426950408889634
SWAP = [(0, 1), (1, 0)]
F32 = jnp.float32
BF16 = jnp.bfloat16
NN = (((1,), (0,)), ((), ()))
NT = (((1,), (1,)), ((), ()))
TN = (((0,), (0,)), ((), ()))


def mm(left, right, dims=NN):
    return lax.dot_general(left, right, dims, preferred_element_type=F32)


def params(mib):
    return pltpu.CompilerParams(vmem_limit_bytes=mib * 2**20)


def cost(flops, moved):
    return pl.CostEstimate(flops=flops, bytes_accessed=moved, transcendentals=0)


def hot(left, right):
    return (left == right).astype(BF16)


def route_kernel(
    rows_dev, capacity, top_ref, gene_ref, know_ref, req_ref, gene_slot_ref, know_slot_ref
):
    tokens = gene_ref.shape[0]
    devices, slots_all = req_ref.shape
    lane = lax.broadcasted_iota(jnp.int32, (tokens, devices), 1)
    top = top_ref[0]
    half = jnp.where((lane & 1) == 0, top, 1 - top)
    first = (half * (devices // 2) + (lane >> 1)) * rows_dev
    earlier = (
        lax.broadcasted_iota(jnp.int32, (tokens, tokens), 0)
        > lax.broadcasted_iota(jnp.int32, (tokens, tokens), 1)
    ).astype(F32).astype(BF16)
    rank_lane = lax.broadcasted_iota(jnp.int32, (tokens, capacity), 1)
    asked = []
    for which, (ids_ref, slot_ref) in enumerate(((gene_ref, gene_slot_ref), (know_ref, know_slot_ref))):
        row = ids_ref[...] - first
        hit = (row >= 0) & (row < rows_dev)
        before = mm(earlier, hit.astype(F32).astype(BF16))
        rank = jnp.sum(jnp.where(hit, before, 0.0), axis=1, keepdims=True)
        owner = jnp.sum(jnp.where(hit, lane, 0).astype(F32), axis=1, keepdims=True)
        slot_ref[...] = (owner * slots_all + rank).astype(jnp.int32) + which * capacity
        rank_hit = (rank_lane == rank.astype(jnp.int32)).astype(F32).astype(BF16)
        coded = jnp.where(hit, row + 1, 0)
        high = (coded >> 4).astype(F32).astype(BF16)
        low = (coded & 15).astype(F32).astype(BF16)
        wanted = (mm(high, rank_hit, TN) * 16.0 + mm(low, rank_hit, TN)).astype(jnp.int32)
        asked.append(jnp.where(wanted > 0, wanted - 1 + which * rows_dev, -1))
    req_ref[:, :capacity] = asked[0]
    req_ref[:, capacity:] = asked[1]


def route(top, gene_ids, know_ids, rows_dev, capacity, devices):
    tokens = gene_ids.shape[0]
    return pl.pallas_call(
        functools.partial(route_kernel, rows_dev, capacity),
        in_specs=[pl.BlockSpec(memory_space=pltpu.SMEM)] + [pl.BlockSpec(memory_space=pltpu.VMEM)] * 2,
        out_shape=(
            jax.ShapeDtypeStruct((devices, 2 * capacity), jnp.int32),
            jax.ShapeDtypeStruct((tokens, 1), jnp.int32),
            jax.ShapeDtypeStruct((tokens, 1), jnp.int32),
        ),
        compiler_params=params(32),
        name="route",
    )(top.reshape(1), gene_ids[:, None], know_ids[:, None])


def fill_keys(aug_ref, key, first_key, count):
    lanes = lax.broadcasted_iota(jnp.int32, key.shape, 1)
    at = lax.broadcasted_iota(jnp.int32, key.shape, 0) + first_key
    bias = jnp.where(at < count, 0.0, -1e30).astype(BF16)
    none = jnp.zeros_like(key)
    aug_ref[:, :PAIR] = jnp.where(lanes < HEAD_DIM, key, jnp.where(lanes == HEAD_DIM, bias, none))
    aug_ref[:, PAIR : 2 * PAIR] = key
    aug_ref[:, 2 * PAIR :] = jnp.where(lanes >= HEAD_DIM, key, jnp.where(lanes == 0, bias, none))


def head_mask(shape, head):
    lanes = lax.broadcasted_iota(jnp.int32, shape, 1)
    return (lanes >= head * HEAD_DIM) & (lanes < (head + 1) * HEAD_DIM)


def spread_query(query, head):
    lanes = lax.broadcasted_iota(jnp.int32, query.shape, 1)
    scaled = query.astype(F32) * (HEAD_DIM ** (-0.5) * LOG2E)
    scaled = jnp.where(head_mask(query.shape, head), scaled, 0.0)
    high = scaled.astype(BF16)
    low = scaled - high.astype(F32)
    low = jnp.where(lanes == (1 - head) * HEAD_DIM, 1.0, low).astype(BF16)
    return jnp.concatenate([low, high] if head == 0 else [high, low], axis=1)


def fold_rows(value, how):
    return how(value.reshape(value.shape[0] // 8, 8, value.shape[1]), axis=0)


def attend_kernel(merge, where_ref, q_ref, k_ref, v_ref, *rest):
    if merge:
        out_in_ref, lse_in_ref, out_ref, lse_ref, aug_ref, vt_ref, score_ref = rest
    else:
        out_ref, lse_ref, aug_ref, vt_ref, score_ref = rest
    spans = [slice(c, c + KEY_CHUNK) for c in range(0, k_ref.shape[0], KEY_CHUNK)]
    fill_keys(aug_ref, k_ref[...], where_ref[0], where_ref[1])
    vt_ref[...] = v_ref[...].T
    outs = []
    for head in range(2):
        own = slice(head * HEAD_DIM, (head + 1) * HEAD_DIM)
        query = spread_query(q_ref[...], head)
        top = None
        for span in spans:
            scores = mm(aug_ref[span, head * PAIR : (head + 2) * PAIR], query, NT)
            score_ref[head, span, :] = scores
            high = fold_rows(scores, jnp.max)
            top = high if top is None else jnp.maximum(top, high)
        top = jnp.max(top, axis=0, keepdims=True)
        total = None
        acc = None
        for span in spans:
            probs = jnp.exp2(score_ref[head, span, :] - top)
            part = fold_rows(probs, jnp.sum)
            total = part if total is None else total + part
            part = mm(vt_ref[own, span], probs.astype(BF16))
            acc = part if acc is None else acc + part
        total = jnp.sum(total, axis=0, keepdims=True)
        lse = top + jnp.log2(total)
        if merge:
            before = lse_in_ref[0, head : head + 1, :]
            both = jnp.maximum(lse, before)
            both = both + jnp.log2(jnp.exp2(lse - both) + jnp.exp2(before - both))
            acc = acc * (jnp.exp2(lse - both) / total)
            acc = acc + out_in_ref[own, :] * jnp.exp2(before - both)
            lse = both
        else:
            acc = acc / total
        lse_ref[0, head : head + 1, :] = lse
        outs.append(acc)
    out = jnp.concatenate(outs, axis=0)
    out_ref[...] = out.T if merge else out


def attend(where, query, key, value, before=()):
    tokens, width = query.shape
    keys = key.shape[0]
    pairs = width // PAIR
    column = lambda rows: pl.BlockSpec((rows, PAIR), lambda p, w: (0, p))
    upright = pl.BlockSpec((PAIR, tokens), lambda p, w: (p, 0))
    stats = pl.BlockSpec((1, 2, tokens), lambda p, w: (p, 0, 0))
    merge = len(before) > 0
    return pl.pallas_call(
        functools.partial(attend_kernel, merge),
        grid_spec=pltpu.PrefetchScalarGridSpec(
            num_scalar_prefetch=1,
            grid=(pairs,),
            in_specs=[column(tokens), column(keys), column(keys)] + ([upright, stats] if merge else []),
            out_specs=[column(tokens) if merge else upright, stats],
            scratch_shapes=[
                pltpu.VMEM((keys, 3 * PAIR), BF16),
                pltpu.VMEM((PAIR, keys), BF16),
                pltpu.VMEM((2, keys, tokens), F32),
            ],
        ),
        out_shape=(
            jax.ShapeDtypeStruct((tokens, width) if merge else (width, tokens), F32),
            jax.ShapeDtypeStruct((pairs, 2, tokens), F32),
        ),
        compiler_params=params(48),
        cost_estimate=cost(16 * tokens * keys * width, 2 * tokens * width * 10),
        name="attend_more" if merge else "attend",
    )(where, query, key, value, *before)


def attend_back_kernel(
    add, untouched, where_ref, q_ref, g_ref, o_ref, lse_ref, k_ref, v_ref, *rest
):
    dq_in_ref = rest[0] if add else None
    dq_ref, dk_ref, dv_ref, aug_ref, kt_ref = rest[int(add) + untouched :]
    fill_keys(aug_ref, k_ref[...], where_ref[0], where_ref[1])
    kt_ref[...] = k_ref[...].T
    grad = g_ref[...]
    picks = (
        lax.broadcasted_iota(jnp.int32, (8, PAIR), 1) // HEAD_DIM
        == lax.broadcasted_iota(jnp.int32, (8, PAIR), 0)
    ).astype(F32)
    inner = lax.dot_general(
        picks,
        grad.astype(F32) * o_ref[...],
        NT,
        precision=lax.Precision.HIGHEST,
        preferred_element_type=F32,
    )
    scaled = q_ref[...] * jnp.asarray(HEAD_DIM ** (-0.5), BF16)
    none = jnp.zeros_like(grad)
    masks = [head_mask(grad.shape, head) for head in range(2)]
    queries = [spread_query(q_ref[...], head) for head in range(2)]
    q_heads = [jnp.where(m, scaled, none) for m in masks]
    g_heads = [jnp.where(m, grad, none) for m in masks]
    dqs = [None, None]
    for first in range(0, k_ref.shape[0], KEY_CHUNK):
        span = slice(first, first + KEY_CHUNK)
        dk = None
        dv = None
        for head in range(2):
            own = slice(head * HEAD_DIM, (head + 1) * HEAD_DIM)
            scores = mm(aug_ref[span, head * PAIR : (head + 2) * PAIR], queries[head], NT)
            probs = jnp.exp2(scores - lse_ref[0, head : head + 1, :])
            grad_probs = mm(v_ref[span, :], g_heads[head], NT)
            grad_scores = (probs * (grad_probs - inner[head : head + 1, :])).astype(BF16)
            part = mm(kt_ref[own, span], grad_scores)
            dqs[head] = part if dqs[head] is None else dqs[head] + part
            part = mm(probs.astype(BF16), g_heads[head])
            dv = part if dv is None else dv + part
            part = mm(grad_scores, q_heads[head])
            dk = part if dk is None else dk + part
        dk_ref[span, :] = dk.astype(BF16)
        dv_ref[span, :] = dv.astype(BF16)
    dq = jnp.concatenate(dqs, axis=0).T * HEAD_DIM ** (-0.5)
    if add:
        dq = dq + dq_in_ref[...]
    dq_ref[...] = dq.astype(dq_ref.dtype)


def attend_back(where, query, grad, out, lse, key, value, first, count, before, into):
    tokens, width = query.shape
    keys = key.shape[0]
    column = lambda rows: pl.BlockSpec((rows, PAIR), lambda p, w: (0, p + first))
    untouched = pl.BlockSpec(memory_space=pl.ANY)
    add = len(before) > 0
    given = 7 + len(before)
    return pl.pallas_call(
        functools.partial(attend_back_kernel, add, len(into)),
        grid_spec=pltpu.PrefetchScalarGridSpec(
            num_scalar_prefetch=1,
            grid=(count,),
            in_specs=[column(tokens)] * 3
            + [pl.BlockSpec((1, 2, tokens), lambda p, w: (p + first, 0, 0))]
            + [column(keys)] * 2
            + [column(tokens)] * len(before)
            + [untouched] * len(into),
            out_specs=[column(tokens), column(keys), column(keys)],
            scratch_shapes=[
                pltpu.VMEM((keys, 3 * PAIR), BF16),
                pltpu.VMEM((PAIR, keys), BF16),
            ],
        ),
        out_shape=(
            jax.ShapeDtypeStruct((tokens, width), BF16 if add else F32),
            jax.ShapeDtypeStruct((keys, width), BF16),
            jax.ShapeDtypeStruct((keys, width), BF16),
        ),
        input_output_aliases={given + i: i for i in range(len(into))},
        compiler_params=params(56),
        cost_estimate=cost(40 * tokens * keys * PAIR * count, 2 * tokens * PAIR * count * 12),
        name=("attend_back_more" if add else "attend_back") + str(first),
    )(where, query, grad, out, lse, key, value, *before, *into)


def norm_parts(value):
    centre = jnp.mean(value, axis=-1, keepdims=True)
    centred = value - centre
    variance = jnp.mean(centred * centred, axis=-1, keepdims=True)
    inverse = lax.rsqrt(variance + 1e-05)
    return centred * inverse, inverse


def norm_back(grad, unit, inverse, gain):
    grad_unit = grad * gain
    return inverse * (
        grad_unit
        - jnp.mean(grad_unit, axis=-1, keepdims=True)
        - unit * jnp.mean(grad_unit * unit, axis=-1, keepdims=True)
    )


def middle_kernel(
    ctx_ref,
    emb_ref,
    cot_ref,
    w_out_ref,
    w_up_ref,
    w_down_ref,
    small_ref,
    b_up_ref,
    out_ref,
    ctx_low_ref,
    normed_ref,
    act_ref,
    gffn_ref,
    gpre_ref,
    gattn_ref,
    gone_ref,
    gctx_ref,
    sums_ref,
    up_sums_ref,
    slope_ref,
):
    step = pl.program_id(0)
    width = emb_ref.shape[1]
    wide = w_up_ref.shape[1]

    @pl.when(step == 0)
    def _():
        sums_ref[...] = jnp.zeros_like(sums_ref)
        up_sums_ref[...] = jnp.zeros_like(up_sums_ref)

    b_out, gain_one, shift_one, b_down, gain_two, shift_two = (
        small_ref[i : i + 1, :] for i in range(6)
    )
    ctx_low = ctx_ref[...].astype(BF16)
    ctx_low_ref[...] = ctx_low
    unit_one, inv_one = norm_parts(emb_ref[...] + mm(ctx_low, w_out_ref[...]) + b_out)
    normed = unit_one * gain_one + shift_one
    normed_low = normed.astype(BF16)
    normed_ref[...] = normed_low
    ffn = None
    for c in range(wide // width):
        span = slice(c * width, (c + 1) * width)
        pre = mm(normed_low, w_up_ref[:, span]) + b_up_ref[:, span]
        below = 0.5 * (1.0 + lax.erf(pre * 0.7071067811865476))
        act = (pre * below).astype(BF16)
        act_ref[:, span] = act
        slope_ref[:, span] = below + pre * (0.3989422804014327 * jnp.exp(-0.5 * pre * pre))
        part = mm(act, w_down_ref[span, :])
        ffn = part if ffn is None else ffn + part
    unit_two, inv_two = norm_parts(normed + ffn + b_down)
    out_ref[...] = (unit_two * gain_two + shift_two).astype(BF16)
    grad = cot_ref[...].astype(F32)
    sums_ref[0:8, :] += fold_rows(grad * unit_two, jnp.sum)
    sums_ref[8:16, :] += fold_rows(grad, jnp.sum)
    grad_two = norm_back(grad, unit_two, inv_two, gain_two)
    gffn = grad_two.astype(BF16)
    gffn_ref[...] = gffn
    sums_ref[16:24, :] += fold_rows(gffn.astype(F32), jnp.sum)
    grad_normed = grad_two
    for c in range(wide // width):
        span = slice(c * width, (c + 1) * width)
        gpre = (mm(gffn, w_down_ref[span, :], NT) * slope_ref[:, span]).astype(BF16)
        gpre_ref[:, span] = gpre
        up_sums_ref[:, span] += fold_rows(gpre.astype(F32), jnp.sum)
        grad_normed = grad_normed + mm(gpre, w_up_ref[:, span], NT)
    sums_ref[24:32, :] += fold_rows(grad_normed * unit_one, jnp.sum)
    sums_ref[32:40, :] += fold_rows(grad_normed, jnp.sum)
    grad_one = norm_back(grad_normed, unit_one, inv_one, gain_one)
    gone_ref[...] = grad_one
    gattn = grad_one.astype(BF16)
    gattn_ref[...] = gattn
    sums_ref[40:48, :] += fold_rows(gattn.astype(F32), jnp.sum)
    gctx_ref[...] = mm(gattn, w_out_ref[...], NT).astype(BF16)


def middle(ctx, embedded, cotangent, w_out, w_up, w_down, small, b_up, block=256):
    tokens, width = embedded.shape
    wide = w_up.shape[1]
    whole = lambda a: pl.BlockSpec(a.shape, lambda i: (0, 0), pipeline_mode=pl.Buffered(1))
    rows = lambda n: pl.BlockSpec((block, n), lambda i: (i, 0))
    fixed = lambda r, n: pl.BlockSpec((r, n), lambda i: (0, 0))
    shape = lambda n, dtype: jax.ShapeDtypeStruct((tokens, n), dtype)
    return pl.pallas_call(
        middle_kernel,
        grid=(tokens // block,),
        in_specs=[rows(width)] * 3 + [whole(w_out), whole(w_up), whole(w_down), whole(small), whole(b_up)],
        out_specs=[
            rows(width),
            rows(width),
            rows(width),
            rows(wide),
            rows(width),
            rows(wide),
            rows(width),
            rows(width),
            rows(width),
            fixed(48, width),
            fixed(8, wide),
        ],
        out_shape=[
            shape(width, BF16),
            shape(width, BF16),
            shape(width, BF16),
            shape(wide, BF16),
            shape(width, BF16),
            shape(wide, BF16),
            shape(width, BF16),
            shape(width, F32),
            shape(width, BF16),
            jax.ShapeDtypeStruct((48, width), F32),
            jax.ShapeDtypeStruct((8, wide), F32),
        ],
        scratch_shapes=[pltpu.VMEM((block, wide), F32)],
        compiler_params=params(60),
        cost_estimate=cost(tokens * width * (8 * wide + 4 * width) * 2, 2 * tokens * (2 * wide + 14 * width)),
        name="middle",
    )(ctx, embedded, cotangent, w_out, w_up, w_down, small, b_up)


def weight_sums_kernel(counts, half_ref, act_ref, gffn_ref, gpre_ref, norm_ref, ctx_ref, gattn_ref, out_ref):
    at = pl.program_id(0) + half_ref[0] * pl.num_programs(0)
    first = 0
    for count, left, right in zip(counts, (act_ref, gpre_ref, ctx_ref), (gffn_ref, norm_ref, gattn_ref)):
        @pl.when((at >= first) & (at < first + count))
        def _(left=left, right=right):
            out_ref[...] = mm(left[...], right[...], TN).astype(BF16)
        first += count


def weight_sums(half, activated, grad_ffn, grad_pre, normed, ctx, grad_attn, block=384):
    tokens, width = grad_ffn.shape
    lefts = (activated, grad_pre, ctx)
    counts = [left.shape[1] // block for left in lefts]
    steps = sum(counts) // 2
    specs = []
    first = 0
    for left, right, count in zip(lefts, (grad_ffn, normed, grad_attn), counts):
        specs.append(
            pl.BlockSpec(
                (tokens, block),
                lambda i, h, first=first, count=count: (0, jnp.clip(i + h[0] * steps - first, 0, count - 1)),
            )
        )
        specs.append(pl.BlockSpec((tokens, width), lambda i, h: (0, 0), pipeline_mode=pl.Buffered(1)))
        first += count
    return pl.pallas_call(
        functools.partial(weight_sums_kernel, counts),
        grid_spec=pltpu.PrefetchScalarGridSpec(
            num_scalar_prefetch=1,
            grid=(steps,),
            in_specs=specs,
            out_specs=pl.BlockSpec((block, width), lambda i, h: (i, 0)),
        ),
        out_shape=jax.ShapeDtypeStruct((steps * block, width), BF16),
        compiler_params=params(60),
        cost_estimate=cost(2 * tokens * width * block * steps, 2 * steps * block * (tokens + width)),
        name="weight_sums",
    )(half.reshape(1), activated, grad_ffn, grad_pre, normed, ctx, grad_attn)


def unpack_kernel(first, half, turn, core_ref, own_ref, other_ref, out_ref):
    at = pl.program_id(0) + first
    mine = (at >= half) == (core_ref[0] == 1)
    rows = jnp.where(mine, own_ref[...], other_ref[...]).astype(F32)
    out_ref[...] = rows.T if turn else rows


def unpack(core, own, other, first, rows, turn, block=384):
    half, width = own.shape[0] // block, own.shape[1]
    first, steps = first // block, rows // block

    def place(i, c, owner):
        at = i + first
        inside = (at >= half) == (c[0] == owner)
        return jnp.where(inside, at % half, half - 1), 0

    return pl.pallas_call(
        functools.partial(unpack_kernel, first, half, turn),
        grid_spec=pltpu.PrefetchScalarGridSpec(
            num_scalar_prefetch=1,
            grid=(steps,),
            in_specs=[
                pl.BlockSpec((block, width), functools.partial(place, owner=1)),
                pl.BlockSpec((block, width), functools.partial(place, owner=0)),
            ],
            out_specs=pl.BlockSpec((width, block), lambda i, c: (0, i))
            if turn
            else pl.BlockSpec((block, width), lambda i, c: (i, 0)),
        ),
        out_shape=jax.ShapeDtypeStruct((width, rows) if turn else (rows, width), F32),
        compiler_params=params(60),
        cost_estimate=cost(rows * width, rows * width * 6),
        name="unpack" + str(first),
    )(core.reshape(1), own, other)


def unpack_whole_kernel(heights, core_ref, own_ref, other_ref, *out_refs):
    half = own_ref.shape[0]
    lower = core_ref[0] == 0
    first = 0
    for height, out_ref in zip(heights, out_refs):
        for part in range(2):
            start, stop = max(first, part * half), min(first + height, (part + 1) * half)
            if start < stop:
                span = slice(start - part * half, stop - part * half)
                near, far = (own_ref, other_ref) if part == 0 else (other_ref, own_ref)
                rows = jnp.where(lower, near[span, :], far[span, :])
                out_ref[start - first : stop - first, :] = rows.astype(F32)
        first += height


def unpack_whole(core, own, other, heights):
    width = own.shape[1]
    vmem = pl.BlockSpec(memory_space=pltpu.VMEM)
    return pl.pallas_call(
        functools.partial(unpack_whole_kernel, heights),
        in_specs=[pl.BlockSpec(memory_space=pltpu.SMEM), vmem, vmem],
        out_specs=[vmem] * len(heights),
        out_shape=[jax.ShapeDtypeStruct((height, width), F32) for height in heights],
        compiler_params=params(60),
        name="unpack_whole",
    )(core.reshape(1), own, other)


def cut(value, axis):
    rows = value.shape[0] // 2
    me = lax.axis_index(axis)
    keep = lax.dynamic_slice_in_dim(value, me * rows, rows, 0)
    return keep, lax.dynamic_slice_in_dim(value, (1 - me) * rows, rows, 0)


def swap(value, axis):
    return lax.ppermute(value, axis, SWAP)


def join(value, other, axis):
    first = lax.axis_index(axis) == 0
    return jnp.concatenate([jnp.where(first, value, other), jnp.where(first, other, value)], axis=0)


def stages_of(dp_axes):
    near, far = dp_axes[-2], dp_axes[-3::-1]
    down = [((near, "seq"), True), (("seq", near), True)] + [((axis,), True) for axis in far]
    return down + [(axes, False) for axes, _ in down[::-1]]


def begin(pieces, stage):
    axes, halves = stage
    if len(pieces) < len(axes):
        pieces = jnp.split(pieces[0], 2, axis=0)
    if len(pieces) > len(axes):
        pieces = [jnp.concatenate(pieces, axis=0)]
    if halves:
        keeps, sends = zip(*(cut(p, axis) for p, axis in zip(pieces, axes)))
        return list(keeps), list(sends)
    return list(pieces), list(pieces)


def travel(sends, stage):
    return [swap(s, axis) for s, axis in zip(sends, stage[0])]


def end(keeps, arrived, stage):
    axes, halves = stage
    if halves:
        return [k + a for k, a in zip(keeps, arrived)]
    return [join(k, a, axis) for k, a, axis in zip(keeps, arrived, axes)]


def run_stages(pieces, stages):
    for stage in stages:
        keeps, sends = begin(pieces, stage)
        pieces = end(keeps, travel(sends, stage), stage)
    return pieces


def local(
    dp_axes,
    gene_ids,
    homolog_ids,
    knowledge_ids,
    expr_bins,
    species,
    cell_lengths,
    gene_table,
    knowledge_tables,
    expr_table,
    w_query,
    b_query,
    w_key,
    w_value,
    b_value,
    w_out,
    b_out,
    gain_one,
    shift_one,
    w_up,
    b_up,
    w_down,
    b_down,
    gain_two,
    shift_two,
    cotangent,
):
    tokens = gene_ids.shape[1]
    rows_dev, width = gene_table.shape
    wide = w_up.shape[1]
    every = (*dp_axes, "seq")
    top_axis, group_axes = dp_axes[0], (*dp_axes[1:], "seq")
    devices = lax.axis_size(every)
    group = devices // 2
    capacity = 2 * tokens // devices
    slots_all = 2 * capacity
    slots = devices * slots_all
    bins = expr_table.shape[0]
    me = lax.axis_index("seq")

    def exchange(value):
        return lax.all_to_all(value, group_axes, split_axis=0, concat_axis=0, tiled=True)

    gene_table, knowledge_tables = lax.optimization_barrier((gene_table, knowledge_tables))
    gene_other = lax.ppermute(gene_table, top_axis, SWAP)
    know_sum = jnp.sum(knowledge_tables.astype(F32), axis=0).astype(BF16)
    chosen = jnp.where(species[0] == 1, homolog_ids, gene_ids).reshape(-1)
    requests, gene_slot, know_slot = route(
        lax.axis_index(top_axis), chosen, knowledge_ids.reshape(-1), rows_dev, capacity, devices
    )
    asked = exchange(requests.reshape(group, 2 * slots_all))
    asked, gene_other, know_sum = lax.optimization_barrier((asked, gene_other, know_sum))
    know_other = lax.ppermute(know_sum, top_axis, SWAP)
    asked = asked.reshape(group, 2, slots_all)
    shift = jnp.arange(2)[None, :, None] * (2 * rows_dev)
    asked = jnp.where(asked >= 0, asked + shift, -1).reshape(group, 2 * slots_all)
    row_at = jnp.arange(4 * rows_dev)
    slot_at = jnp.arange(slots).reshape(group, 2 * slots_all)
    bin_hot = hot(expr_bins.reshape(-1)[:, None], jnp.arange(bins)[None, :])
    embedded = mm(bin_hot, expr_table)
    fetched = gene_other
    tables = jnp.concatenate([gene_table, know_sum, gene_other], axis=0)
    late_rows = slice(slots_all + capacity, 2 * slots_all)
    early_rows = slice(0, slots_all + capacity)
    for columns, rows, table in (
        (early_rows, row_at[: 3 * rows_dev], tables),
        (late_rows, row_at[3 * rows_dev :], know_other),
    ):
        wanted = asked[:, columns].reshape(-1)
        found = mm(hot(wanted[:, None], rows[None, :]), table).astype(BF16)
        found, _ = lax.optimization_barrier((found, fetched))
        fetched = exchange(found.reshape(group, -1, width)).reshape(-1, width)
        at = slot_at[:, columns].reshape(1, -1)
        embedded = embedded + mm(((at == gene_slot) | (at == know_slot)).astype(BF16), fetched)
    asked = asked.reshape(slots)
    slot_at = slot_at.reshape(1, slots)
    slot_hot = ((slot_at == gene_slot) | (slot_at == know_slot)).astype(BF16)
    x_low = embedded.astype(BF16)

    x_other = lax.ppermute(x_low, "seq", SWAP)
    query = (mm(x_low, w_query) + b_query).astype(BF16)
    key, key_other = (mm(x, w_key).astype(BF16) for x in (x_low, x_other))
    value, value_other = ((mm(x, w_value) + b_value).astype(BF16) for x in (x_low, x_other))
    mine = jnp.stack([me * tokens, cell_lengths[0]]).astype(jnp.int32)
    others = jnp.stack([(1 - me) * tokens, cell_lengths[0]]).astype(jnp.int32)
    block_rows = 2 * rows_dev
    owned = [row_at[at : at + block_rows, None] == asked[None, :] for at in (0, block_rows)]
    counts = [jnp.sum(o.astype(jnp.int32), axis=1) for o in owned]
    counts_back = lax.ppermute(counts[1], top_axis, SWAP)
    first_part = attend(mine, query, key, value)
    first_part, counts_back = lax.optimization_barrier((first_part, counts_back))
    row_counts = counts[0] + counts_back
    context, lse = attend(others, query, key_other, value_other, first_part)

    small = jnp.stack([b_out, gain_one, shift_one, b_down, gain_two, shift_two])
    (
        layer_output,
        ctx_low,
        normed_low,
        activated,
        grad_ffn,
        grad_pre,
        grad_attn,
        grad_one,
        grad_ctx,
        sums,
        up_sums,
    ) = middle(
        context, embedded, cotangent.reshape(tokens, width), w_out, w_up, w_down, small, b_up[None, :]
    )

    core = dp_axes[-1]
    stages = stages_of(dp_axes)
    my_core = lax.axis_index(core)
    lefts_rights = (activated, grad_ffn, grad_pre, normed_low, ctx_low, grad_attn)
    sent = weight_sums(1 - my_core, *lefts_rights)
    sent, lefts_rights = lax.optimization_barrier((sent, lefts_rights))
    arrived = swap(sent, core)
    kept = weight_sums(my_core, *lefts_rights)
    kept, arrived, grad_ctx = lax.optimization_barrier((kept, arrived, grad_ctx))
    early = jnp.split(kept + arrived, 2, axis=0)
    pairs = width // PAIR
    third = pairs // 3
    sides = ((others, key_other, value_other), (mine, key, value))
    parts = (((0, 2 * third), (2 * third, third)), ((0, third), (third, third), (2 * third, third)))
    done = 0
    grads = []
    before = ()
    for side, (place, keys, values) in enumerate(sides):
        into = ()
        for first, count in parts[side]:
            keeps, sends = begin(early, stages[done])
            keeps, sends, grad_ctx, into, before = lax.optimization_barrier(
                (keeps, sends, grad_ctx, into, before)
            )
            came = travel(sends, stages[done])
            into = attend_back(
                place, query, grad_ctx, context, lse, keys, values, first, count, before, into
            )
            came, into = lax.optimization_barrier((came, into))
            early = end(keeps, came, stages[done])
            done += 1
        grads.append(into)
        if side == 0:
            before = into[:1]
            dx_other = (mm(into[1], w_key, NT) + mm(into[2], w_value, NT)).astype(BF16)
            dx_other, before = lax.optimization_barrier((dx_other, before))
            dx_from_other = swap(dx_other, "seq")
    (_, dk_other, dv_other), (dq, dk, dv) = grads
    keeps, sends = begin(early, stages[done])
    keeps, sends, dq, dk, dv, dx_from_other = lax.optimization_barrier(
        (keeps, sends, dq, dk, dv, dx_from_other)
    )
    came = travel(sends, stages[done])
    grad_embedded = (
        grad_one
        + mm(dq, w_query, NT)
        + mm(dk, w_key, NT)
        + mm(dv, w_value, NT)
        + dx_from_other.astype(F32)
    )
    grad_low = grad_embedded.astype(BF16)
    grad_low, came = lax.optimization_barrier((grad_low, came))
    keeps, sends = begin(end(keeps, came, stages[done]), stages[done + 1])
    done += 1
    keeps, sends, grad_low = lax.optimization_barrier((keeps, sends, grad_low))
    came = travel(sends, stages[done])

    outgoing = mm(slot_hot, grad_low, TN).astype(BF16)
    outgoing, dq, dk, dv, came = lax.optimization_barrier((outgoing, dq, dk, dv, came))
    early = end(keeps, came, stages[done])
    done += 1
    returned = exchange(outgoing.reshape(group, 2 * slots_all, width)).reshape(slots, width)
    w_query_grad = mm(x_low, dq, TN)
    w_key_grad = mm(x_low, dk, TN) + mm(x_other, dk_other, TN)
    w_value_grad = mm(x_low, dv, TN) + mm(x_other, dv_other, TN)
    b_query_grad = jnp.sum(dq.astype(F32), axis=0)
    b_value_grad = jnp.sum(dv.astype(F32), axis=0) + jnp.sum(dv_other.astype(F32), axis=0)
    grad_rest = (grad_embedded - grad_low.astype(F32)).astype(BF16)
    expr_grad = mm(bin_hot, grad_low, TN) + mm(bin_hot, grad_rest, TN)
    short = jnp.concatenate(
        [
            jnp.sum(sums.reshape(6, 8, width), axis=1),
            jnp.sum(up_sums, axis=0).reshape(wide // width, width),
            b_query_grad[None, :],
            b_value_grad[None, :],
        ],
        axis=0,
    )
    block = 128
    short = jnp.pad(short, ((0, -short.shape[0] % block), (0, 0)))
    late = [w_query_grad, w_key_grad, w_value_grad, expr_grad, short]
    heights = [item.shape[0] for item in late]
    late = jnp.concatenate([item.astype(BF16) for item in late], axis=0)
    keep, send = cut(late, core)
    late = jnp.split(keep + swap(send, core), 2, axis=0)
    keeps, sends = begin(late, stages[0])
    came = travel(sends, stages[0])
    returned, keeps, came, early = lax.optimization_barrier((returned, keeps, came, early))
    late = end(keeps, came, stages[0])
    last = len(stages) - 1
    spread = 4
    early_keeps, early_sends = begin(early, stages[done])
    early_came = []
    early_parts = []
    for at, stage in enumerate(stages[1:], start=1):
        keeps, sends = begin(late, stage)
        if at == last - 1:
            keeps, sends, for_other = lax.optimization_barrier((keeps, sends, for_other))
            from_other = [swap(part, top_axis) for part in jnp.split(for_other, 2, axis=0)]
        if at == last:
            keeps, sends, from_other[0] = lax.optimization_barrier((keeps, sends, from_other[0]))
        came = travel(sends, stage)
        if 2 <= at < 2 + spread:
            rows = early_sends[0].shape[0] // spread
            some = [p[(at - 2) * rows : (at - 1) * rows] for p in early_sends]
            some, came = lax.optimization_barrier((travel(some, stages[done]), came))
            early_came.append(some)
        if at == 2:
            table_own = mm(owned[0].astype(BF16), returned)
            came, table_own = lax.optimization_barrier((came, table_own))
        if at == 3:
            for_other = mm(owned[1].astype(BF16), returned).astype(BF16)
            came, for_other = lax.optimization_barrier((came, for_other))
        if at == last - 1:
            early_came = [jnp.concatenate(parts, axis=0) for parts in zip(*early_came)]
            early = end(early_keeps, early_came, stages[done])
            early = jnp.concatenate(run_stages(early, stages[done + 1 :]), axis=0)
            came, early = lax.optimization_barrier((came, early))
            early_step = (early, swap(early, core))
        if at == last:
            early_parts.append(unpack(my_core, *early_step, 0, wide, False))
            came, early_parts, from_other[1] = lax.optimization_barrier(
                (came, early_parts, from_other[1])
            )
        late = end(keeps, came, stage)
    late = jnp.concatenate(late, axis=0)
    late_other = swap(late, core)
    early_parts.append(unpack(my_core, *early_step, wide, wide, True))
    early_parts.append(unpack(my_core, *early_step, 2 * wide, width, False))
    late_other, early_parts, from_other = lax.optimization_barrier(
        (late_other, early_parts, from_other)
    )
    gene_grad, know_grad = (
        table_own[part * rows_dev : (part + 1) * rows_dev] + from_other[part].astype(F32)
        for part in range(2)
    )
    w_down_grad, w_up_grad, w_out_grad = early_parts
    w_query_grad, w_key_grad, w_value_grad, expr_grad, short = unpack_whole(
        my_core, late, late_other, heights
    )
    gain_two_grad, shift_two_grad, b_down_grad, gain_one_grad, shift_one_grad, b_out_grad = (
        short[i] for i in range(6)
    )
    b_up_grad = short[6 : 6 + wide // width].reshape(wide)
    b_query_grad, b_value_grad = short[6 + wide // width], short[7 + wide // width]
    return (
        layer_output.reshape(1, tokens, width),
        gene_grad,
        know_grad,
        expr_grad,
        w_query_grad,
        b_query_grad,
        w_key_grad,
        w_value_grad,
        b_value_grad,
        w_out_grad,
        b_out_grad,
        gain_one_grad,
        shift_one_grad,
        w_up_grad,
        b_up_grad,
        w_down_grad,
        b_down_grad,
        gain_two_grad,
        shift_two_grad,
        row_counts.reshape(2, rows_dev),
    )


def solution(mesh):
    bits = mesh.shape["dp"].bit_length() - 1
    dp_axes = tuple(f"dp{i}" for i in range(bits))
    fine = Mesh(mesh.devices.reshape((2,) * bits + (mesh.shape["seq"],)), (*dp_axes, "seq"))
    every = (*dp_axes, "seq")
    whole = P()
    placed = (
        (P(dp_axes, "seq"),) * 4
        + (P(dp_axes),) * 2
        + (P(every, None), P(None, every, None))
        + (whole,) * 16
        + (P(dp_axes, "seq", None),)
    )
    given = (
        (P(dp_axes, "seq", None),)
        + (P(every, None),) * 2
        + (whole,) * 16
        + (P(None, every),)
    )
    return jax.shard_map(
        functools.partial(local, dp_axes), mesh=fine, in_specs=placed, out_specs=given, check_vma=False
    )
```

```python
import functools

import jax
import jax.numpy as jnp
from jax import lax
from jax.experimental import pallas as pl
from jax.experimental.pallas import tpu as pltpu
from jax.sharding import Mesh, PartitionSpec as P

HEADS = 12
HEAD_DIM = 64
PAIR = 2 * HEAD_DIM
KEY_CHUNK = 512
LOG2E = 1.4426950408889634
SWAP = [(0, 1), (1, 0)]
F32 = jnp.float32
BF16 = jnp.bfloat16
NN = (((1,), (0,)), ((), ()))
NT = (((1,), (1,)), ((), ()))
TN = (((0,), (0,)), ((), ()))


def mm(left, right, dims=NN):
    return lax.dot_general(left, right, dims, preferred_element_type=F32)


def params(mib):
    return pltpu.CompilerParams(vmem_limit_bytes=mib * 2**20)


def cost(flops, moved):
    return pl.CostEstimate(flops=flops, bytes_accessed=moved, transcendentals=0)


def hot(left, right):
    return (left == right).astype(BF16)


def route_kernel(
    rows_dev, capacity, top_ref, gene_ref, know_ref, req_ref, gene_slot_ref, know_slot_ref
):
    tokens = gene_ref.shape[0]
    devices, slots_all = req_ref.shape
    lane = lax.broadcasted_iota(jnp.int32, (tokens, devices), 1)
    top = top_ref[0]
    half = jnp.where((lane & 1) == 0, top, 1 - top)
    first = (half * (devices // 2) + (lane >> 1)) * rows_dev
    earlier = (
        lax.broadcasted_iota(jnp.int32, (tokens, tokens), 0)
        > lax.broadcasted_iota(jnp.int32, (tokens, tokens), 1)
    ).astype(F32).astype(BF16)
    rank_lane = lax.broadcasted_iota(jnp.int32, (tokens, capacity), 1)
    asked = []
    for which, (ids_ref, slot_ref) in enumerate(((gene_ref, gene_slot_ref), (know_ref, know_slot_ref))):
        row = ids_ref[...] - first
        hit = (row >= 0) & (row < rows_dev)
        before = mm(earlier, hit.astype(F32).astype(BF16))
        rank = jnp.sum(jnp.where(hit, before, 0.0), axis=1, keepdims=True)
        owner = jnp.sum(jnp.where(hit, lane, 0).astype(F32), axis=1, keepdims=True)
        slot_ref[...] = (owner * slots_all + rank).astype(jnp.int32) + which * capacity
        rank_hit = (rank_lane == rank.astype(jnp.int32)).astype(F32).astype(BF16)
        coded = jnp.where(hit, row + 1, 0)
        high = (coded >> 4).astype(F32).astype(BF16)
        low = (coded & 15).astype(F32).astype(BF16)
        wanted = (mm(high, rank_hit, TN) * 16.0 + mm(low, rank_hit, TN)).astype(jnp.int32)
        asked.append(jnp.where(wanted > 0, wanted - 1 + which * rows_dev, -1))
    req_ref[:, :capacity] = asked[0]
    req_ref[:, capacity:] = asked[1]


def route(top, gene_ids, know_ids, rows_dev, capacity, devices):
    tokens = gene_ids.shape[0]
    return pl.pallas_call(
        functools.partial(route_kernel, rows_dev, capacity),
        in_specs=[pl.BlockSpec(memory_space=pltpu.SMEM)] + [pl.BlockSpec(memory_space=pltpu.VMEM)] * 2,
        out_shape=(
            jax.ShapeDtypeStruct((devices, 2 * capacity), jnp.int32),
            jax.ShapeDtypeStruct((tokens, 1), jnp.int32),
            jax.ShapeDtypeStruct((tokens, 1), jnp.int32),
        ),
        compiler_params=params(32),
        name="route",
    )(top.reshape(1), gene_ids[:, None], know_ids[:, None])


def fill_keys(aug_ref, key, first_key, count):
    lanes = lax.broadcasted_iota(jnp.int32, key.shape, 1)
    at = lax.broadcasted_iota(jnp.int32, key.shape, 0) + first_key
    bias = jnp.where(at < count, 0.0, -1e30).astype(BF16)
    none = jnp.zeros_like(key)
    aug_ref[:, :PAIR] = jnp.where(lanes < HEAD_DIM, key, jnp.where(lanes == HEAD_DIM, bias, none))
    aug_ref[:, PAIR : 2 * PAIR] = key
    aug_ref[:, 2 * PAIR :] = jnp.where(lanes >= HEAD_DIM, key, jnp.where(lanes == 0, bias, none))


def head_mask(shape, head):
    lanes = lax.broadcasted_iota(jnp.int32, shape, 1)
    return (lanes >= head * HEAD_DIM) & (lanes < (head + 1) * HEAD_DIM)


def spread_query(query, head):
    lanes = lax.broadcasted_iota(jnp.int32, query.shape, 1)
    scaled = query.astype(F32) * (HEAD_DIM ** (-0.5) * LOG2E)
    scaled = jnp.where(head_mask(query.shape, head), scaled, 0.0)
    high = scaled.astype(BF16)
    low = scaled - high.astype(F32)
    low = jnp.where(lanes == (1 - head) * HEAD_DIM, 1.0, low).astype(BF16)
    return jnp.concatenate([low, high] if head == 0 else [high, low], axis=1)


def fold_rows(value, how):
    return how(value.reshape(value.shape[0] // 8, 8, value.shape[1]), axis=0)


def attend_kernel(merge, where_ref, q_ref, k_ref, v_ref, *rest):
    if merge:
        out_in_ref, lse_in_ref, out_ref, lse_ref, aug_ref, vt_ref, score_ref = rest
    else:
        out_ref, lse_ref, aug_ref, vt_ref, score_ref = rest
    spans = [slice(c, c + KEY_CHUNK) for c in range(0, k_ref.shape[0], KEY_CHUNK)]
    fill_keys(aug_ref, k_ref[...], where_ref[0], where_ref[1])
    vt_ref[...] = v_ref[...].T
    outs = []
    for head in range(2):
        own = slice(head * HEAD_DIM, (head + 1) * HEAD_DIM)
        query = spread_query(q_ref[...], head)
        top = None
        for span in spans:
            scores = mm(aug_ref[span, head * PAIR : (head + 2) * PAIR], query, NT)
            score_ref[head, span, :] = scores
            high = fold_rows(scores, jnp.max)
            top = high if top is None else jnp.maximum(top, high)
        top = jnp.max(top, axis=0, keepdims=True)
        total = None
        acc = None
        for span in spans:
            probs = jnp.exp2(score_ref[head, span, :] - top)
            part = fold_rows(probs, jnp.sum)
            total = part if total is None else total + part
            part = mm(vt_ref[own, span], probs.astype(BF16))
            acc = part if acc is None else acc + part
        total = jnp.sum(total, axis=0, keepdims=True)
        lse = top + jnp.log2(total)
        if merge:
            before = lse_in_ref[0, head : head + 1, :]
            both = jnp.maximum(lse, before)
            both = both + jnp.log2(jnp.exp2(lse - both) + jnp.exp2(before - both))
            acc = acc * (jnp.exp2(lse - both) / total)
            acc = acc + out_in_ref[own, :] * jnp.exp2(before - both)
            lse = both
        else:
            acc = acc / total
        lse_ref[0, head : head + 1, :] = lse
        outs.append(acc)
    out = jnp.concatenate(outs, axis=0)
    out_ref[...] = out.T if merge else out


def attend(where, query, key, value, before=()):
    tokens, width = query.shape
    keys = key.shape[0]
    pairs = width // PAIR
    column = lambda rows: pl.BlockSpec((rows, PAIR), lambda p, w: (0, p))
    upright = pl.BlockSpec((PAIR, tokens), lambda p, w: (p, 0))
    stats = pl.BlockSpec((1, 2, tokens), lambda p, w: (p, 0, 0))
    merge = len(before) > 0
    return pl.pallas_call(
        functools.partial(attend_kernel, merge),
        grid_spec=pltpu.PrefetchScalarGridSpec(
            num_scalar_prefetch=1,
            grid=(pairs,),
            in_specs=[column(tokens), column(keys), column(keys)] + ([upright, stats] if merge else []),
            out_specs=[column(tokens) if merge else upright, stats],
            scratch_shapes=[
                pltpu.VMEM((keys, 3 * PAIR), BF16),
                pltpu.VMEM((PAIR, keys), BF16),
                pltpu.VMEM((2, keys, tokens), F32),
            ],
        ),
        out_shape=(
            jax.ShapeDtypeStruct((tokens, width) if merge else (width, tokens), F32),
            jax.ShapeDtypeStruct((pairs, 2, tokens), F32),
        ),
        compiler_params=params(48),
        cost_estimate=cost(16 * tokens * keys * width, 2 * tokens * width * 10),
        name="attend_more" if merge else "attend",
    )(where, query, key, value, *before)


def attend_back_kernel(
    add, untouched, where_ref, q_ref, g_ref, o_ref, lse_ref, k_ref, v_ref, *rest
):
    dq_in_ref = rest[0] if add else None
    dq_ref, dk_ref, dv_ref, aug_ref, kt_ref = rest[int(add) + untouched :]
    fill_keys(aug_ref, k_ref[...], where_ref[0], where_ref[1])
    kt_ref[...] = k_ref[...].T
    grad = g_ref[...]
    picks = (
        lax.broadcasted_iota(jnp.int32, (8, PAIR), 1) // HEAD_DIM
        == lax.broadcasted_iota(jnp.int32, (8, PAIR), 0)
    ).astype(F32)
    inner = lax.dot_general(
        picks,
        grad.astype(F32) * o_ref[...],
        NT,
        precision=lax.Precision.HIGHEST,
        preferred_element_type=F32,
    )
    scaled = q_ref[...] * jnp.asarray(HEAD_DIM ** (-0.5), BF16)
    none = jnp.zeros_like(grad)
    masks = [head_mask(grad.shape, head) for head in range(2)]
    queries = [spread_query(q_ref[...], head) for head in range(2)]
    q_heads = [jnp.where(m, scaled, none) for m in masks]
    g_heads = [jnp.where(m, grad, none) for m in masks]
    dqs = [None, None]
    for first in range(0, k_ref.shape[0], KEY_CHUNK):
        span = slice(first, first + KEY_CHUNK)
        dk = None
        dv = None
        for head in range(2):
            own = slice(head * HEAD_DIM, (head + 1) * HEAD_DIM)
            scores = mm(aug_ref[span, head * PAIR : (head + 2) * PAIR], queries[head], NT)
            probs = jnp.exp2(scores - lse_ref[0, head : head + 1, :])
            grad_probs = mm(v_ref[span, :], g_heads[head], NT)
            grad_scores = (probs * (grad_probs - inner[head : head + 1, :])).astype(BF16)
            part = mm(kt_ref[own, span], grad_scores)
            dqs[head] = part if dqs[head] is None else dqs[head] + part
            part = mm(probs.astype(BF16), g_heads[head])
            dv = part if dv is None else dv + part
            part = mm(grad_scores, q_heads[head])
            dk = part if dk is None else dk + part
        dk_ref[span, :] = dk.astype(BF16)
        dv_ref[span, :] = dv.astype(BF16)
    dq = jnp.concatenate(dqs, axis=0).T * HEAD_DIM ** (-0.5)
    if add:
        dq = dq + dq_in_ref[...]
    dq_ref[...] = dq.astype(dq_ref.dtype)


def attend_back(where, query, grad, out, lse, key, value, first, count, before, into):
    tokens, width = query.shape
    keys = key.shape[0]
    column = lambda rows: pl.BlockSpec((rows, PAIR), lambda p, w: (0, p + first))
    untouched = pl.BlockSpec(memory_space=pl.ANY)
    add = len(before) > 0
    given = 7 + len(before)
    return pl.pallas_call(
        functools.partial(attend_back_kernel, add, len(into)),
        grid_spec=pltpu.PrefetchScalarGridSpec(
            num_scalar_prefetch=1,
            grid=(count,),
            in_specs=[column(tokens)] * 3
            + [pl.BlockSpec((1, 2, tokens), lambda p, w: (p + first, 0, 0))]
            + [column(keys)] * 2
            + [column(tokens)] * len(before)
            + [untouched] * len(into),
            out_specs=[column(tokens), column(keys), column(keys)],
            scratch_shapes=[
                pltpu.VMEM((keys, 3 * PAIR), BF16),
                pltpu.VMEM((PAIR, keys), BF16),
            ],
        ),
        out_shape=(
            jax.ShapeDtypeStruct((tokens, width), BF16 if add else F32),
            jax.ShapeDtypeStruct((keys, width), BF16),
            jax.ShapeDtypeStruct((keys, width), BF16),
        ),
        input_output_aliases={given + i: i for i in range(len(into))},
        compiler_params=params(56),
        cost_estimate=cost(40 * tokens * keys * PAIR * count, 2 * tokens * PAIR * count * 12),
        name=("attend_back_more" if add else "attend_back") + str(first),
    )(where, query, grad, out, lse, key, value, *before, *into)


def norm_parts(value):
    centre = jnp.mean(value, axis=-1, keepdims=True)
    centred = value - centre
    variance = jnp.mean(centred * centred, axis=-1, keepdims=True)
    inverse = lax.rsqrt(variance + 1e-05)
    return centred * inverse, inverse


def norm_back(grad, unit, inverse, gain):
    grad_unit = grad * gain
    return inverse * (
        grad_unit
        - jnp.mean(grad_unit, axis=-1, keepdims=True)
        - unit * jnp.mean(grad_unit * unit, axis=-1, keepdims=True)
    )


def middle_kernel(
    ctx_ref,
    emb_ref,
    cot_ref,
    w_out_ref,
    w_up_ref,
    w_down_ref,
    small_ref,
    b_up_ref,
    out_ref,
    ctx_low_ref,
    normed_ref,
    act_ref,
    gffn_ref,
    gpre_ref,
    gattn_ref,
    gone_ref,
    gctx_ref,
    sums_ref,
    up_sums_ref,
    slope_ref,
):
    step = pl.program_id(0)
    width = emb_ref.shape[1]
    wide = w_up_ref.shape[1]

    @pl.when(step == 0)
    def _():
        sums_ref[...] = jnp.zeros_like(sums_ref)
        up_sums_ref[...] = jnp.zeros_like(up_sums_ref)

    b_out, gain_one, shift_one, b_down, gain_two, shift_two = (
        small_ref[i : i + 1, :] for i in range(6)
    )
    ctx_low = ctx_ref[...].astype(BF16)
    ctx_low_ref[...] = ctx_low
    unit_one, inv_one = norm_parts(emb_ref[...] + mm(ctx_low, w_out_ref[...]) + b_out)
    normed = unit_one * gain_one + shift_one
    normed_low = normed.astype(BF16)
    normed_ref[...] = normed_low
    ffn = None
    for c in range(wide // width):
        span = slice(c * width, (c + 1) * width)
        pre = mm(normed_low, w_up_ref[:, span]) + b_up_ref[:, span]
        below = 0.5 * (1.0 + lax.erf(pre * 0.7071067811865476))
        act = (pre * below).astype(BF16)
        act_ref[:, span] = act
        slope_ref[:, span] = below + pre * (0.3989422804014327 * jnp.exp(-0.5 * pre * pre))
        part = mm(act, w_down_ref[span, :])
        ffn = part if ffn is None else ffn + part
    unit_two, inv_two = norm_parts(normed + ffn + b_down)
    out_ref[...] = (unit_two * gain_two + shift_two).astype(BF16)
    grad = cot_ref[...].astype(F32)
    sums_ref[0:8, :] += fold_rows(grad * unit_two, jnp.sum)
    sums_ref[8:16, :] += fold_rows(grad, jnp.sum)
    grad_two = norm_back(grad, unit_two, inv_two, gain_two)
    gffn = grad_two.astype(BF16)
    gffn_ref[...] = gffn
    sums_ref[16:24, :] += fold_rows(gffn.astype(F32), jnp.sum)
    grad_normed = grad_two
    for c in range(wide // width):
        span = slice(c * width, (c + 1) * width)
        gpre = (mm(gffn, w_down_ref[span, :], NT) * slope_ref[:, span]).astype(BF16)
        gpre_ref[:, span] = gpre
        up_sums_ref[:, span] += fold_rows(gpre.astype(F32), jnp.sum)
        grad_normed = grad_normed + mm(gpre, w_up_ref[:, span], NT)
    sums_ref[24:32, :] += fold_rows(grad_normed * unit_one, jnp.sum)
    sums_ref[32:40, :] += fold_rows(grad_normed, jnp.sum)
    grad_one = norm_back(grad_normed, unit_one, inv_one, gain_one)
    gone_ref[...] = grad_one
    gattn = grad_one.astype(BF16)
    gattn_ref[...] = gattn
    sums_ref[40:48, :] += fold_rows(gattn.astype(F32), jnp.sum)
    gctx_ref[...] = mm(gattn, w_out_ref[...], NT).astype(BF16)


def middle(ctx, embedded, cotangent, w_out, w_up, w_down, small, b_up, block=256):
    tokens, width = embedded.shape
    wide = w_up.shape[1]
    whole = lambda a: pl.BlockSpec(a.shape, lambda i: (0, 0), pipeline_mode=pl.Buffered(1))
    rows = lambda n: pl.BlockSpec((block, n), lambda i: (i, 0))
    fixed = lambda r, n: pl.BlockSpec((r, n), lambda i: (0, 0))
    shape = lambda n, dtype: jax.ShapeDtypeStruct((tokens, n), dtype)
    return pl.pallas_call(
        middle_kernel,
        grid=(tokens // block,),
        in_specs=[rows(width)] * 3 + [whole(w_out), whole(w_up), whole(w_down), whole(small), whole(b_up)],
        out_specs=[
            rows(width),
            rows(width),
            rows(width),
            rows(wide),
            rows(width),
            rows(wide),
            rows(width),
            rows(width),
            rows(width),
            fixed(48, width),
            fixed(8, wide),
        ],
        out_shape=[
            shape(width, BF16),
            shape(width, BF16),
            shape(width, BF16),
            shape(wide, BF16),
            shape(width, BF16),
            shape(wide, BF16),
            shape(width, BF16),
            shape(width, F32),
            shape(width, BF16),
            jax.ShapeDtypeStruct((48, width), F32),
            jax.ShapeDtypeStruct((8, wide), F32),
        ],
        scratch_shapes=[pltpu.VMEM((block, wide), F32)],
        compiler_params=params(60),
        cost_estimate=cost(tokens * width * (8 * wide + 4 * width) * 2, 2 * tokens * (2 * wide + 14 * width)),
        name="middle",
    )(ctx, embedded, cotangent, w_out, w_up, w_down, small, b_up)


def weight_sums_kernel(counts, half_ref, act_ref, gffn_ref, gpre_ref, norm_ref, ctx_ref, gattn_ref, out_ref):
    at = pl.program_id(0) + half_ref[0] * pl.num_programs(0)
    first = 0
    for count, left, right in zip(counts, (act_ref, gpre_ref, ctx_ref), (gffn_ref, norm_ref, gattn_ref)):
        @pl.when((at >= first) & (at < first + count))
        def _(left=left, right=right):
            out_ref[...] = mm(left[...], right[...], TN).astype(BF16)
        first += count


def weight_sums(half, activated, grad_ffn, grad_pre, normed, ctx, grad_attn, block=384):
    tokens, width = grad_ffn.shape
    lefts = (activated, grad_pre, ctx)
    counts = [left.shape[1] // block for left in lefts]
    steps = sum(counts) // 2
    specs = []
    first = 0
    for left, right, count in zip(lefts, (grad_ffn, normed, grad_attn), counts):
        specs.append(
            pl.BlockSpec(
                (tokens, block),
                lambda i, h, first=first, count=count: (0, jnp.clip(i + h[0] * steps - first, 0, count - 1)),
            )
        )
        specs.append(pl.BlockSpec((tokens, width), lambda i, h: (0, 0), pipeline_mode=pl.Buffered(1)))
        first += count
    return pl.pallas_call(
        functools.partial(weight_sums_kernel, counts),
        grid_spec=pltpu.PrefetchScalarGridSpec(
            num_scalar_prefetch=1,
            grid=(steps,),
            in_specs=specs,
            out_specs=pl.BlockSpec((block, width), lambda i, h: (i, 0)),
        ),
        out_shape=jax.ShapeDtypeStruct((steps * block, width), BF16),
        compiler_params=params(60),
        cost_estimate=cost(2 * tokens * width * block * steps, 2 * steps * block * (tokens + width)),
        name="weight_sums",
    )(half.reshape(1), activated, grad_ffn, grad_pre, normed, ctx, grad_attn)


def unpack_kernel(first, half, turn, core_ref, own_ref, other_ref, out_ref):
    at = pl.program_id(0) + first
    mine = (at >= half) == (core_ref[0] == 1)
    rows = jnp.where(mine, own_ref[...], other_ref[...]).astype(F32)
    out_ref[...] = rows.T if turn else rows


def unpack(core, own, other, first, rows, turn, block=384):
    half, width = own.shape[0] // block, own.shape[1]
    first, steps = first // block, rows // block

    def place(i, c, owner):
        at = i + first
        inside = (at >= half) == (c[0] == owner)
        return jnp.where(inside, at % half, half - 1), 0

    return pl.pallas_call(
        functools.partial(unpack_kernel, first, half, turn),
        grid_spec=pltpu.PrefetchScalarGridSpec(
            num_scalar_prefetch=1,
            grid=(steps,),
            in_specs=[
                pl.BlockSpec((block, width), functools.partial(place, owner=1)),
                pl.BlockSpec((block, width), functools.partial(place, owner=0)),
            ],
            out_specs=pl.BlockSpec((width, block), lambda i, c: (0, i))
            if turn
            else pl.BlockSpec((block, width), lambda i, c: (i, 0)),
        ),
        out_shape=jax.ShapeDtypeStruct((width, rows) if turn else (rows, width), F32),
        compiler_params=params(60),
        cost_estimate=cost(rows * width, rows * width * 6),
        name="unpack" + str(first),
    )(core.reshape(1), own, other)


def unpack_whole_kernel(heights, core_ref, own_ref, other_ref, *out_refs):
    half = own_ref.shape[0]
    lower = core_ref[0] == 0
    first = 0
    for height, out_ref in zip(heights, out_refs):
        for part in range(2):
            start, stop = max(first, part * half), min(first + height, (part + 1) * half)
            if start < stop:
                span = slice(start - part * half, stop - part * half)
                near, far = (own_ref, other_ref) if part == 0 else (other_ref, own_ref)
                rows = jnp.where(lower, near[span, :], far[span, :])
                out_ref[start - first : stop - first, :] = rows.astype(F32)
        first += height


def unpack_whole(core, own, other, heights):
    width = own.shape[1]
    vmem = pl.BlockSpec(memory_space=pltpu.VMEM)
    return pl.pallas_call(
        functools.partial(unpack_whole_kernel, heights),
        in_specs=[pl.BlockSpec(memory_space=pltpu.SMEM), vmem, vmem],
        out_specs=[vmem] * len(heights),
        out_shape=[jax.ShapeDtypeStruct((height, width), F32) for height in heights],
        compiler_params=params(60),
        name="unpack_whole",
    )(core.reshape(1), own, other)


def cut(value, axis):
    rows = value.shape[0] // 2
    me = lax.axis_index(axis)
    keep = lax.dynamic_slice_in_dim(value, me * rows, rows, 0)
    return keep, lax.dynamic_slice_in_dim(value, (1 - me) * rows, rows, 0)


def swap(value, axis):
    return lax.ppermute(value, axis, SWAP)


def join(value, other, axis):
    first = lax.axis_index(axis) == 0
    return jnp.concatenate([jnp.where(first, value, other), jnp.where(first, other, value)], axis=0)


def stages_of(dp_axes):
    near, far = dp_axes[-2], dp_axes[-3::-1]
    down = [((near, "seq"), True), (("seq", near), True)] + [((axis,), True) for axis in far]
    return down + [(axes, False) for axes, _ in down[::-1]]


def begin(pieces, stage):
    axes, halves = stage
    if len(pieces) < len(axes):
        pieces = jnp.split(pieces[0], 2, axis=0)
    if len(pieces) > len(axes):
        pieces = [jnp.concatenate(pieces, axis=0)]
    if halves:
        keeps, sends = zip(*(cut(p, axis) for p, axis in zip(pieces, axes)))
        return list(keeps), list(sends)
    return list(pieces), list(pieces)


def travel(sends, stage):
    return [swap(s, axis) for s, axis in zip(sends, stage[0])]


def end(keeps, arrived, stage):
    axes, halves = stage
    if halves:
        return [k + a for k, a in zip(keeps, arrived)]
    return [join(k, a, axis) for k, a, axis in zip(keeps, arrived, axes)]


def run_stages(pieces, stages):
    for stage in stages:
        keeps, sends = begin(pieces, stage)
        pieces = end(keeps, travel(sends, stage), stage)
    return pieces


def local(
    dp_axes,
    gene_ids,
    homolog_ids,
    knowledge_ids,
    expr_bins,
    species,
    cell_lengths,
    gene_table,
    knowledge_tables,
    expr_table,
    w_query,
    b_query,
    w_key,
    w_value,
    b_value,
    w_out,
    b_out,
    gain_one,
    shift_one,
    w_up,
    b_up,
    w_down,
    b_down,
    gain_two,
    shift_two,
    cotangent,
):
    tokens = gene_ids.shape[1]
    rows_dev, width = gene_table.shape
    wide = w_up.shape[1]
    every = (*dp_axes, "seq")
    top_axis, group_axes = dp_axes[0], (*dp_axes[1:], "seq")
    devices = lax.axis_size(every)
    group = devices // 2
    capacity = 2 * tokens // devices
    slots_all = 2 * capacity
    slots = devices * slots_all
    bins = expr_table.shape[0]
    me = lax.axis_index("seq")

    def exchange(value):
        return lax.all_to_all(value, group_axes, split_axis=0, concat_axis=0, tiled=True)

    gene_table, knowledge_tables = lax.optimization_barrier((gene_table, knowledge_tables))
    gene_other = lax.ppermute(gene_table, top_axis, SWAP)
    know_sum = jnp.sum(knowledge_tables.astype(F32), axis=0).astype(BF16)
    chosen = jnp.where(species[0] == 1, homolog_ids, gene_ids).reshape(-1)
    requests, gene_slot, know_slot = route(
        lax.axis_index(top_axis), chosen, knowledge_ids.reshape(-1), rows_dev, capacity, devices
    )
    asked = exchange(requests.reshape(group, 2 * slots_all))
    asked, gene_other, know_sum = lax.optimization_barrier((asked, gene_other, know_sum))
    know_other = lax.ppermute(know_sum, top_axis, SWAP)
    asked = asked.reshape(group, 2, slots_all)
    shift = jnp.arange(2)[None, :, None] * (2 * rows_dev)
    asked = jnp.where(asked >= 0, asked + shift, -1).reshape(group, 2 * slots_all)
    row_at = jnp.arange(4 * rows_dev)
    slot_at = jnp.arange(slots).reshape(group, 2 * slots_all)
    bin_hot = hot(expr_bins.reshape(-1)[:, None], jnp.arange(bins)[None, :])
    embedded = mm(bin_hot, expr_table)
    fetched = gene_other
    tables = jnp.concatenate([gene_table, know_sum, gene_other], axis=0)
    late_rows = slice(slots_all + capacity, 2 * slots_all)
    early_rows = slice(0, slots_all + capacity)
    for columns, rows, table in (
        (early_rows, row_at[: 3 * rows_dev], tables),
        (late_rows, row_at[3 * rows_dev :], know_other),
    ):
        wanted = asked[:, columns].reshape(-1)
        found = mm(hot(wanted[:, None], rows[None, :]), table).astype(BF16)
        found, _ = lax.optimization_barrier((found, fetched))
        fetched = exchange(found.reshape(group, -1, width)).reshape(-1, width)
        at = slot_at[:, columns].reshape(1, -1)
        embedded = embedded + mm(((at == gene_slot) | (at == know_slot)).astype(BF16), fetched)
    asked = asked.reshape(slots)
    slot_at = slot_at.reshape(1, slots)
    slot_hot = ((slot_at == gene_slot) | (slot_at == know_slot)).astype(BF16)
    x_low = embedded.astype(BF16)

    x_other = lax.ppermute(x_low, "seq", SWAP)
    query = (mm(x_low, w_query) + b_query).astype(BF16)
    key, key_other = (mm(x, w_key).astype(BF16) for x in (x_low, x_other))
    value, value_other = ((mm(x, w_value) + b_value).astype(BF16) for x in (x_low, x_other))
    mine = jnp.stack([me * tokens, cell_lengths[0]]).astype(jnp.int32)
    others = jnp.stack([(1 - me) * tokens, cell_lengths[0]]).astype(jnp.int32)
    block_rows = 2 * rows_dev
    owned = [row_at[at : at + block_rows, None] == asked[None, :] for at in (0, block_rows)]
    counts = [jnp.sum(o.astype(jnp.int32), axis=1) for o in owned]
    counts_back = lax.ppermute(counts[1], top_axis, SWAP)
    first_part = attend(mine, query, key, value)
    first_part, counts_back = lax.optimization_barrier((first_part, counts_back))
    row_counts = counts[0] + counts_back
    context, lse = attend(others, query, key_other, value_other, first_part)

    small = jnp.stack([b_out, gain_one, shift_one, b_down, gain_two, shift_two])
    (
        layer_output,
        ctx_low,
        normed_low,
        activated,
        grad_ffn,
        grad_pre,
        grad_attn,
        grad_one,
        grad_ctx,
        sums,
        up_sums,
    ) = middle(
        context, embedded, cotangent.reshape(tokens, width), w_out, w_up, w_down, small, b_up[None, :]
    )

    core = dp_axes[-1]
    stages = stages_of(dp_axes)
    my_core = lax.axis_index(core)
    lefts_rights = (activated, grad_ffn, grad_pre, normed_low, ctx_low, grad_attn)
    sent = weight_sums(1 - my_core, *lefts_rights)
    sent, lefts_rights = lax.optimization_barrier((sent, lefts_rights))
    arrived = swap(sent, core)
    kept = weight_sums(my_core, *lefts_rights)
    kept, arrived, grad_ctx = lax.optimization_barrier((kept, arrived, grad_ctx))
    early = jnp.split(kept + arrived, 2, axis=0)
    pairs = width // PAIR
    third = pairs // 3
    sides = ((others, key_other, value_other), (mine, key, value))
    parts = (((0, 2 * third), (2 * third, third)), ((0, third), (third, third), (2 * third, third)))
    done = 0
    grads = []
    before = ()
    for side, (place, keys, values) in enumerate(sides):
        into = ()
        for first, count in parts[side]:
            keeps, sends = begin(early, stages[done])
            keeps, sends, grad_ctx, into, before = lax.optimization_barrier(
                (keeps, sends, grad_ctx, into, before)
            )
            came = travel(sends, stages[done])
            into = attend_back(
                place, query, grad_ctx, context, lse, keys, values, first, count, before, into
            )
            came, into = lax.optimization_barrier((came, into))
            early = end(keeps, came, stages[done])
            done += 1
        grads.append(into)
        if side == 0:
            before = into[:1]
            dx_other = (mm(into[1], w_key, NT) + mm(into[2], w_value, NT)).astype(BF16)
            dx_other, before = lax.optimization_barrier((dx_other, before))
            dx_from_other = swap(dx_other, "seq")
    (_, dk_other, dv_other), (dq, dk, dv) = grads
    keeps, sends = begin(early, stages[done])
    keeps, sends, dq, dk, dv, dx_from_other = lax.optimization_barrier(
        (keeps, sends, dq, dk, dv, dx_from_other)
    )
    came = travel(sends, stages[done])
    grad_embedded = (
        grad_one
        + mm(dq, w_query, NT)
        + mm(dk, w_key, NT)
        + mm(dv, w_value, NT)
        + dx_from_other.astype(F32)
    )
    grad_low = grad_embedded.astype(BF16)
    grad_low, came = lax.optimization_barrier((grad_low, came))
    keeps, sends = begin(end(keeps, came, stages[done]), stages[done + 1])
    done += 1
    keeps, sends, grad_low = lax.optimization_barrier((keeps, sends, grad_low))
    came = travel(sends, stages[done])

    outgoing = mm(slot_hot, grad_low, TN).astype(BF16)
    outgoing, dq, dk, dv, came = lax.optimization_barrier((outgoing, dq, dk, dv, came))
    early = end(keeps, came, stages[done])
    done += 1
    returned = exchange(outgoing.reshape(group, 2 * slots_all, width)).reshape(slots, width)
    w_query_grad = mm(x_low, dq, TN)
    w_key_grad = mm(x_low, dk, TN) + mm(x_other, dk_other, TN)
    w_value_grad = mm(x_low, dv, TN) + mm(x_other, dv_other, TN)
    b_query_grad = jnp.sum(dq.astype(F32), axis=0)
    b_value_grad = jnp.sum(dv.astype(F32), axis=0) + jnp.sum(dv_other.astype(F32), axis=0)
    grad_rest = (grad_embedded - grad_low.astype(F32)).astype(BF16)
    expr_grad = mm(bin_hot, grad_low, TN) + mm(bin_hot, grad_rest, TN)
    short = jnp.concatenate(
        [
            jnp.sum(sums.reshape(6, 8, width), axis=1),
            jnp.sum(up_sums, axis=0).reshape(wide // width, width),
            b_query_grad[None, :],
            b_value_grad[None, :],
        ],
        axis=0,
    )
    block = 128
    short = jnp.pad(short, ((0, -short.shape[0] % block), (0, 0)))
    late = [w_query_grad, w_key_grad, w_value_grad, expr_grad, short]
    heights = [item.shape[0] for item in late]
    late = jnp.concatenate([item.astype(BF16) for item in late], axis=0)
    keep, send = cut(late, core)
    late = jnp.split(keep + swap(send, core), 2, axis=0)
    keeps, sends = begin(late, stages[0])
    came = travel(sends, stages[0])
    returned, keeps, came, early = lax.optimization_barrier((returned, keeps, came, early))
    late = end(keeps, came, stages[0])
    last = len(stages) - 1
    spread = 3
    early_keeps, early_sends = begin(early, stages[done])
    early_came = []
    early_parts = []
    from_other = []
    for at, stage in enumerate(stages[1:], start=1):
        keeps, sends = begin(late, stage)
        if at >= last - 1:
            keeps, sends, for_other = lax.optimization_barrier((keeps, sends, for_other))
        if at == last:
            keeps, sends, early_step = lax.optimization_barrier((keeps, sends, early_step))
        came = travel(sends, stage)
        if at >= last - 1:
            quarter = swap(jnp.split(for_other, 4, axis=0)[len(from_other)], top_axis)
            came, quarter = lax.optimization_barrier((came, quarter))
            from_other.append(quarter)
        if 2 <= at < 2 + spread:
            rows = early_sends[0].shape[0] // spread
            some = [p[(at - 2) * rows : (at - 1) * rows] for p in early_sends]
            some, came = lax.optimization_barrier((travel(some, stages[done]), came))
            early_came.append(some)
        if at == 2:
            table_own = mm(owned[0].astype(BF16), returned)
            came, table_own = lax.optimization_barrier((came, table_own))
        if at == 3:
            for_other = mm(owned[1].astype(BF16), returned).astype(BF16)
            came, for_other = lax.optimization_barrier((came, for_other))
        if at == last - 2:
            early_came = [jnp.concatenate(parts, axis=0) for parts in zip(*early_came)]
            early = end(early_keeps, early_came, stages[done])
            early = jnp.concatenate(run_stages(early, stages[done + 1 :]), axis=0)
            came, early = lax.optimization_barrier((came, early))
            early_step = (early, swap(early, core))
        if at == last:
            early_parts.append(unpack(my_core, *early_step, 0, wide, False))
            came, early_parts = lax.optimization_barrier((came, early_parts))
        late = end(keeps, came, stage)
    late = jnp.concatenate(late, axis=0)
    late, for_other = lax.optimization_barrier((late, for_other))
    late_other = swap(late, core)
    quarters = jnp.split(for_other, 4, axis=0)
    from_other.append(swap(quarters[2], top_axis))
    early_parts.append(unpack(my_core, *early_step, wide, wide, True))
    early_parts.append(unpack(my_core, *early_step, 2 * wide, width, False))
    late_other, early_parts, from_other, quarter = lax.optimization_barrier(
        (late_other, early_parts, from_other, quarters[3])
    )
    from_other.append(swap(quarter, top_axis))
    rows = block_rows // 4
    gene_grad, know_grad = (
        jnp.concatenate(
            [
                table_own[part * rows : (part + 1) * rows] + from_other[part].astype(F32)
                for part in parts
            ],
            axis=0,
        )
        for parts in ((0, 1), (2, 3))
    )
    w_down_grad, w_up_grad, w_out_grad = early_parts
    w_query_grad, w_key_grad, w_value_grad, expr_grad, short = unpack_whole(
        my_core, late, late_other, heights
    )
    gain_two_grad, shift_two_grad, b_down_grad, gain_one_grad, shift_one_grad, b_out_grad = (
        short[i] for i in range(6)
    )
    b_up_grad = short[6 : 6 + wide // width].reshape(wide)
    b_query_grad, b_value_grad = short[6 + wide // width], short[7 + wide // width]
    return (
        layer_output.reshape(1, tokens, width),
        gene_grad,
        know_grad,
        expr_grad,
        w_query_grad,
        b_query_grad,
        w_key_grad,
        w_value_grad,
        b_value_grad,
        w_out_grad,
        b_out_grad,
        gain_one_grad,
        shift_one_grad,
        w_up_grad,
        b_up_grad,
        w_down_grad,
        b_down_grad,
        gain_two_grad,
        shift_two_grad,
        row_counts.reshape(2, rows_dev),
    )


def solution(mesh):
    bits = mesh.shape["dp"].bit_length() - 1
    dp_axes = tuple(f"dp{i}" for i in range(bits))
    fine = Mesh(mesh.devices.reshape((2,) * bits + (mesh.shape["seq"],)), (*dp_axes, "seq"))
    every = (*dp_axes, "seq")
    whole = P()
    placed = (
        (P(dp_axes, "seq"),) * 4
        + (P(dp_axes),) * 2
        + (P(every, None), P(None, every, None))
        + (whole,) * 16
        + (P(dp_axes, "seq", None),)
    )
    given = (
        (P(dp_axes, "seq", None),)
        + (P(every, None),) * 2
        + (whole,) * 16
        + (P(None, every),)
    )
    return jax.shard_map(
        functools.partial(local, dp_axes), mesh=fine, in_specs=placed, out_specs=given, check_vma=False
    )
```

```python
import functools

import jax
import jax.numpy as jnp
from jax import lax
from jax.experimental import pallas as pl
from jax.experimental.pallas import tpu as pltpu
from jax.sharding import Mesh, PartitionSpec as P

HEADS = 12
HEAD_DIM = 64
PAIR = 2 * HEAD_DIM
KEY_CHUNK = 512
LOG2E = 1.4426950408889634
SWAP = [(0, 1), (1, 0)]
F32 = jnp.float32
BF16 = jnp.bfloat16
NN = (((1,), (0,)), ((), ()))
NT = (((1,), (1,)), ((), ()))
TN = (((0,), (0,)), ((), ()))


def mm(left, right, dims=NN):
    return lax.dot_general(left, right, dims, preferred_element_type=F32)


def params(mib):
    return pltpu.CompilerParams(vmem_limit_bytes=mib * 2**20)


def cost(flops, moved):
    return pl.CostEstimate(flops=flops, bytes_accessed=moved, transcendentals=0)


def hot(left, right):
    return (left == right).astype(BF16)


def route_kernel(
    rows_dev, capacity, top_ref, gene_ref, know_ref, req_ref, gene_slot_ref, know_slot_ref
):
    tokens = gene_ref.shape[0]
    devices, slots_all = req_ref.shape
    lane = lax.broadcasted_iota(jnp.int32, (tokens, devices), 1)
    top = top_ref[0]
    half = jnp.where((lane & 1) == 0, top, 1 - top)
    first = (half * (devices // 2) + (lane >> 1)) * rows_dev
    earlier = (
        lax.broadcasted_iota(jnp.int32, (tokens, tokens), 0)
        > lax.broadcasted_iota(jnp.int32, (tokens, tokens), 1)
    ).astype(F32).astype(BF16)
    rank_lane = lax.broadcasted_iota(jnp.int32, (tokens, capacity), 1)
    asked = []
    for which, (ids_ref, slot_ref) in enumerate(((gene_ref, gene_slot_ref), (know_ref, know_slot_ref))):
        row = ids_ref[...] - first
        hit = (row >= 0) & (row < rows_dev)
        before = mm(earlier, hit.astype(F32).astype(BF16))
        rank = jnp.sum(jnp.where(hit, before, 0.0), axis=1, keepdims=True)
        owner = jnp.sum(jnp.where(hit, lane, 0).astype(F32), axis=1, keepdims=True)
        slot_ref[...] = (owner * slots_all + rank).astype(jnp.int32) + which * capacity
        rank_hit = (rank_lane == rank.astype(jnp.int32)).astype(F32).astype(BF16)
        coded = jnp.where(hit, row + 1, 0)
        high = (coded >> 4).astype(F32).astype(BF16)
        low = (coded & 15).astype(F32).astype(BF16)
        wanted = (mm(high, rank_hit, TN) * 16.0 + mm(low, rank_hit, TN)).astype(jnp.int32)
        asked.append(jnp.where(wanted > 0, wanted - 1 + which * rows_dev, -1))
    req_ref[:, :capacity] = asked[0]
    req_ref[:, capacity:] = asked[1]


def route(top, gene_ids, know_ids, rows_dev, capacity, devices):
    tokens = gene_ids.shape[0]
    return pl.pallas_call(
        functools.partial(route_kernel, rows_dev, capacity),
        in_specs=[pl.BlockSpec(memory_space=pltpu.SMEM)] + [pl.BlockSpec(memory_space=pltpu.VMEM)] * 2,
        out_shape=(
            jax.ShapeDtypeStruct((devices, 2 * capacity), jnp.int32),
            jax.ShapeDtypeStruct((tokens, 1), jnp.int32),
            jax.ShapeDtypeStruct((tokens, 1), jnp.int32),
        ),
        compiler_params=params(32),
        name="route",
    )(top.reshape(1), gene_ids[:, None], know_ids[:, None])


def fill_keys(aug_ref, key, first_key, count):
    lanes = lax.broadcasted_iota(jnp.int32, key.shape, 1)
    at = lax.broadcasted_iota(jnp.int32, key.shape, 0) + first_key
    bias = jnp.where(at < count, 0.0, -1e30).astype(BF16)
    none = jnp.zeros_like(key)
    aug_ref[:, :PAIR] = jnp.where(lanes < HEAD_DIM, key, jnp.where(lanes == HEAD_DIM, bias, none))
    aug_ref[:, PAIR : 2 * PAIR] = key
    aug_ref[:, 2 * PAIR :] = jnp.where(lanes >= HEAD_DIM, key, jnp.where(lanes == 0, bias, none))


def head_mask(shape, head):
    lanes = lax.broadcasted_iota(jnp.int32, shape, 1)
    return (lanes >= head * HEAD_DIM) & (lanes < (head + 1) * HEAD_DIM)


def spread_query(query, head):
    lanes = lax.broadcasted_iota(jnp.int32, query.shape, 1)
    scaled = query.astype(F32) * (HEAD_DIM ** (-0.5) * LOG2E)
    scaled = jnp.where(head_mask(query.shape, head), scaled, 0.0)
    high = scaled.astype(BF16)
    low = scaled - high.astype(F32)
    low = jnp.where(lanes == (1 - head) * HEAD_DIM, 1.0, low).astype(BF16)
    return jnp.concatenate([low, high] if head == 0 else [high, low], axis=1)


def fold_rows(value, how):
    return how(value.reshape(value.shape[0] // 8, 8, value.shape[1]), axis=0)


def attend_kernel(merge, where_ref, q_ref, k_ref, v_ref, *rest):
    if merge:
        out_in_ref, lse_in_ref, out_ref, lse_ref, aug_ref, vt_ref, score_ref = rest
    else:
        out_ref, lse_ref, aug_ref, vt_ref, score_ref = rest
    spans = [slice(c, c + KEY_CHUNK) for c in range(0, k_ref.shape[0], KEY_CHUNK)]
    fill_keys(aug_ref, k_ref[...], where_ref[0], where_ref[1])
    vt_ref[...] = v_ref[...].T
    outs = []
    for head in range(2):
        own = slice(head * HEAD_DIM, (head + 1) * HEAD_DIM)
        query = spread_query(q_ref[...], head)
        top = None
        for span in spans:
            scores = mm(aug_ref[span, head * PAIR : (head + 2) * PAIR], query, NT)
            score_ref[head, span, :] = scores
            high = fold_rows(scores, jnp.max)
            top = high if top is None else jnp.maximum(top, high)
        top = jnp.max(top, axis=0, keepdims=True)
        total = None
        acc = None
        for span in spans:
            probs = jnp.exp2(score_ref[head, span, :] - top)
            part = fold_rows(probs, jnp.sum)
            total = part if total is None else total + part
            part = mm(vt_ref[own, span], probs.astype(BF16))
            acc = part if acc is None else acc + part
        total = jnp.sum(total, axis=0, keepdims=True)
        lse = top + jnp.log2(total)
        if merge:
            before = lse_in_ref[0, head : head + 1, :]
            both = jnp.maximum(lse, before)
            both = both + jnp.log2(jnp.exp2(lse - both) + jnp.exp2(before - both))
            acc = acc * (jnp.exp2(lse - both) / total)
            acc = acc + out_in_ref[own, :] * jnp.exp2(before - both)
            lse = both
        else:
            acc = acc / total
        lse_ref[0, head : head + 1, :] = lse
        outs.append(acc)
    out = jnp.concatenate(outs, axis=0)
    out_ref[...] = out.T if merge else out


def attend(where, query, key, value, before=()):
    tokens, width = query.shape
    keys = key.shape[0]
    pairs = width // PAIR
    column = lambda rows: pl.BlockSpec((rows, PAIR), lambda p, w: (0, p))
    upright = pl.BlockSpec((PAIR, tokens), lambda p, w: (p, 0))
    stats = pl.BlockSpec((1, 2, tokens), lambda p, w: (p, 0, 0))
    merge = len(before) > 0
    return pl.pallas_call(
        functools.partial(attend_kernel, merge),
        grid_spec=pltpu.PrefetchScalarGridSpec(
            num_scalar_prefetch=1,
            grid=(pairs,),
            in_specs=[column(tokens), column(keys), column(keys)] + ([upright, stats] if merge else []),
            out_specs=[column(tokens) if merge else upright, stats],
            scratch_shapes=[
                pltpu.VMEM((keys, 3 * PAIR), BF16),
                pltpu.VMEM((PAIR, keys), BF16),
                pltpu.VMEM((2, keys, tokens), F32),
            ],
        ),
        out_shape=(
            jax.ShapeDtypeStruct((tokens, width) if merge else (width, tokens), F32),
            jax.ShapeDtypeStruct((pairs, 2, tokens), F32),
        ),
        compiler_params=params(48),
        cost_estimate=cost(16 * tokens * keys * width, 2 * tokens * width * 10),
        name="attend_more" if merge else "attend",
    )(where, query, key, value, *before)


def attend_back_kernel(
    add, untouched, where_ref, q_ref, g_ref, o_ref, lse_ref, k_ref, v_ref, *rest
):
    dq_in_ref = rest[0] if add else None
    dq_ref, dk_ref, dv_ref, aug_ref, kt_ref = rest[int(add) + untouched :]
    fill_keys(aug_ref, k_ref[...], where_ref[0], where_ref[1])
    kt_ref[...] = k_ref[...].T
    grad = g_ref[...]
    picks = (
        lax.broadcasted_iota(jnp.int32, (8, PAIR), 1) // HEAD_DIM
        == lax.broadcasted_iota(jnp.int32, (8, PAIR), 0)
    ).astype(F32)
    inner = lax.dot_general(
        picks,
        grad.astype(F32) * o_ref[...],
        NT,
        precision=lax.Precision.HIGHEST,
        preferred_element_type=F32,
    )
    scaled = q_ref[...] * jnp.asarray(HEAD_DIM ** (-0.5), BF16)
    none = jnp.zeros_like(grad)
    masks = [head_mask(grad.shape, head) for head in range(2)]
    queries = [spread_query(q_ref[...], head) for head in range(2)]
    q_heads = [jnp.where(m, scaled, none) for m in masks]
    g_heads = [jnp.where(m, grad, none) for m in masks]
    dqs = [None, None]
    for first in range(0, k_ref.shape[0], KEY_CHUNK):
        span = slice(first, first + KEY_CHUNK)
        dk = None
        dv = None
        for head in range(2):
            own = slice(head * HEAD_DIM, (head + 1) * HEAD_DIM)
            scores = mm(aug_ref[span, head * PAIR : (head + 2) * PAIR], queries[head], NT)
            probs = jnp.exp2(scores - lse_ref[0, head : head + 1, :])
            grad_probs = mm(v_ref[span, :], g_heads[head], NT)
            grad_scores = (probs * (grad_probs - inner[head : head + 1, :])).astype(BF16)
            part = mm(kt_ref[own, span], grad_scores)
            dqs[head] = part if dqs[head] is None else dqs[head] + part
            part = mm(probs.astype(BF16), g_heads[head])
            dv = part if dv is None else dv + part
            part = mm(grad_scores, q_heads[head])
            dk = part if dk is None else dk + part
        dk_ref[span, :] = dk.astype(BF16)
        dv_ref[span, :] = dv.astype(BF16)
    dq = jnp.concatenate(dqs, axis=0).T * HEAD_DIM ** (-0.5)
    if add:
        dq = dq + dq_in_ref[...]
    dq_ref[...] = dq.astype(dq_ref.dtype)


def attend_back(where, query, grad, out, lse, key, value, first, count, before, into):
    tokens, width = query.shape
    keys = key.shape[0]
    column = lambda rows: pl.BlockSpec((rows, PAIR), lambda p, w: (0, p + first))
    untouched = pl.BlockSpec(memory_space=pl.ANY)
    add = len(before) > 0
    given = 7 + len(before)
    return pl.pallas_call(
        functools.partial(attend_back_kernel, add, len(into)),
        grid_spec=pltpu.PrefetchScalarGridSpec(
            num_scalar_prefetch=1,
            grid=(count,),
            in_specs=[column(tokens)] * 3
            + [pl.BlockSpec((1, 2, tokens), lambda p, w: (p + first, 0, 0))]
            + [column(keys)] * 2
            + [column(tokens)] * len(before)
            + [untouched] * len(into),
            out_specs=[column(tokens), column(keys), column(keys)],
            scratch_shapes=[
                pltpu.VMEM((keys, 3 * PAIR), BF16),
                pltpu.VMEM((PAIR, keys), BF16),
            ],
        ),
        out_shape=(
            jax.ShapeDtypeStruct((tokens, width), BF16 if add else F32),
            jax.ShapeDtypeStruct((keys, width), BF16),
            jax.ShapeDtypeStruct((keys, width), BF16),
        ),
        input_output_aliases={given + i: i for i in range(len(into))},
        compiler_params=params(56),
        cost_estimate=cost(40 * tokens * keys * PAIR * count, 2 * tokens * PAIR * count * 12),
        name=("attend_back_more" if add else "attend_back") + str(first),
    )(where, query, grad, out, lse, key, value, *before, *into)


def norm_parts(value):
    centre = jnp.mean(value, axis=-1, keepdims=True)
    centred = value - centre
    variance = jnp.mean(centred * centred, axis=-1, keepdims=True)
    inverse = lax.rsqrt(variance + 1e-05)
    return centred * inverse, inverse


def norm_back(grad, unit, inverse, gain):
    grad_unit = grad * gain
    return inverse * (
        grad_unit
        - jnp.mean(grad_unit, axis=-1, keepdims=True)
        - unit * jnp.mean(grad_unit * unit, axis=-1, keepdims=True)
    )


def middle_kernel(
    ctx_ref,
    emb_ref,
    cot_ref,
    w_out_ref,
    w_up_ref,
    w_down_ref,
    small_ref,
    b_up_ref,
    out_ref,
    ctx_low_ref,
    normed_ref,
    act_ref,
    gffn_ref,
    gpre_ref,
    gattn_ref,
    gone_ref,
    gctx_ref,
    sums_ref,
    up_sums_ref,
    slope_ref,
):
    step = pl.program_id(0)
    width = emb_ref.shape[1]
    wide = w_up_ref.shape[1]

    @pl.when(step == 0)
    def _():
        sums_ref[...] = jnp.zeros_like(sums_ref)
        up_sums_ref[...] = jnp.zeros_like(up_sums_ref)

    b_out, gain_one, shift_one, b_down, gain_two, shift_two = (
        small_ref[i : i + 1, :] for i in range(6)
    )
    ctx_low = ctx_ref[...].astype(BF16)
    ctx_low_ref[...] = ctx_low
    unit_one, inv_one = norm_parts(emb_ref[...] + mm(ctx_low, w_out_ref[...]) + b_out)
    normed = unit_one * gain_one + shift_one
    normed_low = normed.astype(BF16)
    normed_ref[...] = normed_low
    ffn = None
    for c in range(wide // width):
        span = slice(c * width, (c + 1) * width)
        pre = mm(normed_low, w_up_ref[:, span]) + b_up_ref[:, span]
        below = 0.5 * (1.0 + lax.erf(pre * 0.7071067811865476))
        act = (pre * below).astype(BF16)
        act_ref[:, span] = act
        slope_ref[:, span] = below + pre * (0.3989422804014327 * jnp.exp(-0.5 * pre * pre))
        part = mm(act, w_down_ref[span, :])
        ffn = part if ffn is None else ffn + part
    unit_two, inv_two = norm_parts(normed + ffn + b_down)
    out_ref[...] = (unit_two * gain_two + shift_two).astype(BF16)
    grad = cot_ref[...].astype(F32)
    sums_ref[0:8, :] += fold_rows(grad * unit_two, jnp.sum)
    sums_ref[8:16, :] += fold_rows(grad, jnp.sum)
    grad_two = norm_back(grad, unit_two, inv_two, gain_two)
    gffn = grad_two.astype(BF16)
    gffn_ref[...] = gffn
    sums_ref[16:24, :] += fold_rows(gffn.astype(F32), jnp.sum)
    grad_normed = grad_two
    for c in range(wide // width):
        span = slice(c * width, (c + 1) * width)
        gpre = (mm(gffn, w_down_ref[span, :], NT) * slope_ref[:, span]).astype(BF16)
        gpre_ref[:, span] = gpre
        up_sums_ref[:, span] += fold_rows(gpre.astype(F32), jnp.sum)
        grad_normed = grad_normed + mm(gpre, w_up_ref[:, span], NT)
    sums_ref[24:32, :] += fold_rows(grad_normed * unit_one, jnp.sum)
    sums_ref[32:40, :] += fold_rows(grad_normed, jnp.sum)
    grad_one = norm_back(grad_normed, unit_one, inv_one, gain_one)
    gone_ref[...] = grad_one
    gattn = grad_one.astype(BF16)
    gattn_ref[...] = gattn
    sums_ref[40:48, :] += fold_rows(gattn.astype(F32), jnp.sum)
    gctx_ref[...] = mm(gattn, w_out_ref[...], NT).astype(BF16)


def middle(ctx, embedded, cotangent, w_out, w_up, w_down, small, b_up, block=512):
    tokens, width = embedded.shape
    wide = w_up.shape[1]
    whole = lambda a: pl.BlockSpec(a.shape, lambda i: (0, 0), pipeline_mode=pl.Buffered(1))
    rows = lambda n: pl.BlockSpec((block, n), lambda i: (i, 0))
    fixed = lambda r, n: pl.BlockSpec((r, n), lambda i: (0, 0))
    shape = lambda n, dtype: jax.ShapeDtypeStruct((tokens, n), dtype)
    return pl.pallas_call(
        middle_kernel,
        grid=(tokens // block,),
        in_specs=[rows(width)] * 3 + [whole(w_out), whole(w_up), whole(w_down), whole(small), whole(b_up)],
        out_specs=[
            rows(width),
            rows(width),
            rows(width),
            rows(wide),
            rows(width),
            rows(wide),
            rows(width),
            rows(width),
            rows(width),
            fixed(48, width),
            fixed(8, wide),
        ],
        out_shape=[
            shape(width, BF16),
            shape(width, BF16),
            shape(width, BF16),
            shape(wide, BF16),
            shape(width, BF16),
            shape(wide, BF16),
            shape(width, BF16),
            shape(width, F32),
            shape(width, BF16),
            jax.ShapeDtypeStruct((48, width), F32),
            jax.ShapeDtypeStruct((8, wide), F32),
        ],
        scratch_shapes=[pltpu.VMEM((block, wide), F32)],
        compiler_params=params(60),
        cost_estimate=cost(tokens * width * (8 * wide + 4 * width) * 2, 2 * tokens * (2 * wide + 14 * width)),
        name="middle",
    )(ctx, embedded, cotangent, w_out, w_up, w_down, small, b_up)


def weight_sums_kernel(counts, half_ref, act_ref, gffn_ref, gpre_ref, norm_ref, ctx_ref, gattn_ref, out_ref):
    at = pl.program_id(0) + half_ref[0] * pl.num_programs(0)
    first = 0
    for count, left, right in zip(counts, (act_ref, gpre_ref, ctx_ref), (gffn_ref, norm_ref, gattn_ref)):
        @pl.when((at >= first) & (at < first + count))
        def _(left=left, right=right):
            out_ref[...] = mm(left[...], right[...], TN).astype(BF16)
        first += count


def weight_sums(half, activated, grad_ffn, grad_pre, normed, ctx, grad_attn, block=384):
    tokens, width = grad_ffn.shape
    lefts = (activated, grad_pre, ctx)
    counts = [left.shape[1] // block for left in lefts]
    steps = sum(counts) // 2
    specs = []
    first = 0
    for left, right, count in zip(lefts, (grad_ffn, normed, grad_attn), counts):
        specs.append(
            pl.BlockSpec(
                (tokens, block),
                lambda i, h, first=first, count=count: (0, jnp.clip(i + h[0] * steps - first, 0, count - 1)),
            )
        )
        specs.append(pl.BlockSpec((tokens, width), lambda i, h: (0, 0), pipeline_mode=pl.Buffered(1)))
        first += count
    return pl.pallas_call(
        functools.partial(weight_sums_kernel, counts),
        grid_spec=pltpu.PrefetchScalarGridSpec(
            num_scalar_prefetch=1,
            grid=(steps,),
            in_specs=specs,
            out_specs=pl.BlockSpec((block, width), lambda i, h: (i, 0)),
        ),
        out_shape=jax.ShapeDtypeStruct((steps * block, width), BF16),
        compiler_params=params(60),
        cost_estimate=cost(2 * tokens * width * block * steps, 2 * steps * block * (tokens + width)),
        name="weight_sums",
    )(half.reshape(1), activated, grad_ffn, grad_pre, normed, ctx, grad_attn)


def unpack_kernel(first, half, turn, core_ref, own_ref, other_ref, out_ref):
    at = pl.program_id(0) + first
    mine = (at >= half) == (core_ref[0] == 1)
    rows = jnp.where(mine, own_ref[...], other_ref[...]).astype(F32)
    out_ref[...] = rows.T if turn else rows


def unpack(core, own, other, first, rows, turn, block=384):
    half, width = own.shape[0] // block, own.shape[1]
    first, steps = first // block, rows // block

    def place(i, c, owner):
        at = i + first
        inside = (at >= half) == (c[0] == owner)
        return jnp.where(inside, at % half, half - 1), 0

    return pl.pallas_call(
        functools.partial(unpack_kernel, first, half, turn),
        grid_spec=pltpu.PrefetchScalarGridSpec(
            num_scalar_prefetch=1,
            grid=(steps,),
            in_specs=[
                pl.BlockSpec((block, width), functools.partial(place, owner=1)),
                pl.BlockSpec((block, width), functools.partial(place, owner=0)),
            ],
            out_specs=pl.BlockSpec((width, block), lambda i, c: (0, i))
            if turn
            else pl.BlockSpec((block, width), lambda i, c: (i, 0)),
        ),
        out_shape=jax.ShapeDtypeStruct((width, rows) if turn else (rows, width), F32),
        compiler_params=params(60),
        cost_estimate=cost(rows * width, rows * width * 6),
        name="unpack" + str(first),
    )(core.reshape(1), own, other)


def unpack_whole_kernel(heights, core_ref, own_ref, other_ref, *out_refs):
    half = own_ref.shape[0]
    lower = core_ref[0] == 0
    first = 0
    for height, out_ref in zip(heights, out_refs):
        for part in range(2):
            start, stop = max(first, part * half), min(first + height, (part + 1) * half)
            if start < stop:
                span = slice(start - part * half, stop - part * half)
                near, far = (own_ref, other_ref) if part == 0 else (other_ref, own_ref)
                rows = jnp.where(lower, near[span, :], far[span, :])
                out_ref[start - first : stop - first, :] = rows.astype(F32)
        first += height


def unpack_whole(core, own, other, heights):
    width = own.shape[1]
    vmem = pl.BlockSpec(memory_space=pltpu.VMEM)
    return pl.pallas_call(
        functools.partial(unpack_whole_kernel, heights),
        in_specs=[pl.BlockSpec(memory_space=pltpu.SMEM), vmem, vmem],
        out_specs=[vmem] * len(heights),
        out_shape=[jax.ShapeDtypeStruct((height, width), F32) for height in heights],
        compiler_params=params(60),
        name="unpack_whole",
    )(core.reshape(1), own, other)


def cut(value, axis):
    rows = value.shape[0] // 2
    me = lax.axis_index(axis)
    keep = lax.dynamic_slice_in_dim(value, me * rows, rows, 0)
    return keep, lax.dynamic_slice_in_dim(value, (1 - me) * rows, rows, 0)


def swap(value, axis):
    return lax.ppermute(value, axis, SWAP)


def join(value, other, axis):
    first = lax.axis_index(axis) == 0
    return jnp.concatenate([jnp.where(first, value, other), jnp.where(first, other, value)], axis=0)


def stages_of(dp_axes):
    near, far = dp_axes[-2], dp_axes[-3::-1]
    down = [((near, "seq"), True), (("seq", near), True)] + [((axis,), True) for axis in far]
    return down + [(axes, False) for axes, _ in down[::-1]]


def begin(pieces, stage):
    axes, halves = stage
    if len(pieces) < len(axes):
        pieces = jnp.split(pieces[0], 2, axis=0)
    if len(pieces) > len(axes):
        pieces = [jnp.concatenate(pieces, axis=0)]
    if halves:
        keeps, sends = zip(*(cut(p, axis) for p, axis in zip(pieces, axes)))
        return list(keeps), list(sends)
    return list(pieces), list(pieces)


def travel(sends, stage):
    return [swap(s, axis) for s, axis in zip(sends, stage[0])]


def end(keeps, arrived, stage):
    axes, halves = stage
    if halves:
        return [k + a for k, a in zip(keeps, arrived)]
    return [join(k, a, axis) for k, a, axis in zip(keeps, arrived, axes)]


def run_stages(pieces, stages):
    for stage in stages:
        keeps, sends = begin(pieces, stage)
        pieces = end(keeps, travel(sends, stage), stage)
    return pieces


def local(
    dp_axes,
    gene_ids,
    homolog_ids,
    knowledge_ids,
    expr_bins,
    species,
    cell_lengths,
    gene_table,
    knowledge_tables,
    expr_table,
    w_query,
    b_query,
    w_key,
    w_value,
    b_value,
    w_out,
    b_out,
    gain_one,
    shift_one,
    w_up,
    b_up,
    w_down,
    b_down,
    gain_two,
    shift_two,
    cotangent,
):
    tokens = gene_ids.shape[1]
    rows_dev, width = gene_table.shape
    wide = w_up.shape[1]
    every = (*dp_axes, "seq")
    top_axis, group_axes = dp_axes[0], (*dp_axes[1:], "seq")
    devices = lax.axis_size(every)
    group = devices // 2
    capacity = 2 * tokens // devices
    slots_all = 2 * capacity
    slots = devices * slots_all
    bins = expr_table.shape[0]
    me = lax.axis_index("seq")

    def exchange(value):
        return lax.all_to_all(value, group_axes, split_axis=0, concat_axis=0, tiled=True)

    gene_table, knowledge_tables = lax.optimization_barrier((gene_table, knowledge_tables))
    gene_other = lax.ppermute(gene_table, top_axis, SWAP)
    know_sum = jnp.sum(knowledge_tables.astype(F32), axis=0).astype(BF16)
    chosen = jnp.where(species[0] == 1, homolog_ids, gene_ids).reshape(-1)
    requests, gene_slot, know_slot = route(
        lax.axis_index(top_axis), chosen, knowledge_ids.reshape(-1), rows_dev, capacity, devices
    )
    asked = exchange(requests.reshape(group, 2 * slots_all))
    asked, gene_other, know_sum = lax.optimization_barrier((asked, gene_other, know_sum))
    know_other = lax.ppermute(know_sum, top_axis, SWAP)
    asked = asked.reshape(group, 2, slots_all)
    shift = jnp.arange(2)[None, :, None] * (2 * rows_dev)
    asked = jnp.where(asked >= 0, asked + shift, -1).reshape(group, 2 * slots_all)
    row_at = jnp.arange(4 * rows_dev)
    slot_at = jnp.arange(slots).reshape(group, 2 * slots_all)
    bin_hot = hot(expr_bins.reshape(-1)[:, None], jnp.arange(bins)[None, :])
    embedded = mm(bin_hot, expr_table)
    fetched = gene_other
    tables = jnp.concatenate([gene_table, know_sum, gene_other], axis=0)
    late_rows = slice(slots_all + capacity, 2 * slots_all)
    early_rows = slice(0, slots_all + capacity)
    for columns, rows, table in (
        (early_rows, row_at[: 3 * rows_dev], tables),
        (late_rows, row_at[3 * rows_dev :], know_other),
    ):
        wanted = asked[:, columns].reshape(-1)
        found = mm(hot(wanted[:, None], rows[None, :]), table).astype(BF16)
        found, _ = lax.optimization_barrier((found, fetched))
        fetched = exchange(found.reshape(group, -1, width)).reshape(-1, width)
        at = slot_at[:, columns].reshape(1, -1)
        embedded = embedded + mm(((at == gene_slot) | (at == know_slot)).astype(BF16), fetched)
    asked = asked.reshape(slots)
    slot_at = slot_at.reshape(1, slots)
    slot_hot = ((slot_at == gene_slot) | (slot_at == know_slot)).astype(BF16)
    x_low = embedded.astype(BF16)

    x_other = lax.ppermute(x_low, "seq", SWAP)
    query = (mm(x_low, w_query) + b_query).astype(BF16)
    key, key_other = (mm(x, w_key).astype(BF16) for x in (x_low, x_other))
    value, value_other = ((mm(x, w_value) + b_value).astype(BF16) for x in (x_low, x_other))
    mine = jnp.stack([me * tokens, cell_lengths[0]]).astype(jnp.int32)
    others = jnp.stack([(1 - me) * tokens, cell_lengths[0]]).astype(jnp.int32)
    block_rows = 2 * rows_dev
    owned = [row_at[at : at + block_rows, None] == asked[None, :] for at in (0, block_rows)]
    counts = [jnp.sum(o.astype(jnp.int32), axis=1) for o in owned]
    counts_back = lax.ppermute(counts[1], top_axis, SWAP)
    first_part = attend(mine, query, key, value)
    first_part, counts_back = lax.optimization_barrier((first_part, counts_back))
    row_counts = counts[0] + counts_back
    context, lse = attend(others, query, key_other, value_other, first_part)

    small = jnp.stack([b_out, gain_one, shift_one, b_down, gain_two, shift_two])
    (
        layer_output,
        ctx_low,
        normed_low,
        activated,
        grad_ffn,
        grad_pre,
        grad_attn,
        grad_one,
        grad_ctx,
        sums,
        up_sums,
    ) = middle(
        context, embedded, cotangent.reshape(tokens, width), w_out, w_up, w_down, small, b_up[None, :]
    )

    core = dp_axes[-1]
    stages = stages_of(dp_axes)
    my_core = lax.axis_index(core)
    lefts_rights = (activated, grad_ffn, grad_pre, normed_low, ctx_low, grad_attn)
    sent = weight_sums(1 - my_core, *lefts_rights)
    sent, lefts_rights = lax.optimization_barrier((sent, lefts_rights))
    arrived = swap(sent, core)
    kept = weight_sums(my_core, *lefts_rights)
    kept, arrived, grad_ctx = lax.optimization_barrier((kept, arrived, grad_ctx))
    early = jnp.split(kept + arrived, 2, axis=0)
    pairs = width // PAIR
    third = pairs // 3
    sides = ((others, key_other, value_other), (mine, key, value))
    parts = (((0, 2 * third), (2 * third, third)), ((0, third), (third, third), (2 * third, third)))
    done = 0
    grads = []
    before = ()
    for side, (place, keys, values) in enumerate(sides):
        into = ()
        for first, count in parts[side]:
            keeps, sends = begin(early, stages[done])
            keeps, sends, grad_ctx, into, before = lax.optimization_barrier(
                (keeps, sends, grad_ctx, into, before)
            )
            came = travel(sends, stages[done])
            into = attend_back(
                place, query, grad_ctx, context, lse, keys, values, first, count, before, into
            )
            came, into = lax.optimization_barrier((came, into))
            early = end(keeps, came, stages[done])
            done += 1
        grads.append(into)
        if side == 0:
            before = into[:1]
            dx_other = (mm(into[1], w_key, NT) + mm(into[2], w_value, NT)).astype(BF16)
            dx_other, before = lax.optimization_barrier((dx_other, before))
            dx_from_other = swap(dx_other, "seq")
    (_, dk_other, dv_other), (dq, dk, dv) = grads
    keeps, sends = begin(early, stages[done])
    keeps, sends, dq, dk, dv, dx_from_other = lax.optimization_barrier(
        (keeps, sends, dq, dk, dv, dx_from_other)
    )
    came = travel(sends, stages[done])
    grad_embedded = (
        grad_one
        + mm(dq, w_query, NT)
        + mm(dk, w_key, NT)
        + mm(dv, w_value, NT)
        + dx_from_other.astype(F32)
    )
    grad_low = grad_embedded.astype(BF16)
    grad_low, came = lax.optimization_barrier((grad_low, came))
    keeps, sends = begin(end(keeps, came, stages[done]), stages[done + 1])
    done += 1
    keeps, sends, grad_low = lax.optimization_barrier((keeps, sends, grad_low))
    came = travel(sends, stages[done])

    outgoing = mm(slot_hot, grad_low, TN).astype(BF16)
    outgoing, dq, dk, dv, came = lax.optimization_barrier((outgoing, dq, dk, dv, came))
    early = end(keeps, came, stages[done])
    done += 1
    returned = exchange(outgoing.reshape(group, 2 * slots_all, width)).reshape(slots, width)
    w_query_grad = mm(x_low, dq, TN)
    w_key_grad = mm(x_low, dk, TN) + mm(x_other, dk_other, TN)
    w_value_grad = mm(x_low, dv, TN) + mm(x_other, dv_other, TN)
    b_query_grad = jnp.sum(dq.astype(F32), axis=0)
    b_value_grad = jnp.sum(dv.astype(F32), axis=0) + jnp.sum(dv_other.astype(F32), axis=0)
    grad_rest = (grad_embedded - grad_low.astype(F32)).astype(BF16)
    expr_grad = mm(bin_hot, grad_low, TN) + mm(bin_hot, grad_rest, TN)
    short = jnp.concatenate(
        [
            jnp.sum(sums.reshape(6, 8, width), axis=1),
            jnp.sum(up_sums, axis=0).reshape(wide // width, width),
            b_query_grad[None, :],
            b_value_grad[None, :],
        ],
        axis=0,
    )
    block = 128
    short = jnp.pad(short, ((0, -short.shape[0] % block), (0, 0)))
    late = [w_query_grad, w_key_grad, w_value_grad, expr_grad, short]
    heights = [item.shape[0] for item in late]
    late = jnp.concatenate([item.astype(BF16) for item in late], axis=0)
    keep, send = cut(late, core)
    late = jnp.split(keep + swap(send, core), 2, axis=0)
    keeps, sends = begin(late, stages[0])
    came = travel(sends, stages[0])
    returned, keeps, came, early = lax.optimization_barrier((returned, keeps, came, early))
    late = end(keeps, came, stages[0])
    last = len(stages) - 1
    spread = 3
    early_keeps, early_sends = begin(early, stages[done])
    early_came = []
    early_parts = []
    from_other = []
    for at, stage in enumerate(stages[1:], start=1):
        keeps, sends = begin(late, stage)
        if at >= last - 1:
            keeps, sends, for_other = lax.optimization_barrier((keeps, sends, for_other))
        if at == last:
            keeps, sends, early_step = lax.optimization_barrier((keeps, sends, early_step))
        if at == 4:
            keeps, sends, rows_then = lax.optimization_barrier((keeps, sends, returned))
        came = travel(sends, stage)
        if at >= last - 1:
            quarter = swap(jnp.split(for_other, 4, axis=0)[len(from_other)], top_axis)
            came, quarter = lax.optimization_barrier((came, quarter))
            from_other.append(quarter)
        if 2 <= at < 2 + spread:
            rows = early_sends[0].shape[0] // spread
            some = [p[(at - 2) * rows : (at - 1) * rows] for p in early_sends]
            some, came = lax.optimization_barrier((travel(some, stages[done]), came))
            early_came.append(some)
        if at == 2:
            table_own = mm(owned[0].astype(BF16), returned)
            came, table_own = lax.optimization_barrier((came, table_own))
        if at == 4:
            for_other = mm(owned[1].astype(BF16), rows_then).astype(BF16)
            came, for_other = lax.optimization_barrier((came, for_other))
        if at == last - 2:
            early_came = [jnp.concatenate(parts, axis=0) for parts in zip(*early_came)]
            early = end(early_keeps, early_came, stages[done])
            early = jnp.concatenate(run_stages(early, stages[done + 1 :]), axis=0)
            came, early = lax.optimization_barrier((came, early))
            early_step = (early, swap(early, core))
        if at == last:
            early_parts.append(unpack(my_core, *early_step, 0, wide, False))
            early_parts.append(unpack(my_core, *early_step, 2 * wide, width, False))
            came, early_parts = lax.optimization_barrier((came, early_parts))
        late = end(keeps, came, stage)
    late = jnp.concatenate(late, axis=0)
    late, for_other = lax.optimization_barrier((late, for_other))
    late_other = swap(late, core)
    quarters = jnp.split(for_other, 4, axis=0)
    from_other.append(swap(quarters[2], top_axis))
    early_parts.append(unpack(my_core, *early_step, wide, wide, True))
    late_other, early_parts, from_other, quarter = lax.optimization_barrier(
        (late_other, early_parts, from_other, quarters[3])
    )
    from_other.append(swap(quarter, top_axis))
    rows = block_rows // 4
    gene_grad, know_grad = (
        jnp.concatenate(
            [
                table_own[part * rows : (part + 1) * rows] + from_other[part].astype(F32)
                for part in parts
            ],
            axis=0,
        )
        for parts in ((0, 1), (2, 3))
    )
    w_down_grad, w_out_grad, w_up_grad = early_parts
    w_query_grad, w_key_grad, w_value_grad, expr_grad, short = unpack_whole(
        my_core, late, late_other, heights
    )
    gain_two_grad, shift_two_grad, b_down_grad, gain_one_grad, shift_one_grad, b_out_grad = (
        short[i] for i in range(6)
    )
    b_up_grad = short[6 : 6 + wide // width].reshape(wide)
    b_query_grad, b_value_grad = short[6 + wide // width], short[7 + wide // width]
    return (
        layer_output.reshape(1, tokens, width),
        gene_grad,
        know_grad,
        expr_grad,
        w_query_grad,
        b_query_grad,
        w_key_grad,
        w_value_grad,
        b_value_grad,
        w_out_grad,
        b_out_grad,
        gain_one_grad,
        shift_one_grad,
        w_up_grad,
        b_up_grad,
        w_down_grad,
        b_down_grad,
        gain_two_grad,
        shift_two_grad,
        row_counts.reshape(2, rows_dev),
    )


def solution(mesh):
    bits = mesh.shape["dp"].bit_length() - 1
    dp_axes = tuple(f"dp{i}" for i in range(bits))
    fine = Mesh(mesh.devices.reshape((2,) * bits + (mesh.shape["seq"],)), (*dp_axes, "seq"))
    every = (*dp_axes, "seq")
    whole = P()
    placed = (
        (P(dp_axes, "seq"),) * 4
        + (P(dp_axes),) * 2
        + (P(every, None), P(None, every, None))
        + (whole,) * 16
        + (P(dp_axes, "seq", None),)
    )
    given = (
        (P(dp_axes, "seq", None),)
        + (P(every, None),) * 2
        + (whole,) * 16
        + (P(None, every),)
    )
    return jax.shard_map(
        functools.partial(local, dp_axes), mesh=fine, in_specs=placed, out_specs=given, check_vma=False
    )
```

```python
import functools

import jax
import jax.numpy as jnp
from jax import lax
from jax.experimental import pallas as pl
from jax.experimental.pallas import tpu as pltpu
from jax.sharding import Mesh, PartitionSpec as P

HEADS = 12
HEAD_DIM = 64
PAIR = 2 * HEAD_DIM
KEY_CHUNK = 512
LOG2E = 1.4426950408889634
SWAP = [(0, 1), (1, 0)]
F32 = jnp.float32
BF16 = jnp.bfloat16
NN = (((1,), (0,)), ((), ()))
NT = (((1,), (1,)), ((), ()))
TN = (((0,), (0,)), ((), ()))


def mm(left, right, dims=NN):
    return lax.dot_general(left, right, dims, preferred_element_type=F32)


def params(mib):
    return pltpu.CompilerParams(vmem_limit_bytes=mib * 2**20)


def cost(flops, moved):
    return pl.CostEstimate(flops=flops, bytes_accessed=moved, transcendentals=0)


def hot(left, right):
    return (left == right).astype(BF16)


def route_kernel(
    rows_dev, capacity, top_ref, gene_ref, know_ref, req_ref, gene_slot_ref, know_slot_ref
):
    tokens = gene_ref.shape[0]
    devices, slots_all = req_ref.shape
    lane = lax.broadcasted_iota(jnp.int32, (tokens, devices), 1)
    top = top_ref[0]
    half = jnp.where((lane & 1) == 0, top, 1 - top)
    first = (half * (devices // 2) + (lane >> 1)) * rows_dev
    earlier = (
        lax.broadcasted_iota(jnp.int32, (tokens, tokens), 0)
        > lax.broadcasted_iota(jnp.int32, (tokens, tokens), 1)
    ).astype(F32).astype(BF16)
    rank_lane = lax.broadcasted_iota(jnp.int32, (tokens, capacity), 1)
    asked = []
    for which, (ids_ref, slot_ref) in enumerate(((gene_ref, gene_slot_ref), (know_ref, know_slot_ref))):
        row = ids_ref[...] - first
        hit = (row >= 0) & (row < rows_dev)
        before = mm(earlier, hit.astype(F32).astype(BF16))
        rank = jnp.sum(jnp.where(hit, before, 0.0), axis=1, keepdims=True)
        owner = jnp.sum(jnp.where(hit, lane, 0).astype(F32), axis=1, keepdims=True)
        slot_ref[...] = (owner * slots_all + rank).astype(jnp.int32) + which * capacity
        rank_hit = (rank_lane == rank.astype(jnp.int32)).astype(F32).astype(BF16)
        coded = jnp.where(hit, row + 1, 0)
        high = (coded >> 4).astype(F32).astype(BF16)
        low = (coded & 15).astype(F32).astype(BF16)
        wanted = (mm(high, rank_hit, TN) * 16.0 + mm(low, rank_hit, TN)).astype(jnp.int32)
        asked.append(jnp.where(wanted > 0, wanted - 1 + which * rows_dev, -1))
    req_ref[:, :capacity] = asked[0]
    req_ref[:, capacity:] = asked[1]


def route(top, gene_ids, know_ids, rows_dev, capacity, devices):
    tokens = gene_ids.shape[0]
    return pl.pallas_call(
        functools.partial(route_kernel, rows_dev, capacity),
        in_specs=[pl.BlockSpec(memory_space=pltpu.SMEM)] + [pl.BlockSpec(memory_space=pltpu.VMEM)] * 2,
        out_shape=(
            jax.ShapeDtypeStruct((devices, 2 * capacity), jnp.int32),
            jax.ShapeDtypeStruct((tokens, 1), jnp.int32),
            jax.ShapeDtypeStruct((tokens, 1), jnp.int32),
        ),
        compiler_params=params(32),
        name="route",
    )(top.reshape(1), gene_ids[:, None], know_ids[:, None])


def fill_keys(aug_ref, key, first_key, count):
    lanes = lax.broadcasted_iota(jnp.int32, key.shape, 1)
    at = lax.broadcasted_iota(jnp.int32, key.shape, 0) + first_key
    bias = jnp.where(at < count, 0.0, -1e30).astype(BF16)
    none = jnp.zeros_like(key)
    aug_ref[:, :PAIR] = jnp.where(lanes < HEAD_DIM, key, jnp.where(lanes == HEAD_DIM, bias, none))
    aug_ref[:, PAIR : 2 * PAIR] = key
    aug_ref[:, 2 * PAIR :] = jnp.where(lanes >= HEAD_DIM, key, jnp.where(lanes == 0, bias, none))


def head_mask(shape, head):
    lanes = lax.broadcasted_iota(jnp.int32, shape, 1)
    return (lanes >= head * HEAD_DIM) & (lanes < (head + 1) * HEAD_DIM)


def spread_query(query, head):
    lanes = lax.broadcasted_iota(jnp.int32, query.shape, 1)
    scaled = query.astype(F32) * (HEAD_DIM ** (-0.5) * LOG2E)
    scaled = jnp.where(head_mask(query.shape, head), scaled, 0.0)
    high = scaled.astype(BF16)
    low = scaled - high.astype(F32)
    low = jnp.where(lanes == (1 - head) * HEAD_DIM, 1.0, low).astype(BF16)
    return jnp.concatenate([low, high] if head == 0 else [high, low], axis=1)


def fold_rows(value, how):
    return how(value.reshape(value.shape[0] // 8, 8, value.shape[1]), axis=0)


def attend_kernel(merge, where_ref, q_ref, k_ref, v_ref, *rest):
    if merge:
        out_in_ref, lse_in_ref, out_ref, lse_ref, aug_ref, vt_ref, score_ref = rest
    else:
        out_ref, lse_ref, aug_ref, vt_ref, score_ref = rest
    spans = [slice(c, c + KEY_CHUNK) for c in range(0, k_ref.shape[0], KEY_CHUNK)]
    fill_keys(aug_ref, k_ref[...], where_ref[0], where_ref[1])
    vt_ref[...] = v_ref[...].T
    outs = []
    for head in range(2):
        own = slice(head * HEAD_DIM, (head + 1) * HEAD_DIM)
        query = spread_query(q_ref[...], head)
        top = None
        for span in spans:
            scores = mm(aug_ref[span, head * PAIR : (head + 2) * PAIR], query, NT)
            score_ref[head, span, :] = scores
            high = fold_rows(scores, jnp.max)
            top = high if top is None else jnp.maximum(top, high)
        top = jnp.max(top, axis=0, keepdims=True)
        total = None
        acc = None
        for span in spans:
            probs = jnp.exp2(score_ref[head, span, :] - top)
            part = fold_rows(probs, jnp.sum)
            total = part if total is None else total + part
            part = mm(vt_ref[own, span], probs.astype(BF16))
            acc = part if acc is None else acc + part
        total = jnp.sum(total, axis=0, keepdims=True)
        lse = top + jnp.log2(total)
        if merge:
            before = lse_in_ref[0, head : head + 1, :]
            both = jnp.maximum(lse, before)
            both = both + jnp.log2(jnp.exp2(lse - both) + jnp.exp2(before - both))
            acc = acc * (jnp.exp2(lse - both) / total)
            acc = acc + out_in_ref[own, :] * jnp.exp2(before - both)
            lse = both
        else:
            acc = acc / total
        lse_ref[0, head : head + 1, :] = lse
        outs.append(acc)
    out = jnp.concatenate(outs, axis=0)
    out_ref[...] = out.T if merge else out


def attend(where, query, key, value, before=()):
    tokens, width = query.shape
    keys = key.shape[0]
    pairs = width // PAIR
    column = lambda rows: pl.BlockSpec((rows, PAIR), lambda p, w: (0, p))
    upright = pl.BlockSpec((PAIR, tokens), lambda p, w: (p, 0))
    stats = pl.BlockSpec((1, 2, tokens), lambda p, w: (p, 0, 0))
    merge = len(before) > 0
    return pl.pallas_call(
        functools.partial(attend_kernel, merge),
        grid_spec=pltpu.PrefetchScalarGridSpec(
            num_scalar_prefetch=1,
            grid=(pairs,),
            in_specs=[column(tokens), column(keys), column(keys)] + ([upright, stats] if merge else []),
            out_specs=[column(tokens) if merge else upright, stats],
            scratch_shapes=[
                pltpu.VMEM((keys, 3 * PAIR), BF16),
                pltpu.VMEM((PAIR, keys), BF16),
                pltpu.VMEM((2, keys, tokens), F32),
            ],
        ),
        out_shape=(
            jax.ShapeDtypeStruct((tokens, width) if merge else (width, tokens), F32),
            jax.ShapeDtypeStruct((pairs, 2, tokens), F32),
        ),
        compiler_params=params(48),
        cost_estimate=cost(16 * tokens * keys * width, 2 * tokens * width * 10),
        name="attend_more" if merge else "attend",
    )(where, query, key, value, *before)


def attend_back_kernel(
    add, untouched, where_ref, q_ref, g_ref, o_ref, lse_ref, k_ref, v_ref, *rest
):
    dq_in_ref = rest[0] if add else None
    dq_ref, dk_ref, dv_ref, aug_ref, kt_ref = rest[int(add) + untouched :]
    fill_keys(aug_ref, k_ref[...], where_ref[0], where_ref[1])
    kt_ref[...] = k_ref[...].T
    grad = g_ref[...]
    picks = (
        lax.broadcasted_iota(jnp.int32, (8, PAIR), 1) // HEAD_DIM
        == lax.broadcasted_iota(jnp.int32, (8, PAIR), 0)
    ).astype(F32)
    inner = lax.dot_general(
        picks,
        grad.astype(F32) * o_ref[...],
        NT,
        precision=lax.Precision.HIGHEST,
        preferred_element_type=F32,
    )
    scaled = q_ref[...] * jnp.asarray(HEAD_DIM ** (-0.5), BF16)
    none = jnp.zeros_like(grad)
    masks = [head_mask(grad.shape, head) for head in range(2)]
    queries = [spread_query(q_ref[...], head) for head in range(2)]
    q_heads = [jnp.where(m, scaled, none) for m in masks]
    g_heads = [jnp.where(m, grad, none) for m in masks]
    dqs = [None, None]
    for first in range(0, k_ref.shape[0], KEY_CHUNK):
        span = slice(first, first + KEY_CHUNK)
        dk = None
        dv = None
        for head in range(2):
            own = slice(head * HEAD_DIM, (head + 1) * HEAD_DIM)
            scores = mm(aug_ref[span, head * PAIR : (head + 2) * PAIR], queries[head], NT)
            probs = jnp.exp2(scores - lse_ref[0, head : head + 1, :])
            grad_probs = mm(v_ref[span, :], g_heads[head], NT)
            grad_scores = (probs * (grad_probs - inner[head : head + 1, :])).astype(BF16)
            part = mm(kt_ref[own, span], grad_scores)
            dqs[head] = part if dqs[head] is None else dqs[head] + part
            part = mm(probs.astype(BF16), g_heads[head])
            dv = part if dv is None else dv + part
            part = mm(grad_scores, q_heads[head])
            dk = part if dk is None else dk + part
        dk_ref[span, :] = dk.astype(BF16)
        dv_ref[span, :] = dv.astype(BF16)
    dq = jnp.concatenate(dqs, axis=0).T * HEAD_DIM ** (-0.5)
    if add:
        dq = dq + dq_in_ref[...]
    dq_ref[...] = dq.astype(dq_ref.dtype)


def attend_back(where, query, grad, out, lse, key, value, first, count, before, into):
    tokens, width = query.shape
    keys = key.shape[0]
    column = lambda rows: pl.BlockSpec((rows, PAIR), lambda p, w: (0, p + first))
    untouched = pl.BlockSpec(memory_space=pl.ANY)
    add = len(before) > 0
    given = 7 + len(before)
    return pl.pallas_call(
        functools.partial(attend_back_kernel, add, len(into)),
        grid_spec=pltpu.PrefetchScalarGridSpec(
            num_scalar_prefetch=1,
            grid=(count,),
            in_specs=[column(tokens)] * 3
            + [pl.BlockSpec((1, 2, tokens), lambda p, w: (p + first, 0, 0))]
            + [column(keys)] * 2
            + [column(tokens)] * len(before)
            + [untouched] * len(into),
            out_specs=[column(tokens), column(keys), column(keys)],
            scratch_shapes=[
                pltpu.VMEM((keys, 3 * PAIR), BF16),
                pltpu.VMEM((PAIR, keys), BF16),
            ],
        ),
        out_shape=(
            jax.ShapeDtypeStruct((tokens, width), BF16 if add else F32),
            jax.ShapeDtypeStruct((keys, width), BF16),
            jax.ShapeDtypeStruct((keys, width), BF16),
        ),
        input_output_aliases={given + i: i for i in range(len(into))},
        compiler_params=params(56),
        cost_estimate=cost(40 * tokens * keys * PAIR * count, 2 * tokens * PAIR * count * 12),
        name=("attend_back_more" if add else "attend_back") + str(first),
    )(where, query, grad, out, lse, key, value, *before, *into)


def norm_parts(value):
    centre = jnp.mean(value, axis=-1, keepdims=True)
    centred = value - centre
    variance = jnp.mean(centred * centred, axis=-1, keepdims=True)
    inverse = lax.rsqrt(variance + 1e-05)
    return centred * inverse, inverse


def norm_back(grad, unit, inverse, gain):
    grad_unit = grad * gain
    return inverse * (
        grad_unit
        - jnp.mean(grad_unit, axis=-1, keepdims=True)
        - unit * jnp.mean(grad_unit * unit, axis=-1, keepdims=True)
    )


def middle_kernel(
    ctx_ref,
    emb_ref,
    cot_ref,
    w_out_ref,
    w_up_ref,
    w_down_ref,
    small_ref,
    b_up_ref,
    out_ref,
    ctx_low_ref,
    normed_ref,
    act_ref,
    gffn_ref,
    gpre_ref,
    gattn_ref,
    gone_ref,
    gctx_ref,
    sums_ref,
    up_sums_ref,
    slope_ref,
):
    step = pl.program_id(0)
    width = emb_ref.shape[1]
    wide = w_up_ref.shape[1]

    @pl.when(step == 0)
    def _():
        sums_ref[...] = jnp.zeros_like(sums_ref)
        up_sums_ref[...] = jnp.zeros_like(up_sums_ref)

    b_out, gain_one, shift_one, b_down, gain_two, shift_two = (
        small_ref[i : i + 1, :] for i in range(6)
    )
    ctx_low = ctx_ref[...].astype(BF16)
    ctx_low_ref[...] = ctx_low
    unit_one, inv_one = norm_parts(emb_ref[...] + mm(ctx_low, w_out_ref[...]) + b_out)
    normed = unit_one * gain_one + shift_one
    normed_low = normed.astype(BF16)
    normed_ref[...] = normed_low
    ffn = None
    for c in range(wide // width):
        span = slice(c * width, (c + 1) * width)
        pre = mm(normed_low, w_up_ref[:, span]) + b_up_ref[:, span]
        below = 0.5 * (1.0 + lax.erf(pre * 0.7071067811865476))
        act = (pre * below).astype(BF16)
        act_ref[:, span] = act
        slope_ref[:, span] = below + pre * (0.3989422804014327 * jnp.exp(-0.5 * pre * pre))
        part = mm(act, w_down_ref[span, :])
        ffn = part if ffn is None else ffn + part
    unit_two, inv_two = norm_parts(normed + ffn + b_down)
    out_ref[...] = (unit_two * gain_two + shift_two).astype(BF16)
    grad = cot_ref[...].astype(F32)
    sums_ref[0:8, :] += fold_rows(grad * unit_two, jnp.sum)
    sums_ref[8:16, :] += fold_rows(grad, jnp.sum)
    grad_two = norm_back(grad, unit_two, inv_two, gain_two)
    gffn = grad_two.astype(BF16)
    gffn_ref[...] = gffn
    sums_ref[16:24, :] += fold_rows(gffn.astype(F32), jnp.sum)
    grad_normed = grad_two
    for c in range(wide // width):
        span = slice(c * width, (c + 1) * width)
        gpre = (mm(gffn, w_down_ref[span, :], NT) * slope_ref[:, span]).astype(BF16)
        gpre_ref[:, span] = gpre
        up_sums_ref[:, span] += fold_rows(gpre.astype(F32), jnp.sum)
        grad_normed = grad_normed + mm(gpre, w_up_ref[:, span], NT)
    sums_ref[24:32, :] += fold_rows(grad_normed * unit_one, jnp.sum)
    sums_ref[32:40, :] += fold_rows(grad_normed, jnp.sum)
    grad_one = norm_back(grad_normed, unit_one, inv_one, gain_one)
    gone_ref[...] = grad_one
    gattn = grad_one.astype(BF16)
    gattn_ref[...] = gattn
    sums_ref[40:48, :] += fold_rows(gattn.astype(F32), jnp.sum)
    gctx_ref[...] = mm(gattn, w_out_ref[...], NT).astype(BF16)


def middle(ctx, embedded, cotangent, w_out, w_up, w_down, small, b_up, block=512):
    tokens, width = embedded.shape
    wide = w_up.shape[1]
    whole = lambda a: pl.BlockSpec(a.shape, lambda i: (0, 0), pipeline_mode=pl.Buffered(1))
    rows = lambda n: pl.BlockSpec((block, n), lambda i: (i, 0))
    fixed = lambda r, n: pl.BlockSpec((r, n), lambda i: (0, 0))
    shape = lambda n, dtype: jax.ShapeDtypeStruct((tokens, n), dtype)
    return pl.pallas_call(
        middle_kernel,
        grid=(tokens // block,),
        in_specs=[rows(width)] * 3 + [whole(w_out), whole(w_up), whole(w_down), whole(small), whole(b_up)],
        out_specs=[
            rows(width),
            rows(width),
            rows(width),
            rows(wide),
            rows(width),
            rows(wide),
            rows(width),
            rows(width),
            rows(width),
            fixed(48, width),
            fixed(8, wide),
        ],
        out_shape=[
            shape(width, BF16),
            shape(width, BF16),
            shape(width, BF16),
            shape(wide, BF16),
            shape(width, BF16),
            shape(wide, BF16),
            shape(width, BF16),
            shape(width, F32),
            shape(width, BF16),
            jax.ShapeDtypeStruct((48, width), F32),
            jax.ShapeDtypeStruct((8, wide), F32),
        ],
        scratch_shapes=[pltpu.VMEM((block, wide), F32)],
        compiler_params=params(60),
        cost_estimate=cost(tokens * width * (8 * wide + 4 * width) * 2, 2 * tokens * (2 * wide + 14 * width)),
        name="middle",
    )(ctx, embedded, cotangent, w_out, w_up, w_down, small, b_up)


def weight_sums_kernel(counts, half_ref, act_ref, gffn_ref, gpre_ref, norm_ref, ctx_ref, gattn_ref, out_ref):
    at = pl.program_id(0) + half_ref[0] * pl.num_programs(0)
    first = 0
    for count, left, right in zip(counts, (act_ref, gpre_ref, ctx_ref), (gffn_ref, norm_ref, gattn_ref)):
        @pl.when((at >= first) & (at < first + count))
        def _(left=left, right=right):
            out_ref[...] = mm(left[...], right[...], TN).astype(BF16)
        first += count


def weight_sums(half, activated, grad_ffn, grad_pre, normed, ctx, grad_attn, block=384):
    tokens, width = grad_ffn.shape
    lefts = (activated, grad_pre, ctx)
    counts = [left.shape[1] // block for left in lefts]
    steps = sum(counts) // 2
    specs = []
    first = 0
    for left, right, count in zip(lefts, (grad_ffn, normed, grad_attn), counts):
        specs.append(
            pl.BlockSpec(
                (tokens, block),
                lambda i, h, first=first, count=count: (0, jnp.clip(i + h[0] * steps - first, 0, count - 1)),
            )
        )
        specs.append(pl.BlockSpec((tokens, width), lambda i, h: (0, 0), pipeline_mode=pl.Buffered(1)))
        first += count
    return pl.pallas_call(
        functools.partial(weight_sums_kernel, counts),
        grid_spec=pltpu.PrefetchScalarGridSpec(
            num_scalar_prefetch=1,
            grid=(steps,),
            in_specs=specs,
            out_specs=pl.BlockSpec((block, width), lambda i, h: (i, 0)),
        ),
        out_shape=jax.ShapeDtypeStruct((steps * block, width), BF16),
        compiler_params=params(60),
        cost_estimate=cost(2 * tokens * width * block * steps, 2 * steps * block * (tokens + width)),
        name="weight_sums",
    )(half.reshape(1), activated, grad_ffn, grad_pre, normed, ctx, grad_attn)


def unpack_kernel(first, half, turn, core_ref, own_ref, other_ref, out_ref):
    at = pl.program_id(0) + first
    mine = (at >= half) == (core_ref[0] == 1)
    rows = jnp.where(mine, own_ref[...], other_ref[...]).astype(F32)
    out_ref[...] = rows.T if turn else rows


def unpack(core, own, other, first, rows, turn, block=384):
    half, width = own.shape[0] // block, own.shape[1]
    first, steps = first // block, rows // block

    def place(i, c, owner):
        at = i + first
        inside = (at >= half) == (c[0] == owner)
        return jnp.where(inside, at % half, half - 1), 0

    return pl.pallas_call(
        functools.partial(unpack_kernel, first, half, turn),
        grid_spec=pltpu.PrefetchScalarGridSpec(
            num_scalar_prefetch=1,
            grid=(steps,),
            in_specs=[
                pl.BlockSpec((block, width), functools.partial(place, owner=1)),
                pl.BlockSpec((block, width), functools.partial(place, owner=0)),
            ],
            out_specs=pl.BlockSpec((width, block), lambda i, c: (0, i))
            if turn
            else pl.BlockSpec((block, width), lambda i, c: (i, 0)),
        ),
        out_shape=jax.ShapeDtypeStruct((width, rows) if turn else (rows, width), F32),
        compiler_params=params(60),
        cost_estimate=cost(rows * width, rows * width * 6),
        name="unpack" + str(first),
    )(core.reshape(1), own, other)


def unpack_whole_kernel(heights, core_ref, own_ref, other_ref, *out_refs):
    half = own_ref.shape[0]
    lower = core_ref[0] == 0
    first = 0
    for height, out_ref in zip(heights, out_refs):
        for part in range(2):
            start, stop = max(first, part * half), min(first + height, (part + 1) * half)
            if start < stop:
                span = slice(start - part * half, stop - part * half)
                near, far = (own_ref, other_ref) if part == 0 else (other_ref, own_ref)
                rows = jnp.where(lower, near[span, :], far[span, :])
                out_ref[start - first : stop - first, :] = rows.astype(F32)
        first += height


def unpack_whole(core, own, other, heights):
    width = own.shape[1]
    vmem = pl.BlockSpec(memory_space=pltpu.VMEM)
    return pl.pallas_call(
        functools.partial(unpack_whole_kernel, heights),
        in_specs=[pl.BlockSpec(memory_space=pltpu.SMEM), vmem, vmem],
        out_specs=[vmem] * len(heights),
        out_shape=[jax.ShapeDtypeStruct((height, width), F32) for height in heights],
        compiler_params=params(60),
        name="unpack_whole",
    )(core.reshape(1), own, other)


def cut(value, axis):
    rows = value.shape[0] // 2
    me = lax.axis_index(axis)
    keep = lax.dynamic_slice_in_dim(value, me * rows, rows, 0)
    return keep, lax.dynamic_slice_in_dim(value, (1 - me) * rows, rows, 0)


def swap(value, axis):
    return lax.ppermute(value, axis, SWAP)


def join(value, other, axis):
    first = lax.axis_index(axis) == 0
    return jnp.concatenate([jnp.where(first, value, other), jnp.where(first, other, value)], axis=0)


def stages_of(dp_axes):
    near, far = dp_axes[-2], dp_axes[-3::-1]
    down = [((near, "seq"), True), (("seq", near), True)] + [((axis,), True) for axis in far]
    return down + [(axes, False) for axes, _ in down[::-1]]


def begin(pieces, stage):
    axes, halves = stage
    if len(pieces) < len(axes):
        pieces = jnp.split(pieces[0], 2, axis=0)
    if len(pieces) > len(axes):
        pieces = [jnp.concatenate(pieces, axis=0)]
    if halves:
        keeps, sends = zip(*(cut(p, axis) for p, axis in zip(pieces, axes)))
        return list(keeps), list(sends)
    return list(pieces), list(pieces)


def travel(sends, stage):
    return [swap(s, axis) for s, axis in zip(sends, stage[0])]


def end(keeps, arrived, stage):
    axes, halves = stage
    if halves:
        return [k + a for k, a in zip(keeps, arrived)]
    return [join(k, a, axis) for k, a, axis in zip(keeps, arrived, axes)]


def run_stages(pieces, stages):
    for stage in stages:
        keeps, sends = begin(pieces, stage)
        pieces = end(keeps, travel(sends, stage), stage)
    return pieces


def local(
    dp_axes,
    gene_ids,
    homolog_ids,
    knowledge_ids,
    expr_bins,
    species,
    cell_lengths,
    gene_table,
    knowledge_tables,
    expr_table,
    w_query,
    b_query,
    w_key,
    w_value,
    b_value,
    w_out,
    b_out,
    gain_one,
    shift_one,
    w_up,
    b_up,
    w_down,
    b_down,
    gain_two,
    shift_two,
    cotangent,
):
    tokens = gene_ids.shape[1]
    rows_dev, width = gene_table.shape
    wide = w_up.shape[1]
    every = (*dp_axes, "seq")
    top_axis, group_axes = dp_axes[0], (*dp_axes[1:], "seq")
    devices = lax.axis_size(every)
    group = devices // 2
    capacity = 2 * tokens // devices
    slots_all = 2 * capacity
    slots = devices * slots_all
    bins = expr_table.shape[0]
    me = lax.axis_index("seq")

    def exchange(value):
        return lax.all_to_all(value, group_axes, split_axis=0, concat_axis=0, tiled=True)

    gene_table, knowledge_tables = lax.optimization_barrier((gene_table, knowledge_tables))
    gene_other = lax.ppermute(gene_table, top_axis, SWAP)
    know_sum = jnp.sum(knowledge_tables.astype(F32), axis=0).astype(BF16)
    chosen = jnp.where(species[0] == 1, homolog_ids, gene_ids).reshape(-1)
    requests, gene_slot, know_slot = route(
        lax.axis_index(top_axis), chosen, knowledge_ids.reshape(-1), rows_dev, capacity, devices
    )
    asked = exchange(requests.reshape(group, 2 * slots_all))
    asked, gene_other, know_sum = lax.optimization_barrier((asked, gene_other, know_sum))
    know_other = lax.ppermute(know_sum, top_axis, SWAP)
    asked = asked.reshape(group, 2, slots_all)
    shift = jnp.arange(2)[None, :, None] * (2 * rows_dev)
    asked = jnp.where(asked >= 0, asked + shift, -1).reshape(group, 2 * slots_all)
    row_at = jnp.arange(4 * rows_dev)
    slot_at = jnp.arange(slots).reshape(group, 2 * slots_all)
    bin_hot = hot(expr_bins.reshape(-1)[:, None], jnp.arange(bins)[None, :])
    embedded = mm(bin_hot, expr_table)
    fetched = gene_other
    tables = jnp.concatenate([gene_table, know_sum, gene_other], axis=0)
    late_rows = slice(slots_all + capacity, 2 * slots_all)
    early_rows = slice(0, slots_all + capacity)
    for columns, rows, table in (
        (early_rows, row_at[: 3 * rows_dev], tables),
        (late_rows, row_at[3 * rows_dev :], know_other),
    ):
        wanted = asked[:, columns].reshape(-1)
        found = mm(hot(wanted[:, None], rows[None, :]), table).astype(BF16)
        found, _ = lax.optimization_barrier((found, fetched))
        fetched = exchange(found.reshape(group, -1, width)).reshape(-1, width)
        at = slot_at[:, columns].reshape(1, -1)
        embedded = embedded + mm(((at == gene_slot) | (at == know_slot)).astype(BF16), fetched)
    asked = asked.reshape(slots)
    slot_at = slot_at.reshape(1, slots)
    slot_hot = ((slot_at == gene_slot) | (slot_at == know_slot)).astype(BF16)
    x_low = embedded.astype(BF16)

    x_other = lax.ppermute(x_low, "seq", SWAP)
    query = (mm(x_low, w_query) + b_query).astype(BF16)
    key, key_other = (mm(x, w_key).astype(BF16) for x in (x_low, x_other))
    value, value_other = ((mm(x, w_value) + b_value).astype(BF16) for x in (x_low, x_other))
    mine = jnp.stack([me * tokens, cell_lengths[0]]).astype(jnp.int32)
    others = jnp.stack([(1 - me) * tokens, cell_lengths[0]]).astype(jnp.int32)
    block_rows = 2 * rows_dev
    owned = [row_at[at : at + block_rows, None] == asked[None, :] for at in (0, block_rows)]
    counts = [jnp.sum(o.astype(jnp.int32), axis=1) for o in owned]
    counts_back = lax.ppermute(counts[1], top_axis, SWAP)
    first_part = attend(mine, query, key, value)
    first_part, counts_back = lax.optimization_barrier((first_part, counts_back))
    row_counts = counts[0] + counts_back
    context, lse = attend(others, query, key_other, value_other, first_part)

    small = jnp.stack([b_out, gain_one, shift_one, b_down, gain_two, shift_two])
    (
        layer_output,
        ctx_low,
        normed_low,
        activated,
        grad_ffn,
        grad_pre,
        grad_attn,
        grad_one,
        grad_ctx,
        sums,
        up_sums,
    ) = middle(
        context, embedded, cotangent.reshape(tokens, width), w_out, w_up, w_down, small, b_up[None, :]
    )

    core = dp_axes[-1]
    stages = stages_of(dp_axes)
    my_core = lax.axis_index(core)
    lefts_rights = (activated, grad_ffn, grad_pre, normed_low, ctx_low, grad_attn)
    sent = weight_sums(1 - my_core, *lefts_rights)
    sent, lefts_rights = lax.optimization_barrier((sent, lefts_rights))
    arrived = swap(sent, core)
    kept = weight_sums(my_core, *lefts_rights)
    kept, arrived, grad_ctx = lax.optimization_barrier((kept, arrived, grad_ctx))
    early = jnp.split(kept + arrived, 2, axis=0)
    pairs = width // PAIR
    third = pairs // 3
    sides = ((others, key_other, value_other), (mine, key, value))
    parts = (((0, 2 * third), (2 * third, third)), ((0, third), (third, third), (2 * third, third)))
    done = 0
    grads = []
    before = ()
    for side, (place, keys, values) in enumerate(sides):
        into = ()
        for first, count in parts[side]:
            keeps, sends = begin(early, stages[done])
            keeps, sends, grad_ctx, into, before = lax.optimization_barrier(
                (keeps, sends, grad_ctx, into, before)
            )
            came = travel(sends, stages[done])
            into = attend_back(
                place, query, grad_ctx, context, lse, keys, values, first, count, before, into
            )
            came, into = lax.optimization_barrier((came, into))
            early = end(keeps, came, stages[done])
            done += 1
        grads.append(into)
        if side == 0:
            before = into[:1]
            dx_other = (mm(into[1], w_key, NT) + mm(into[2], w_value, NT)).astype(BF16)
            dx_other, before = lax.optimization_barrier((dx_other, before))
            dx_from_other = swap(dx_other, "seq")
    (_, dk_other, dv_other), (dq, dk, dv) = grads
    keeps, sends = begin(early, stages[done])
    keeps, sends, dq, dk, dv, dx_from_other = lax.optimization_barrier(
        (keeps, sends, dq, dk, dv, dx_from_other)
    )
    came = travel(sends, stages[done])
    grad_embedded = (
        grad_one
        + mm(dq, w_query, NT)
        + mm(dk, w_key, NT)
        + mm(dv, w_value, NT)
        + dx_from_other.astype(F32)
    )
    grad_low = grad_embedded.astype(BF16)
    grad_low, came = lax.optimization_barrier((grad_low, came))
    keeps, sends = begin(end(keeps, came, stages[done]), stages[done + 1])
    done += 1
    keeps, sends, grad_low = lax.optimization_barrier((keeps, sends, grad_low))
    came = travel(sends, stages[done])

    outgoing = mm(slot_hot, grad_low, TN).astype(BF16)
    outgoing, dq, dk, dv, came = lax.optimization_barrier((outgoing, dq, dk, dv, came))
    early = end(keeps, came, stages[done])
    done += 1
    returned = exchange(outgoing.reshape(group, 2 * slots_all, width)).reshape(slots, width)
    w_query_grad = mm(x_low, dq, TN)
    w_key_grad = mm(x_low, dk, TN) + mm(x_other, dk_other, TN)
    w_value_grad = mm(x_low, dv, TN) + mm(x_other, dv_other, TN)
    b_query_grad = jnp.sum(dq.astype(F32), axis=0)
    b_value_grad = jnp.sum(dv.astype(F32), axis=0) + jnp.sum(dv_other.astype(F32), axis=0)
    grad_rest = (grad_embedded - grad_low.astype(F32)).astype(BF16)
    expr_grad = mm(bin_hot, grad_low, TN) + mm(bin_hot, grad_rest, TN)
    short = jnp.concatenate(
        [
            jnp.sum(sums.reshape(6, 8, width), axis=1),
            jnp.sum(up_sums, axis=0).reshape(wide // width, width),
            b_query_grad[None, :],
            b_value_grad[None, :],
        ],
        axis=0,
    )
    block = 128
    short = jnp.pad(short, ((0, -short.shape[0] % block), (0, 0)))
    late = [w_query_grad, w_key_grad, w_value_grad, expr_grad, short]
    heights = [item.shape[0] for item in late]
    late = jnp.concatenate([item.astype(BF16) for item in late], axis=0)
    keep, send = cut(late, core)
    late = jnp.split(keep + swap(send, core), 2, axis=0)
    keeps, sends = begin(late, stages[0])
    came = travel(sends, stages[0])
    returned, keeps, came, early = lax.optimization_barrier((returned, keeps, came, early))
    late = end(keeps, came, stages[0])
    last = len(stages) - 1
    spread = 3
    early_keeps, early_sends = begin(early, stages[done])
    early_came = []
    early_parts = []
    from_other = []
    for at, stage in enumerate(stages[1:], start=1):
        keeps, sends = begin(late, stage)
        if at >= last - 1:
            keeps, sends, for_other = lax.optimization_barrier((keeps, sends, for_other))
        early_then = early_sends
        if 2 < at < 2 + spread:
            keeps, sends, early_then = lax.optimization_barrier((keeps, sends, early_sends))
        if at == last:
            keeps, sends, early_step = lax.optimization_barrier((keeps, sends, early_step))
        if at == 4:
            keeps, sends, rows_then = lax.optimization_barrier((keeps, sends, returned))
        came = travel(sends, stage)
        if at >= last - 1:
            third = swap(jnp.split(for_other, 3, axis=0)[len(from_other)], top_axis)
            came, third = lax.optimization_barrier((came, third))
            from_other.append(third)
        if 2 <= at < 2 + spread:
            rows = early_sends[0].shape[0] // spread
            some = [p[(at - 2) * rows : (at - 1) * rows] for p in early_then]
            some, came = lax.optimization_barrier((travel(some, stages[done]), came))
            early_came.append(some)
        if at == 2:
            table_own = mm(owned[0].astype(BF16), returned)
            came, table_own = lax.optimization_barrier((came, table_own))
        if at == 4:
            for_other = mm(owned[1].astype(BF16), rows_then).astype(BF16)
            came, for_other = lax.optimization_barrier((came, for_other))
        if at == last - 2:
            early_came = [jnp.concatenate(parts, axis=0) for parts in zip(*early_came)]
            early = end(early_keeps, early_came, stages[done])
            early = jnp.concatenate(run_stages(early, stages[done + 1 :]), axis=0)
            came, early = lax.optimization_barrier((came, early))
            early_step = (early, swap(early, core))
        if at == last:
            early_parts.append(unpack(my_core, *early_step, 0, wide, False))
            early_parts.append(unpack(my_core, *early_step, 2 * wide, width, False))
            came, early_parts = lax.optimization_barrier((came, early_parts))
        late = end(keeps, came, stage)
    late = jnp.concatenate(late, axis=0)
    late, for_other = lax.optimization_barrier((late, for_other))
    late_other = swap(late, core)
    from_other.append(swap(jnp.split(for_other, 3, axis=0)[2], top_axis))
    early_parts.append(unpack(my_core, *early_step, wide, wide, True))
    late_other, early_parts, from_other = lax.optimization_barrier(
        (late_other, early_parts, from_other)
    )
    table_grads = table_own + jnp.concatenate(from_other, axis=0).astype(F32)
    w_down_grad, w_out_grad, w_up_grad = early_parts
    w_query_grad, w_key_grad, w_value_grad, expr_grad, short = unpack_whole(
        my_core, late, late_other, heights
    )
    gain_two_grad, shift_two_grad, b_down_grad, gain_one_grad, shift_one_grad, b_out_grad = (
        short[i] for i in range(6)
    )
    b_up_grad = short[6 : 6 + wide // width].reshape(wide)
    b_query_grad, b_value_grad = short[6 + wide // width], short[7 + wide // width]
    return (
        layer_output.reshape(1, tokens, width),
        table_grads[:rows_dev],
        table_grads[rows_dev:],
        expr_grad,
        w_query_grad,
        b_query_grad,
        w_key_grad,
        w_value_grad,
        b_value_grad,
        w_out_grad,
        b_out_grad,
        gain_one_grad,
        shift_one_grad,
        w_up_grad,
        b_up_grad,
        w_down_grad,
        b_down_grad,
        gain_two_grad,
        shift_two_grad,
        row_counts.reshape(2, rows_dev),
    )


def solution(mesh):
    bits = mesh.shape["dp"].bit_length() - 1
    dp_axes = tuple(f"dp{i}" for i in range(bits))
    fine = Mesh(mesh.devices.reshape((2,) * bits + (mesh.shape["seq"],)), (*dp_axes, "seq"))
    every = (*dp_axes, "seq")
    whole = P()
    placed = (
        (P(dp_axes, "seq"),) * 4
        + (P(dp_axes),) * 2
        + (P(every, None), P(None, every, None))
        + (whole,) * 16
        + (P(dp_axes, "seq", None),)
    )
    given = (
        (P(dp_axes, "seq", None),)
        + (P(every, None),) * 2
        + (whole,) * 16
        + (P(None, every),)
    )
    return jax.shard_map(
        functools.partial(local, dp_axes), mesh=fine, in_specs=placed, out_specs=given, check_vma=False
    )
```
